32 devices in a mesh: dp: 8 (over z, y), tensor: 4 (over x, core).
Axes of the slice: x: 2, y: 2, z: 4, core: 2. Of those that a mesh axis runs over, the one named last changes fastest.
Arguments:
- tokens: bfloat16 [4096, 2048], P(('dp', 'tensor')), may hold values from -6 to 6
- lengths: int32 [8, 4], P('dp'), may hold values from 0 to 512, as said below
- w_query: bfloat16 [2048, 2048], P(None, 'tensor'), may hold values from -0.125 to 0.125
- w_key: bfloat16 [2048, 2048], P(None, 'tensor'), may hold values from -0.125 to 0.125
- w_value: bfloat16 [2048, 2048], P(None, 'tensor'), may hold values from -0.125 to 0.125
- w_out: bfloat16 [2048, 2048], P('tensor'), may hold values from -0.125 to 0.125
- w_gate: bfloat16 [2048, 8192], P(None, 'tensor'), may hold values from -0.125 to 0.125
- w_up: bfloat16 [2048, 8192], P(None, 'tensor'), may hold values from -0.125 to 0.125
- w_down: bfloat16 [8192, 2048], P('tensor'), may hold values from -0.0625 to 0.0625
- gain_query: float32 [2048], P('tensor'), may hold values from 0.1 to 1.9
- gain_key: float32 [2048], P('tensor'), may hold values from 0.1 to 1.9
- gain_attn: float32 [2048], replicated, may hold values from 0.1 to 1.9
- gain_mlp: float32 [2048], replicated, may hold values from 0.1 to 1.9
- cotangent: bfloat16 [4096, 2048], P(('dp', 'tensor')), may hold values from -6 to 6
Outputs:
- output: bfloat16 [4096, 2048], P(('dp', 'tensor'))
- grad_tokens: bfloat16 [4096, 2048], P(('dp', 'tensor'))
- grad_w_query: float32 [2048, 2048], P('dp', 'tensor')
- grad_w_key: float32 [2048, 2048], P('dp', 'tensor')
- grad_w_value: float32 [2048, 2048], P('dp', 'tensor')
- grad_w_out: float32 [2048, 2048], P('tensor', 'dp')
- grad_w_gate: float32 [2048, 8192], P('dp', 'tensor')
- grad_w_up: float32 [2048, 8192], P('dp', 'tensor')
- grad_w_down: float32 [8192, 2048], P('tensor', 'dp')
- grad_gain_query: float32 [2048], P('tensor')
- grad_gain_key: float32 [2048], P('tensor')
- grad_gain_attn: float32 [2048], replicated
- grad_gain_mlp: float32 [2048], replicated
The draws below stay inside these ranges and needn't reach their ends.
Inputs may be any that keep to these rules, and one draw needn't show every extreme that they name: Each row lists the lengths of its sequences in order, then zeros; every nonzero length is 128 or more and they sum to 512; row 0 holds one sequence of 512 tokens.
All inputs are finite; a program needn't handle non-finite values.
Results may differ from the reference program's by a relative error of at most 0.023.
Values may be sent and summed in bfloat16 or wider, within the bound.
A program may use at most 256 MiB of HBM per device.

```python
import math
import jax
import jax.numpy as jnp
from jax import lax

D = 2048
H = 16
HD = 128
FF = 8192
ROW_LEN = 512
MIN_SEG = 128
SEGS = 4
ROWS = 8
TOKENS = 4096


def draw_lengths(key, part):
    counts_key, cuts_key = jax.random.split(key)
    pieces = jax.random.randint(counts_key, (ROWS, 1), 1, SEGS + 1).astype(jnp.int32)
    pieces = jnp.where(jnp.arange(ROWS, dtype=jnp.int32)[:, None] == 0, 1, pieces).astype(jnp.int32)
    spare = (ROW_LEN - pieces * MIN_SEG).astype(jnp.int32)
    cuts = jax.random.randint(cuts_key, (ROWS, SEGS - 1), 0, spare + 1).astype(jnp.int32)
    slots = jnp.arange(SEGS - 1, dtype=jnp.int32)[None, :]
    cuts = jnp.where(slots < pieces - 1, cuts, spare).astype(jnp.int32)
    cuts = jnp.sort(cuts, axis=1)
    edges = jnp.concatenate([jnp.zeros((ROWS, 1), jnp.int32), cuts, spare], axis=1)
    parts_len = edges[:, 1:] - edges[:, :-1]
    used = (jnp.arange(SEGS, dtype=jnp.int32)[None, :] < pieces).astype(jnp.int32)
    return (parts_len + MIN_SEG * used).astype(jnp.int32)


def strengthened(values, own_key, source, target, parts, factor):
    owner, partner = [(jnp.arange(values.shape[dim]) // (values.shape[dim] // parts)).reshape([-1 if axis == dim else 1 for axis in range(values.ndim)]) for dim in (source, target)]
    chosen = jax.random.permutation(own_key, parts)[partner]
    strong = (owner == chosen) | (owner == (partner + parts // 2) % parts)
    return jnp.where(strong, factor * values, values)


def levels(key, dims, cuts, smallest, high):
    def one(dim, blocks):
        heights = jax.random.uniform(jax.random.fold_in(jax.random.fold_in(key, 6), dim), (blocks,), jnp.float32, smallest / len(cuts), high / len(cuts))
        return jnp.repeat(jnp.exp(heights), dims[dim] // blocks).reshape((-1,) + (1,) * (len(dims) - dim - 1))

    gain = one(*cuts[0])
    for cut in cuts[1:]:
        gain = gain * one(*cut)
    return gain


def gaussian(rng, extent, spread, reach, cuts=(), held_as=jnp.bfloat16):
    array = jax.random.normal(rng, extent, jnp.float32) * spread
    if len(cuts) > 0:
        array = levels(rng, extent, cuts, -0.22, 0.18) * array
    return jnp.clip(array, min=-reach, max=reach).astype(held_as)


def noise_with(rng, extent, width, limit, cuts, heavy, kind=jnp.bfloat16):
    array = width * jax.random.normal(rng, extent, jnp.float32)
    if cuts:
        array = array * levels(rng, extent, cuts, -0.22, 0.18)
    return jnp.clip(strengthened(array, jax.random.fold_in(rng, 3), *heavy), -limit, limit).astype(kind)


def setup_inputs(seed: int = 0) -> dict:
    streams_of = jax.random.split(jax.random.key(seed), 15)
    tokens = gaussian(streams_of[0], (TOKENS, D), 1.0, 6.0, ((0, 32),))
    lengths = draw_lengths(jax.random.fold_in(streams_of[14], 71), 0)
    w_query = gaussian(streams_of[2], (D, D), D ** -0.5, 0.125, ((1, 4),))
    w_key = gaussian(streams_of[3], (D, D), D ** -0.5, 0.125, ((1, 4),))
    w_value = gaussian(streams_of[4], (D, D), D ** -0.5, 0.125, ((1, 4),))
    w_out = gaussian(streams_of[5], (D, D), D ** -0.5, 0.125, ((0, 4),))
    w_gate = gaussian(streams_of[6], (D, FF), D ** -0.5, 0.125, ((1, 4),))
    w_up = gaussian(streams_of[7], (D, FF), D ** -0.5, 0.125, ((1, 4),))
    w_down = gaussian(streams_of[8], (FF, D), FF ** -0.5, 0.0625, ((0, 4),))
    gain_query = jnp.clip(1.0 + 0.18 * jax.random.normal(streams_of[9], (D,), jnp.float32), 0.1, 1.9)
    gain_key = jnp.clip(1.0 + 0.18 * jax.random.normal(streams_of[10], (D,), jnp.float32), 0.1, 1.9)
    gain_attn = jnp.clip(1.0 + 0.18 * jax.random.normal(streams_of[11], (D,), jnp.float32), 0.1, 1.9)
    gain_mlp = jnp.clip(1.0 + 0.18 * jax.random.normal(streams_of[12], (D,), jnp.float32), 0.1, 1.9)
    cotangent = noise_with(streams_of[13], (TOKENS, D), 1.0, 6.0, ((0, 32),), (0, 1, 32, 2.75))
    return dict(tokens=tokens, lengths=lengths, w_query=w_query, w_key=w_key, w_value=w_value, w_out=w_out, w_gate=w_gate, w_up=w_up, w_down=w_down, gain_query=gain_query, gain_key=gain_key, gain_attn=gain_attn, gain_mlp=gain_mlp, cotangent=cotangent)


EPS = 1e-06
THETA = 500000.0

@jax.custom_vjp
def low(v):
    return lax.optimization_barrier(v.astype(jnp.bfloat16)).astype(jnp.float32)

@jax.custom_vjp
def low_back(v):
    return v

def low_keep(v):
    return (low(v), None)

def low_pass(kept, grad):
    return (grad,)

def back_keep(v):
    return (v, None)

def back_low(kept, grad):
    return (low(grad),)
low.defvjp(low_keep, low_pass)
low_back.defvjp(back_keep, back_low)

def mat(left_mat, right_mat):
    return jnp.dot(left_mat, right_mat, preferred_element_type=jnp.float32, precision=lax.Precision.HIGHEST)

def rotate(values, offsets, rot_sign):
    half_width = values.shape[-1] // 2
    frequency = jnp.exp(jnp.arange(half_width, dtype=jnp.float32) * (-2.0 * math.log(THETA) / values.shape[-1]))
    angles = offsets.astype(jnp.float32)[..., None, None] * frequency
    cosines = jnp.cos(angles)
    sine_part = rot_sign * jnp.sin(angles)
    first_half = values[..., :half_width]
    second_half = values[..., half_width:]
    return jnp.concatenate([first_half * cosines - second_half * sine_part, second_half * cosines + first_half * sine_part], axis=-1)

def row_layout(lengths_row):
    seq_ends = jnp.cumsum(lengths_row).astype(jnp.int32)
    position = jnp.arange(ROW_LEN, dtype=jnp.int32)
    passed = (position[:, None] >= seq_ends[None, :]).astype(jnp.int32)
    segment = lax.optimization_barrier(jnp.sum(passed, axis=1))
    seq_start = lax.optimization_barrier(jnp.sum(passed * lengths_row[None, :], axis=1))
    return (segment, position - seq_start)

def allowed_mask(segment):
    position = jnp.arange(segment.shape[0], dtype=jnp.int32)
    return (segment[:, None] == segment[None, :]) & (position[None, :] <= position[:, None])

def rms_scale(values):
    return lax.rsqrt(lax.optimization_barrier(jnp.mean(values * values, axis=-1, keepdims=True)) + EPS)

def row_forward(params, block_item):
    tokens_row, lengths_row = block_item
    w_query, w_key, w_value, w_out, w_gate, w_up, w_down, gain_query, gain_key, gain_attn, gain_mlp = params
    segment, offsets = row_layout(lengths_row)
    queries = low_back(mat(tokens_row, w_query))
    keys_raw = low_back(mat(tokens_row, w_key))
    values_low = low(low_back(mat(tokens_row, w_value)))
    q_rot = low(rotate((queries * rms_scale(queries) * gain_query).reshape(ROW_LEN, H, HD), offsets, 1.0))
    k_rot = low(rotate((keys_raw * rms_scale(keys_raw) * gain_key).reshape(ROW_LEN, H, HD), offsets, 1.0))
    scale_factor = 1.0 / math.sqrt(HD)
    scores = low_back(jnp.einsum('qhd,khd->hqk', q_rot, k_rot, precision=lax.Precision.HIGHEST) * scale_factor)
    scores = jnp.where(allowed_mask(segment)[None], scores, -1e+30)
    row_max = lax.optimization_barrier(jnp.max(scores, axis=-1, keepdims=True))
    shifted = jnp.exp(scores - row_max)
    attn_weights = low(shifted / lax.optimization_barrier(jnp.sum(shifted, axis=-1, keepdims=True)))
    mixed = jnp.einsum('hqk,khd->qhd', attn_weights, values_low.reshape(ROW_LEN, H, HD), precision=lax.Precision.HIGHEST)
    mixed = low_back(low(mixed.reshape(ROW_LEN, D)))
    attn_out = low_back(mat(mixed, w_out))
    hidden = tokens_row + attn_out * rms_scale(attn_out) * gain_attn
    hidden_low = low(hidden)
    gate_acts = low_back(mat(hidden_low, w_gate))
    up_acts = low_back(mat(hidden_low, w_up))
    inner = low(gate_acts * jax.nn.sigmoid(gate_acts) * up_acts)
    mlp_out = low_back(mat(inner, w_down))
    return hidden + mlp_out * rms_scale(mlp_out) * gain_mlp

def reference(tokens, lengths, w_query, w_key, w_value, w_out, w_gate, w_up, w_down, gain_query, gain_key, gain_attn, gain_mlp, cotangent):
    params = tuple((weight.astype(jnp.float32) for weight in (w_query, w_key, w_value, w_out, w_gate, w_up, w_down, gain_query, gain_key, gain_attn, gain_mlp)))
    row_step = jax.checkpoint(row_forward)

    def forward(token_rows, *params_in):
        row_blocks = token_rows.reshape(ROWS, ROW_LEN, D)
        result = lax.map(lambda block_item: row_step(params_in, block_item), (row_blocks, lengths))
        return result.reshape(TOKENS, D)
    output, pullback = jax.vjp(forward, tokens.astype(jnp.float32), *params)
    grads = pullback(cotangent.astype(jnp.float32))
    return (output.astype(jnp.bfloat16), grads[0].astype(jnp.bfloat16), grads[1], grads[2], grads[3], grads[4], grads[5], grads[6], grads[7], grads[8], grads[9], grads[10], grads[11])
```

```python
import math

import jax
import jax.numpy as jnp
from jax import lax
from jax.sharding import PartitionSpec as P

HD = 128
ROW_LEN = 512


EPS = 1e-06
THETA = 500000.0


def rotate(values, offsets, rot_sign):
    half_width = values.shape[-1] // 2
    frequency = jnp.exp(
        jnp.arange(half_width, dtype=jnp.float32) * (-2.0 * math.log(THETA) / values.shape[-1])
    )
    angles = offsets.astype(jnp.float32)[..., None, None] * frequency
    cosines = jnp.cos(angles)
    sine_part = rot_sign * jnp.sin(angles)
    first_half = values[..., :half_width]
    second_half = values[..., half_width:]
    return jnp.concatenate(
        [
            first_half * cosines - second_half * sine_part,
            second_half * cosines + first_half * sine_part,
        ],
        axis=-1,
    )


def row_layout(lengths_row):
    slots = jnp.arange(lengths_row.shape[0], dtype=jnp.int32)
    seq_ends = jnp.sum(
        jnp.where(slots[None, :] <= slots[:, None], lengths_row[None, :], 0), axis=1
    )
    position = jnp.arange(ROW_LEN, dtype=jnp.int32)
    passed = (position[:, None] >= seq_ends[None, :]).astype(jnp.int32)
    segment = jnp.sum(passed, axis=1)
    seq_start = jnp.sum(passed * lengths_row[None, :], axis=1)
    return (segment, position - seq_start)


def allowed_mask(segment):
    position = jnp.arange(segment.shape[0], dtype=jnp.int32)
    return (segment[:, None] == segment[None, :]) & (position[None, :] <= position[:, None])


def times_t(left_mat, right_mat):
    return lax.dot_general(
        left_mat, right_mat, (((1,), (1,)), ((), ())), preferred_element_type=jnp.float32
    )


def t_times(left_mat, right_mat):
    return lax.dot_general(
        left_mat, right_mat, (((0,), (0,)), ((), ())), preferred_element_type=jnp.float32
    )


def masked_scores(queries_low, keys_low, segment):
    scale_factor = 1.0 / math.sqrt(queries_low.shape[-1])
    scores = (
        jnp.einsum("qhd,khd->hqk", queries_low, keys_low, preferred_element_type=jnp.float32)
        * scale_factor
    )
    return jnp.where(allowed_mask(segment)[None], scores, -1e30)


def attend(block_item):
    queries_low, keys_low, values_low, segment = block_item
    scores = masked_scores(queries_low, keys_low, segment)
    row_max = jnp.max(scores, axis=-1, keepdims=True)
    shifted = jnp.exp(scores - row_max)
    row_total = jnp.sum(shifted, axis=-1, keepdims=True)
    attn_weights = (shifted / row_total).astype(jnp.bfloat16)
    mixed = jnp.einsum("hqk,khd->qhd", attn_weights, values_low, preferred_element_type=jnp.float32)
    return (mixed.astype(jnp.bfloat16), (row_max + jnp.log(row_total))[..., 0])


def attend_back(block_item):
    queries_low, keys_low, values_low, segment, log_total, grad_mixed = block_item
    scale_factor = 1.0 / math.sqrt(queries_low.shape[-1])
    scores = masked_scores(queries_low, keys_low, segment)
    attn_weights = jnp.exp(scores - log_total[..., None])
    grad_weights = jnp.einsum(
        "qhd,khd->hqk", grad_mixed, values_low, preferred_element_type=jnp.float32
    )
    row_dots = jnp.sum(attn_weights * grad_weights, axis=-1, keepdims=True)
    grad_scores = (attn_weights * (grad_weights - row_dots)).astype(jnp.bfloat16)
    grad_queries = scale_factor * jnp.einsum(
        "hqk,khd->qhd", grad_scores, keys_low, preferred_element_type=jnp.float32
    )
    grad_keys = scale_factor * jnp.einsum(
        "hqk,qhd->khd", grad_scores, queries_low, preferred_element_type=jnp.float32
    )
    grad_values = jnp.einsum(
        "hqk,qhd->khd",
        attn_weights.astype(jnp.bfloat16),
        grad_mixed,
        preferred_element_type=jnp.float32,
    )
    return (grad_queries, grad_keys, grad_values.astype(jnp.bfloat16))


def post_norm_back(grad_in, unit_rows, inv_scale, gain_vec):
    scaled = grad_in * gain_vec
    mean_dots = jnp.mean(scaled * unit_rows, axis=-1, keepdims=True)
    return (inv_scale * (scaled - unit_rows * mean_dots), jnp.sum(grad_in * unit_rows, axis=0))


OUTER = 4


def swap(value, shift):
    size = lax.axis_size("dp")
    return lax.ppermute(value, "dp", [(d, d ^ shift) for d in range(size)])


def pick(parts, index):
    return lax.dynamic_index_in_dim(parts, index, 0, keepdims=False)


def sum_inner(parts):
    inner = parts.shape[0]
    mine = lax.axis_index("dp") % inner
    total = pick(parts, mine)
    for k in range(1, inner):
        sent = pick(parts, mine ^ k).astype(jnp.bfloat16)
        total = total + swap(sent, k).astype(jnp.float32)
    return total


def trade_outer(parts, inner):
    mine = lax.axis_index("dp") // inner
    got = [(mine, pick(parts, mine))]
    for k in range(1, OUTER):
        got.append((mine ^ k, swap(pick(parts, mine ^ k), k * inner)))
    return got


def split_rows(grad, inner):
    cols = grad.shape[1]
    return grad.reshape(OUTER, inner, -1, cols).transpose(1, 0, 2, 3)


def split_cols(grad, inner):
    rows = grad.shape[0]
    return grad.reshape(rows, OUTER, inner, -1).transpose(2, 1, 0, 3)


def scatter_sum(parts, inner):
    half = sum_inner(parts).astype(jnp.bfloat16)
    got = trade_outer(half, inner)
    return sum(g.astype(jnp.float32) for _, g in got)


def scatter_join(parts, inner, axis):
    half = sum_inner(parts).astype(jnp.bfloat16)
    got = trade_outer(half, inner)
    stack = jnp.zeros((OUTER, *got[0][1].shape), jnp.bfloat16)
    for place, block in got:
        stack = lax.dynamic_update_index_in_dim(stack, block, place, 0)
    joined = jnp.concatenate([stack[z] for z in range(OUTER)], axis=axis)
    return joined.astype(jnp.float32)


def body(
    tokens,
    lengths,
    w_query,
    w_key,
    w_value,
    w_out,
    w_gate,
    w_up,
    w_down,
    gain_query,
    gain_key,
    gain_attn,
    gain_mlp,
    cotangent,
):
    rows_dev = lengths.shape[0]
    model_width = w_query.shape[0]
    local_width = w_query.shape[1]
    head_count = local_width // HD
    gathered = lax.all_gather(tokens, "tensor", axis=0, tiled=True)
    row_count = gathered.shape[0]
    segment, offsets = jax.vmap(row_layout)(lengths)
    queries = jnp.dot(gathered, w_query, preferred_element_type=jnp.float32)
    keys_raw = jnp.dot(gathered, w_key, preferred_element_type=jnp.float32)
    values_low = jnp.dot(gathered, w_value, preferred_element_type=jnp.float32).astype(jnp.bfloat16)
    q_total, k_total = lax.psum(
        (jnp.sum(queries * queries, axis=1), jnp.sum(keys_raw * keys_raw, axis=1)), "tensor"
    )
    q_inv = lax.rsqrt(q_total / model_width + EPS)[:, None]
    k_inv = lax.rsqrt(k_total / model_width + EPS)[:, None]
    q_unit = queries * q_inv
    k_unit = keys_raw * k_inv

    def to_heads(values):
        return values.reshape(rows_dev, ROW_LEN, head_count, HD)

    queries_low = rotate(to_heads(q_unit * gain_query), offsets, 1.0).astype(jnp.bfloat16)
    keys_low = rotate(to_heads(k_unit * gain_key), offsets, 1.0).astype(jnp.bfloat16)
    values_heads = to_heads(values_low)
    mixed_heads, log_total = jax.vmap(lambda *a: attend(a))(
        queries_low, keys_low, values_heads, segment
    )
    mixed_low = mixed_heads.reshape(row_count, local_width)
    attn_out = lax.psum_scatter(
        jnp.dot(mixed_low, w_out, preferred_element_type=jnp.float32).astype(jnp.bfloat16),
        "tensor",
        scatter_dimension=0,
        tiled=True,
    ).astype(jnp.float32)
    a_inv = lax.rsqrt(jnp.mean(attn_out * attn_out, axis=1, keepdims=True) + EPS)
    a_unit = attn_out * a_inv
    hidden = tokens.astype(jnp.float32) + a_unit * gain_attn
    hidden_low = hidden.astype(jnp.bfloat16)
    hidden_all = lax.all_gather(hidden_low, "tensor", axis=0, tiled=True)
    inner_count = lax.axis_size("dp") // OUTER
    outer_index = lax.axis_index("dp") // inner_count

    def gather_group(shard):
        groups = [[z * inner_count + i for z in range(OUTER)] for i in range(inner_count)]
        part = lax.all_gather(shard, "dp", axis=0, tiled=True, axis_index_groups=groups)
        return lax.all_gather(part, "tensor", axis=0, tiled=True)

    hidden_group = gather_group(hidden_low)
    gate_acts = jnp.dot(hidden_all, w_gate, preferred_element_type=jnp.float32)
    up_acts = jnp.dot(hidden_all, w_up, preferred_element_type=jnp.float32)
    gate_sigmoid = jax.nn.sigmoid(gate_acts)
    inner_low = (gate_acts * gate_sigmoid * up_acts).astype(jnp.bfloat16)
    mlp_out = lax.psum_scatter(
        jnp.dot(inner_low, w_down, preferred_element_type=jnp.float32).astype(jnp.bfloat16),
        "tensor",
        scatter_dimension=0,
        tiled=True,
    ).astype(jnp.float32)
    f_inv = lax.rsqrt(jnp.mean(mlp_out * mlp_out, axis=1, keepdims=True) + EPS)
    f_unit = mlp_out * f_inv
    output = (hidden + f_unit * gain_mlp).astype(jnp.bfloat16)
    grad_output = cotangent.astype(jnp.float32)
    grad_mlp, grad_gain_mlp_part = post_norm_back(grad_output, f_unit, f_inv, gain_mlp)
    grad_mlp_low = grad_mlp.astype(jnp.bfloat16)
    mlp_grad_all = lax.all_gather(grad_mlp_low, "tensor", axis=0, tiled=True)
    mlp_grad_group = gather_group(grad_mlp_low)
    grad_inner = times_t(mlp_grad_all, w_down)
    grad_gate_low = (
        grad_inner * up_acts * gate_sigmoid * (1.0 + gate_acts * (1.0 - gate_sigmoid))
    ).astype(jnp.bfloat16)
    grad_up_low = (grad_inner * gate_acts * gate_sigmoid).astype(jnp.bfloat16)
    part_width = w_gate.shape[1] // OUTER
    gate_part = lax.dynamic_slice_in_dim(w_gate, outer_index * part_width, part_width, 1)
    up_part = lax.dynamic_slice_in_dim(w_up, outer_index * part_width, part_width, 1)
    down_part = lax.dynamic_slice_in_dim(w_down, outer_index * part_width, part_width, 0)
    gate_g = jnp.dot(hidden_group, gate_part, preferred_element_type=jnp.float32)
    up_g = jnp.dot(hidden_group, up_part, preferred_element_type=jnp.float32)
    sig_g = jax.nn.sigmoid(gate_g)
    inner_g = (gate_g * sig_g * up_g).astype(jnp.bfloat16)
    grad_inner_g = times_t(mlp_grad_group, down_part)
    grad_gate_g = (grad_inner_g * up_g * sig_g * (1.0 + gate_g * (1.0 - sig_g))).astype(
        jnp.bfloat16
    )
    grad_up_g = (grad_inner_g * gate_g * sig_g).astype(jnp.bfloat16)
    sum_down = scatter_join(split_cols(t_times(inner_g, mlp_grad_group), inner_count), inner_count, 0)
    sum_gate = scatter_join(split_rows(t_times(hidden_group, grad_gate_g), inner_count), inner_count, 1)
    sum_up = scatter_join(split_rows(t_times(hidden_group, grad_up_g), inner_count), inner_count, 1)
    grad_hidden = grad_output + lax.psum_scatter(
        (times_t(grad_gate_low, w_gate) + times_t(grad_up_low, w_up)).astype(jnp.bfloat16),
        "tensor",
        scatter_dimension=0,
        tiled=True,
    ).astype(jnp.float32)
    grad_attn, grad_gain_attn_part = post_norm_back(grad_hidden, a_unit, a_inv, gain_attn)
    attn_grad_all = lax.all_gather(grad_attn.astype(jnp.bfloat16), "tensor", axis=0, tiled=True)
    grad_w_out = t_times(mixed_low, attn_grad_all)
    grad_mixed = times_t(attn_grad_all, w_out).astype(jnp.bfloat16)
    grad_q_rot, grad_k_rot, grad_values_low = jax.vmap(lambda *a: attend_back(a))(
        queries_low, keys_low, values_heads, segment, log_total, to_heads(grad_mixed)
    )
    grad_q_norm = rotate(grad_q_rot, offsets, -1.0).reshape(row_count, local_width)
    grad_k_norm = rotate(grad_k_rot, offsets, -1.0).reshape(row_count, local_width)
    grad_gain_query_part = jnp.sum(grad_q_norm * q_unit, axis=0)
    grad_gain_key_part = jnp.sum(grad_k_norm * k_unit, axis=0)
    q_scaled = grad_q_norm * gain_query
    k_scaled = grad_k_norm * gain_key
    q_dots, k_dots = lax.psum(
        (jnp.sum(q_scaled * q_unit, axis=1), jnp.sum(k_scaled * k_unit, axis=1)), "tensor"
    )
    grad_queries_low = (q_inv * (q_scaled - q_unit * (q_dots / model_width)[:, None])).astype(
        jnp.bfloat16
    )
    grad_keys_low = (k_inv * (k_scaled - k_unit * (k_dots / model_width)[:, None])).astype(
        jnp.bfloat16
    )
    grad_values_flat = grad_values_low.reshape(row_count, local_width)
    grad_w_query = t_times(gathered, grad_queries_low)
    grad_w_key = t_times(gathered, grad_keys_low)
    grad_w_value = t_times(gathered, grad_values_flat)
    grad_tokens = (
        grad_hidden
        + lax.psum_scatter(
            (
                times_t(grad_queries_low, w_query)
                + times_t(grad_keys_low, w_key)
                + times_t(grad_values_flat, w_value)
            ).astype(jnp.bfloat16),
            "tensor",
            scatter_dimension=0,
            tiled=True,
        ).astype(jnp.float32)
    ).astype(jnp.bfloat16)
    tensor_start = lax.axis_index("tensor") * local_width
    zero_row = jnp.zeros((model_width,), jnp.float32)
    q_full = lax.dynamic_update_slice(zero_row, grad_gain_query_part, (tensor_start,))
    k_full = lax.dynamic_update_slice(zero_row, grad_gain_key_part, (tensor_start,))
    gain_stack = jnp.stack([q_full, k_full, grad_gain_attn_part, grad_gain_mlp_part])
    gain_total = lax.psum(gain_stack, ("dp", "tensor"))
    grad_gain_query = lax.dynamic_slice(gain_total[0], (tensor_start,), (local_width,))
    grad_gain_key = lax.dynamic_slice(gain_total[1], (tensor_start,), (local_width,))
    summed = (
        scatter_sum(split_rows(grad_w_query, inner_count), inner_count),
        scatter_sum(split_rows(grad_w_key, inner_count), inner_count),
        scatter_sum(split_rows(grad_w_value, inner_count), inner_count),
        scatter_sum(split_cols(grad_w_out, inner_count), inner_count),
        sum_gate,
        sum_up,
        sum_down,
    )
    return (
        output,
        grad_tokens,
        summed[0],
        summed[1],
        summed[2],
        summed[3],
        summed[4],
        summed[5],
        summed[6],
        grad_gain_query,
        grad_gain_key,
        gain_total[2],
        gain_total[3],
    )


def solution(mesh):
    placed = (
        P(("dp", "tensor"), None),
        P("dp", None),
        P(None, "tensor"),
        P(None, "tensor"),
        P(None, "tensor"),
        P("tensor", None),
        P(None, "tensor"),
        P(None, "tensor"),
        P("tensor", None),
        P("tensor"),
        P("tensor"),
        P(),
        P(),
        P(("dp", "tensor"), None),
    )
    return jax.shard_map(
        body,
        mesh=mesh,
        in_specs=placed,
        out_specs=(
            P(("dp", "tensor"), None),
            P(("dp", "tensor"), None),
            P("dp", "tensor"),
            P("dp", "tensor"),
            P("dp", "tensor"),
            P("tensor", "dp"),
            P("dp", "tensor"),
            P("dp", "tensor"),
            P("tensor", "dp"),
            P("tensor"),
            P("tensor"),
            P(),
            P(),
        ),
        check_vma=False,
    )
```

```python
import math

import jax
import jax.numpy as jnp
from jax import lax
from jax.experimental import pallas as pl
from jax.experimental.pallas import tpu as pltpu
from jax.sharding import PartitionSpec as P

HD = 128
ROW_LEN = 512


EPS = 1e-06
THETA = 500000.0


def rotate(values, offsets, rot_sign):
    half_width = values.shape[-1] // 2
    frequency = jnp.exp(
        jnp.arange(half_width, dtype=jnp.float32) * (-2.0 * math.log(THETA) / values.shape[-1])
    )
    angles = offsets.astype(jnp.float32)[..., None, None] * frequency
    cosines = jnp.cos(angles)
    sine_part = rot_sign * jnp.sin(angles)
    first_half = values[..., :half_width]
    second_half = values[..., half_width:]
    return jnp.concatenate(
        [
            first_half * cosines - second_half * sine_part,
            second_half * cosines + first_half * sine_part,
        ],
        axis=-1,
    )


def row_layout(lengths_row):
    slots = jnp.arange(lengths_row.shape[0], dtype=jnp.int32)
    seq_ends = jnp.sum(
        jnp.where(slots[None, :] <= slots[:, None], lengths_row[None, :], 0), axis=1
    )
    position = jnp.arange(ROW_LEN, dtype=jnp.int32)
    passed = (position[:, None] >= seq_ends[None, :]).astype(jnp.int32)
    segment = jnp.sum(passed, axis=1)
    seq_start = jnp.sum(passed * lengths_row[None, :], axis=1)
    return (segment, position - seq_start)


def allowed_mask(segment):
    position = jnp.arange(segment.shape[0], dtype=jnp.int32)
    return (segment[:, None] == segment[None, :]) & (position[None, :] <= position[:, None])


def times_t(left_mat, right_mat):
    return lax.dot_general(
        left_mat, right_mat, (((1,), (1,)), ((), ())), preferred_element_type=jnp.float32
    )


def t_times(left_mat, right_mat):
    return lax.dot_general(
        left_mat, right_mat, (((0,), (0,)), ((), ())), preferred_element_type=jnp.float32
    )


def masked_scores(queries_low, keys_low, segment):
    scale_factor = 1.0 / math.sqrt(queries_low.shape[-1])
    scores = (
        jnp.einsum("qhd,khd->hqk", queries_low, keys_low, preferred_element_type=jnp.float32)
        * scale_factor
    )
    return jnp.where(allowed_mask(segment)[None], scores, -1e30)


def attend(block_item):
    queries_low, keys_low, values_low, segment = block_item
    scores = masked_scores(queries_low, keys_low, segment)
    row_max = jnp.max(scores, axis=-1, keepdims=True)
    shifted = jnp.exp(scores - row_max)
    row_total = jnp.sum(shifted, axis=-1, keepdims=True)
    attn_weights = (shifted / row_total).astype(jnp.bfloat16)
    mixed = jnp.einsum("hqk,khd->qhd", attn_weights, values_low, preferred_element_type=jnp.float32)
    return (mixed.astype(jnp.bfloat16), (row_max + jnp.log(row_total))[..., 0])


def attend_back(block_item):
    queries_low, keys_low, values_low, segment, log_total, grad_mixed = block_item
    scale_factor = 1.0 / math.sqrt(queries_low.shape[-1])
    scores = masked_scores(queries_low, keys_low, segment)
    attn_weights = jnp.exp(scores - log_total[..., None])
    grad_weights = jnp.einsum(
        "qhd,khd->hqk", grad_mixed, values_low, preferred_element_type=jnp.float32
    )
    row_dots = jnp.sum(attn_weights * grad_weights, axis=-1, keepdims=True)
    grad_scores = (attn_weights * (grad_weights - row_dots)).astype(jnp.bfloat16)
    grad_queries = scale_factor * jnp.einsum(
        "hqk,khd->qhd", grad_scores, keys_low, preferred_element_type=jnp.float32
    )
    grad_keys = scale_factor * jnp.einsum(
        "hqk,qhd->khd", grad_scores, queries_low, preferred_element_type=jnp.float32
    )
    grad_values = jnp.einsum(
        "hqk,qhd->khd",
        attn_weights.astype(jnp.bfloat16),
        grad_mixed,
        preferred_element_type=jnp.float32,
    )
    return (grad_queries, grad_keys, grad_values.astype(jnp.bfloat16))


def post_norm_back(grad_in, unit_rows, inv_scale, gain_vec):
    scaled = grad_in * gain_vec
    mean_dots = jnp.mean(scaled * unit_rows, axis=-1, keepdims=True)
    return (inv_scale * (scaled - unit_rows * mean_dots), jnp.sum(grad_in * unit_rows, axis=0))


OUTER = 4


def swap(value, shift):
    size = lax.axis_size("dp")
    return lax.ppermute(value, "dp", [(d, d ^ shift) for d in range(size)])


def pick(parts, index):
    return lax.dynamic_index_in_dim(parts, index, 0, keepdims=False)


def sum_inner(parts):
    inner = parts.shape[0]
    mine = lax.axis_index("dp") % inner
    total = pick(parts, mine)
    for k in range(1, inner):
        sent = pick(parts, mine ^ k).astype(jnp.bfloat16)
        total = total + swap(sent, k).astype(jnp.float32)
    return total


def trade_outer(parts, inner):
    mine = lax.axis_index("dp") // inner
    got = [(mine, pick(parts, mine))]
    for k in range(1, OUTER):
        got.append((mine ^ k, swap(pick(parts, mine ^ k), k * inner)))
    return got


def split_rows(grad, inner):
    cols = grad.shape[1]
    return grad.reshape(OUTER, inner, -1, cols).transpose(1, 0, 2, 3)


def split_cols(grad, inner):
    rows = grad.shape[0]
    return grad.reshape(rows, OUTER, inner, -1).transpose(2, 1, 0, 3)


def scatter_sum(parts, inner):
    half = sum_inner(parts).astype(jnp.bfloat16)
    got = trade_outer(half, inner)
    return sum(g.astype(jnp.float32) for _, g in got)


def scatter_join(parts, inner, axis):
    half = sum_inner(parts).astype(jnp.bfloat16)
    got = trade_outer(half, inner)
    stack = jnp.zeros((OUTER, *got[0][1].shape), jnp.bfloat16)
    for place, block in got:
        stack = lax.dynamic_update_index_in_dim(stack, block, place, 0)
    joined = jnp.concatenate([stack[z] for z in range(OUTER)], axis=axis)
    return joined.astype(jnp.float32)


MESH = pl.DeviceIdType.MESH
FULL = pl.BlockSpec(memory_space=pl.ANY)


def grads_kernel(
    hid_ref, dml_ref, hall_ref, dall_ref, wg_ref, wu_ref, wd_ref, tok_ref, dat_ref, dq_ref, dk_ref, dv_ref, mix_ref,
    out_ref, gh_ref, gm_ref,
    rows_v, wg_v, wu_v, wd_v, lhs_in, lhs_t, acc, full, part,
    ld_sem, zs_s, zs_r, xs_s, xs_r, cs_s, cs_r, ys_s, ys_r, ts_s, ts_r, own_s,
):
    d = lax.axis_index("dp")
    t = lax.axis_index("tensor")
    z = d // 2
    y = d % 2
    mate = t + 1 - 2 * (t % 2)
    across = (t + 2) % 4
    far = (mate + 2) % 4
    twin = z * 2 + 1 - y

    def remote(src, dst, ss, rs, dd, tt):
        return pltpu.make_async_remote_copy(
            src_ref=src, dst_ref=dst, send_sem=ss, recv_sem=rs, device_id=(dd, tt), device_id_type=MESH
        )

    def peer(k):
        return ((z + k) % 4) * 2 + y

    f = wg_v.shape[1]
    loads = [
        pltpu.make_async_copy(tok_ref, rows_v.at[1, 0], ld_sem.at[0]),
        pltpu.make_async_copy(dat_ref, rows_v.at[1, 1], ld_sem.at[1]),
        pltpu.make_async_copy(dv_ref, lhs_in.at[0], ld_sem.at[2]),
        pltpu.make_async_copy(dq_ref, lhs_in.at[1], ld_sem.at[3]),
        pltpu.make_async_copy(dk_ref, lhs_in.at[2], ld_sem.at[4]),
        pltpu.make_async_copy(mix_ref, lhs_in.at[3], ld_sem.at[5]),
        pltpu.make_async_copy(hall_ref, rows_v.at[0, 0], ld_sem.at[6]),
        pltpu.make_async_copy(dall_ref, rows_v.at[0, 1], ld_sem.at[7]),
        pltpu.make_async_copy(wg_ref.at[:, pl.ds(z * f, f)], wg_v, ld_sem.at[8]),
        pltpu.make_async_copy(wu_ref.at[:, pl.ds(z * f, f)], wu_v, ld_sem.at[9]),
        pltpu.make_async_copy(wd_ref.at[pl.ds(z * f, f), :], wd_v, ld_sem.at[10]),
    ]
    for c in loads:
        c.start()

    barrier = pltpu.get_barrier_semaphore()
    for dd, tt in [(peer(1), t), (peer(2), t), (peer(3), t), (twin, t), (d, mate), (d, across)]:
        pl.semaphore_signal(barrier, inc=1, device_id=(dd, tt), device_id_type=MESH)
    pl.semaphore_wait(barrier, 6)

    shards = (hid_ref, dml_ref)
    groups = (gh_ref, gm_ref)

    def gather_z(a, k):
        return remote(shards[a], groups[a].at[z, t], zs_s.at[a, k - 1], zs_r.at[a, k - 1], peer(k), t)

    def forward_x(a, k):
        r = (z + 4 - k) % 4
        return remote(groups[a].at[r, t], groups[a].at[r, t], xs_s.at[a, k - 1], xs_r.at[a, k - 1], d, across)

    def forward_c(a, k, h):
        r = (z + 4 - k) % 4
        q = t if h == 0 else across
        return remote(groups[a].at[r, q], groups[a].at[r, q], cs_s.at[a, k - 1, h], cs_r.at[a, k - 1, h], d, mate)

    order = (1, 3, 2)
    for k in order:
        for a in range(2):
            gather_z(a, k).start()

    def swap_y(w):
        return remote(full.at[w, :, 1 - y], part.at[w], ys_s.at[w], ys_r.at[w], twin, t)

    def trade_z(w, k):
        return remote(
            part.at[w, (z + k) % 4], out_ref.at[w, z], ts_s.at[w, k - 1], ts_r.at[w, k - 1], peer(k), t
        )

    def keep(w):
        return pltpu.make_async_copy(part.at[w, z], out_ref.at[w, z], own_s.at[w])

    def finish_y(w):
        swap_y(w).wait()
        for b in range(4):
            part[w, b] = (part[w, b].astype(jnp.float32) + full[w, b, y].astype(jnp.float32)).astype(
                jnp.bfloat16
            )
        for k in (2, 1, 3):
            trade_z(w, k).start()
        keep(w).start()

    width = full.shape[4]

    def attn_grad(w, side):
        lhs_t[0] = lhs_in[w].astype(jnp.float32).T.astype(jnp.bfloat16)

        def tile(j, carry):
            cols = pl.ds(pl.multiple_of(j * width, width), width)
            full[w, j // 2, j % 2] = jnp.dot(
                lhs_t[0], rows_v[1, side, :, cols], preferred_element_type=jnp.float32
            ).astype(jnp.bfloat16)
            return carry

        lax.fori_loop(0, 8, tile, 0)
        swap_y(w).start()

    loads[1].wait()
    loads[5].wait()
    attn_grad(3, 1)
    for i in (0, 2, 3, 4):
        loads[i].wait()
    for w in range(3):
        attn_grad(w, 0)

    step = 256

    def mlp_row(slot, first):
        def wide(j, carry):
            cols = pl.ds(pl.multiple_of(j * step, step), step)
            g = jnp.dot(rows_v[slot, 0], wg_v[:, cols], preferred_element_type=jnp.float32)
            u = jnp.dot(rows_v[slot, 0], wu_v[:, cols], preferred_element_type=jnp.float32)
            di = lax.dot_general(
                rows_v[slot, 1], wd_v[cols, :], (((1,), (1,)), ((), ())), preferred_element_type=jnp.float32
            )
            sg = jax.nn.sigmoid(g)
            gs = g * sg
            lhs_t[0, cols, :] = (gs * u).T.astype(jnp.bfloat16)
            lhs_t[1, cols, :] = (di * u * sg * (1.0 + g * (1.0 - sg))).T.astype(jnp.bfloat16)
            lhs_t[2, cols, :] = (di * gs).T.astype(jnp.bfloat16)
            return carry

        lax.fori_loop(0, f // step, wide, 0)

        def deep(j, carry):
            cols = pl.ds(pl.multiple_of(j * step, step), step)
            for w, side in ((0, 1), (1, 0), (2, 0)):
                new = jnp.dot(lhs_t[w], rows_v[slot, side, :, cols], preferred_element_type=jnp.float32)
                if first:
                    acc[w, :, cols] = new
                else:
                    acc[w, :, cols] += new
            return carry

        lax.fori_loop(0, acc.shape[2] // step, deep, 0)

    for i in range(6, 11):
        loads[i].wait()
    mlp_row(0, True)

    def advance_x(k):
        for a in range(2):
            gather_z(a, k).wait_recv()
            forward_x(a, k).start()

    def advance_c(k):
        for a in range(2):
            forward_x(a, k).wait_recv()
            for h in range(2):
                forward_c(a, k, h).start()

    def row_loads(k, slot):
        r = (z + 4 - k) % 4
        return [
            pltpu.make_async_copy(groups[a].at[r, q], rows_v.at[slot, a, pl.ds(q * 128, 128)], ld_sem.at[a * 4 + q])
            for a in range(2)
            for q in range(4)
        ]

    advance_x(order[0])
    finish_y(3)
    advance_c(order[0])
    advance_x(order[1])
    finish_y(0)
    for n, k in enumerate(order):
        slot = (n + 1) % 2
        for a in range(2):
            for h in range(2):
                forward_c(a, k, h).wait_recv()
        copies = row_loads(k, slot)
        for c in copies:
            c.start()
        if n + 1 < 3:
            advance_c(order[n + 1])
        if n + 2 < 3:
            advance_x(order[n + 2])
        for c in copies:
            c.wait()
        mlp_row(slot, False)
        if n < 2:
            finish_y(n + 1)

    def emit(w):
        def tile(j, carry):
            cols = pl.ds(pl.multiple_of(j * width, width), width)
            full[4 + w, j // 2, j % 2] = acc[w, :, cols].astype(jnp.bfloat16)
            return carry

        lax.fori_loop(0, 8, tile, 0)
        swap_y(4 + w).start()

    for w in range(3):
        emit(w)
    for w in range(3):
        finish_y(4 + w)
    for k in order:
        for a in range(2):
            gather_z(a, k).wait_send()
            forward_x(a, k).wait_send()
            for h in range(2):
                forward_c(a, k, h).wait_send()
    for w in range(7):
        keep(w).wait()
        for k in range(1, 4):
            trade_z(w, k).wait()


def weight_grads(hid, dml, hall, dall, wg, wu, wd, tok, dat, dq, dk, dv, mix):
    rows, width = hall.shape
    f = wg.shape[1] // 4
    block = width // 8
    bf = jnp.bfloat16
    dma = pltpu.SemaphoreType.DMA
    flops = 2 * rows * width * f * (4 + 24)
    return pl.pallas_call(
        grads_kernel,
        name="weight_grads",
        out_shape=(
            jax.ShapeDtypeStruct((7, 4, f, block), bf),
            jax.ShapeDtypeStruct((4, 4, rows // 4, width), bf),
            jax.ShapeDtypeStruct((4, 4, rows // 4, width), bf),
        ),
        in_specs=[FULL] * 13,
        out_specs=(FULL,) * 3,
        scratch_shapes=[
            pltpu.VMEM((2, 2, rows, width), bf),
            pltpu.VMEM((width, f), bf),
            pltpu.VMEM((width, f), bf),
            pltpu.VMEM((f, width), bf),
            pltpu.VMEM((4, rows, f), bf),
            pltpu.VMEM((3, f, rows), bf),
            pltpu.VMEM((3, f, width), jnp.float32),
            pltpu.VMEM((7, 4, 2, f, block), bf),
            pltpu.VMEM((7, 4, f, block), bf),
            dma((11,)),
            dma((2, 3)),
            dma((2, 3)),
            dma((2, 3)),
            dma((2, 3)),
            dma((2, 3, 2)),
            dma((2, 3, 2)),
            dma((7,)),
            dma((7,)),
            dma((7, 3)),
            dma((7, 3)),
            dma((7,)),
        ],
        compiler_params=pltpu.CompilerParams(
            collective_id=0, has_side_effects=True, vmem_limit_bytes=60 * 1024 * 1024
        ),
        cost_estimate=pl.CostEstimate(flops=flops, bytes_accessed=60 * 1024 * 1024, transcendentals=0),
    )(hid, dml, hall, dall, wg, wu, wd, tok, dat, dq, dk, dv, mix)


def body(
    tokens,
    lengths,
    w_query,
    w_key,
    w_value,
    w_out,
    w_gate,
    w_up,
    w_down,
    gain_query,
    gain_key,
    gain_attn,
    gain_mlp,
    cotangent,
):
    rows_dev = lengths.shape[0]
    model_width = w_query.shape[0]
    local_width = w_query.shape[1]
    head_count = local_width // HD
    gathered = lax.all_gather(tokens, "tensor", axis=0, tiled=True)
    row_count = gathered.shape[0]
    segment, offsets = jax.vmap(row_layout)(lengths)
    queries = jnp.dot(gathered, w_query, preferred_element_type=jnp.float32)
    keys_raw = jnp.dot(gathered, w_key, preferred_element_type=jnp.float32)
    values_low = jnp.dot(gathered, w_value, preferred_element_type=jnp.float32).astype(jnp.bfloat16)
    q_total, k_total = lax.psum(
        (jnp.sum(queries * queries, axis=1), jnp.sum(keys_raw * keys_raw, axis=1)), "tensor"
    )
    q_inv = lax.rsqrt(q_total / model_width + EPS)[:, None]
    k_inv = lax.rsqrt(k_total / model_width + EPS)[:, None]
    q_unit = queries * q_inv
    k_unit = keys_raw * k_inv

    def to_heads(values):
        return values.reshape(rows_dev, ROW_LEN, head_count, HD)

    queries_low = rotate(to_heads(q_unit * gain_query), offsets, 1.0).astype(jnp.bfloat16)
    keys_low = rotate(to_heads(k_unit * gain_key), offsets, 1.0).astype(jnp.bfloat16)
    values_heads = to_heads(values_low)
    mixed_heads, log_total = jax.vmap(lambda *a: attend(a))(
        queries_low, keys_low, values_heads, segment
    )
    mixed_low = mixed_heads.reshape(row_count, local_width)
    attn_out = lax.psum_scatter(
        jnp.dot(mixed_low, w_out, preferred_element_type=jnp.float32).astype(jnp.bfloat16),
        "tensor",
        scatter_dimension=0,
        tiled=True,
    ).astype(jnp.float32)
    a_inv = lax.rsqrt(jnp.mean(attn_out * attn_out, axis=1, keepdims=True) + EPS)
    a_unit = attn_out * a_inv
    hidden = tokens.astype(jnp.float32) + a_unit * gain_attn
    hidden_low = hidden.astype(jnp.bfloat16)
    hidden_all = lax.all_gather(hidden_low, "tensor", axis=0, tiled=True)
    inner_count = lax.axis_size("dp") // OUTER
    outer_index = lax.axis_index("dp") // inner_count

    def gather_group(shard):
        groups = [[z * inner_count + i for z in range(OUTER)] for i in range(inner_count)]
        part = lax.all_gather(shard, "dp", axis=0, tiled=True, axis_index_groups=groups)
        return lax.all_gather(part, "tensor", axis=0, tiled=True)

    fused = lax.axis_size("dp") == 8
    if not fused:
        hidden_group = gather_group(hidden_low)
    gate_acts = jnp.dot(hidden_all, w_gate, preferred_element_type=jnp.float32)
    up_acts = jnp.dot(hidden_all, w_up, preferred_element_type=jnp.float32)
    gate_sigmoid = jax.nn.sigmoid(gate_acts)
    inner_low = (gate_acts * gate_sigmoid * up_acts).astype(jnp.bfloat16)
    mlp_out = lax.psum_scatter(
        jnp.dot(inner_low, w_down, preferred_element_type=jnp.float32).astype(jnp.bfloat16),
        "tensor",
        scatter_dimension=0,
        tiled=True,
    ).astype(jnp.float32)
    f_inv = lax.rsqrt(jnp.mean(mlp_out * mlp_out, axis=1, keepdims=True) + EPS)
    f_unit = mlp_out * f_inv
    output = (hidden + f_unit * gain_mlp).astype(jnp.bfloat16)
    grad_output = cotangent.astype(jnp.float32)
    grad_mlp, grad_gain_mlp_part = post_norm_back(grad_output, f_unit, f_inv, gain_mlp)
    grad_mlp_low = grad_mlp.astype(jnp.bfloat16)
    mlp_grad_all = lax.all_gather(grad_mlp_low, "tensor", axis=0, tiled=True)
    if not fused:
        mlp_grad_group = gather_group(grad_mlp_low)
    grad_inner = times_t(mlp_grad_all, w_down)
    grad_gate_low = (
        grad_inner * up_acts * gate_sigmoid * (1.0 + gate_acts * (1.0 - gate_sigmoid))
    ).astype(jnp.bfloat16)
    grad_up_low = (grad_inner * gate_acts * gate_sigmoid).astype(jnp.bfloat16)
    if not fused:
        part_width = w_gate.shape[1] // OUTER
        gate_part = lax.dynamic_slice_in_dim(w_gate, outer_index * part_width, part_width, 1)
        up_part = lax.dynamic_slice_in_dim(w_up, outer_index * part_width, part_width, 1)
        down_part = lax.dynamic_slice_in_dim(w_down, outer_index * part_width, part_width, 0)
        gate_g = jnp.dot(hidden_group, gate_part, preferred_element_type=jnp.float32)
        up_g = jnp.dot(hidden_group, up_part, preferred_element_type=jnp.float32)
        sig_g = jax.nn.sigmoid(gate_g)
        inner_g = (gate_g * sig_g * up_g).astype(jnp.bfloat16)
        grad_inner_g = times_t(mlp_grad_group, down_part)
        grad_gate_g = (grad_inner_g * up_g * sig_g * (1.0 + gate_g * (1.0 - sig_g))).astype(
            jnp.bfloat16
        )
        grad_up_g = (grad_inner_g * gate_g * sig_g).astype(jnp.bfloat16)
        sum_down = scatter_join(split_cols(t_times(inner_g, mlp_grad_group), inner_count), inner_count, 0)
        sum_gate = scatter_join(split_rows(t_times(hidden_group, grad_gate_g), inner_count), inner_count, 1)
        sum_up = scatter_join(split_rows(t_times(hidden_group, grad_up_g), inner_count), inner_count, 1)
    grad_hidden = grad_output + lax.psum_scatter(
        (times_t(grad_gate_low, w_gate) + times_t(grad_up_low, w_up)).astype(jnp.bfloat16),
        "tensor",
        scatter_dimension=0,
        tiled=True,
    ).astype(jnp.float32)
    grad_attn, grad_gain_attn_part = post_norm_back(grad_hidden, a_unit, a_inv, gain_attn)
    attn_grad_all = lax.all_gather(grad_attn.astype(jnp.bfloat16), "tensor", axis=0, tiled=True)
    grad_mixed = times_t(attn_grad_all, w_out).astype(jnp.bfloat16)
    grad_q_rot, grad_k_rot, grad_values_low = jax.vmap(lambda *a: attend_back(a))(
        queries_low, keys_low, values_heads, segment, log_total, to_heads(grad_mixed)
    )
    grad_q_norm = rotate(grad_q_rot, offsets, -1.0).reshape(row_count, local_width)
    grad_k_norm = rotate(grad_k_rot, offsets, -1.0).reshape(row_count, local_width)
    grad_gain_query_part = jnp.sum(grad_q_norm * q_unit, axis=0)
    grad_gain_key_part = jnp.sum(grad_k_norm * k_unit, axis=0)
    q_scaled = grad_q_norm * gain_query
    k_scaled = grad_k_norm * gain_key
    q_dots, k_dots = lax.psum(
        (jnp.sum(q_scaled * q_unit, axis=1), jnp.sum(k_scaled * k_unit, axis=1)), "tensor"
    )
    grad_queries_low = (q_inv * (q_scaled - q_unit * (q_dots / model_width)[:, None])).astype(
        jnp.bfloat16
    )
    grad_keys_low = (k_inv * (k_scaled - k_unit * (k_dots / model_width)[:, None])).astype(
        jnp.bfloat16
    )
    grad_values_flat = grad_values_low.reshape(row_count, local_width)
    grad_tokens = (
        grad_hidden
        + lax.psum_scatter(
            (
                times_t(grad_queries_low, w_query)
                + times_t(grad_keys_low, w_key)
                + times_t(grad_values_flat, w_value)
            ).astype(jnp.bfloat16),
            "tensor",
            scatter_dimension=0,
            tiled=True,
        ).astype(jnp.float32)
    ).astype(jnp.bfloat16)
    tensor_start = lax.axis_index("tensor") * local_width
    zero_row = jnp.zeros((model_width,), jnp.float32)
    q_full = lax.dynamic_update_slice(zero_row, grad_gain_query_part, (tensor_start,))
    k_full = lax.dynamic_update_slice(zero_row, grad_gain_key_part, (tensor_start,))
    gain_stack = jnp.stack([q_full, k_full, grad_gain_attn_part, grad_gain_mlp_part])
    gain_total = lax.psum(gain_stack, ("dp", "tensor"))
    grad_gain_query = lax.dynamic_slice(gain_total[0], (tensor_start,), (local_width,))
    grad_gain_key = lax.dynamic_slice(gain_total[1], (tensor_start,), (local_width,))
    if fused:
        blocks, _, _ = weight_grads(
            hidden_low,
            grad_mlp_low,
            hidden_all,
            mlp_grad_all,
            w_gate,
            w_up,
            w_down,
            gathered,
            attn_grad_all,
            grad_queries_low,
            grad_keys_low,
            grad_values_flat,
            mixed_low,
        )
        summed_attn = jnp.sum(blocks[:4].astype(jnp.float32), axis=1)
        joined = blocks[4:].astype(jnp.float32)
        width = joined.shape[3]
        summed = (
            summed_attn[1].T,
            summed_attn[2].T,
            summed_attn[0].T,
            summed_attn[3],
            joined[1].transpose(2, 0, 1).reshape(width, -1),
            joined[2].transpose(2, 0, 1).reshape(width, -1),
            joined[0].reshape(-1, width),
        )
    else:
        summed = (
            scatter_sum(split_rows(t_times(gathered, grad_queries_low), inner_count), inner_count),
            scatter_sum(split_rows(t_times(gathered, grad_keys_low), inner_count), inner_count),
            scatter_sum(split_rows(t_times(gathered, grad_values_flat), inner_count), inner_count),
            scatter_sum(split_cols(t_times(mixed_low, attn_grad_all), inner_count), inner_count),
            sum_gate,
            sum_up,
            sum_down,
        )
    return (
        output,
        grad_tokens,
        summed[0],
        summed[1],
        summed[2],
        summed[3],
        summed[4],
        summed[5],
        summed[6],
        grad_gain_query,
        grad_gain_key,
        gain_total[2],
        gain_total[3],
    )


def solution(mesh):
    placed = (
        P(("dp", "tensor"), None),
        P("dp", None),
        P(None, "tensor"),
        P(None, "tensor"),
        P(None, "tensor"),
        P("tensor", None),
        P(None, "tensor"),
        P(None, "tensor"),
        P("tensor", None),
        P("tensor"),
        P("tensor"),
        P(),
        P(),
        P(("dp", "tensor"), None),
    )
    return jax.shard_map(
        body,
        mesh=mesh,
        in_specs=placed,
        out_specs=(
            P(("dp", "tensor"), None),
            P(("dp", "tensor"), None),
            P("dp", "tensor"),
            P("dp", "tensor"),
            P("dp", "tensor"),
            P("tensor", "dp"),
            P("dp", "tensor"),
            P("dp", "tensor"),
            P("tensor", "dp"),
            P("tensor"),
            P("tensor"),
            P(),
            P(),
        ),
        check_vma=False,
    )
```

```python
import math

import jax
import jax.numpy as jnp
from jax import lax
from jax.experimental import pallas as pl
from jax.experimental.pallas import tpu as pltpu
from jax.sharding import PartitionSpec as P

HD = 128
ROW_LEN = 512


EPS = 1e-06
THETA = 500000.0


def rotate(values, offsets, rot_sign):
    half_width = values.shape[-1] // 2
    frequency = jnp.exp(
        jnp.arange(half_width, dtype=jnp.float32) * (-2.0 * math.log(THETA) / values.shape[-1])
    )
    angles = offsets.astype(jnp.float32)[..., None, None] * frequency
    cosines = jnp.cos(angles)
    sine_part = rot_sign * jnp.sin(angles)
    first_half = values[..., :half_width]
    second_half = values[..., half_width:]
    return jnp.concatenate(
        [
            first_half * cosines - second_half * sine_part,
            second_half * cosines + first_half * sine_part,
        ],
        axis=-1,
    )


def row_layout(lengths_row):
    slots = jnp.arange(lengths_row.shape[0], dtype=jnp.int32)
    seq_ends = jnp.sum(
        jnp.where(slots[None, :] <= slots[:, None], lengths_row[None, :], 0), axis=1
    )
    position = jnp.arange(ROW_LEN, dtype=jnp.int32)
    passed = (position[:, None] >= seq_ends[None, :]).astype(jnp.int32)
    segment = jnp.sum(passed, axis=1)
    seq_start = jnp.sum(passed * lengths_row[None, :], axis=1)
    return (segment, position - seq_start)


def allowed_mask(segment):
    position = jnp.arange(segment.shape[0], dtype=jnp.int32)
    return (segment[:, None] == segment[None, :]) & (position[None, :] <= position[:, None])


def times_t(left_mat, right_mat):
    return lax.dot_general(
        left_mat, right_mat, (((1,), (1,)), ((), ())), preferred_element_type=jnp.float32
    )


def t_times(left_mat, right_mat):
    return lax.dot_general(
        left_mat, right_mat, (((0,), (0,)), ((), ())), preferred_element_type=jnp.float32
    )


def masked_scores(queries_low, keys_low, segment):
    scale_factor = 1.0 / math.sqrt(queries_low.shape[-1])
    scores = (
        jnp.einsum("qhd,khd->hqk", queries_low, keys_low, preferred_element_type=jnp.float32)
        * scale_factor
    )
    return jnp.where(allowed_mask(segment)[None], scores, -1e30)


def attend(block_item):
    queries_low, keys_low, values_low, segment = block_item
    scores = masked_scores(queries_low, keys_low, segment)
    row_max = jnp.max(scores, axis=-1, keepdims=True)
    shifted = jnp.exp(scores - row_max)
    row_total = jnp.sum(shifted, axis=-1, keepdims=True)
    attn_weights = (shifted / row_total).astype(jnp.bfloat16)
    mixed = jnp.einsum("hqk,khd->qhd", attn_weights, values_low, preferred_element_type=jnp.float32)
    return (mixed.astype(jnp.bfloat16), (row_max + jnp.log(row_total))[..., 0])


def attend_back(block_item):
    queries_low, keys_low, values_low, segment, log_total, grad_mixed = block_item
    scale_factor = 1.0 / math.sqrt(queries_low.shape[-1])
    scores = masked_scores(queries_low, keys_low, segment)
    attn_weights = jnp.exp(scores - log_total[..., None])
    grad_weights = jnp.einsum(
        "qhd,khd->hqk", grad_mixed, values_low, preferred_element_type=jnp.float32
    )
    row_dots = jnp.sum(attn_weights * grad_weights, axis=-1, keepdims=True)
    grad_scores = (attn_weights * (grad_weights - row_dots)).astype(jnp.bfloat16)
    grad_queries = scale_factor * jnp.einsum(
        "hqk,khd->qhd", grad_scores, keys_low, preferred_element_type=jnp.float32
    )
    grad_keys = scale_factor * jnp.einsum(
        "hqk,qhd->khd", grad_scores, queries_low, preferred_element_type=jnp.float32
    )
    grad_values = jnp.einsum(
        "hqk,qhd->khd",
        attn_weights.astype(jnp.bfloat16),
        grad_mixed,
        preferred_element_type=jnp.float32,
    )
    return (grad_queries, grad_keys, grad_values.astype(jnp.bfloat16))


def post_norm_back(grad_in, unit_rows, inv_scale, gain_vec):
    scaled = grad_in * gain_vec
    mean_dots = jnp.mean(scaled * unit_rows, axis=-1, keepdims=True)
    return (inv_scale * (scaled - unit_rows * mean_dots), jnp.sum(grad_in * unit_rows, axis=0))


OUTER = 4


def swap(value, shift):
    size = lax.axis_size("dp")
    return lax.ppermute(value, "dp", [(d, d ^ shift) for d in range(size)])


def pick(parts, index):
    return lax.dynamic_index_in_dim(parts, index, 0, keepdims=False)


def sum_inner(parts):
    inner = parts.shape[0]
    mine = lax.axis_index("dp") % inner
    total = pick(parts, mine)
    for k in range(1, inner):
        sent = pick(parts, mine ^ k).astype(jnp.bfloat16)
        total = total + swap(sent, k).astype(jnp.float32)
    return total


def trade_outer(parts, inner):
    mine = lax.axis_index("dp") // inner
    got = [(mine, pick(parts, mine))]
    for k in range(1, OUTER):
        got.append((mine ^ k, swap(pick(parts, mine ^ k), k * inner)))
    return got


def split_rows(grad, inner):
    cols = grad.shape[1]
    return grad.reshape(OUTER, inner, -1, cols).transpose(1, 0, 2, 3)


def split_cols(grad, inner):
    rows = grad.shape[0]
    return grad.reshape(rows, OUTER, inner, -1).transpose(2, 1, 0, 3)


def scatter_sum(parts, inner):
    half = sum_inner(parts).astype(jnp.bfloat16)
    got = trade_outer(half, inner)
    return sum(g.astype(jnp.float32) for _, g in got)


def scatter_join(parts, inner, axis):
    half = sum_inner(parts).astype(jnp.bfloat16)
    got = trade_outer(half, inner)
    stack = jnp.zeros((OUTER, *got[0][1].shape), jnp.bfloat16)
    for place, block in got:
        stack = lax.dynamic_update_index_in_dim(stack, block, place, 0)
    joined = jnp.concatenate([stack[z] for z in range(OUTER)], axis=axis)
    return joined.astype(jnp.float32)


MESH = pl.DeviceIdType.MESH
FULL = pl.BlockSpec(memory_space=pl.ANY)


def grads_kernel(
    dml_ref, gh_in, gm_in, wg_ref, wu_ref, wd_ref, tok_ref, dat_ref, dq_ref, dk_ref, dv_ref, mix_ref,
    out_ref, gh_ref, gm_ref,
    rows_v, wg_v, wu_v, wd_v, lhs_in, lhs_t, acc, full, part,
    ld_sem, zs_s, zs_r, xs_s, xs_r, cs_s, cs_r, ys_s, ys_r, ts_s, ts_r, own_s,
):
    d = lax.axis_index("dp")
    t = lax.axis_index("tensor")
    z = d // 2
    y = d % 2
    mate = t + 1 - 2 * (t % 2)
    across = (t + 2) % 4
    far = (mate + 2) % 4
    twin = z * 2 + 1 - y

    def remote(src, dst, ss, rs, dd, tt):
        return pltpu.make_async_remote_copy(
            src_ref=src, dst_ref=dst, send_sem=ss, recv_sem=rs, device_id=(dd, tt), device_id_type=MESH
        )

    def peer(k):
        return ((z + k) % 4) * 2 + y

    f = wg_v.shape[1]
    loads = [
        pltpu.make_async_copy(tok_ref, rows_v.at[1, 0], ld_sem.at[0]),
        pltpu.make_async_copy(dat_ref, rows_v.at[1, 1], ld_sem.at[1]),
        pltpu.make_async_copy(dv_ref, lhs_in.at[0], ld_sem.at[2]),
        pltpu.make_async_copy(dq_ref, lhs_in.at[1], ld_sem.at[3]),
        pltpu.make_async_copy(dk_ref, lhs_in.at[2], ld_sem.at[4]),
        pltpu.make_async_copy(mix_ref, lhs_in.at[3], ld_sem.at[5]),
        pltpu.make_async_copy(gh_ref.at[z], rows_v.at[0, 0], ld_sem.at[6]),
        pltpu.make_async_copy(gm_ref.at[z], rows_v.at[0, 1], ld_sem.at[7]),
        pltpu.make_async_copy(wg_ref.at[:, pl.ds(z * f, f)], wg_v, ld_sem.at[8]),
        pltpu.make_async_copy(wu_ref.at[:, pl.ds(z * f, f)], wu_v, ld_sem.at[9]),
        pltpu.make_async_copy(wd_ref.at[pl.ds(z * f, f), :], wd_v, ld_sem.at[10]),
    ]
    for c in loads:
        c.start()

    barrier = pltpu.get_barrier_semaphore()
    for dd, tt in [(peer(1), t), (peer(2), t), (peer(3), t), (twin, t), (d, mate), (d, across)]:
        pl.semaphore_signal(barrier, inc=1, device_id=(dd, tt), device_id_type=MESH)
    pl.semaphore_wait(barrier, 6)

    groups = (gh_ref, gm_ref)

    def gather_z(k):
        return remote(dml_ref, gm_ref.at[z, t], zs_s.at[k - 1], zs_r.at[k - 1], peer(k), t)

    def forward_x(a, k):
        r = (z + 4 - k) % 4
        return remote(groups[a].at[r, t], groups[a].at[r, t], xs_s.at[a, k - 1], xs_r.at[a, k - 1], d, across)

    def forward_c(a, k, h):
        r = (z + 4 - k) % 4
        q = t if h == 0 else across
        return remote(groups[a].at[r, q], groups[a].at[r, q], cs_s.at[a, k - 1, h], cs_r.at[a, k - 1, h], d, mate)

    order = (1, 3, 2)
    for k in order:
        forward_x(0, k).start()
        gather_z(k).start()

    def swap_y(w):
        return remote(full.at[w, :, 1 - y], part.at[w], ys_s.at[w], ys_r.at[w], twin, t)

    def trade_z(w, k):
        return remote(
            part.at[w, (z + k) % 4], out_ref.at[w, z], ts_s.at[w, k - 1], ts_r.at[w, k - 1], peer(k), t
        )

    def keep(w):
        return pltpu.make_async_copy(part.at[w, z], out_ref.at[w, z], own_s.at[w])

    def finish_y(w):
        swap_y(w).wait()
        for b in range(4):
            part[w, b] = (part[w, b].astype(jnp.float32) + full[w, b, y].astype(jnp.float32)).astype(
                jnp.bfloat16
            )
        for k in (2, 1, 3):
            trade_z(w, k).start()
        keep(w).start()

    width = full.shape[4]

    def attn_grad(w, side):
        lhs_t[0] = lhs_in[w].astype(jnp.float32).T.astype(jnp.bfloat16)

        def tile(j, carry):
            cols = pl.ds(pl.multiple_of(j * width, width), width)
            full[w, j // 2, j % 2] = jnp.dot(
                lhs_t[0], rows_v[1, side, :, :, cols].reshape(lhs_t.shape[2], width), preferred_element_type=jnp.float32
            ).astype(jnp.bfloat16)
            return carry

        lax.fori_loop(0, 8, tile, 0)
        swap_y(w).start()

    loads[1].wait()
    loads[5].wait()
    attn_grad(3, 1)
    for i in (0, 2, 3, 4):
        loads[i].wait()
    for w in range(3):
        attn_grad(w, 0)

    step = 256
    tall = (lhs_t.shape[2], acc.shape[2])

    def mlp_row(slot, first):
        def wide(j, carry):
            cols = pl.ds(pl.multiple_of(j * step, step), step)
            g = jnp.dot(rows_v[slot, 0].reshape(tall), wg_v[:, cols], preferred_element_type=jnp.float32)
            u = jnp.dot(rows_v[slot, 0].reshape(tall), wu_v[:, cols], preferred_element_type=jnp.float32)
            di = lax.dot_general(
                rows_v[slot, 1].reshape(tall), wd_v[cols, :], (((1,), (1,)), ((), ())), preferred_element_type=jnp.float32
            )
            sg = jax.nn.sigmoid(g)
            gs = g * sg
            lhs_t[0, cols, :] = (gs * u).T.astype(jnp.bfloat16)
            lhs_t[1, cols, :] = (di * u * sg * (1.0 + g * (1.0 - sg))).T.astype(jnp.bfloat16)
            lhs_t[2, cols, :] = (di * gs).T.astype(jnp.bfloat16)
            return carry

        lax.fori_loop(0, f // step, wide, 0)

        def deep(j, carry):
            cols = pl.ds(pl.multiple_of(j * step, step), step)
            for w, side in ((0, 1), (1, 0), (2, 0)):
                new = jnp.dot(lhs_t[w], rows_v[slot, side, :, :, cols].reshape(lhs_t.shape[2], step), preferred_element_type=jnp.float32)
                if first:
                    acc[w, :, cols] = new
                else:
                    acc[w, :, cols] += new
            return carry

        lax.fori_loop(0, acc.shape[2] // step, deep, 0)

    for i in range(6, 11):
        loads[i].wait()
    mlp_row(0, True)

    def advance_x(k):
        gather_z(k).wait_recv()
        forward_x(1, k).start()

    def advance_c(k):
        for a in range(2):
            forward_x(a, k).wait_recv()
            for h in range(2):
                forward_c(a, k, h).start()

    def row_loads(k, slot):
        r = (z + 4 - k) % 4
        return [
            pltpu.make_async_copy(groups[a].at[r, q], rows_v.at[slot, a, q], ld_sem.at[a * 4 + q])
            for a in range(2)
            for q in range(4)
        ]

    advance_x(order[0])
    finish_y(3)
    advance_c(order[0])
    advance_x(order[1])
    finish_y(0)
    for n, k in enumerate(order):
        slot = (n + 1) % 2
        for a in range(2):
            for h in range(2):
                forward_c(a, k, h).wait_recv()
        copies = row_loads(k, slot)
        for c in copies:
            c.start()
        if n + 1 < 3:
            advance_c(order[n + 1])
        if n + 2 < 3:
            advance_x(order[n + 2])
        for c in copies:
            c.wait()
        mlp_row(slot, False)
        if n < 2:
            finish_y(n + 1)

    def emit(w):
        def tile(j, carry):
            cols = pl.ds(pl.multiple_of(j * width, width), width)
            full[4 + w, j // 2, j % 2] = acc[w, :, cols].astype(jnp.bfloat16)
            return carry

        lax.fori_loop(0, 8, tile, 0)
        swap_y(4 + w).start()

    for w in range(3):
        emit(w)
    for w in range(3):
        finish_y(4 + w)
    for k in order:
        gather_z(k).wait_send()
        for a in range(2):
            forward_x(a, k).wait_send()
            for h in range(2):
                forward_c(a, k, h).wait_send()
    for w in range(7):
        keep(w).wait()
        for k in range(1, 4):
            trade_z(w, k).wait()


def weight_grads(dml, gh, gd, wg, wu, wd, tok, dat, dq, dk, dv, mix):
    rows, width = tok.shape
    tok = tok.reshape(4, rows // 4, width)
    dat = dat.reshape(4, rows // 4, width)
    f = wg.shape[1] // 4
    block = width // 8
    bf = jnp.bfloat16
    dma = pltpu.SemaphoreType.DMA
    flops = 2 * rows * width * f * (4 + 24)
    return pl.pallas_call(
        grads_kernel,
        name="weight_grads",
        input_output_aliases={1: 1, 2: 2},
        out_shape=(
            jax.ShapeDtypeStruct((7, 4, f, block), bf),
            jax.ShapeDtypeStruct((4, 4, rows // 4, width), bf),
            jax.ShapeDtypeStruct((4, 4, rows // 4, width), bf),
        ),
        in_specs=[FULL] * 12,
        out_specs=(FULL,) * 3,
        scratch_shapes=[
            pltpu.VMEM((2, 2, 4, rows // 4, width), bf),
            pltpu.VMEM((width, f), bf),
            pltpu.VMEM((width, f), bf),
            pltpu.VMEM((f, width), bf),
            pltpu.VMEM((4, rows, f), bf),
            pltpu.VMEM((3, f, rows), bf),
            pltpu.VMEM((3, f, width), jnp.float32),
            pltpu.VMEM((7, 4, 2, f, block), bf),
            pltpu.VMEM((7, 4, f, block), bf),
            dma((11,)),
            dma((3,)),
            dma((3,)),
            dma((2, 3)),
            dma((2, 3)),
            dma((2, 3, 2)),
            dma((2, 3, 2)),
            dma((7,)),
            dma((7,)),
            dma((7, 3)),
            dma((7, 3)),
            dma((7,)),
        ],
        compiler_params=pltpu.CompilerParams(
            collective_id=0, has_side_effects=True, vmem_limit_bytes=60 * 1024 * 1024
        ),
        cost_estimate=pl.CostEstimate(flops=flops, bytes_accessed=60 * 1024 * 1024, transcendentals=0),
    )(dml, gh, gd, wg, wu, wd, tok, dat, dq, dk, dv, mix)


def far_copy(src, dst, ss, rs, dd, tt):
    return pltpu.make_async_remote_copy(
        src_ref=src, dst_ref=dst, send_sem=ss, recv_sem=rs, device_id=(dd, tt), device_id_type=MESH
    )


def mean_inv(values):
    return lax.rsqrt(jnp.mean(values * values, axis=1, keepdims=True) + EPS)


def mlp_kernel(
    att_ref, tok_ref, cot_ref, ga_ref, gm_ref, wg_ref, wu_ref, wd_ref,
    out_ref, ghid_ref, dat_ref, dml_ref, gain_ref, gh_ref, gd_ref,
    wg_v, wu_v, wd_v, slope_g, slope_u, own, oth, low_a, low_b, pown, pmate, xsend, xrecv, qown, qmate, hid,
    w_sem, as_s, as_r, ax_s, ax_r, af_s, af_r, ps_s, ps_r, px_s, px_r, pq_s, pq_r, zs_s, zs_r, st_sem,
):
    d = lax.axis_index("dp")
    t = lax.axis_index("tensor")
    z = d // 2
    y = d % 2
    c = t % 2
    chip = t // 2
    mate = t + 1 - 2 * c
    across = (t + 2) % 4
    shard, width = att_ref.shape
    ff = wg_v.shape[1]
    bf = jnp.bfloat16
    f32 = jnp.float32
    tile = 512
    tiles = ff // tile

    def wcopy(i, j):
        cols = pl.ds(j * tile, tile)
        if i == 0:
            return pltpu.make_async_copy(wg_ref.at[:, cols], wg_v.at[:, cols], w_sem.at[0, j])
        if i == 1:
            return pltpu.make_async_copy(wu_ref.at[:, cols], wu_v.at[:, cols], w_sem.at[1, j])
        return pltpu.make_async_copy(wd_ref.at[cols, :], wd_v.at[cols, :], w_sem.at[2, j])

    for j in range(tiles):
        wcopy(0, j).start()
        wcopy(1, j).start()
    for j in range(tiles):
        wcopy(2, j).start()

    barrier = pltpu.get_barrier_semaphore()
    peers = [((z + k) % 4) * 2 + y for k in range(1, 4)]
    for dd, tt in [(peers[0], t), (peers[1], t), (peers[2], t), (d, mate), (d, across)]:
        pl.semaphore_signal(barrier, inc=1, device_id=(dd, tt), device_id_type=MESH)
    pl.semaphore_wait(barrier, 5)

    def send_mate(p):
        return far_copy(own.at[p, c], own.at[p, c], as_s.at[p], as_r.at[p], d, mate)

    def send_across(p):
        return far_copy(own.at[p, c], oth.at[p, c], ax_s.at[p], ax_r.at[p], d, across)

    def forward(p):
        return far_copy(oth.at[p, c], oth.at[p, c], af_s.at[p], af_r.at[p], d, mate)

    half = width // 2

    def part_mate(p, h):
        return far_copy(
            pown.at[p, h, 1 - c], pmate.at[p, h], ps_s.at[p, h], ps_r.at[p, h], d, mate
        )

    def part_across(p, h):
        return far_copy(xsend.at[p, h], xrecv.at[p, h], px_s.at[p, h], px_r.at[p, h], d, across)

    def part_own(p):
        return far_copy(qown.at[p, 1 - c], qmate.at[p], pq_s.at[p], pq_r.at[p], d, mate)

    def gather_z(k):
        return far_copy(
            own.at[0, c], gh_ref.at[z, t], zs_s.at[k - 1], zs_r.at[k - 1], ((z + k) % 4) * 2 + y, t
        )

    def store_row(p, ref):
        mine = ref.at[z]
        return [
            pltpu.make_async_copy(own.at[p, 0], mine.at[chip * 2], st_sem.at[p, 0]),
            pltpu.make_async_copy(own.at[p, 1], mine.at[chip * 2 + 1], st_sem.at[p, 1]),
            pltpu.make_async_copy(oth.at[p, 0], mine.at[2 - chip * 2], st_sem.at[p, 2]),
            pltpu.make_async_copy(oth.at[p, 1], mine.at[3 - chip * 2], st_sem.at[p, 3]),
        ]

    two = 2 * shard

    def forward_in(lhs, base, wait):
        for j in range(tiles):
            if wait:
                wcopy(0, j).wait()
                wcopy(1, j).wait()
            cols = pl.ds(j * tile, tile)
            for s in range(2):
                rows = pl.ds(s * shard, shard)
                g = jnp.dot(lhs[s], wg_v[:, cols], preferred_element_type=f32)
                u = jnp.dot(lhs[s], wu_v[:, cols], preferred_element_type=f32)
                sg = jax.nn.sigmoid(g)
                gs = g * sg
                low_a[rows, cols] = (gs * u).astype(bf)
                slope_u[pl.ds(base + s * shard, shard), cols] = gs
                slope_g[pl.ds(base + s * shard, shard), cols] = u * sg * (1.0 + g * (1.0 - sg))

    def backward_in(lhs, base, wait):
        for j in range(tiles):
            cols = pl.ds(j * tile, tile)
            for s in range(2):
                rows = pl.ds(s * shard, shard)
                di = lax.dot_general(
                    lhs[s], wd_v[cols, :], (((1,), (1,)), ((), ())), preferred_element_type=f32
                )
                low_a[rows, cols] = (di * slope_g[pl.ds(base + s * shard, shard), cols]).astype(bf)
                low_b[rows, cols] = (di * slope_u[pl.ds(base + s * shard, shard), cols]).astype(bf)

    def result(p, cols):
        if p == 0:
            return jnp.dot(low_a[...], wd_v[:, cols], preferred_element_type=f32)
        nt = (((1,), (1,)), ((), ()))
        return lax.dot_general(
            low_a[...], wg_v[cols, :], nt, preferred_element_type=f32
        ) + lax.dot_general(low_b[...], wu_v[cols, :], nt, preferred_element_type=f32)

    def run(p, first, wait):
        send_across(p).start()
        send_mate(p).start()
        if p == 0:
            for k in (1, 3, 2):
                gather_z(k).start()
        send_mate(p).wait_recv()
        first(own.at[p], 0, wait)
        if wait:
            for j in range(tiles):
                wcopy(2, j).wait()
        for j in range(width // tile):
            cols = pl.ds(j * tile, tile)
            new = result(p, cols).astype(bf)
            for s in range(2):
                qown[p, s, :, cols] = new[s * shard : (s + 1) * shard]
        part_own(p).start()
        send_across(p).wait_recv()
        forward(p).start()
        forward(p).wait_recv()
        for cp in store_row(p, gh_ref if p == 0 else gd_ref):
            cp.start()
        first(oth.at[p], two, False)
        for h in range(2):
            for j in range(half // tile):
                new = result(p, pl.ds(h * half + j * tile, tile)).astype(bf)
                for s in range(2):
                    pown[p, h, s, :, pl.ds(j * tile, tile)] = new[s * shard : (s + 1) * shard]
            part_mate(p, h).start()
            part_mate(p, h).wait_recv()
            xsend[p, h] = (pown[p, h, c].astype(f32) + pmate[p, h].astype(f32)).astype(bf)
            part_across(p, h).start()
        part_own(p).wait_recv()
        sums = []
        for h in range(2):
            part_across(p, h).wait_recv()
            cols = slice(h * half, (h + 1) * half)
            sums.append(
                qown[p, c, :, cols].astype(f32) + qmate[p, :, cols].astype(f32) + xrecv[p, h].astype(f32)
            )
        return jnp.concatenate(sums, axis=1)

    att = att_ref[...]
    hid[...] = tok_ref[...].astype(f32) + att * mean_inv(att) * ga_ref[...]
    own[0, c] = hid[...].astype(bf)
    mlp = run(0, forward_in, True)
    rf = mean_inv(mlp)
    fh = mlp * rf
    gy = cot_ref[...].astype(f32)
    out_ref[...] = (hid[...] + fh * gm_ref[...]).astype(bf)
    scaled = gy * gm_ref[...]
    dm = (rf * (scaled - fh * jnp.mean(scaled * fh, axis=1, keepdims=True))).astype(bf)
    gain_ref[1:2, :] = jnp.sum(gy * fh, axis=0, keepdims=True)
    own[1, c] = dm
    dml_ref[...] = dm
    back = run(1, backward_in, False)
    gh = cot_ref[...].astype(f32) + back
    ghid_ref[...] = gh
    ra = mean_inv(att_ref[...])
    ah = att_ref[...] * ra
    gain_ref[0:1, :] = jnp.sum(gh * ah, axis=0, keepdims=True)
    scaled = gh * ga_ref[...]
    dat_ref[...] = (ra * (scaled - ah * jnp.mean(scaled * ah, axis=1, keepdims=True))).astype(bf)

    for p in range(2):
        send_across(p).wait_send()
        send_mate(p).wait_send()
        forward(p).wait_send()
        part_own(p).wait_send()
        for h in range(2):
            part_mate(p, h).wait_send()
            part_across(p, h).wait_send()
        for cp in store_row(p, gh_ref if p == 0 else gd_ref):
            cp.wait()
    for k in range(1, 4):
        gather_z(k).wait()


def mlp_both(att, tok, cot, ga, gm, wg, wu, wd):
    shard, width = tok.shape
    ff = wg.shape[1]
    bf = jnp.bfloat16
    f32 = jnp.float32
    dma = pltpu.SemaphoreType.DMA
    half = width // 2
    vm = pl.BlockSpec(memory_space=pltpu.VMEM)
    shape = jax.ShapeDtypeStruct
    return pl.pallas_call(
        mlp_kernel,
        name="feed_forward",
        out_shape=(
            shape((shard, width), bf),
            shape((shard, width), f32),
            shape((shard, width), bf),
            shape((shard, width), bf),
            shape((2, width), f32),
            shape((4, 4, shard, width), bf),
            shape((4, 4, shard, width), bf),
        ),
        in_specs=[vm] * 5 + [FULL] * 3,
        out_specs=(vm,) * 5 + (FULL,) * 2,
        scratch_shapes=[
            pltpu.VMEM((width, ff), bf),
            pltpu.VMEM((width, ff), bf),
            pltpu.VMEM((ff, width), bf),
            pltpu.VMEM((4 * shard, ff), f32),
            pltpu.VMEM((4 * shard, ff), f32),
            pltpu.VMEM((2, 2, shard, width), bf),
            pltpu.VMEM((2, 2, shard, width), bf),
            pltpu.VMEM((2 * shard, ff), bf),
            pltpu.VMEM((2 * shard, ff), bf),
            pltpu.VMEM((2, 2, 2, shard, half), bf),
            pltpu.VMEM((2, 2, shard, half), bf),
            pltpu.VMEM((2, 2, shard, half), bf),
            pltpu.VMEM((2, 2, shard, half), bf),
            pltpu.VMEM((2, 2, shard, width), bf),
            pltpu.VMEM((2, shard, width), bf),
            pltpu.VMEM((shard, width), f32),
            dma((3, ff // 512)),
            dma((2,)), dma((2,)), dma((2,)), dma((2,)), dma((2,)), dma((2,)),
            dma((2, 2)), dma((2, 2)), dma((2, 2)), dma((2, 2)),
            dma((2,)), dma((2,)),
            dma((3,)), dma((3,)),
            dma((2, 4)),
        ],
        compiler_params=pltpu.CompilerParams(
            collective_id=1, has_side_effects=True, vmem_limit_bytes=60 * 1024 * 1024
        ),
        cost_estimate=pl.CostEstimate(
            flops=2 * 6 * 4 * shard * width * ff, bytes_accessed=40 * 1024 * 1024, transcendentals=4 * shard * ff
        ),
    )(att, tok, cot, ga.reshape(1, -1), gm.reshape(1, -1), wg, wu, wd)


def body(
    tokens,
    lengths,
    w_query,
    w_key,
    w_value,
    w_out,
    w_gate,
    w_up,
    w_down,
    gain_query,
    gain_key,
    gain_attn,
    gain_mlp,
    cotangent,
):
    rows_dev = lengths.shape[0]
    model_width = w_query.shape[0]
    local_width = w_query.shape[1]
    head_count = local_width // HD
    gathered = lax.all_gather(tokens, "tensor", axis=0, tiled=True)
    row_count = gathered.shape[0]
    segment, offsets = jax.vmap(row_layout)(lengths)
    queries = jnp.dot(gathered, w_query, preferred_element_type=jnp.float32)
    keys_raw = jnp.dot(gathered, w_key, preferred_element_type=jnp.float32)
    values_low = jnp.dot(gathered, w_value, preferred_element_type=jnp.float32).astype(jnp.bfloat16)
    q_total, k_total = lax.psum(
        (jnp.sum(queries * queries, axis=1), jnp.sum(keys_raw * keys_raw, axis=1)), "tensor"
    )
    q_inv = lax.rsqrt(q_total / model_width + EPS)[:, None]
    k_inv = lax.rsqrt(k_total / model_width + EPS)[:, None]
    q_unit = queries * q_inv
    k_unit = keys_raw * k_inv

    def to_heads(values):
        return values.reshape(rows_dev, ROW_LEN, head_count, HD)

    queries_low = rotate(to_heads(q_unit * gain_query), offsets, 1.0).astype(jnp.bfloat16)
    keys_low = rotate(to_heads(k_unit * gain_key), offsets, 1.0).astype(jnp.bfloat16)
    values_heads = to_heads(values_low)
    mixed_heads, log_total = jax.vmap(lambda *a: attend(a))(
        queries_low, keys_low, values_heads, segment
    )
    mixed_low = mixed_heads.reshape(row_count, local_width)
    attn_out = lax.psum_scatter(
        jnp.dot(mixed_low, w_out, preferred_element_type=jnp.float32).astype(jnp.bfloat16),
        "tensor",
        scatter_dimension=0,
        tiled=True,
    ).astype(jnp.float32)
    fused = lax.axis_size("dp") == 8
    inner_count = lax.axis_size("dp") // OUTER
    if fused:
        output, grad_hidden, grad_attn_low, grad_mlp_low, gain_parts, group_h, group_d = mlp_both(
            attn_out, tokens, cotangent, gain_attn, gain_mlp, w_gate, w_up, w_down
        )
        grad_gain_attn_part, grad_gain_mlp_part = gain_parts[0], gain_parts[1]
    else:
        a_inv = lax.rsqrt(jnp.mean(attn_out * attn_out, axis=1, keepdims=True) + EPS)
        a_unit = attn_out * a_inv
        hidden = tokens.astype(jnp.float32) + a_unit * gain_attn
        hidden_low = hidden.astype(jnp.bfloat16)
        hidden_all = lax.all_gather(hidden_low, "tensor", axis=0, tiled=True)
        outer_index = lax.axis_index("dp") // inner_count

        def gather_group(shard):
            groups = [[z * inner_count + i for z in range(OUTER)] for i in range(inner_count)]
            part = lax.all_gather(shard, "dp", axis=0, tiled=True, axis_index_groups=groups)
            return lax.all_gather(part, "tensor", axis=0, tiled=True)

        hidden_group = gather_group(hidden_low)
        gate_acts = jnp.dot(hidden_all, w_gate, preferred_element_type=jnp.float32)
        up_acts = jnp.dot(hidden_all, w_up, preferred_element_type=jnp.float32)
        gate_sigmoid = jax.nn.sigmoid(gate_acts)
        inner_low = (gate_acts * gate_sigmoid * up_acts).astype(jnp.bfloat16)
        mlp_out = lax.psum_scatter(
            jnp.dot(inner_low, w_down, preferred_element_type=jnp.float32).astype(jnp.bfloat16),
            "tensor",
            scatter_dimension=0,
            tiled=True,
        ).astype(jnp.float32)
        f_inv = lax.rsqrt(jnp.mean(mlp_out * mlp_out, axis=1, keepdims=True) + EPS)
        f_unit = mlp_out * f_inv
        output = (hidden + f_unit * gain_mlp).astype(jnp.bfloat16)
        grad_output = cotangent.astype(jnp.float32)
        grad_mlp, grad_gain_mlp_part = post_norm_back(grad_output, f_unit, f_inv, gain_mlp)
        grad_mlp_low = grad_mlp.astype(jnp.bfloat16)
        mlp_grad_all = lax.all_gather(grad_mlp_low, "tensor", axis=0, tiled=True)
        mlp_grad_group = gather_group(grad_mlp_low)
        grad_inner = times_t(mlp_grad_all, w_down)
        grad_gate_low = (
            grad_inner * up_acts * gate_sigmoid * (1.0 + gate_acts * (1.0 - gate_sigmoid))
        ).astype(jnp.bfloat16)
        grad_up_low = (grad_inner * gate_acts * gate_sigmoid).astype(jnp.bfloat16)
        part_width = w_gate.shape[1] // OUTER
        gate_part = lax.dynamic_slice_in_dim(w_gate, outer_index * part_width, part_width, 1)
        up_part = lax.dynamic_slice_in_dim(w_up, outer_index * part_width, part_width, 1)
        down_part = lax.dynamic_slice_in_dim(w_down, outer_index * part_width, part_width, 0)
        gate_g = jnp.dot(hidden_group, gate_part, preferred_element_type=jnp.float32)
        up_g = jnp.dot(hidden_group, up_part, preferred_element_type=jnp.float32)
        sig_g = jax.nn.sigmoid(gate_g)
        inner_g = (gate_g * sig_g * up_g).astype(jnp.bfloat16)
        grad_inner_g = times_t(mlp_grad_group, down_part)
        grad_gate_g = (grad_inner_g * up_g * sig_g * (1.0 + gate_g * (1.0 - sig_g))).astype(
            jnp.bfloat16
        )
        grad_up_g = (grad_inner_g * gate_g * sig_g).astype(jnp.bfloat16)
        sum_down = scatter_join(split_cols(t_times(inner_g, mlp_grad_group), inner_count), inner_count, 0)
        sum_gate = scatter_join(split_rows(t_times(hidden_group, grad_gate_g), inner_count), inner_count, 1)
        sum_up = scatter_join(split_rows(t_times(hidden_group, grad_up_g), inner_count), inner_count, 1)
        grad_hidden = grad_output + lax.psum_scatter(
            (times_t(grad_gate_low, w_gate) + times_t(grad_up_low, w_up)).astype(jnp.bfloat16),
            "tensor",
            scatter_dimension=0,
            tiled=True,
        ).astype(jnp.float32)
        grad_attn, grad_gain_attn_part = post_norm_back(grad_hidden, a_unit, a_inv, gain_attn)
        grad_attn_low = grad_attn.astype(jnp.bfloat16)
    attn_grad_all = lax.all_gather(grad_attn_low, "tensor", axis=0, tiled=True)
    grad_mixed = times_t(attn_grad_all, w_out).astype(jnp.bfloat16)
    grad_q_rot, grad_k_rot, grad_values_low = jax.vmap(lambda *a: attend_back(a))(
        queries_low, keys_low, values_heads, segment, log_total, to_heads(grad_mixed)
    )
    grad_q_norm = rotate(grad_q_rot, offsets, -1.0).reshape(row_count, local_width)
    grad_k_norm = rotate(grad_k_rot, offsets, -1.0).reshape(row_count, local_width)
    grad_gain_query_part = jnp.sum(grad_q_norm * q_unit, axis=0)
    grad_gain_key_part = jnp.sum(grad_k_norm * k_unit, axis=0)
    q_scaled = grad_q_norm * gain_query
    k_scaled = grad_k_norm * gain_key
    q_dots, k_dots = lax.psum(
        (jnp.sum(q_scaled * q_unit, axis=1), jnp.sum(k_scaled * k_unit, axis=1)), "tensor"
    )
    grad_queries_low = (q_inv * (q_scaled - q_unit * (q_dots / model_width)[:, None])).astype(
        jnp.bfloat16
    )
    grad_keys_low = (k_inv * (k_scaled - k_unit * (k_dots / model_width)[:, None])).astype(
        jnp.bfloat16
    )
    grad_values_flat = grad_values_low.reshape(row_count, local_width)
    grad_tokens = (
        grad_hidden
        + lax.psum_scatter(
            (
                times_t(grad_queries_low, w_query)
                + times_t(grad_keys_low, w_key)
                + times_t(grad_values_flat, w_value)
            ).astype(jnp.bfloat16),
            "tensor",
            scatter_dimension=0,
            tiled=True,
        ).astype(jnp.float32)
    ).astype(jnp.bfloat16)
    tensor_start = lax.axis_index("tensor") * local_width
    zero_row = jnp.zeros((model_width,), jnp.float32)
    q_full = lax.dynamic_update_slice(zero_row, grad_gain_query_part, (tensor_start,))
    k_full = lax.dynamic_update_slice(zero_row, grad_gain_key_part, (tensor_start,))
    gain_stack = jnp.stack([q_full, k_full, grad_gain_attn_part, grad_gain_mlp_part])
    gain_total = lax.psum(gain_stack, ("dp", "tensor"))
    grad_gain_query = lax.dynamic_slice(gain_total[0], (tensor_start,), (local_width,))
    grad_gain_key = lax.dynamic_slice(gain_total[1], (tensor_start,), (local_width,))
    if fused:
        blocks, _, _ = weight_grads(
            grad_mlp_low,
            group_h,
            group_d,
            w_gate,
            w_up,
            w_down,
            gathered,
            attn_grad_all,
            grad_queries_low,
            grad_keys_low,
            grad_values_flat,
            mixed_low,
        )
        summed_attn = jnp.sum(blocks[:4].astype(jnp.float32), axis=1)
        joined = blocks[4:].astype(jnp.float32)
        width = joined.shape[3]
        summed = (
            summed_attn[1].T,
            summed_attn[2].T,
            summed_attn[0].T,
            summed_attn[3],
            joined[1].transpose(2, 0, 1).reshape(width, -1),
            joined[2].transpose(2, 0, 1).reshape(width, -1),
            joined[0].reshape(-1, width),
        )
    else:
        summed = (
            scatter_sum(split_rows(t_times(gathered, grad_queries_low), inner_count), inner_count),
            scatter_sum(split_rows(t_times(gathered, grad_keys_low), inner_count), inner_count),
            scatter_sum(split_rows(t_times(gathered, grad_values_flat), inner_count), inner_count),
            scatter_sum(split_cols(t_times(mixed_low, attn_grad_all), inner_count), inner_count),
            sum_gate,
            sum_up,
            sum_down,
        )
    return (
        output,
        grad_tokens,
        summed[0],
        summed[1],
        summed[2],
        summed[3],
        summed[4],
        summed[5],
        summed[6],
        grad_gain_query,
        grad_gain_key,
        gain_total[2],
        gain_total[3],
    )


def solution(mesh):
    placed = (
        P(("dp", "tensor"), None),
        P("dp", None),
        P(None, "tensor"),
        P(None, "tensor"),
        P(None, "tensor"),
        P("tensor", None),
        P(None, "tensor"),
        P(None, "tensor"),
        P("tensor", None),
        P("tensor"),
        P("tensor"),
        P(),
        P(),
        P(("dp", "tensor"), None),
    )
    return jax.shard_map(
        body,
        mesh=mesh,
        in_specs=placed,
        out_specs=(
            P(("dp", "tensor"), None),
            P(("dp", "tensor"), None),
            P("dp", "tensor"),
            P("dp", "tensor"),
            P("dp", "tensor"),
            P("tensor", "dp"),
            P("dp", "tensor"),
            P("dp", "tensor"),
            P("tensor", "dp"),
            P("tensor"),
            P("tensor"),
            P(),
            P(),
        ),
        check_vma=False,
    )
```

```python
import math

import jax
import jax.numpy as jnp
from jax import lax
from jax.experimental import pallas as pl
from jax.experimental.pallas import tpu as pltpu
from jax.sharding import PartitionSpec as P

HD = 128
ROW_LEN = 512


EPS = 1e-06
THETA = 500000.0


def rotate(values, offsets, rot_sign):
    half_width = values.shape[-1] // 2
    frequency = jnp.exp(
        jnp.arange(half_width, dtype=jnp.float32) * (-2.0 * math.log(THETA) / values.shape[-1])
    )
    angles = offsets.astype(jnp.float32)[..., None, None] * frequency
    cosines = jnp.cos(angles)
    sine_part = rot_sign * jnp.sin(angles)
    first_half = values[..., :half_width]
    second_half = values[..., half_width:]
    return jnp.concatenate(
        [
            first_half * cosines - second_half * sine_part,
            second_half * cosines + first_half * sine_part,
        ],
        axis=-1,
    )


def row_layout(lengths_row):
    slots = jnp.arange(lengths_row.shape[0], dtype=jnp.int32)
    seq_ends = jnp.sum(
        jnp.where(slots[None, :] <= slots[:, None], lengths_row[None, :], 0), axis=1
    )
    position = jnp.arange(ROW_LEN, dtype=jnp.int32)
    passed = (position[:, None] >= seq_ends[None, :]).astype(jnp.int32)
    segment = jnp.sum(passed, axis=1)
    seq_start = jnp.sum(passed * lengths_row[None, :], axis=1)
    return (segment, position - seq_start)


def allowed_mask(segment):
    position = jnp.arange(segment.shape[0], dtype=jnp.int32)
    return (segment[:, None] == segment[None, :]) & (position[None, :] <= position[:, None])


def times_t(left_mat, right_mat):
    return lax.dot_general(
        left_mat, right_mat, (((1,), (1,)), ((), ())), preferred_element_type=jnp.float32
    )


def t_times(left_mat, right_mat):
    return lax.dot_general(
        left_mat, right_mat, (((0,), (0,)), ((), ())), preferred_element_type=jnp.float32
    )


def masked_scores(queries_low, keys_low, segment):
    scale_factor = 1.0 / math.sqrt(queries_low.shape[-1])
    scores = (
        jnp.einsum("qhd,khd->hqk", queries_low, keys_low, preferred_element_type=jnp.float32)
        * scale_factor
    )
    return jnp.where(allowed_mask(segment)[None], scores, -1e30)


def attend(block_item):
    queries_low, keys_low, values_low, segment = block_item
    scores = masked_scores(queries_low, keys_low, segment)
    row_max = jnp.max(scores, axis=-1, keepdims=True)
    shifted = jnp.exp(scores - row_max)
    row_total = jnp.sum(shifted, axis=-1, keepdims=True)
    attn_weights = (shifted / row_total).astype(jnp.bfloat16)
    mixed = jnp.einsum("hqk,khd->qhd", attn_weights, values_low, preferred_element_type=jnp.float32)
    return (mixed.astype(jnp.bfloat16), (row_max + jnp.log(row_total))[..., 0])


def attend_back(block_item):
    queries_low, keys_low, values_low, segment, log_total, grad_mixed = block_item
    scale_factor = 1.0 / math.sqrt(queries_low.shape[-1])
    scores = masked_scores(queries_low, keys_low, segment)
    attn_weights = jnp.exp(scores - log_total[..., None])
    grad_weights = jnp.einsum(
        "qhd,khd->hqk", grad_mixed, values_low, preferred_element_type=jnp.float32
    )
    row_dots = jnp.sum(attn_weights * grad_weights, axis=-1, keepdims=True)
    grad_scores = (attn_weights * (grad_weights - row_dots)).astype(jnp.bfloat16)
    grad_queries = scale_factor * jnp.einsum(
        "hqk,khd->qhd", grad_scores, keys_low, preferred_element_type=jnp.float32
    )
    grad_keys = scale_factor * jnp.einsum(
        "hqk,qhd->khd", grad_scores, queries_low, preferred_element_type=jnp.float32
    )
    grad_values = jnp.einsum(
        "hqk,qhd->khd",
        attn_weights.astype(jnp.bfloat16),
        grad_mixed,
        preferred_element_type=jnp.float32,
    )
    return (grad_queries, grad_keys, grad_values.astype(jnp.bfloat16))


def post_norm_back(grad_in, unit_rows, inv_scale, gain_vec):
    scaled = grad_in * gain_vec
    mean_dots = jnp.mean(scaled * unit_rows, axis=-1, keepdims=True)
    return (inv_scale * (scaled - unit_rows * mean_dots), jnp.sum(grad_in * unit_rows, axis=0))


OUTER = 4


def swap(value, shift):
    size = lax.axis_size("dp")
    return lax.ppermute(value, "dp", [(d, d ^ shift) for d in range(size)])


def pick(parts, index):
    return lax.dynamic_index_in_dim(parts, index, 0, keepdims=False)


def sum_inner(parts):
    inner = parts.shape[0]
    mine = lax.axis_index("dp") % inner
    total = pick(parts, mine)
    for k in range(1, inner):
        sent = pick(parts, mine ^ k).astype(jnp.bfloat16)
        total = total + swap(sent, k).astype(jnp.float32)
    return total


def trade_outer(parts, inner):
    mine = lax.axis_index("dp") // inner
    got = [(mine, pick(parts, mine))]
    for k in range(1, OUTER):
        got.append((mine ^ k, swap(pick(parts, mine ^ k), k * inner)))
    return got


def split_rows(grad, inner):
    cols = grad.shape[1]
    return grad.reshape(OUTER, inner, -1, cols).transpose(1, 0, 2, 3)


def split_cols(grad, inner):
    rows = grad.shape[0]
    return grad.reshape(rows, OUTER, inner, -1).transpose(2, 1, 0, 3)


def scatter_sum(parts, inner):
    half = sum_inner(parts).astype(jnp.bfloat16)
    got = trade_outer(half, inner)
    return sum(g.astype(jnp.float32) for _, g in got)


def scatter_join(parts, inner, axis):
    half = sum_inner(parts).astype(jnp.bfloat16)
    got = trade_outer(half, inner)
    stack = jnp.zeros((OUTER, *got[0][1].shape), jnp.bfloat16)
    for place, block in got:
        stack = lax.dynamic_update_index_in_dim(stack, block, place, 0)
    joined = jnp.concatenate([stack[z] for z in range(OUTER)], axis=axis)
    return joined.astype(jnp.float32)


MESH = pl.DeviceIdType.MESH
FULL = pl.BlockSpec(memory_space=pl.ANY)


def grads_kernel(
    gp_ref, gqk_ref, gh_in, gm_in, wg_ref, wu_ref, wd_ref, tok_ref, dat_ref, dq_ref, dk_ref, dv_ref, mix_ref,
    gain_ref, out_ref, gh_ref, gm_ref,
    rows_v, wg_v, wu_v, wd_v, lhs_in, lhs_t, acc, full, part,
    gbuf, gin,
    ld_sem, xs_s, xs_r, cs_s, cs_r, ys_s, ys_r, ts_s, ts_r, own_s, gs_s, gs_r,
):
    d = lax.axis_index("dp")
    t = lax.axis_index("tensor")
    z = d // 2
    y = d % 2
    mate = t + 1 - 2 * (t % 2)
    across = (t + 2) % 4
    far = (mate + 2) % 4
    twin = z * 2 + 1 - y

    def remote(src, dst, ss, rs, dd, tt):
        return pltpu.make_async_remote_copy(
            src_ref=src, dst_ref=dst, send_sem=ss, recv_sem=rs, device_id=(dd, tt), device_id_type=MESH
        )

    def peer(k):
        return ((z + k) % 4) * 2 + y

    f = wg_v.shape[1]
    loads = [
        pltpu.make_async_copy(tok_ref, rows_v.at[1, 0], ld_sem.at[0]),
        pltpu.make_async_copy(dat_ref, rows_v.at[1, 1], ld_sem.at[1]),
        pltpu.make_async_copy(dv_ref, lhs_in.at[0], ld_sem.at[2]),
        pltpu.make_async_copy(dq_ref, lhs_in.at[1], ld_sem.at[3]),
        pltpu.make_async_copy(dk_ref, lhs_in.at[2], ld_sem.at[4]),
        pltpu.make_async_copy(mix_ref, lhs_in.at[3], ld_sem.at[5]),
        pltpu.make_async_copy(gh_ref.at[z], rows_v.at[0, 0], ld_sem.at[6]),
        pltpu.make_async_copy(gm_ref.at[z], rows_v.at[0, 1], ld_sem.at[7]),
        pltpu.make_async_copy(wg_ref.at[:, pl.ds(z * f, f)], wg_v, ld_sem.at[8]),
        pltpu.make_async_copy(wu_ref.at[:, pl.ds(z * f, f)], wu_v, ld_sem.at[9]),
        pltpu.make_async_copy(wd_ref.at[pl.ds(z * f, f), :], wd_v, ld_sem.at[10]),
    ]
    for c in loads:
        c.start()

    barrier = pltpu.get_barrier_semaphore()
    for dd, tt in [(peer(1), t), (peer(2), t), (peer(3), t), (twin, t), (d, mate), (d, across)]:
        pl.semaphore_signal(barrier, inc=1, device_id=(dd, tt), device_id_type=MESH)
    pl.semaphore_wait(barrier, 6)

    groups = (gh_ref, gm_ref)

    def forward_x(a, k):
        r = (z + 4 - k) % 4
        return remote(groups[a].at[r, t], groups[a].at[r, t], xs_s.at[a, k - 1], xs_r.at[a, k - 1], d, across)

    def forward_c(a, k, h):
        r = (z + 4 - k) % 4
        q = t if h == 0 else across
        return remote(groups[a].at[r, q], groups[a].at[r, q], cs_s.at[a, k - 1, h], cs_r.at[a, k - 1, h], d, mate)

    order = (1, 3, 2)
    for k in order:
        for a in range(2):
            forward_x(a, k).start()

    def gain_copy(i):
        stage, who = ((0, (peer(1), t)), (0, (peer(2), t)), (0, (peer(3), t)), (1, (twin, t)), (2, (d, across)), (3, (d, mate)))[i]
        return remote(gbuf.at[stage], gin.at[i], gs_s.at[i], gs_r.at[i], *who)

    gbuf[0] = jnp.zeros_like(gbuf[0])
    gbuf[0, 0:2, :] = gp_ref[...]
    gbuf[0, 2:4, 0 : gqk_ref.shape[1]] = gqk_ref[...]
    for i in range(3):
        gain_copy(i).start()

    def gain_step(stage):
        new = gbuf[stage]
        for i in ((0, 1, 2), (3,), (4,), (5,))[stage]:
            gain_copy(i).wait_recv()
            new = new + gin[i]
        if stage < 3:
            gbuf[stage + 1] = new
            gain_copy(stage + 3).start()
        if stage == 1:
            gain_ref[2:4, :] = new[2:4, :]
        if stage == 3:
            gain_ref[0:2, :] = new[0:2, :]

    def swap_y(w):
        return remote(full.at[w, :, 1 - y], part.at[w], ys_s.at[w], ys_r.at[w], twin, t)

    def trade_z(w, k):
        return remote(
            part.at[w, (z + k) % 4], out_ref.at[w, z], ts_s.at[w, k - 1], ts_r.at[w, k - 1], peer(k), t
        )

    def keep(w):
        return pltpu.make_async_copy(part.at[w, z], out_ref.at[w, z], own_s.at[w])

    def finish_y(w):
        swap_y(w).wait()
        for b in range(4):
            part[w, b] = (part[w, b].astype(jnp.float32) + full[w, b, y].astype(jnp.float32)).astype(
                jnp.bfloat16
            )
        for k in (2, 1, 3):
            trade_z(w, k).start()
        keep(w).start()

    width = full.shape[4]

    def attn_grad(w, side):
        lhs_t[0] = lhs_in[w].reshape(lhs_t.shape[2], f).astype(jnp.float32).T.astype(jnp.bfloat16)

        def tile(j, carry):
            cols = pl.ds(pl.multiple_of(j * width, width), width)
            full[w, j // 2, j % 2] = jnp.dot(
                lhs_t[0], rows_v[1, side, :, :, cols].reshape(lhs_t.shape[2], width), preferred_element_type=jnp.float32
            ).astype(jnp.bfloat16)
            return carry

        lax.fori_loop(0, 8, tile, 0)
        swap_y(w).start()

    loads[1].wait()
    loads[5].wait()
    attn_grad(3, 1)
    for i in (0, 2, 3, 4):
        loads[i].wait()
    for w in range(3):
        attn_grad(w, 0)

    step = 256
    tall = (lhs_t.shape[2], acc.shape[2])

    def mlp_row(slot, first):
        def wide(j, carry):
            cols = pl.ds(pl.multiple_of(j * step, step), step)
            g = jnp.dot(rows_v[slot, 0].reshape(tall), wg_v[:, cols], preferred_element_type=jnp.float32)
            u = jnp.dot(rows_v[slot, 0].reshape(tall), wu_v[:, cols], preferred_element_type=jnp.float32)
            di = lax.dot_general(
                rows_v[slot, 1].reshape(tall), wd_v[cols, :], (((1,), (1,)), ((), ())), preferred_element_type=jnp.float32
            )
            sg = jax.nn.sigmoid(g)
            gs = g * sg
            lhs_t[0, cols, :] = (gs * u).T.astype(jnp.bfloat16)
            lhs_t[1, cols, :] = (di * u * sg * (1.0 + g * (1.0 - sg))).T.astype(jnp.bfloat16)
            lhs_t[2, cols, :] = (di * gs).T.astype(jnp.bfloat16)
            return carry

        lax.fori_loop(0, f // step, wide, 0)

        def deep(j, carry):
            cols = pl.ds(pl.multiple_of(j * step, step), step)
            for w, side in ((0, 1), (1, 0), (2, 0)):
                new = jnp.dot(lhs_t[w], rows_v[slot, side, :, :, cols].reshape(lhs_t.shape[2], step), preferred_element_type=jnp.float32)
                if first:
                    acc[w, :, cols] = new
                else:
                    acc[w, :, cols] += new
            return carry

        lax.fori_loop(0, acc.shape[2] // step, deep, 0)

    for i in range(6, 11):
        loads[i].wait()
    mlp_row(0, True)

    def advance_c(k):
        for a in range(2):
            forward_x(a, k).wait_recv()
            for h in range(2):
                forward_c(a, k, h).start()

    def row_loads(k, slot):
        r = (z + 4 - k) % 4
        return [
            pltpu.make_async_copy(groups[a].at[r, q], rows_v.at[slot, a, q], ld_sem.at[a * 4 + q])
            for a in range(2)
            for q in range(4)
        ]

    gain_step(0)
    finish_y(3)
    advance_c(order[0])
    finish_y(0)
    gain_step(1)
    for n, k in enumerate(order):
        slot = (n + 1) % 2
        for a in range(2):
            for h in range(2):
                forward_c(a, k, h).wait_recv()
        copies = row_loads(k, slot)
        for c in copies:
            c.start()
        if n + 1 < 3:
            advance_c(order[n + 1])
        for c in copies:
            c.wait()
        mlp_row(slot, False)
        if n < 2:
            finish_y(n + 1)
            gain_step(n + 2)

    def emit(w):
        def tile(j, carry):
            cols = pl.ds(pl.multiple_of(j * width, width), width)
            full[4 + w, j // 2, j % 2] = acc[w, :, cols].astype(jnp.bfloat16)
            return carry

        lax.fori_loop(0, 8, tile, 0)
        swap_y(4 + w).start()

    for w in range(3):
        emit(w)
    for w in range(3):
        finish_y(4 + w)
    for i in range(6):
        gain_copy(i).wait_send()
    for k in order:
        for a in range(2):
            forward_x(a, k).wait_send()
            for h in range(2):
                forward_c(a, k, h).wait_send()
    for w in range(7):
        keep(w).wait()
        for k in range(1, 4):
            trade_z(w, k).wait()


def weight_grads(gp, gqk, gh, gd, wg, wu, wd, tok, dat, dq, dk, dv, mix):
    rows, width = 4 * tok.shape[1], tok.shape[2]
    f = wg.shape[1] // 4
    block = width // 8
    bf = jnp.bfloat16
    dma = pltpu.SemaphoreType.DMA
    flops = 2 * rows * width * f * (4 + 24)
    return pl.pallas_call(
        grads_kernel,
        name="weight_grads",
        input_output_aliases={2: 2, 3: 3},
        out_shape=(
            jax.ShapeDtypeStruct((4, width), jnp.float32),
            jax.ShapeDtypeStruct((7, 4, f, block), bf),
            jax.ShapeDtypeStruct((4, 4, rows // 4, width), bf),
            jax.ShapeDtypeStruct((4, 4, rows // 4, width), bf),
        ),
        in_specs=[pl.BlockSpec(memory_space=pltpu.VMEM)] * 2 + [FULL] * 11,
        out_specs=(pl.BlockSpec(memory_space=pltpu.VMEM),) + (FULL,) * 3,
        scratch_shapes=[
            pltpu.VMEM((2, 2, 4, rows // 4, width), bf),
            pltpu.VMEM((width, f), bf),
            pltpu.VMEM((width, f), bf),
            pltpu.VMEM((f, width), bf),
            pltpu.VMEM((4, 4, rows // 4, f), bf),
            pltpu.VMEM((3, f, rows), bf),
            pltpu.VMEM((3, f, width), jnp.float32),
            pltpu.VMEM((7, 4, 2, f, block), bf),
            pltpu.VMEM((7, 4, f, block), bf),
            pltpu.VMEM((4, 8, width), jnp.float32),
            pltpu.VMEM((6, 8, width), jnp.float32),
            dma((11,)),
            dma((2, 3)),
            dma((2, 3)),
            dma((2, 3, 2)),
            dma((2, 3, 2)),
            dma((7,)),
            dma((7,)),
            dma((7, 3)),
            dma((7, 3)),
            dma((7,)),
            dma((6,)),
            dma((6,)),
        ],
        compiler_params=pltpu.CompilerParams(
            collective_id=0, has_side_effects=True, vmem_limit_bytes=60 * 1024 * 1024
        ),
        cost_estimate=pl.CostEstimate(flops=flops, bytes_accessed=60 * 1024 * 1024, transcendentals=0),
    )(gp, gqk, gh, gd, wg, wu, wd, tok, dat, dq, dk, dv, mix)


def far_copy(src, dst, ss, rs, dd, tt):
    return pltpu.make_async_remote_copy(
        src_ref=src, dst_ref=dst, send_sem=ss, recv_sem=rs, device_id=(dd, tt), device_id_type=MESH
    )


def mean_inv(values):
    return lax.rsqrt(jnp.mean(values * values, axis=1, keepdims=True) + EPS)


def mlp_kernel(
    att_ref, tok_ref, cot_ref, ga_ref, gm_ref, wg_ref, wu_ref, wd_ref,
    out_ref, ghid_ref, dat_ref, dml_ref, gain_ref, gh_ref, gd_ref,
    wg_v, wu_v, wd_v, slope_g, slope_u, own, oth, low_a, low_b, pown, pmate, xsend, xrecv, qown, qmate, hid,
    w_sem, as_s, as_r, ax_s, ax_r, af_s, af_r, ps_s, ps_r, px_s, px_r, pq_s, pq_r, zs_s, zs_r, st_sem,
):
    d = lax.axis_index("dp")
    t = lax.axis_index("tensor")
    z = d // 2
    y = d % 2
    c = t % 2
    chip = t // 2
    mate = t + 1 - 2 * c
    across = (t + 2) % 4
    shard, width = att_ref.shape
    ff = wg_v.shape[1]
    bf = jnp.bfloat16
    f32 = jnp.float32
    tile = 512
    tiles = ff // tile

    def wcopy(i, j):
        cols = pl.ds(j * tile, tile)
        if i == 0:
            return pltpu.make_async_copy(wg_ref.at[:, cols], wg_v.at[:, cols], w_sem.at[0, j])
        if i == 1:
            return pltpu.make_async_copy(wu_ref.at[:, cols], wu_v.at[:, cols], w_sem.at[1, j])
        return pltpu.make_async_copy(wd_ref.at[cols, :], wd_v.at[cols, :], w_sem.at[2, j])

    for j in range(tiles):
        wcopy(0, j).start()
        wcopy(1, j).start()
    for j in range(tiles):
        wcopy(2, j).start()

    barrier = pltpu.get_barrier_semaphore()
    peers = [((z + k) % 4) * 2 + y for k in range(1, 4)]
    for dd, tt in [(peers[0], t), (peers[1], t), (peers[2], t), (d, mate), (d, across)]:
        pl.semaphore_signal(barrier, inc=1, device_id=(dd, tt), device_id_type=MESH)
    pl.semaphore_wait(barrier, 5)

    def send_mate(p):
        return far_copy(own.at[p, c], own.at[p, c], as_s.at[p], as_r.at[p], d, mate)

    def send_across(p):
        return far_copy(own.at[p, c], oth.at[p, c], ax_s.at[p], ax_r.at[p], d, across)

    def forward(p):
        return far_copy(oth.at[p, c], oth.at[p, c], af_s.at[p], af_r.at[p], d, mate)

    half = width // 2

    def part_mate(p, h):
        return far_copy(
            pown.at[p, h, 1 - c], pmate.at[p, h], ps_s.at[p, h], ps_r.at[p, h], d, mate
        )

    def part_across(p, h):
        return far_copy(xsend.at[p, h], xrecv.at[p, h], px_s.at[p, h], px_r.at[p, h], d, across)

    def part_own(p):
        return far_copy(qown.at[p, 1 - c], qmate.at[p], pq_s.at[p], pq_r.at[p], d, mate)

    def gather_z(k):
        return far_copy(
            own.at[0, c], gh_ref.at[z, t], zs_s.at[k - 1], zs_r.at[k - 1], ((z + k) % 4) * 2 + y, t
        )

    def store_row(p, ref):
        mine = ref.at[z]
        return [
            pltpu.make_async_copy(own.at[p, 0], mine.at[chip * 2], st_sem.at[p, 0]),
            pltpu.make_async_copy(own.at[p, 1], mine.at[chip * 2 + 1], st_sem.at[p, 1]),
            pltpu.make_async_copy(oth.at[p, 0], mine.at[2 - chip * 2], st_sem.at[p, 2]),
            pltpu.make_async_copy(oth.at[p, 1], mine.at[3 - chip * 2], st_sem.at[p, 3]),
        ]

    two = 2 * shard

    def forward_in(lhs, base, wait):
        for j in range(tiles):
            if wait:
                wcopy(0, j).wait()
                wcopy(1, j).wait()
            cols = pl.ds(j * tile, tile)
            for s in range(2):
                rows = pl.ds(s * shard, shard)
                g = jnp.dot(lhs[s], wg_v[:, cols], preferred_element_type=f32)
                u = jnp.dot(lhs[s], wu_v[:, cols], preferred_element_type=f32)
                sg = jax.nn.sigmoid(g)
                gs = g * sg
                low_a[rows, cols] = (gs * u).astype(bf)
                slope_u[pl.ds(base + s * shard, shard), cols] = gs
                slope_g[pl.ds(base + s * shard, shard), cols] = u * sg * (1.0 + g * (1.0 - sg))

    def backward_in(lhs, base, wait):
        for j in range(tiles):
            cols = pl.ds(j * tile, tile)
            for s in range(2):
                rows = pl.ds(s * shard, shard)
                di = lax.dot_general(
                    lhs[s], wd_v[cols, :], (((1,), (1,)), ((), ())), preferred_element_type=f32
                )
                low_a[rows, cols] = (di * slope_g[pl.ds(base + s * shard, shard), cols]).astype(bf)
                low_b[rows, cols] = (di * slope_u[pl.ds(base + s * shard, shard), cols]).astype(bf)

    def result(p, cols):
        if p == 0:
            return jnp.dot(low_a[...], wd_v[:, cols], preferred_element_type=f32)
        nt = (((1,), (1,)), ((), ()))
        return lax.dot_general(
            low_a[...], wg_v[cols, :], nt, preferred_element_type=f32
        ) + lax.dot_general(low_b[...], wu_v[cols, :], nt, preferred_element_type=f32)

    def run(p, first, wait):
        send_across(p).start()
        send_mate(p).start()
        if p == 0:
            for k in (1, 3, 2):
                gather_z(k).start()
        send_mate(p).wait_recv()
        first(own.at[p], 0, wait)
        if wait:
            for j in range(tiles):
                wcopy(2, j).wait()
        for j in range(width // tile):
            cols = pl.ds(j * tile, tile)
            new = result(p, cols).astype(bf)
            for s in range(2):
                qown[p, s, :, cols] = new[s * shard : (s + 1) * shard]
        part_own(p).start()
        send_across(p).wait_recv()
        forward(p).start()
        forward(p).wait_recv()
        for cp in store_row(p, gh_ref if p == 0 else gd_ref):
            cp.start()
        first(oth.at[p], two, False)
        for h in range(2):
            for j in range(half // tile):
                new = result(p, pl.ds(h * half + j * tile, tile)).astype(bf)
                for s in range(2):
                    pown[p, h, s, :, pl.ds(j * tile, tile)] = new[s * shard : (s + 1) * shard]
            part_mate(p, h).start()
            part_mate(p, h).wait_recv()
            xsend[p, h] = (pown[p, h, c].astype(f32) + pmate[p, h].astype(f32)).astype(bf)
            part_across(p, h).start()
        part_own(p).wait_recv()
        sums = []
        for h in range(2):
            part_across(p, h).wait_recv()
            cols = slice(h * half, (h + 1) * half)
            sums.append(
                qown[p, c, :, cols].astype(f32) + qmate[p, :, cols].astype(f32) + xrecv[p, h].astype(f32)
            )
        return jnp.concatenate(sums, axis=1)

    att = att_ref[...]
    hid[...] = tok_ref[...].astype(f32) + att * mean_inv(att) * ga_ref[...]
    own[0, c] = hid[...].astype(bf)
    mlp = run(0, forward_in, True)
    rf = mean_inv(mlp)
    fh = mlp * rf
    gy = cot_ref[...].astype(f32)
    out_ref[...] = (hid[...] + fh * gm_ref[...]).astype(bf)
    scaled = gy * gm_ref[...]
    dm = (rf * (scaled - fh * jnp.mean(scaled * fh, axis=1, keepdims=True))).astype(bf)
    gain_ref[1:2, :] = jnp.sum(gy * fh, axis=0, keepdims=True)
    own[1, c] = dm
    dml_ref[...] = dm
    back = run(1, backward_in, False)
    gh = cot_ref[...].astype(f32) + back
    ghid_ref[...] = gh
    ra = mean_inv(att_ref[...])
    ah = att_ref[...] * ra
    gain_ref[0:1, :] = jnp.sum(gh * ah, axis=0, keepdims=True)
    scaled = gh * ga_ref[...]
    dat_ref[...] = (ra * (scaled - ah * jnp.mean(scaled * ah, axis=1, keepdims=True))).astype(bf)

    for p in range(2):
        send_across(p).wait_send()
        send_mate(p).wait_send()
        forward(p).wait_send()
        part_own(p).wait_send()
        for h in range(2):
            part_mate(p, h).wait_send()
            part_across(p, h).wait_send()
        for cp in store_row(p, gh_ref if p == 0 else gd_ref):
            cp.wait()
    for k in range(1, 4):
        gather_z(k).wait()


def mlp_both(att, tok, cot, ga, gm, wg, wu, wd):
    shard, width = tok.shape
    ff = wg.shape[1]
    bf = jnp.bfloat16
    f32 = jnp.float32
    dma = pltpu.SemaphoreType.DMA
    half = width // 2
    vm = pl.BlockSpec(memory_space=pltpu.VMEM)
    shape = jax.ShapeDtypeStruct
    return pl.pallas_call(
        mlp_kernel,
        name="feed_forward",
        out_shape=(
            shape((shard, width), bf),
            shape((shard, width), f32),
            shape((shard, width), bf),
            shape((shard, width), bf),
            shape((2, width), f32),
            shape((4, 4, shard, width), bf),
            shape((4, 4, shard, width), bf),
        ),
        in_specs=[vm] * 5 + [FULL] * 3,
        out_specs=(vm,) * 5 + (FULL,) * 2,
        scratch_shapes=[
            pltpu.VMEM((width, ff), bf),
            pltpu.VMEM((width, ff), bf),
            pltpu.VMEM((ff, width), bf),
            pltpu.VMEM((4 * shard, ff), f32),
            pltpu.VMEM((4 * shard, ff), f32),
            pltpu.VMEM((2, 2, shard, width), bf),
            pltpu.VMEM((2, 2, shard, width), bf),
            pltpu.VMEM((2 * shard, ff), bf),
            pltpu.VMEM((2 * shard, ff), bf),
            pltpu.VMEM((2, 2, 2, shard, half), bf),
            pltpu.VMEM((2, 2, shard, half), bf),
            pltpu.VMEM((2, 2, shard, half), bf),
            pltpu.VMEM((2, 2, shard, half), bf),
            pltpu.VMEM((2, 2, shard, width), bf),
            pltpu.VMEM((2, shard, width), bf),
            pltpu.VMEM((shard, width), f32),
            dma((3, ff // 512)),
            dma((2,)), dma((2,)), dma((2,)), dma((2,)), dma((2,)), dma((2,)),
            dma((2, 2)), dma((2, 2)), dma((2, 2)), dma((2, 2)),
            dma((2,)), dma((2,)),
            dma((3,)), dma((3,)),
            dma((2, 4)),
        ],
        compiler_params=pltpu.CompilerParams(
            collective_id=1, has_side_effects=True, vmem_limit_bytes=60 * 1024 * 1024
        ),
        cost_estimate=pl.CostEstimate(
            flops=2 * 6 * 4 * shard * width * ff, bytes_accessed=40 * 1024 * 1024, transcendentals=4 * shard * ff
        ),
    )(att, tok, cot, ga.reshape(1, -1), gm.reshape(1, -1), wg, wu, wd)


NT = (((1,), (1,)), ((), ()))
TN = (((0,), (0,)), ((), ()))


def places():
    d = lax.axis_index("dp")
    t = lax.axis_index("tensor")
    c = t % 2
    return d, t, d // 2, d % 2, c, t // 2, t + 1 - 2 * c, (t + 2) % 4


def greet(targets):
    barrier = pltpu.get_barrier_semaphore()
    for dd, tt in targets:
        pl.semaphore_signal(barrier, inc=1, device_id=(dd, tt), device_id_type=MESH)
    pl.semaphore_wait(barrier, len(targets))


def to_rows(column):
    n = column.shape[0]
    return jnp.broadcast_to(column, (n, n)).T[0:8, :]


def to_column(rows):
    n = rows.shape[1]
    return jnp.broadcast_to(rows[0:1, :], (n, n)).T[:, 0:1]


def attend_kernel(
    tok_ref, cos_ref, sin_ref, segc_ref, segr_ref, gq_ref, gk_ref, wq_ref, wk_ref, wv_ref, wo_ref,
    att_ref, tall_ref, qh_ref, kh_ref, qr_ref, kr_ref, v_ref, mix_ref, p_ref, inv_ref,
    w_v, wo_v, tall, raw, rot, val, mixed, prob, stat, stat_in, pown, pmate, xsend, xrecv, qown, qmate,
    w_sem, as_s, as_r, ss_s, ss_r, ps_s, ps_r, px_s, px_r, pq_s, pq_r, st_sem,
):
    d, t, z, y, c, chip, mate, across = places()
    far = (mate + 2) % 4
    shard, width = tok_ref.shape
    local = w_v.shape[2]
    bf = jnp.bfloat16
    f32 = jnp.float32
    heads = local // HD
    weights = [
        pltpu.make_async_copy(r, w_v.at[i], w_sem.at[i]) for i, r in enumerate((wq_ref, wk_ref, wv_ref))
    ] + [pltpu.make_async_copy(wo_ref, wo_v, w_sem.at[3])]
    for cp in weights:
        cp.start()
    tall[t] = tok_ref[...]
    greet([(d, mate), (d, across), (d, far)])

    send_x = far_copy(tall.at[t], tall.at[t], as_s.at[0], as_r.at[0], d, across)
    send_m = far_copy(tall.at[t], tall.at[t], as_s.at[1], as_r.at[1], d, mate)
    forward = far_copy(tall.at[across], tall.at[across], as_s.at[2], as_r.at[2], d, mate)
    send_x.start()
    send_m.start()

    def project(first):
        rows = tall[pl.ds(first, 2)].reshape(2 * shard, width)
        for i in range(3):
            new = jnp.dot(rows, w_v[i], preferred_element_type=f32).reshape(2, shard, local)
            if i == 2:
                val[pl.ds(first, 2)] = new.astype(bf)
            else:
                raw[i, pl.ds(first, 2)] = new
                for s in range(2):
                    stat[first + s, i * 8 : i * 8 + 8, :] = to_rows(
                        jnp.sum(new[s] * new[s], axis=1, keepdims=True)
                    )

    here = chip * 2
    there = 2 - chip * 2
    for cp in weights[:3]:
        cp.wait()
    send_m.wait_recv()
    project(here)
    send_x.wait_recv()
    forward.start()
    forward.wait_recv()
    project(there)

    stats = [
        far_copy(stat, stat_in.at[i], ss_s.at[i], ss_r.at[i], d, who)
        for i, who in enumerate((mate, across, far))
    ]
    for cp in stats:
        cp.start()
    stores = [
        pltpu.make_async_copy(tall, tall_ref, st_sem.at[0]),
        pltpu.make_async_copy(val, v_ref, st_sem.at[1]),
    ]
    for cp in stores:
        cp.start()
    for cp in stats:
        cp.wait_recv()

    for q in range(4):
        inv = lax.rsqrt((stat[q] + stat_in[0, q] + stat_in[1, q] + stat_in[2, q]) / width + EPS)
        inv_ref[q] = inv
        for i, gain in ((0, gq_ref), (1, gk_ref)):
            unit = raw[i, q] * to_column(inv[i * 8 : i * 8 + 8])
            raw[i, q] = unit
            unit = unit * gain[...]
            for h in range(heads):
                cols = slice(h * HD, (h + 1) * HD)
                one = unit[:, cols]
                rot[i, q, :, cols] = (
                    one * cos_ref[q] + pltpu.roll(one, HD // 2, 1) * sin_ref[q]
                ).astype(bf)
    more = [
        pltpu.make_async_copy(raw.at[0], qh_ref, st_sem.at[2]),
        pltpu.make_async_copy(raw.at[1], kh_ref, st_sem.at[3]),
        pltpu.make_async_copy(rot.at[0], qr_ref, st_sem.at[4]),
        pltpu.make_async_copy(rot.at[1], kr_ref, st_sem.at[5]),
    ]
    for cp in more:
        cp.start()
    stores += more

    scale = 1.0 / math.sqrt(HD)
    total = 4 * shard

    def mix(first, n):
        ids = first * shard + lax.broadcasted_iota(jnp.int32, (2 * shard, total), 0)
        keys = lax.broadcasted_iota(jnp.int32, (2 * shard, total), 1)
        same = segc_ref[pl.ds(first, 2)].reshape(2 * shard, 1) == segr_ref[...]
        ok = same & (keys <= ids)
        for h in range(heads):
            cols = slice(h * HD, (h + 1) * HD)
            s = lax.dot_general(
                rot[0, pl.ds(first, 2), :, cols].reshape(2 * shard, HD),
                rot[1, :, :, cols].reshape(total, HD),
                NT,
                preferred_element_type=f32,
            )
            s = jnp.where(ok, s * scale, -1e30)
            e = jnp.exp(s - jnp.max(s, axis=1, keepdims=True))
            p = e / jnp.sum(e, axis=1, keepdims=True)
            prob[pl.ds(first, 2), h] = p.reshape(2, shard, total)
            mixed[pl.ds(first, 2), :, cols] = (
                jnp.dot(p.astype(bf), val[:, :, cols].reshape(total, HD), preferred_element_type=f32)
                .astype(bf)
                .reshape(2, shard, HD)
            )
        cp = pltpu.make_async_copy(prob.at[pl.ds(first, 2)], p_ref.at[pl.ds(first, 2)], st_sem.at[6 + n])
        cp.start()
        stores.append(cp)

    half = width // 2
    tile = 512

    def part_mate(h):
        return far_copy(pown.at[h, 1 - c], pmate.at[h], ps_s.at[h], ps_r.at[h], d, mate)

    def part_across(h):
        return far_copy(xsend.at[h], xrecv.at[h], px_s.at[h], px_r.at[h], d, across)

    part_own = far_copy(qown.at[1 - c], qmate, pq_s, pq_r, d, mate)

    mix(there, 0)
    weights[3].wait()
    for h in range(2):
        for j in range(half // tile):
            new = jnp.dot(
                mixed[pl.ds(there, 2)].reshape(2 * shard, local),
                wo_v[:, pl.ds(h * half + j * tile, tile)],
                preferred_element_type=f32,
            ).astype(bf)
            pown[h, :, :, pl.ds(j * tile, tile)] = new.reshape(2, shard, tile)
        part_mate(h).start()
    for h in range(2):
        part_mate(h).wait_recv()
        xsend[h] = (pown[h, c].astype(f32) + pmate[h].astype(f32)).astype(bf)
        part_across(h).start()
    mix(here, 1)
    for j in range(width // tile):
        new = jnp.dot(
            mixed[pl.ds(here, 2)].reshape(2 * shard, local),
            wo_v[:, pl.ds(j * tile, tile)],
            preferred_element_type=f32,
        ).astype(bf)
        qown[:, :, pl.ds(j * tile, tile)] = new.reshape(2, shard, tile)
    part_own.start()
    cp = pltpu.make_async_copy(mixed, mix_ref, st_sem.at[8])
    cp.start()
    stores.append(cp)
    part_own.wait_recv()
    for h in range(2):
        part_across(h).wait_recv()
        cols = slice(h * half, (h + 1) * half)
        att_ref[:, cols] = (
            qown[c, :, cols].astype(f32) + qmate[:, cols].astype(f32) + xrecv[h].astype(f32)
        )
    for cp in stores:
        cp.wait()
    for cp in [send_x, send_m, forward, part_own] + stats:
        cp.wait_send()
    for h in range(2):
        part_mate(h).wait_send()
        part_across(h).wait_send()


def attend_both(tok, cos, sin, seg, gq, gk, wq, wk, wv, wo):
    shard, width = tok.shape
    local = wq.shape[1]
    heads = local // HD
    bf = jnp.bfloat16
    f32 = jnp.float32
    dma = pltpu.SemaphoreType.DMA
    vm = pl.BlockSpec(memory_space=pltpu.VMEM)
    shape = jax.ShapeDtypeStruct
    half = width // 2
    total = 4 * shard
    return pl.pallas_call(
        attend_kernel,
        name="attend_forward",
        out_shape=(
            shape((shard, width), f32),
            shape((4, shard, width), bf),
            shape((4, shard, local), f32),
            shape((4, shard, local), f32),
            shape((4, shard, local), bf),
            shape((4, shard, local), bf),
            shape((4, shard, local), bf),
            shape((4, shard, local), bf),
            shape((4, heads, shard, total), f32),
            shape((4, 16, shard), f32),
        ),
        in_specs=[vm] * 7 + [FULL] * 4,
        out_specs=(vm,) + (FULL,) * 8 + (vm,),
        scratch_shapes=[
            pltpu.VMEM((3, width, local), bf),
            pltpu.VMEM((local, width), bf),
            pltpu.VMEM((4, shard, width), bf),
            pltpu.VMEM((2, 4, shard, local), f32),
            pltpu.VMEM((2, 4, shard, local), bf),
            pltpu.VMEM((4, shard, local), bf),
            pltpu.VMEM((4, shard, local), bf),
            pltpu.VMEM((4, heads, shard, total), f32),
            pltpu.VMEM((4, 16, shard), f32),
            pltpu.VMEM((3, 4, 16, shard), f32),
            pltpu.VMEM((2, 2, shard, half), bf),
            pltpu.VMEM((2, shard, half), bf),
            pltpu.VMEM((2, shard, half), bf),
            pltpu.VMEM((2, shard, half), bf),
            pltpu.VMEM((2, shard, width), bf),
            pltpu.VMEM((shard, width), bf),
            dma((4,)),
            dma((3,)), dma((3,)), dma((3,)), dma((3,)),
            dma((2,)), dma((2,)), dma((2,)), dma((2,)),
            dma(()), dma(()),
            dma((9,)),
        ],
        compiler_params=pltpu.CompilerParams(
            collective_id=2, has_side_effects=True, vmem_limit_bytes=56 * 1024 * 1024
        ),
        cost_estimate=pl.CostEstimate(
            flops=2 * total * width * local * 4, bytes_accessed=24 * 1024 * 1024, transcendentals=heads * total * total
        ),
    )(
        tok, cos.reshape(4, shard, HD), sin.reshape(4, shard, HD), seg.reshape(4, shard, 1), seg.reshape(1, total),
        gq.reshape(1, -1), gk.reshape(1, -1), wq, wk, wv, wo,
    )


def attend_back_kernel(
    dat_ref, ghid_ref, cos_ref, sin_ref, gq_ref, gk_ref, inv_ref,
    wq_ref, wk_ref, wv_ref, wo_ref, qh_ref, kh_ref, qr_ref, kr_ref, v_ref, p_ref, dml_ref, gd_in,
    gt_ref, gain_ref, dall_ref, dq_ref, dk_ref, dv_ref, gd_ref,
    w_v, wo_v, dall, unit, rot, val, dmix, prob, scaled, low, stat, stat_in, pown, pmate, xsend, xrecv, qown, qmate,
    w_sem, as_s, as_r, ss_s, ss_r, ps_s, ps_r, px_s, px_r, pq_s, pq_r, zs_s, zs_r, st_sem,
):
    d, t, z, y, c, chip, mate, across = places()
    far = (mate + 2) % 4
    shard, width = dat_ref.shape
    local = w_v.shape[2]
    bf = jnp.bfloat16
    f32 = jnp.float32
    heads = local // HD
    total = 4 * shard
    sources = (wo_ref, v_ref, p_ref, qr_ref, kr_ref, qh_ref, kh_ref, wq_ref, wk_ref, wv_ref)
    homes = (wo_v, val, prob, rot.at[0], rot.at[1], unit.at[0], unit.at[1], w_v.at[0], w_v.at[1], w_v.at[2])
    loads = [pltpu.make_async_copy(a, b, w_sem.at[i]) for i, (a, b) in enumerate(zip(sources, homes))]
    for cp in loads:
        cp.start()
    dall[t] = dat_ref[...]
    peers = [((z + k) % 4) * 2 + y for k in range(1, 4)]
    greet([(d, mate), (d, across), (d, far)] + [(p, t) for p in peers])

    send_x = far_copy(dall.at[t], dall.at[t], as_s.at[0], as_r.at[0], d, across)
    send_m = far_copy(dall.at[t], dall.at[t], as_s.at[1], as_r.at[1], d, mate)
    forward = far_copy(dall.at[across], dall.at[across], as_s.at[2], as_r.at[2], d, mate)
    send_x.start()
    send_m.start()
    gather = [
        far_copy(dml_ref, gd_ref.at[z, t], zs_s.at[k], zs_r.at[k], peers[k], t) for k in (0, 2, 1)
    ]
    for cp in gather:
        cp.start()

    def project(first):
        rows = dall[pl.ds(first, 2)].reshape(2 * shard, width)
        dmix[pl.ds(first, 2)] = (
            lax.dot_general(rows, wo_v[...], NT, preferred_element_type=f32).astype(bf).reshape(2, shard, local)
        )

    here = chip * 2
    there = 2 - chip * 2
    loads[0].wait()
    send_m.wait_recv()
    project(here)
    for cp in loads[1:]:
        cp.wait()
    send_x.wait_recv()
    forward.start()
    forward.wait_recv()
    project(there)
    stores = [pltpu.make_async_copy(dall, dall_ref, st_sem.at[0])]
    stores[0].start()

    scale = 1.0 / math.sqrt(HD)
    cos = cos_ref[...].reshape(total, HD)
    sin = sin_ref[...].reshape(total, HD)
    dots = [jnp.zeros((total, 1), f32), jnp.zeros((total, 1), f32)]
    for h in range(heads):
        cols = slice(h * HD, (h + 1) * HD)
        dm = dmix[:, :, cols].reshape(total, HD)
        p = prob[:, h].reshape(total, total)
        dp = lax.dot_general(dm, val[:, :, cols].reshape(total, HD), NT, preferred_element_type=f32)
        ds = (p * (dp - jnp.sum(p * dp, axis=1, keepdims=True))).astype(bf)
        low[2, :, :, cols] = (
            lax.dot_general(p.astype(bf), dm, TN, preferred_element_type=f32).astype(bf).reshape(4, shard, HD)
        )
        back = (
            jnp.dot(ds, rot[1, :, :, cols].reshape(total, HD), preferred_element_type=f32) * scale,
            lax.dot_general(ds, rot[0, :, :, cols].reshape(total, HD), TN, preferred_element_type=f32) * scale,
        )
        for i, gain in ((0, gq_ref), (1, gk_ref)):
            g = back[i]
            g = g * cos - pltpu.roll(g, HD // 2, 1) * sin
            u = unit[i, :, :, cols].reshape(total, HD)
            prod = g * u
            gain_ref[i : i + 1, cols] = jnp.sum(prod, axis=0, keepdims=True)
            dots[i] = dots[i] + jnp.sum(prod * gain[:, cols], axis=1, keepdims=True)
            scaled[i, :, :, cols] = (g * gain[:, cols]).reshape(4, shard, HD)
    for q in range(4):
        for i in range(2):
            stat[q, i * 8 : i * 8 + 8, :] = to_rows(dots[i][q * shard : (q + 1) * shard])
    stats = [
        far_copy(stat, stat_in.at[i], ss_s.at[i], ss_r.at[i], d, who)
        for i, who in enumerate((mate, across, far))
    ]
    for cp in stats:
        cp.start()
    for cp in stats:
        cp.wait_recv()

    def finish(first):
        for s in range(2):
            q = first + s
            mean = (stat[q] + stat_in[0, q] + stat_in[1, q] + stat_in[2, q]) / width
            inv = inv_ref[q]
            for i in range(2):
                low[i, q] = (
                    to_column(inv[i * 8 : i * 8 + 8])
                    * (scaled[i, q] - unit[i, q] * to_column(mean[i * 8 : i * 8 + 8]))
                ).astype(bf)

    half = width // 2
    tile = 512

    def part_mate(h):
        return far_copy(pown.at[h, 1 - c], pmate.at[h], ps_s.at[h], ps_r.at[h], d, mate)

    def part_across(h):
        return far_copy(xsend.at[h], xrecv.at[h], px_s.at[h], px_r.at[h], d, across)

    part_own = far_copy(qown.at[1 - c], qmate, pq_s, pq_r, d, mate)

    def result(first, start):
        new = None
        for i in range(3):
            one = lax.dot_general(
                low[i, pl.ds(first, 2)].reshape(2 * shard, local),
                w_v[i, pl.ds(start, tile), :],
                NT,
                preferred_element_type=f32,
            )
            new = one if new is None else new + one
        return new.astype(bf).reshape(2, shard, tile)

    finish(there)
    for h in range(2):
        for j in range(half // tile):
            pown[h, :, :, pl.ds(j * tile, tile)] = result(there, h * half + j * tile)
        part_mate(h).start()
        part_mate(h).wait_recv()
        xsend[h] = (pown[h, c].astype(f32) + pmate[h].astype(f32)).astype(bf)
        part_across(h).start()
    finish(here)
    more = [
        pltpu.make_async_copy(low.at[i], r, st_sem.at[1 + i]) for i, r in enumerate((dq_ref, dk_ref, dv_ref))
    ]
    for cp in more:
        cp.start()
    stores += more
    for j in range(width // tile):
        qown[:, :, pl.ds(j * tile, tile)] = result(here, j * tile)
    part_own.start()
    part_own.wait_recv()
    for h in range(2):
        part_across(h).wait_recv()
        cols = slice(h * half, (h + 1) * half)
        gt_ref[:, cols] = (
            ghid_ref[:, cols]
            + (qown[c, :, cols].astype(f32) + qmate[:, cols].astype(f32) + xrecv[h].astype(f32))
        ).astype(bf)
    for cp in stores:
        cp.wait()
    for cp in [send_x, send_m, forward, part_own] + stats:
        cp.wait_send()
    for h in range(2):
        part_mate(h).wait_send()
        part_across(h).wait_send()
    for cp in gather:
        cp.wait()


def attend_back_both(dat, ghid, cos, sin, gq, gk, inv, wq, wk, wv, wo, qh, kh, qr, kr, v, p, dml, gd):
    shard, width = dat.shape
    local = wq.shape[1]
    heads = local // HD
    bf = jnp.bfloat16
    f32 = jnp.float32
    dma = pltpu.SemaphoreType.DMA
    vm = pl.BlockSpec(memory_space=pltpu.VMEM)
    shape = jax.ShapeDtypeStruct
    half = width // 2
    total = 4 * shard
    return pl.pallas_call(
        attend_back_kernel,
        name="attend_backward",
        out_shape=(
            shape((shard, width), bf),
            shape((2, local), f32),
            shape((4, shard, width), bf),
            shape((4, shard, local), bf),
            shape((4, shard, local), bf),
            shape((4, shard, local), bf),
            shape(gd.shape, bf),
        ),
        in_specs=[vm] * 7 + [FULL] * 12,
        out_specs=(vm,) * 2 + (FULL,) * 5,
        input_output_aliases={18: 6},
        scratch_shapes=[
            pltpu.VMEM((3, width, local), bf),
            pltpu.VMEM((local, width), bf),
            pltpu.VMEM((4, shard, width), bf),
            pltpu.VMEM((2, 4, shard, local), f32),
            pltpu.VMEM((2, 4, shard, local), bf),
            pltpu.VMEM((4, shard, local), bf),
            pltpu.VMEM((4, shard, local), bf),
            pltpu.VMEM((4, heads, shard, total), f32),
            pltpu.VMEM((2, 4, shard, local), f32),
            pltpu.VMEM((3, 4, shard, local), bf),
            pltpu.VMEM((4, 16, shard), f32),
            pltpu.VMEM((3, 4, 16, shard), f32),
            pltpu.VMEM((2, 2, shard, half), bf),
            pltpu.VMEM((2, shard, half), bf),
            pltpu.VMEM((2, shard, half), bf),
            pltpu.VMEM((2, shard, half), bf),
            pltpu.VMEM((2, shard, width), bf),
            pltpu.VMEM((shard, width), bf),
            dma((10,)),
            dma((3,)), dma((3,)), dma((3,)), dma((3,)),
            dma((2,)), dma((2,)), dma((2,)), dma((2,)),
            dma(()), dma(()), dma((3,)), dma((3,)),
            dma((4,)),
        ],
        compiler_params=pltpu.CompilerParams(
            collective_id=3, has_side_effects=True, vmem_limit_bytes=56 * 1024 * 1024
        ),
        cost_estimate=pl.CostEstimate(
            flops=2 * total * width * local * 4 + 10 * heads * total * total * HD,
            bytes_accessed=24 * 1024 * 1024,
            transcendentals=0,
        ),
    )(
        dat, ghid, cos.reshape(4, shard, HD), sin.reshape(4, shard, HD), gq.reshape(1, -1), gk.reshape(1, -1), inv,
        wq, wk, wv, wo, qh, kh, qr, kr, v, p, dml, gd,
    )


def place_kernel(b_ref, q_ref, k_ref, v_ref, o_ref, g_ref, u_ref, d_ref):
    f32 = jnp.float32
    f = b_ref.shape[2]
    for w, ref in ((0, v_ref), (1, q_ref), (2, k_ref), (3, o_ref)):
        new = b_ref[w, 0].astype(f32)
        for i in range(1, 4):
            new = new + b_ref[w, i].astype(f32)
        ref[...] = new if w == 3 else new.T
    for i in range(4):
        d_ref[i * f : (i + 1) * f, :] = b_ref[4, i].astype(f32)
        g_ref[:, i * f : (i + 1) * f] = b_ref[5, i].astype(f32).T
        u_ref[:, i * f : (i + 1) * f] = b_ref[6, i].astype(f32).T


def place_grads(blocks):
    _, _, f, block = blocks.shape
    f32 = jnp.float32
    vm = pl.BlockSpec(memory_space=pltpu.VMEM)
    shape = jax.ShapeDtypeStruct
    return pl.pallas_call(
        place_kernel,
        name="place_grads",
        out_shape=(
            shape((block, f), f32),
            shape((block, f), f32),
            shape((block, f), f32),
            shape((f, block), f32),
            shape((block, 4 * f), f32),
            shape((block, 4 * f), f32),
            shape((4 * f, block), f32),
        ),
        in_specs=[vm],
        out_specs=(vm,) * 7,
        compiler_params=pltpu.CompilerParams(vmem_limit_bytes=40 * 1024 * 1024),
    )(blocks)


def plain_body(
    tokens,
    lengths,
    w_query,
    w_key,
    w_value,
    w_out,
    w_gate,
    w_up,
    w_down,
    gain_query,
    gain_key,
    gain_attn,
    gain_mlp,
    cotangent,
):
    rows_dev = lengths.shape[0]
    model_width = w_query.shape[0]
    local_width = w_query.shape[1]
    head_count = local_width // HD
    gathered = lax.all_gather(tokens, "tensor", axis=0, tiled=True)
    row_count = gathered.shape[0]
    segment, offsets = jax.vmap(row_layout)(lengths)
    queries = jnp.dot(gathered, w_query, preferred_element_type=jnp.float32)
    keys_raw = jnp.dot(gathered, w_key, preferred_element_type=jnp.float32)
    values_low = jnp.dot(gathered, w_value, preferred_element_type=jnp.float32).astype(jnp.bfloat16)
    q_total, k_total = lax.psum(
        (jnp.sum(queries * queries, axis=1), jnp.sum(keys_raw * keys_raw, axis=1)), "tensor"
    )
    q_inv = lax.rsqrt(q_total / model_width + EPS)[:, None]
    k_inv = lax.rsqrt(k_total / model_width + EPS)[:, None]
    q_unit = queries * q_inv
    k_unit = keys_raw * k_inv

    def to_heads(values):
        return values.reshape(rows_dev, ROW_LEN, head_count, HD)

    queries_low = rotate(to_heads(q_unit * gain_query), offsets, 1.0).astype(jnp.bfloat16)
    keys_low = rotate(to_heads(k_unit * gain_key), offsets, 1.0).astype(jnp.bfloat16)
    values_heads = to_heads(values_low)
    mixed_heads, log_total = jax.vmap(lambda *a: attend(a))(
        queries_low, keys_low, values_heads, segment
    )
    mixed_low = mixed_heads.reshape(row_count, local_width)
    attn_out = lax.psum_scatter(
        jnp.dot(mixed_low, w_out, preferred_element_type=jnp.float32).astype(jnp.bfloat16),
        "tensor",
        scatter_dimension=0,
        tiled=True,
    ).astype(jnp.float32)
    inner_count = lax.axis_size("dp") // OUTER
    a_inv = lax.rsqrt(jnp.mean(attn_out * attn_out, axis=1, keepdims=True) + EPS)
    a_unit = attn_out * a_inv
    hidden = tokens.astype(jnp.float32) + a_unit * gain_attn
    hidden_low = hidden.astype(jnp.bfloat16)
    hidden_all = lax.all_gather(hidden_low, "tensor", axis=0, tiled=True)
    outer_index = lax.axis_index("dp") // inner_count

    def gather_group(shard):
        groups = [[z * inner_count + i for z in range(OUTER)] for i in range(inner_count)]
        part = lax.all_gather(shard, "dp", axis=0, tiled=True, axis_index_groups=groups)
        return lax.all_gather(part, "tensor", axis=0, tiled=True)

    hidden_group = gather_group(hidden_low)
    gate_acts = jnp.dot(hidden_all, w_gate, preferred_element_type=jnp.float32)
    up_acts = jnp.dot(hidden_all, w_up, preferred_element_type=jnp.float32)
    gate_sigmoid = jax.nn.sigmoid(gate_acts)
    inner_low = (gate_acts * gate_sigmoid * up_acts).astype(jnp.bfloat16)
    mlp_out = lax.psum_scatter(
        jnp.dot(inner_low, w_down, preferred_element_type=jnp.float32).astype(jnp.bfloat16),
        "tensor",
        scatter_dimension=0,
        tiled=True,
    ).astype(jnp.float32)
    f_inv = lax.rsqrt(jnp.mean(mlp_out * mlp_out, axis=1, keepdims=True) + EPS)
    f_unit = mlp_out * f_inv
    output = (hidden + f_unit * gain_mlp).astype(jnp.bfloat16)
    grad_output = cotangent.astype(jnp.float32)
    grad_mlp, grad_gain_mlp_part = post_norm_back(grad_output, f_unit, f_inv, gain_mlp)
    grad_mlp_low = grad_mlp.astype(jnp.bfloat16)
    mlp_grad_all = lax.all_gather(grad_mlp_low, "tensor", axis=0, tiled=True)
    mlp_grad_group = gather_group(grad_mlp_low)
    grad_inner = times_t(mlp_grad_all, w_down)
    grad_gate_low = (
        grad_inner * up_acts * gate_sigmoid * (1.0 + gate_acts * (1.0 - gate_sigmoid))
    ).astype(jnp.bfloat16)
    grad_up_low = (grad_inner * gate_acts * gate_sigmoid).astype(jnp.bfloat16)
    part_width = w_gate.shape[1] // OUTER
    gate_part = lax.dynamic_slice_in_dim(w_gate, outer_index * part_width, part_width, 1)
    up_part = lax.dynamic_slice_in_dim(w_up, outer_index * part_width, part_width, 1)
    down_part = lax.dynamic_slice_in_dim(w_down, outer_index * part_width, part_width, 0)
    gate_g = jnp.dot(hidden_group, gate_part, preferred_element_type=jnp.float32)
    up_g = jnp.dot(hidden_group, up_part, preferred_element_type=jnp.float32)
    sig_g = jax.nn.sigmoid(gate_g)
    inner_g = (gate_g * sig_g * up_g).astype(jnp.bfloat16)
    grad_inner_g = times_t(mlp_grad_group, down_part)
    grad_gate_g = (grad_inner_g * up_g * sig_g * (1.0 + gate_g * (1.0 - sig_g))).astype(
        jnp.bfloat16
    )
    grad_up_g = (grad_inner_g * gate_g * sig_g).astype(jnp.bfloat16)
    sum_down = scatter_join(split_cols(t_times(inner_g, mlp_grad_group), inner_count), inner_count, 0)
    sum_gate = scatter_join(split_rows(t_times(hidden_group, grad_gate_g), inner_count), inner_count, 1)
    sum_up = scatter_join(split_rows(t_times(hidden_group, grad_up_g), inner_count), inner_count, 1)
    grad_hidden = grad_output + lax.psum_scatter(
        (times_t(grad_gate_low, w_gate) + times_t(grad_up_low, w_up)).astype(jnp.bfloat16),
        "tensor",
        scatter_dimension=0,
        tiled=True,
    ).astype(jnp.float32)
    grad_attn, grad_gain_attn_part = post_norm_back(grad_hidden, a_unit, a_inv, gain_attn)
    grad_attn_low = grad_attn.astype(jnp.bfloat16)
    attn_grad_all = lax.all_gather(grad_attn_low, "tensor", axis=0, tiled=True)
    grad_mixed = times_t(attn_grad_all, w_out).astype(jnp.bfloat16)
    grad_q_rot, grad_k_rot, grad_values_low = jax.vmap(lambda *a: attend_back(a))(
        queries_low, keys_low, values_heads, segment, log_total, to_heads(grad_mixed)
    )
    grad_q_norm = rotate(grad_q_rot, offsets, -1.0).reshape(row_count, local_width)
    grad_k_norm = rotate(grad_k_rot, offsets, -1.0).reshape(row_count, local_width)
    grad_gain_query_part = jnp.sum(grad_q_norm * q_unit, axis=0)
    grad_gain_key_part = jnp.sum(grad_k_norm * k_unit, axis=0)
    q_scaled = grad_q_norm * gain_query
    k_scaled = grad_k_norm * gain_key
    q_dots, k_dots = lax.psum(
        (jnp.sum(q_scaled * q_unit, axis=1), jnp.sum(k_scaled * k_unit, axis=1)), "tensor"
    )
    grad_queries_low = (q_inv * (q_scaled - q_unit * (q_dots / model_width)[:, None])).astype(
        jnp.bfloat16
    )
    grad_keys_low = (k_inv * (k_scaled - k_unit * (k_dots / model_width)[:, None])).astype(
        jnp.bfloat16
    )
    grad_values_flat = grad_values_low.reshape(row_count, local_width)
    grad_tokens = (
        grad_hidden
        + lax.psum_scatter(
            (
                times_t(grad_queries_low, w_query)
                + times_t(grad_keys_low, w_key)
                + times_t(grad_values_flat, w_value)
            ).astype(jnp.bfloat16),
            "tensor",
            scatter_dimension=0,
            tiled=True,
        ).astype(jnp.float32)
    ).astype(jnp.bfloat16)
    tensor_start = lax.axis_index("tensor") * local_width
    zero_row = jnp.zeros((model_width,), jnp.float32)
    q_full = lax.dynamic_update_slice(zero_row, grad_gain_query_part, (tensor_start,))
    k_full = lax.dynamic_update_slice(zero_row, grad_gain_key_part, (tensor_start,))
    gain_stack = jnp.stack([q_full, k_full, grad_gain_attn_part, grad_gain_mlp_part])
    gain_total = lax.psum(gain_stack, ("dp", "tensor"))
    grad_gain_query = lax.dynamic_slice(gain_total[0], (tensor_start,), (local_width,))
    grad_gain_key = lax.dynamic_slice(gain_total[1], (tensor_start,), (local_width,))
    summed = (
        scatter_sum(split_rows(t_times(gathered, grad_queries_low), inner_count), inner_count),
        scatter_sum(split_rows(t_times(gathered, grad_keys_low), inner_count), inner_count),
        scatter_sum(split_rows(t_times(gathered, grad_values_flat), inner_count), inner_count),
        scatter_sum(split_cols(t_times(mixed_low, attn_grad_all), inner_count), inner_count),
        sum_gate,
        sum_up,
        sum_down,
    )
    return (
        output,
        grad_tokens,
        summed[0],
        summed[1],
        summed[2],
        summed[3],
        summed[4],
        summed[5],
        summed[6],
        grad_gain_query,
        grad_gain_key,
        gain_total[2],
        gain_total[3],
    )


def fused_body(
    tokens,
    lengths,
    w_query,
    w_key,
    w_value,
    w_out,
    w_gate,
    w_up,
    w_down,
    gain_query,
    gain_key,
    gain_attn,
    gain_mlp,
    cotangent,
):
    local_width = w_query.shape[1]
    segment, offsets = row_layout(lengths[0])
    half_width = HD // 2
    frequency = jnp.exp(
        jnp.arange(half_width, dtype=jnp.float32) * (-2.0 * math.log(THETA) / HD)
    )
    angles = offsets.astype(jnp.float32)[:, None] * frequency
    cosines = jnp.cos(angles)
    sines = jnp.sin(angles)
    cosines = jnp.concatenate([cosines, cosines], axis=1)
    sines = jnp.concatenate([-sines, sines], axis=1)
    attn_out, tokens_all, q_unit, k_unit, q_rot, k_rot, values, mixed, weights, inverse = attend_both(
        tokens, cosines, sines, segment, gain_query, gain_key, w_query, w_key, w_value, w_out
    )
    output, grad_hidden, grad_attn, grad_mlp, gain_parts, group_h, group_d = mlp_both(
        attn_out, tokens, cotangent, gain_attn, gain_mlp, w_gate, w_up, w_down
    )
    grad_tokens, head_gains, grad_attn_all, grad_q, grad_k, grad_v, group_d = attend_back_both(
        grad_attn, grad_hidden, cosines, sines, gain_query, gain_key, inverse,
        w_query, w_key, w_value, w_out, q_unit, k_unit, q_rot, k_rot, values, weights, grad_mlp, group_d,
    )
    gains, blocks, _, _ = weight_grads(
        gain_parts, head_gains, group_h, group_d, w_gate, w_up, w_down, tokens_all, grad_attn_all,
        grad_q, grad_k, grad_v, mixed,
    )
    return (
        output,
        grad_tokens,
        *place_grads(blocks),
        gains[2, :local_width],
        gains[3, :local_width],
        gains[0],
        gains[1],
    )


def solution(mesh):
    placed = (
        P(("dp", "tensor"), None),
        P("dp", None),
        P(None, "tensor"),
        P(None, "tensor"),
        P(None, "tensor"),
        P("tensor", None),
        P(None, "tensor"),
        P(None, "tensor"),
        P("tensor", None),
        P("tensor"),
        P("tensor"),
        P(),
        P(),
        P(("dp", "tensor"), None),
    )
    return jax.shard_map(
        fused_body if tuple(mesh.shape.values()) == (8, 4) else plain_body,
        mesh=mesh,
        in_specs=placed,
        out_specs=(
            P(("dp", "tensor"), None),
            P(("dp", "tensor"), None),
            P("dp", "tensor"),
            P("dp", "tensor"),
            P("dp", "tensor"),
            P("tensor", "dp"),
            P("dp", "tensor"),
            P("dp", "tensor"),
            P("tensor", "dp"),
            P("tensor"),
            P("tensor"),
            P(),
            P(),
        ),
        check_vma=False,
    )
```

```python
import math

import jax
import jax.numpy as jnp
from jax import lax
from jax.experimental import pallas as pl
from jax.experimental.pallas import tpu as pltpu
from jax.sharding import PartitionSpec as P

HD = 128
ROW_LEN = 512


EPS = 1e-06
THETA = 500000.0


def rotate(values, offsets, rot_sign):
    half_width = values.shape[-1] // 2
    frequency = jnp.exp(
        jnp.arange(half_width, dtype=jnp.float32) * (-2.0 * math.log(THETA) / values.shape[-1])
    )
    angles = offsets.astype(jnp.float32)[..., None, None] * frequency
    cosines = jnp.cos(angles)
    sine_part = rot_sign * jnp.sin(angles)
    first_half = values[..., :half_width]
    second_half = values[..., half_width:]
    return jnp.concatenate(
        [
            first_half * cosines - second_half * sine_part,
            second_half * cosines + first_half * sine_part,
        ],
        axis=-1,
    )


def row_layout(lengths_row):
    slots = jnp.arange(lengths_row.shape[0], dtype=jnp.int32)
    seq_ends = jnp.sum(
        jnp.where(slots[None, :] <= slots[:, None], lengths_row[None, :], 0), axis=1
    )
    position = jnp.arange(ROW_LEN, dtype=jnp.int32)
    passed = (position[:, None] >= seq_ends[None, :]).astype(jnp.int32)
    segment = jnp.sum(passed, axis=1)
    seq_start = jnp.sum(passed * lengths_row[None, :], axis=1)
    return (segment, position - seq_start)


def allowed_mask(segment):
    position = jnp.arange(segment.shape[0], dtype=jnp.int32)
    return (segment[:, None] == segment[None, :]) & (position[None, :] <= position[:, None])


def times_t(left_mat, right_mat):
    return lax.dot_general(
        left_mat, right_mat, (((1,), (1,)), ((), ())), preferred_element_type=jnp.float32
    )


def t_times(left_mat, right_mat):
    return lax.dot_general(
        left_mat, right_mat, (((0,), (0,)), ((), ())), preferred_element_type=jnp.float32
    )


def masked_scores(queries_low, keys_low, segment):
    scale_factor = 1.0 / math.sqrt(queries_low.shape[-1])
    scores = (
        jnp.einsum("qhd,khd->hqk", queries_low, keys_low, preferred_element_type=jnp.float32)
        * scale_factor
    )
    return jnp.where(allowed_mask(segment)[None], scores, -1e30)


def attend(block_item):
    queries_low, keys_low, values_low, segment = block_item
    scores = masked_scores(queries_low, keys_low, segment)
    row_max = jnp.max(scores, axis=-1, keepdims=True)
    shifted = jnp.exp(scores - row_max)
    row_total = jnp.sum(shifted, axis=-1, keepdims=True)
    attn_weights = (shifted / row_total).astype(jnp.bfloat16)
    mixed = jnp.einsum("hqk,khd->qhd", attn_weights, values_low, preferred_element_type=jnp.float32)
    return (mixed.astype(jnp.bfloat16), (row_max + jnp.log(row_total))[..., 0])


def attend_back(block_item):
    queries_low, keys_low, values_low, segment, log_total, grad_mixed = block_item
    scale_factor = 1.0 / math.sqrt(queries_low.shape[-1])
    scores = masked_scores(queries_low, keys_low, segment)
    attn_weights = jnp.exp(scores - log_total[..., None])
    grad_weights = jnp.einsum(
        "qhd,khd->hqk", grad_mixed, values_low, preferred_element_type=jnp.float32
    )
    row_dots = jnp.sum(attn_weights * grad_weights, axis=-1, keepdims=True)
    grad_scores = (attn_weights * (grad_weights - row_dots)).astype(jnp.bfloat16)
    grad_queries = scale_factor * jnp.einsum(
        "hqk,khd->qhd", grad_scores, keys_low, preferred_element_type=jnp.float32
    )
    grad_keys = scale_factor * jnp.einsum(
        "hqk,qhd->khd", grad_scores, queries_low, preferred_element_type=jnp.float32
    )
    grad_values = jnp.einsum(
        "hqk,qhd->khd",
        attn_weights.astype(jnp.bfloat16),
        grad_mixed,
        preferred_element_type=jnp.float32,
    )
    return (grad_queries, grad_keys, grad_values.astype(jnp.bfloat16))


def post_norm_back(grad_in, unit_rows, inv_scale, gain_vec):
    scaled = grad_in * gain_vec
    mean_dots = jnp.mean(scaled * unit_rows, axis=-1, keepdims=True)
    return (inv_scale * (scaled - unit_rows * mean_dots), jnp.sum(grad_in * unit_rows, axis=0))


OUTER = 4


def swap(value, shift):
    size = lax.axis_size("dp")
    return lax.ppermute(value, "dp", [(d, d ^ shift) for d in range(size)])


def pick(parts, index):
    return lax.dynamic_index_in_dim(parts, index, 0, keepdims=False)


def sum_inner(parts):
    inner = parts.shape[0]
    mine = lax.axis_index("dp") % inner
    total = pick(parts, mine)
    for k in range(1, inner):
        sent = pick(parts, mine ^ k).astype(jnp.bfloat16)
        total = total + swap(sent, k).astype(jnp.float32)
    return total


def trade_outer(parts, inner):
    mine = lax.axis_index("dp") // inner
    got = [(mine, pick(parts, mine))]
    for k in range(1, OUTER):
        got.append((mine ^ k, swap(pick(parts, mine ^ k), k * inner)))
    return got


def split_rows(grad, inner):
    cols = grad.shape[1]
    return grad.reshape(OUTER, inner, -1, cols).transpose(1, 0, 2, 3)


def split_cols(grad, inner):
    rows = grad.shape[0]
    return grad.reshape(rows, OUTER, inner, -1).transpose(2, 1, 0, 3)


def scatter_sum(parts, inner):
    half = sum_inner(parts).astype(jnp.bfloat16)
    got = trade_outer(half, inner)
    return sum(g.astype(jnp.float32) for _, g in got)


def scatter_join(parts, inner, axis):
    half = sum_inner(parts).astype(jnp.bfloat16)
    got = trade_outer(half, inner)
    stack = jnp.zeros((OUTER, *got[0][1].shape), jnp.bfloat16)
    for place, block in got:
        stack = lax.dynamic_update_index_in_dim(stack, block, place, 0)
    joined = jnp.concatenate([stack[z] for z in range(OUTER)], axis=axis)
    return joined.astype(jnp.float32)


MESH = pl.DeviceIdType.MESH
FULL = pl.BlockSpec(memory_space=pl.ANY)


def grads_kernel(
    gp_ref, gqk_ref, gh_in, gm_in, wg_ref, wu_ref, wd_ref, tok_ref, nxt_ref, dq_ref, dk_ref, dv_ref, po_ref,
    gain_ref, attn_ref, proj_ref, mlp_ref, gh_ref, gm_ref,
    hb_v, dm_v, wg_v, wu_v, wd_v, lhs_in, lhs_q, lhs_t, quad, quad_in, pair, full, part, gbuf, gin,
    ld_sem, xs_s, xs_r, cs_s, cs_r, qs_s, qs_r, os_s, os_r, qz_s, qz_r, qy_s, qy_r, ys_s, ys_r, ts_s, ts_r, own_s, gs_s, gs_r,
):
    d = lax.axis_index("dp")
    t = lax.axis_index("tensor")
    z = d // 2
    y = d % 2
    side = z % 2
    top = z // 2
    mate = t + 1 - 2 * (t % 2)
    across = (t + 2) % 4
    twin = z * 2 + 1 - y
    pal = (z + 1 - 2 * side) * 2 + y
    bf = jnp.bfloat16
    f32 = jnp.float32
    f = wg_v.shape[1]
    width = wg_v.shape[0]
    shard = hb_v.shape[2]
    span = width // 2
    hc = lhs_in.shape[4]
    total = 4 * shard

    def peer(k):
        return ((z + k) % 4) * 2 + y

    def wide_load(r, slot):
        return pltpu.make_async_copy(gh_ref.at[r], hb_v.at[slot], ld_sem.at[slot])

    heads = (dv_ref, dq_ref, dk_ref)
    parts = (top, 1 - top)
    loads = [
        wide_load(z, 0),
        pltpu.make_async_copy(wg_ref.at[:, pl.ds(side * f, f)], wg_v, ld_sem.at[2]),
        pltpu.make_async_copy(wu_ref.at[:, pl.ds(side * f, f)], wu_v, ld_sem.at[3]),
    ]
    slow = [
        pltpu.make_async_copy(
            wd_ref.at[pl.ds(side * f, f), pl.ds(parts[i] * span, span)], wd_v.at[i], ld_sem.at[4 + i]
        )
        for i in range(2)
    ] + [
        pltpu.make_async_copy(r.at[:, :, pl.ds(y * hc, hc)], lhs_in.at[w, 0], ld_sem.at[6 + w])
        for w, r in enumerate(heads)
    ]
    for cp in loads + slow:
        cp.start()

    greet([(peer(1), t), (peer(2), t), (peer(3), t), (twin, t), (d, mate), (d, across)])

    groups = (gh_ref, gm_ref)
    order = (1, 3, 2)

    def head_swap(w):
        return far_copy(
            heads[w].at[:, :, pl.ds((1 - y) * hc, hc)], lhs_in.at[w, 1], qs_s.at[w], qs_r.at[w], twin, t
        )

    def proj_trade(k):
        return far_copy(po_ref.at[(z + k) % 4], proj_ref.at[z], os_s.at[k - 1], os_r.at[k - 1], peer(k), t)

    def piece(i):
        if i == 0:
            return gh_ref, (z + 2) % 4, None
        return gm_ref, (z + 4 - order[(i - 1) % 3]) % 4, pl.ds(parts[(i - 1) // 3] * span, span)

    def cell(i, q):
        ref, r, cols = piece(i)
        return ref.at[r, q] if cols is None else ref.at[r, q, :, cols]

    def forward_x(i):
        return far_copy(cell(i, t), cell(i, t), xs_s.at[i], xs_r.at[i], d, across)

    def forward_c(i, h):
        q = t if h == 0 else across
        return far_copy(cell(i, q), cell(i, q), cs_s.at[i, h], cs_r.at[i, h], d, mate)

    def advance(i):
        forward_x(i).wait_recv()
        for h in range(2):
            forward_c(i, h).start()

    def arrive(i):
        for h in range(2):
            forward_c(i, h).wait_recv()

    def gain_copy(i):
        stage, who = ((0, (peer(1), t)), (0, (peer(2), t)), (0, (peer(3), t)), (1, (twin, t)), (2, (d, across)), (3, (d, mate)))[i]
        return far_copy(gbuf.at[stage], gin.at[i], gs_s.at[i], gs_r.at[i], *who)

    gbuf[0] = jnp.zeros_like(gbuf[0])
    gbuf[0, 0:2, :] = gp_ref[...]
    gbuf[0, 2:4, 0 : gqk_ref.shape[1]] = gqk_ref[...]
    for i in range(3):
        gain_copy(i).start()
    for w in range(3):
        head_swap(w).start()
    for i in range(7):
        forward_x(i).start()
    for k in (2, 1, 3):
        proj_trade(k).start()
    keep_proj = pltpu.make_async_copy(po_ref.at[z], proj_ref.at[z], own_s.at[0])
    keep_proj.start()

    def gain_step(stage):
        new = gbuf[stage]
        for i in ((0, 1, 2), (3,), (4,), (5,))[stage]:
            gain_copy(i).wait_recv()
            new = new + gin[i]
        if stage < 3:
            gbuf[stage + 1] = new
            gain_copy(stage + 3).start()
        if stage == 1:
            gain_ref[2:4, :] = new[2:4, :]
        if stage == 3:
            gain_ref[0:2, :] = new[0:2, :]

    step = 256

    def remake(slot, n):
        def wide(j, carry):
            cols = pl.ds(pl.multiple_of(j * step, step), step)
            hb = hb_v[slot].reshape(total, width)
            g = jnp.dot(hb, wg_v[:, cols], preferred_element_type=f32)
            u = jnp.dot(hb, wu_v[:, cols], preferred_element_type=f32)
            sg = jax.nn.sigmoid(g)
            gs = g * sg
            toks = slice(n * total, (n + 1) * total)
            lhs_t[0, cols, toks] = (gs * u).T.astype(bf)
            lhs_t[1, cols, toks] = (u * sg * (1.0 + g * (1.0 - sg))).T.astype(bf)
            lhs_t[2, cols, toks] = gs.T.astype(bf)
            return carry

        lax.fori_loop(0, f // step, wide, 0)

    def scale_back(n):
        def wide(j, carry):
            cols = pl.ds(pl.multiple_of(j * step, step), step)
            di = None
            for i in range(2):
                one = lax.dot_general(
                    wd_v[i, cols, :], dm_v[n, i].reshape(total, span), NT, preferred_element_type=f32
                )
                di = one if di is None else di + one
            toks = slice(n * total, (n + 1) * total)
            for w in (1, 2):
                lhs_t[w, cols, toks] = (lhs_t[w, cols, toks].astype(f32) * di).astype(bf)
            return carry

        lax.fori_loop(0, f // step, wide, 0)

    ranks = (0,) + order

    def dm_load(n, i):
        return pltpu.make_async_copy(
            gm_ref.at[(z + 4 - ranks[n]) % 4, :, :, pl.ds(parts[i] * span, span)],
            dm_v.at[n, i],
            ld_sem.at[9 + n * 2 + i],
        )

    def hb_half(n):
        return pltpu.make_async_copy(
            gh_ref.at[(z + 4 - ranks[n]) % 4, :, :, pl.ds(top * span, span)],
            hb_v.at[n // 2, :, :, pl.ds((n % 2) * span, span)],
            ld_sem.at[17 + n],
        )

    for i in range(2):
        dm_load(0, i).start()
    for cp in loads:
        cp.wait()
    nexts = [wide_load((z + 4 - k) % 4, (n + 1) % 2) for n, k in enumerate(order)]
    nexts[0].start()
    remake(0, 0)
    gain_step(0)
    nexts[1].start()
    nexts[0].wait()
    remake(1, 1)
    advance(0)
    nexts[1].wait()
    remake(0, 2)
    arrive(0)
    nexts[2].start()
    advance(1)
    advance(2)
    nexts[2].wait()
    remake(1, 3)

    block = quad.shape[4]

    def quad_trade(w, k):
        return far_copy(quad.at[w, (z + k) % 4], quad_in.at[w, k - 1], qz_s.at[w, k - 1], qz_r.at[w, k - 1], peer(k), t)

    def head_grad(w):
        slow[2 + w].wait()
        head_swap(w).wait_recv()
        for i in range(2):
            lhs_q[:, i * total : (i + 1) * total] = lhs_in[w, i].reshape(total, hc).astype(f32).T.astype(bf)

        def tile(j, carry):
            cols = pl.ds(pl.multiple_of(j * block, block), block)
            quad[w, j // 2, j % 2] = jnp.dot(
                lhs_q[...], hb_v[:, :, :, cols].reshape(2 * total, block), preferred_element_type=f32
            ).astype(bf)
            return carry

        lax.fori_loop(0, 8, tile, 0)
        for k in (2, 1, 3):
            quad_trade(w, k).start()

    toks = [
        pltpu.make_async_copy(r, hb_v.at[i], ld_sem.at[i]) for i, r in enumerate((tok_ref, nxt_ref))
    ]
    for cp in toks:
        cp.start()
    arrive(1)
    arrive(2)
    advance(3)
    for n in (1, 2):
        dm_load(n, 0).start()
    gain_step(1)
    for cp in toks:
        cp.wait()
    for w in range(3):
        head_grad(w)
    for n in range(4):
        hb_half(n).start()
    arrive(3)
    dm_load(3, 0).start()

    def swap_y(w):
        return far_copy(full.at[w, :, 1 - y], part.at[w], ys_s.at[w], ys_r.at[w], twin, t)

    def trade_z(w):
        return far_copy(part.at[w, 1 - side], mlp_ref.at[w, side], ts_s.at[w], ts_r.at[w], pal, t)

    def keep(w):
        return pltpu.make_async_copy(part.at[w, side], mlp_ref.at[w, side], own_s.at[1 + w])

    def finish_y(w):
        swap_y(w).wait()
        for b in range(2):
            part[w, b] = (part[w, b].astype(f32) + full[w, b, y].astype(f32)).astype(bf)
        trade_z(w).start()
        keep(w).start()

    def emit(w):
        for b in range(4):
            new = None
            for n in range(4):
                one = jnp.dot(
                    lhs_t[w, :, n * total : (n + 1) * total],
                    (dm_v[n, 0, :, :, b * block : (b + 1) * block] if w == 0 else hb_v[
                        n // 2, :, :, (n % 2) * span + b * block : (n % 2) * span + (b + 1) * block
                    ]).reshape(total, block),
                    preferred_element_type=f32,
                )
                new = one if new is None else new + one
            full[w, b // 2, b % 2] = new.astype(bf)
        swap_y(w).start()

    for n in range(4):
        dm_load(n, 0).wait()
    emit(0)
    advance(4)
    dm_load(0, 1).wait()
    for cp in slow[:2]:
        cp.wait()
    scale_back(0)
    for n in (1, 2, 3):
        arrive(3 + n)
        dm_load(n, 1).start()
        if n < 3:
            advance(4 + n)
        dm_load(n, 1).wait()
        scale_back(n)
    gain_step(2)
    for n in range(4):
        hb_half(n).wait()
    emit(1)
    emit(2)
    gain_step(3)

    def head_swap_back(w):
        return far_copy(pair.at[w, 1 - y], attn_ref.at[w, y], qy_s.at[w], qy_r.at[w], twin, t)

    def head_keep(w):
        return pltpu.make_async_copy(pair.at[w, y], attn_ref.at[w, y], own_s.at[4 + w])

    def finish_head(w):
        for k in range(1, 4):
            quad_trade(w, k).wait_recv()
        for b in range(2):
            new = quad[w, z, b].astype(f32)
            for i in range(3):
                new = new + quad_in[w, i, b].astype(f32)
            pair[w, b] = new.astype(bf)
        head_swap_back(w).start()
        head_keep(w).start()

    finish_y(0)
    finish_head(0)
    finish_y(1)
    finish_head(1)
    finish_head(2)
    finish_y(2)

    keep_proj.wait()
    for i in range(6):
        gain_copy(i).wait_send()
    for i in range(7):
        forward_x(i).wait_send()
        for h in range(2):
            forward_c(i, h).wait_send()
    for k in range(1, 4):
        proj_trade(k).wait()
    for w in range(3):
        head_swap(w).wait_send()
        for k in range(1, 4):
            quad_trade(w, k).wait_send()
        head_keep(w).wait()
        keep(w).wait()
        head_swap_back(w).wait()
        trade_z(w).wait()


def weight_grads(gp, gqk, gh, gd, wg, wu, wd, tok, nxt, dq, dk, dv, po):
    shard, width = tok.shape[1], tok.shape[2]
    f = wg.shape[1] // 2
    local = dq.shape[2]
    block = width // 8
    bf = jnp.bfloat16
    f32 = jnp.float32
    dma = pltpu.SemaphoreType.DMA
    shape = jax.ShapeDtypeStruct
    vm = pl.BlockSpec(memory_space=pltpu.VMEM)
    flops = 2 * 4 * shard * 4 * f * (3 * width + 3 * width // 2)
    return pl.pallas_call(
        grads_kernel,
        name="weight_grads",
        input_output_aliases={2: 4, 3: 5},
        out_shape=(
            shape((4, width), f32),
            shape((3, 2, local // 2, block), bf),
            shape((4, local, block), bf),
            shape((3, 2, f, block), bf),
            shape(gh.shape, bf),
            shape(gd.shape, bf),
        ),
        in_specs=[vm] * 2 + [FULL] * 11,
        out_specs=(vm,) + (FULL,) * 5,
        scratch_shapes=[
            pltpu.VMEM((2, 4, shard, width), bf),
            pltpu.VMEM((4, 2, 4, shard, width // 2), bf),
            pltpu.VMEM((width, f), bf),
            pltpu.VMEM((width, f), bf),
            pltpu.VMEM((2, f, width // 2), bf),
            pltpu.VMEM((3, 2, 4, shard, local // 2), bf),
            pltpu.VMEM((local // 2, 8 * shard), bf),
            pltpu.VMEM((3, f, 16 * shard), bf),
            pltpu.VMEM((3, 4, 2, local // 2, block), bf),
            pltpu.VMEM((3, 3, 2, local // 2, block), bf),
            pltpu.VMEM((3, 2, local // 2, block), bf),
            pltpu.VMEM((3, 2, 2, f, block), bf),
            pltpu.VMEM((3, 2, f, block), bf),
            pltpu.VMEM((4, 8, width), f32),
            pltpu.VMEM((6, 8, width), f32),
            dma((21,)),
            dma((7,)), dma((7,)), dma((7, 2)), dma((7, 2)),
            dma((3,)), dma((3,)), dma((3,)), dma((3,)),
            dma((3, 3)), dma((3, 3)), dma((3,)), dma((3,)),
            dma((3,)), dma((3,)), dma((3,)), dma((3,)),
            dma((7,)), dma((6,)), dma((6,)),
        ],
        compiler_params=pltpu.CompilerParams(
            collective_id=0, has_side_effects=True, vmem_limit_bytes=60 * 1024 * 1024
        ),
        cost_estimate=pl.CostEstimate(flops=flops, bytes_accessed=60 * 1024 * 1024, transcendentals=0),
    )(gp, gqk, gh, gd, wg, wu, wd, tok, nxt, dq, dk, dv, po)


def far_copy(src, dst, ss, rs, dd, tt):
    return pltpu.make_async_remote_copy(
        src_ref=src, dst_ref=dst, send_sem=ss, recv_sem=rs, device_id=(dd, tt), device_id_type=MESH
    )


def mean_inv(values):
    return lax.rsqrt(jnp.mean(values * values, axis=1, keepdims=True) + EPS)


def mlp_kernel(
    att_ref, tok_ref, cot_ref, ga_ref, gm_ref, wg_ref, wu_ref, wd_ref,
    out_ref, ghid_ref, dat_ref, gain_ref, gh_ref, gd_ref,
    wg_v, wu_v, wd_v, slope_g, slope_u, own, oth, low_a, low_b, pown, pmate, xsend, xrecv, qown, qmate, hid,
    w_sem, as_s, as_r, ax_s, ax_r, af_s, af_r, ps_s, ps_r, px_s, px_r, pq_s, pq_r, zs_s, zs_r, st_sem,
):
    d = lax.axis_index("dp")
    t = lax.axis_index("tensor")
    z = d // 2
    y = d % 2
    c = t % 2
    chip = t // 2
    mate = t + 1 - 2 * c
    across = (t + 2) % 4
    shard, width = att_ref.shape
    ff = wg_v.shape[1]
    bf = jnp.bfloat16
    f32 = jnp.float32
    tile = 512
    tiles = ff // tile

    def wcopy(i, j):
        cols = pl.ds(j * tile, tile)
        if i == 0:
            return pltpu.make_async_copy(wg_ref.at[:, cols], wg_v.at[:, cols], w_sem.at[0, j])
        if i == 1:
            return pltpu.make_async_copy(wu_ref.at[:, cols], wu_v.at[:, cols], w_sem.at[1, j])
        return pltpu.make_async_copy(wd_ref.at[cols, :], wd_v.at[cols, :], w_sem.at[2, j])

    for j in range(tiles):
        wcopy(0, j).start()
        wcopy(1, j).start()
    for j in range(tiles):
        wcopy(2, j).start()

    barrier = pltpu.get_barrier_semaphore()
    peers = [((z + k) % 4) * 2 + y for k in range(1, 4)]
    for dd, tt in [(peers[0], t), (peers[1], t), (peers[2], t), (d, mate), (d, across)]:
        pl.semaphore_signal(barrier, inc=1, device_id=(dd, tt), device_id_type=MESH)
    pl.semaphore_wait(barrier, 5)

    def send_mate(p):
        return far_copy(own.at[p, c], own.at[p, c], as_s.at[p], as_r.at[p], d, mate)

    def send_across(p):
        return far_copy(own.at[p, c], oth.at[p, c], ax_s.at[p], ax_r.at[p], d, across)

    def forward(p):
        return far_copy(oth.at[p, c], oth.at[p, c], af_s.at[p], af_r.at[p], d, mate)

    half = width // 2

    def part_mate(p, h):
        return far_copy(
            pown.at[p, h, 1 - c], pmate.at[p, h], ps_s.at[p, h], ps_r.at[p, h], d, mate
        )

    def part_across(p, h):
        return far_copy(xsend.at[p, h], xrecv.at[p, h], px_s.at[p, h], px_r.at[p, h], d, across)

    def part_own(p):
        return far_copy(qown.at[p, 1 - c], qmate.at[p], pq_s.at[p], pq_r.at[p], d, mate)

    def gather_z(k):
        return far_copy(
            own.at[0, c], gh_ref.at[z, t], zs_s.at[0, k - 1], zs_r.at[0, k - 1], ((z + k) % 4) * 2 + y, t
        )

    def gather_near(k):
        return far_copy(
            own.at[1, c], gd_ref.at[z, t], zs_s.at[1, k - 1], zs_r.at[1, k - 1], ((z + k) % 4) * 2 + y, t
        )

    def store_row(p, ref):
        mine = ref.at[z]
        return [
            pltpu.make_async_copy(own.at[p, 0], mine.at[chip * 2], st_sem.at[p, 0]),
            pltpu.make_async_copy(own.at[p, 1], mine.at[chip * 2 + 1], st_sem.at[p, 1]),
            pltpu.make_async_copy(oth.at[p, 0], mine.at[2 - chip * 2], st_sem.at[p, 2]),
            pltpu.make_async_copy(oth.at[p, 1], mine.at[3 - chip * 2], st_sem.at[p, 3]),
        ]

    two = 2 * shard

    def forward_in(lhs, base, wait):
        for j in range(tiles):
            if wait:
                wcopy(0, j).wait()
                wcopy(1, j).wait()
            cols = pl.ds(j * tile, tile)
            rows = pl.ds(base, two)
            both = lhs[...].reshape(two, width)
            g = jnp.dot(both, wg_v[:, cols], preferred_element_type=f32)
            u = jnp.dot(both, wu_v[:, cols], preferred_element_type=f32)
            sg = jax.nn.sigmoid(g)
            gs = g * sg
            low_a[:, cols] = (gs * u).astype(bf)
            slope_u[rows, cols] = gs
            slope_g[rows, cols] = u * sg * (1.0 + g * (1.0 - sg))

    def backward_in(lhs, base, wait):
        for j in range(tiles):
            cols = pl.ds(j * tile, tile)
            rows = pl.ds(base, two)
            di = lax.dot_general(
                lhs[...].reshape(two, width), wd_v[cols, :], (((1,), (1,)), ((), ())), preferred_element_type=f32
            )
            low_a[:, cols] = (di * slope_g[rows, cols]).astype(bf)
            low_b[:, cols] = (di * slope_u[rows, cols]).astype(bf)

    def result(p, cols):
        if p == 0:
            return jnp.dot(low_a[...], wd_v[:, cols], preferred_element_type=f32)
        nt = (((1,), (1,)), ((), ()))
        return lax.dot_general(
            low_a[...], wg_v[cols, :], nt, preferred_element_type=f32
        ) + lax.dot_general(low_b[...], wu_v[cols, :], nt, preferred_element_type=f32)

    def run(p, first, wait):
        send_across(p).start()
        send_mate(p).start()
        if p == 0:
            for k in (1, 3, 2):
                gather_z(k).start()
        else:
            pl.when(z < 3)(gather_near(1).start)
            pl.when(z > 0)(gather_near(3).start)
        send_mate(p).wait_recv()
        first(own.at[p], 0, wait)
        if wait:
            for j in range(tiles):
                wcopy(2, j).wait()
        for j in range(width // tile):
            cols = pl.ds(j * tile, tile)
            new = result(p, cols).astype(bf)
            for s in range(2):
                qown[p, s, :, cols] = new[s * shard : (s + 1) * shard]
        part_own(p).start()
        send_across(p).wait_recv()
        forward(p).start()
        forward(p).wait_recv()
        for cp in store_row(p, gh_ref if p == 0 else gd_ref):
            cp.start()
        first(oth.at[p], two, False)
        for h in range(2):
            for j in range(half // tile):
                new = result(p, pl.ds(h * half + j * tile, tile)).astype(bf)
                for s in range(2):
                    pown[p, h, s, :, pl.ds(j * tile, tile)] = new[s * shard : (s + 1) * shard]
            part_mate(p, h).start()
            part_mate(p, h).wait_recv()
            xsend[p, h] = (pown[p, h, c].astype(f32) + pmate[p, h].astype(f32)).astype(bf)
            part_across(p, h).start()
        part_own(p).wait_recv()
        sums = []
        for h in range(2):
            part_across(p, h).wait_recv()
            cols = slice(h * half, (h + 1) * half)
            sums.append(
                qown[p, c, :, cols].astype(f32) + qmate[p, :, cols].astype(f32) + xrecv[p, h].astype(f32)
            )
        return jnp.concatenate(sums, axis=1)

    att = att_ref[...]
    hid[...] = tok_ref[...].astype(f32) + att * mean_inv(att) * ga_ref[...]
    own[0, c] = hid[...].astype(bf)
    mlp = run(0, forward_in, True)
    rf = mean_inv(mlp)
    fh = mlp * rf
    gy = cot_ref[...].astype(f32)
    out_ref[...] = (hid[...] + fh * gm_ref[...]).astype(bf)
    scaled = gy * gm_ref[...]
    dm = (rf * (scaled - fh * jnp.mean(scaled * fh, axis=1, keepdims=True))).astype(bf)
    gain_ref[1:2, :] = jnp.sum(gy * fh, axis=0, keepdims=True)
    own[1, c] = dm
    back = run(1, backward_in, False)
    gh = cot_ref[...].astype(f32) + back
    ghid_ref[...] = gh
    ra = mean_inv(att_ref[...])
    ah = att_ref[...] * ra
    gain_ref[0:1, :] = jnp.sum(gh * ah, axis=0, keepdims=True)
    scaled = gh * ga_ref[...]
    dat_ref[...] = (ra * (scaled - ah * jnp.mean(scaled * ah, axis=1, keepdims=True))).astype(bf)

    for p in range(2):
        send_across(p).wait_send()
        send_mate(p).wait_send()
        forward(p).wait_send()
        part_own(p).wait_send()
        for h in range(2):
            part_mate(p, h).wait_send()
            part_across(p, h).wait_send()
        for cp in store_row(p, gh_ref if p == 0 else gd_ref):
            cp.wait()
    for k in range(1, 4):
        gather_z(k).wait()
    pl.when(z < 3)(gather_near(1).wait_send)
    pl.when(z > 0)(gather_near(3).wait_send)
    pl.when(z > 0)(gather_near(1).wait_recv)
    pl.when(z < 3)(gather_near(3).wait_recv)


def mlp_both(att, tok, cot, ga, gm, wg, wu, wd):
    shard, width = tok.shape
    ff = wg.shape[1]
    bf = jnp.bfloat16
    f32 = jnp.float32
    dma = pltpu.SemaphoreType.DMA
    half = width // 2
    vm = pl.BlockSpec(memory_space=pltpu.VMEM)
    shape = jax.ShapeDtypeStruct
    return pl.pallas_call(
        mlp_kernel,
        name="feed_forward",
        out_shape=(
            shape((shard, width), bf),
            shape((shard, width), f32),
            shape((shard, width), bf),
            shape((2, width), f32),
            shape((4, 4, shard, width), bf),
            shape((4, 4, shard, width), bf),
        ),
        in_specs=[vm] * 5 + [FULL] * 3,
        out_specs=(vm,) * 4 + (FULL,) * 2,
        scratch_shapes=[
            pltpu.VMEM((width, ff), bf),
            pltpu.VMEM((width, ff), bf),
            pltpu.VMEM((ff, width), bf),
            pltpu.VMEM((4 * shard, ff), f32),
            pltpu.VMEM((4 * shard, ff), f32),
            pltpu.VMEM((2, 2, shard, width), bf),
            pltpu.VMEM((2, 2, shard, width), bf),
            pltpu.VMEM((2 * shard, ff), bf),
            pltpu.VMEM((2 * shard, ff), bf),
            pltpu.VMEM((2, 2, 2, shard, half), bf),
            pltpu.VMEM((2, 2, shard, half), bf),
            pltpu.VMEM((2, 2, shard, half), bf),
            pltpu.VMEM((2, 2, shard, half), bf),
            pltpu.VMEM((2, 2, shard, width), bf),
            pltpu.VMEM((2, shard, width), bf),
            pltpu.VMEM((shard, width), f32),
            dma((3, ff // 512)),
            dma((2,)), dma((2,)), dma((2,)), dma((2,)), dma((2,)), dma((2,)),
            dma((2, 2)), dma((2, 2)), dma((2, 2)), dma((2, 2)),
            dma((2,)), dma((2,)),
            dma((2, 3)), dma((2, 3)),
            dma((2, 4)),
        ],
        compiler_params=pltpu.CompilerParams(
            collective_id=1, has_side_effects=True, vmem_limit_bytes=60 * 1024 * 1024
        ),
        cost_estimate=pl.CostEstimate(
            flops=2 * 6 * 4 * shard * width * ff, bytes_accessed=40 * 1024 * 1024, transcendentals=4 * shard * ff
        ),
    )(att, tok, cot, ga.reshape(1, -1), gm.reshape(1, -1), wg, wu, wd)


NT = (((1,), (1,)), ((), ()))
TN = (((0,), (0,)), ((), ()))


def places():
    d = lax.axis_index("dp")
    t = lax.axis_index("tensor")
    c = t % 2
    return d, t, d // 2, d % 2, c, t // 2, t + 1 - 2 * c, (t + 2) % 4


def greet(targets):
    barrier = pltpu.get_barrier_semaphore()
    for dd, tt in targets:
        pl.semaphore_signal(barrier, inc=1, device_id=(dd, tt), device_id_type=MESH)
    pl.semaphore_wait(barrier, len(targets))


def to_rows(column):
    n = column.shape[0]
    return jnp.broadcast_to(column, (n, n)).T[0:8, :]


def to_column(rows):
    n = rows.shape[1]
    return jnp.broadcast_to(rows[0:1, :], (n, n)).T[:, 0:1]


def attend_kernel(
    tok_ref, cos_ref, sin_ref, segc_ref, segr_ref, gq_ref, gk_ref, wq_ref, wk_ref, wv_ref, wo_ref,
    att_ref, tall_ref, tnext_ref, qh_ref, kh_ref, qr_ref, kr_ref, v_ref, mix_ref, p_ref, inv_ref,
    w_v, wo_v, tall, raw, rot, val, mixed, prob, stat, stat_in, pown, pmate, xsend, xrecv, qown, qmate,
    w_sem, as_s, as_r, ss_s, ss_r, ps_s, ps_r, px_s, px_r, pq_s, pq_r, st_sem, ns_s, ns_r,
):
    d, t, z, y, c, chip, mate, across = places()
    far = (mate + 2) % 4
    shard, width = tok_ref.shape
    local = w_v.shape[2]
    bf = jnp.bfloat16
    f32 = jnp.float32
    heads = local // HD
    weights = [
        pltpu.make_async_copy(r, w_v.at[i], w_sem.at[i]) for i, r in enumerate((wq_ref, wk_ref, wv_ref))
    ] + [pltpu.make_async_copy(wo_ref, wo_v, w_sem.at[3])]
    for cp in weights:
        cp.start()
    tall[t] = tok_ref[...]
    twin = z * 2 + 1 - y
    greet([(d, mate), (d, across), (d, far), (twin, t)])

    send_x = far_copy(tall.at[t], tall.at[t], as_s.at[0], as_r.at[0], d, across)
    send_m = far_copy(tall.at[t], tall.at[t], as_s.at[1], as_r.at[1], d, mate)
    forward = far_copy(tall.at[across], tall.at[across], as_s.at[2], as_r.at[2], d, mate)
    send_x.start()
    send_m.start()
    next_y = far_copy(tall.at[t], tnext_ref.at[t], ns_s.at[0], ns_r.at[0], twin, t)
    halves = (pl.ds(0, shard // 2), pl.ds(shard // 2, shard // 2))
    next_x = [
        far_copy(tnext_ref.at[t, rows], tnext_ref.at[t, rows], ns_s.at[i], ns_r.at[i], d, across)
        for i, rows in ((1, halves[0]), (4, halves[1]))
    ]
    next_c = [
        far_copy(tnext_ref.at[q], tnext_ref.at[q], ns_s.at[2 + i], ns_r.at[2 + i], d, mate)
        for i, q in enumerate((t, across))
    ]
    next_y.start()

    def project(first):
        rows = tall[pl.ds(first, 2)].reshape(2 * shard, width)
        for i in range(3):
            new = jnp.dot(rows, w_v[i], preferred_element_type=f32).reshape(2, shard, local)
            if i == 2:
                val[pl.ds(first, 2)] = new.astype(bf)
            else:
                raw[i, pl.ds(first, 2)] = new
                for s in range(2):
                    stat[first + s, i * 8 : i * 8 + 8, :] = to_rows(
                        jnp.sum(new[s] * new[s], axis=1, keepdims=True)
                    )

    here = chip * 2
    there = 2 - chip * 2
    for cp in weights[:3]:
        cp.wait()
    send_m.wait_recv()
    project(here)
    send_x.wait_recv()
    forward.start()
    forward.wait_recv()
    next_y.wait_recv()
    next_x[0].start()
    project(there)

    stats = [
        far_copy(stat, stat_in.at[i], ss_s.at[i], ss_r.at[i], d, who)
        for i, who in enumerate((mate, across, far))
    ]
    for cp in stats:
        cp.start()
    next_x[1].start()
    stores = [
        pltpu.make_async_copy(tall, tall_ref, st_sem.at[0]),
        pltpu.make_async_copy(val, v_ref, st_sem.at[1]),
    ]
    for cp in stores:
        cp.start()
    for cp in stats:
        cp.wait_recv()

    for q in range(4):
        inv = lax.rsqrt((stat[q] + stat_in[0, q] + stat_in[1, q] + stat_in[2, q]) / width + EPS)
        inv_ref[q] = inv
        for i, gain in ((0, gq_ref), (1, gk_ref)):
            unit = raw[i, q] * to_column(inv[i * 8 : i * 8 + 8])
            raw[i, q] = unit
            unit = unit * gain[...]
            for h in range(heads):
                cols = slice(h * HD, (h + 1) * HD)
                one = unit[:, cols]
                rot[i, q, :, cols] = (
                    one * cos_ref[q] + pltpu.roll(one, HD // 2, 1) * sin_ref[q]
                ).astype(bf)
    more = [
        pltpu.make_async_copy(raw.at[0], qh_ref, st_sem.at[2]),
        pltpu.make_async_copy(raw.at[1], kh_ref, st_sem.at[3]),
        pltpu.make_async_copy(rot.at[0], qr_ref, st_sem.at[4]),
        pltpu.make_async_copy(rot.at[1], kr_ref, st_sem.at[5]),
    ]
    for cp in more:
        cp.start()
    stores += more

    scale = 1.0 / math.sqrt(HD)
    total = 4 * shard

    def mix(first, n):
        ids = first * shard + lax.broadcasted_iota(jnp.int32, (2 * shard, total), 0)
        keys = lax.broadcasted_iota(jnp.int32, (2 * shard, total), 1)
        same = segc_ref[pl.ds(first, 2)].reshape(2 * shard, 1) == segr_ref[...]
        ok = same & (keys <= ids)
        for h in range(heads):
            cols = slice(h * HD, (h + 1) * HD)
            s = lax.dot_general(
                rot[0, pl.ds(first, 2), :, cols].reshape(2 * shard, HD),
                rot[1, :, :, cols].reshape(total, HD),
                NT,
                preferred_element_type=f32,
            )
            s = jnp.where(ok, s * scale, -1e30)
            e = jnp.exp(s - jnp.max(s, axis=1, keepdims=True))
            p = e / jnp.sum(e, axis=1, keepdims=True)
            prob[pl.ds(first, 2), h] = p.reshape(2, shard, total)
            mixed[pl.ds(first, 2), :, cols] = (
                jnp.dot(p.astype(bf), val[:, :, cols].reshape(total, HD), preferred_element_type=f32)
                .astype(bf)
                .reshape(2, shard, HD)
            )
        cp = pltpu.make_async_copy(prob.at[pl.ds(first, 2)], p_ref.at[pl.ds(first, 2)], st_sem.at[6 + n])
        cp.start()
        stores.append(cp)

    half = width // 2
    tile = 512

    def part_mate(h):
        return far_copy(pown.at[h, 1 - c], pmate.at[h], ps_s.at[h], ps_r.at[h], d, mate)

    def part_across(h):
        return far_copy(xsend.at[h], xrecv.at[h], px_s.at[h], px_r.at[h], d, across)

    part_own = far_copy(qown.at[1 - c], qmate, pq_s, pq_r, d, mate)

    mix(there, 0)
    for cp in next_x:
        cp.wait_recv()
    for cp in next_c:
        cp.start()
    weights[3].wait()
    for h in range(2):
        for j in range(half // tile):
            new = jnp.dot(
                mixed[pl.ds(there, 2)].reshape(2 * shard, local),
                wo_v[:, pl.ds(h * half + j * tile, tile)],
                preferred_element_type=f32,
            ).astype(bf)
            pown[h, :, :, pl.ds(j * tile, tile)] = new.reshape(2, shard, tile)
        part_mate(h).start()
    for h in range(2):
        part_mate(h).wait_recv()
        xsend[h] = (pown[h, c].astype(f32) + pmate[h].astype(f32)).astype(bf)
        part_across(h).start()
    mix(here, 1)
    for j in range(width // tile):
        new = jnp.dot(
            mixed[pl.ds(here, 2)].reshape(2 * shard, local),
            wo_v[:, pl.ds(j * tile, tile)],
            preferred_element_type=f32,
        ).astype(bf)
        qown[:, :, pl.ds(j * tile, tile)] = new.reshape(2, shard, tile)
    part_own.start()
    cp = pltpu.make_async_copy(mixed, mix_ref, st_sem.at[8])
    cp.start()
    stores.append(cp)
    part_own.wait_recv()
    for h in range(2):
        part_across(h).wait_recv()
        cols = slice(h * half, (h + 1) * half)
        att_ref[:, cols] = (
            qown[c, :, cols].astype(f32) + qmate[:, cols].astype(f32) + xrecv[h].astype(f32)
        )
    for cp in stores:
        cp.wait()
    for cp in next_c:
        cp.wait_recv()
    for cp in [send_x, send_m, forward, part_own, next_y] + next_x + next_c + stats:
        cp.wait_send()
    for h in range(2):
        part_mate(h).wait_send()
        part_across(h).wait_send()


def attend_both(tok, cos, sin, seg, gq, gk, wq, wk, wv, wo):
    shard, width = tok.shape
    local = wq.shape[1]
    heads = local // HD
    bf = jnp.bfloat16
    f32 = jnp.float32
    dma = pltpu.SemaphoreType.DMA
    vm = pl.BlockSpec(memory_space=pltpu.VMEM)
    shape = jax.ShapeDtypeStruct
    half = width // 2
    total = 4 * shard
    return pl.pallas_call(
        attend_kernel,
        name="attend_forward",
        out_shape=(
            shape((shard, width), f32),
            shape((4, shard, width), bf),
            shape((4, shard, width), bf),
            shape((4, shard, local), f32),
            shape((4, shard, local), f32),
            shape((4, shard, local), bf),
            shape((4, shard, local), bf),
            shape((4, shard, local), bf),
            shape((4, shard, local), bf),
            shape((4, heads, shard, total), f32),
            shape((4, 16, shard), f32),
        ),
        in_specs=[vm] * 7 + [FULL] * 4,
        out_specs=(vm,) + (FULL,) * 9 + (vm,),
        scratch_shapes=[
            pltpu.VMEM((3, width, local), bf),
            pltpu.VMEM((local, width), bf),
            pltpu.VMEM((4, shard, width), bf),
            pltpu.VMEM((2, 4, shard, local), f32),
            pltpu.VMEM((2, 4, shard, local), bf),
            pltpu.VMEM((4, shard, local), bf),
            pltpu.VMEM((4, shard, local), bf),
            pltpu.VMEM((4, heads, shard, total), f32),
            pltpu.VMEM((4, 16, shard), f32),
            pltpu.VMEM((3, 4, 16, shard), f32),
            pltpu.VMEM((2, 2, shard, half), bf),
            pltpu.VMEM((2, shard, half), bf),
            pltpu.VMEM((2, shard, half), bf),
            pltpu.VMEM((2, shard, half), bf),
            pltpu.VMEM((2, shard, width), bf),
            pltpu.VMEM((shard, width), bf),
            dma((4,)),
            dma((3,)), dma((3,)), dma((3,)), dma((3,)),
            dma((2,)), dma((2,)), dma((2,)), dma((2,)),
            dma(()), dma(()),
            dma((9,)),
            dma((5,)), dma((5,)),
        ],
        compiler_params=pltpu.CompilerParams(
            collective_id=2, has_side_effects=True, vmem_limit_bytes=56 * 1024 * 1024
        ),
        cost_estimate=pl.CostEstimate(
            flops=2 * total * width * local * 4, bytes_accessed=24 * 1024 * 1024, transcendentals=heads * total * total
        ),
    )(
        tok, cos.reshape(4, shard, HD), sin.reshape(4, shard, HD), seg.reshape(4, shard, 1), seg.reshape(1, total),
        gq.reshape(1, -1), gk.reshape(1, -1), wq, wk, wv, wo,
    )


EARLY = (1, 3)


def attend_back_kernel(
    dat_ref, ghid_ref, cos_ref, sin_ref, gq_ref, gk_ref, inv_ref,
    wq_ref, wk_ref, wv_ref, wo_ref, qh_ref, kh_ref, qr_ref, kr_ref, v_ref, p_ref, mix_ref, gh_in, gd_in,
    gt_ref, gain_ref, dq_ref, dk_ref, dv_ref, po_ref, gh_ref, gd_ref,
    w_v, wo_v, dall, unit, rot, val, dmix, prob, scaled, low, mixed, lhs_t, full, part, stat, stat_in, pown, pmate, xsend, xrecv, qown, qmate,
    w_sem, as_s, as_r, ss_s, ss_r, ps_s, ps_r, px_s, px_r, pq_s, pq_r, hx_s, hx_r, hc_s, hc_r, ys_s, ys_r, zs_s, zs_r, st_sem,
):
    d, t, z, y, c, chip, mate, across = places()
    far = (mate + 2) % 4
    shard, width = dat_ref.shape
    local = w_v.shape[2]
    bf = jnp.bfloat16
    f32 = jnp.float32
    heads = local // HD
    total = 4 * shard
    sources = (wo_ref, mix_ref, v_ref, p_ref, qr_ref, kr_ref, qh_ref, kh_ref, wq_ref, wk_ref, wv_ref)
    homes = (wo_v, mixed, val, prob, rot.at[0], rot.at[1], unit.at[0], unit.at[1], w_v.at[0], w_v.at[1], w_v.at[2])
    loads = [pltpu.make_async_copy(a, b, w_sem.at[i]) for i, (a, b) in enumerate(zip(sources, homes))]
    for cp in loads:
        cp.start()
    dall[t] = dat_ref[...]
    twin = z * 2 + 1 - y
    above = ((z + 1) % 4) * 2 + y
    below = ((z + 3) % 4) * 2 + y
    greet([(d, mate), (d, across), (d, far), (twin, t), (above, t), (below, t)])

    def climb(i, r):
        return far_copy(gd_ref.at[r, t], gd_ref.at[r, t], zs_s.at[0, i], zs_r.at[0, i], above, t)

    def sink(i, r):
        return far_copy(gd_ref.at[r, t], gd_ref.at[r, t], zs_s.at[1, i], zs_r.at[1, i], below, t)

    middle = (z > 0) & (z < 3)
    pl.when(middle)(climb(0, (z + 3) % 4).start)
    pl.when(middle)(sink(0, (z + 1) % 4).start)

    send_x = far_copy(dall.at[t], dall.at[t], as_s.at[0], as_r.at[0], d, across)
    send_m = far_copy(dall.at[t], dall.at[t], as_s.at[1], as_r.at[1], d, mate)
    forward = far_copy(dall.at[across], dall.at[across], as_s.at[2], as_r.at[2], d, mate)
    send_x.start()
    send_m.start()
    ahead = [(z + 4 - k) % 4 for k in EARLY]
    rows_x = [
        far_copy(gh_ref.at[r, t], gh_ref.at[r, t], hx_s.at[i], hx_r.at[i], d, across) for i, r in enumerate(ahead)
    ]
    rows_c = [
        far_copy(gh_ref.at[r, q], gh_ref.at[r, q], hc_s.at[i, j], hc_r.at[i, j], d, mate)
        for i, r in enumerate(ahead)
        for j, q in enumerate((t, across))
    ]
    swap_y = far_copy(full.at[:, 1 - y], part, ys_s, ys_r, twin, t)

    def project(first):
        rows = dall[pl.ds(first, 2)].reshape(2 * shard, width)
        dmix[pl.ds(first, 2)] = (
            lax.dot_general(rows, wo_v[...], NT, preferred_element_type=f32).astype(bf).reshape(2, shard, local)
        )

    here = chip * 2
    there = 2 - chip * 2
    loads[0].wait()
    send_m.wait_recv()
    project(here)
    for cp in loads[1:]:
        cp.wait()
    send_x.wait_recv()
    forward.start()
    forward.wait_recv()
    rows_x[0].start()
    project(there)
    lhs_t[...] = mixed[...].reshape(total, local).astype(f32).T.astype(bf)
    block = full.shape[3]
    for b in range(8):
        full[b // 2, b % 2] = jnp.dot(
            lhs_t[...], dall[:, :, b * block : (b + 1) * block].reshape(total, block), preferred_element_type=f32
        ).astype(bf)
    swap_y.start()
    stores = []
    pl.when(z > 1)(climb(0, (z + 2) % 4).wait_recv)
    pl.when(z < 2)(sink(0, (z + 2) % 4).wait_recv)
    pl.when(z == 2)(climb(1, 0).start)
    pl.when(z == 1)(sink(1, 3).start)

    scale = 1.0 / math.sqrt(HD)
    cos = cos_ref[...].reshape(total, HD)
    sin = sin_ref[...].reshape(total, HD)
    dots = [jnp.zeros((total, 1), f32), jnp.zeros((total, 1), f32)]
    for h in range(heads):
        cols = slice(h * HD, (h + 1) * HD)
        dm = dmix[:, :, cols].reshape(total, HD)
        p = prob[:, h].reshape(total, total)
        dp = lax.dot_general(dm, val[:, :, cols].reshape(total, HD), NT, preferred_element_type=f32)
        ds = (p * (dp - jnp.sum(p * dp, axis=1, keepdims=True))).astype(bf)
        low[2, :, :, cols] = (
            lax.dot_general(p.astype(bf), dm, TN, preferred_element_type=f32).astype(bf).reshape(4, shard, HD)
        )
        back = (
            jnp.dot(ds, rot[1, :, :, cols].reshape(total, HD), preferred_element_type=f32) * scale,
            lax.dot_general(ds, rot[0, :, :, cols].reshape(total, HD), TN, preferred_element_type=f32) * scale,
        )
        for i, gain in ((0, gq_ref), (1, gk_ref)):
            g = back[i]
            g = g * cos - pltpu.roll(g, HD // 2, 1) * sin
            u = unit[i, :, :, cols].reshape(total, HD)
            prod = g * u
            gain_ref[i : i + 1, cols] = jnp.sum(prod, axis=0, keepdims=True)
            dots[i] = dots[i] + jnp.sum(prod * gain[:, cols], axis=1, keepdims=True)
            scaled[i, :, :, cols] = (g * gain[:, cols]).reshape(4, shard, HD)
    for q in range(4):
        for i in range(2):
            stat[q, i * 8 : i * 8 + 8, :] = to_rows(dots[i][q * shard : (q + 1) * shard])
    stats = [
        far_copy(stat, stat_in.at[i], ss_s.at[i], ss_r.at[i], d, who)
        for i, who in enumerate((mate, across, far))
    ]
    for cp in stats:
        cp.start()
    rows_x[1].start()
    for cp in stats:
        cp.wait_recv()

    def finish(first):
        for s in range(2):
            q = first + s
            mean = (stat[q] + stat_in[0, q] + stat_in[1, q] + stat_in[2, q]) / width
            inv = inv_ref[q]
            for i in range(2):
                low[i, q] = (
                    to_column(inv[i * 8 : i * 8 + 8])
                    * (scaled[i, q] - unit[i, q] * to_column(mean[i * 8 : i * 8 + 8]))
                ).astype(bf)

    half = width // 2
    tile = 512

    def part_mate(h):
        return far_copy(pown.at[h, 1 - c], pmate.at[h], ps_s.at[h], ps_r.at[h], d, mate)

    def part_across(h):
        return far_copy(xsend.at[h], xrecv.at[h], px_s.at[h], px_r.at[h], d, across)

    part_own = far_copy(qown.at[1 - c], qmate, pq_s, pq_r, d, mate)

    def result(first, start):
        new = None
        for i in range(3):
            one = lax.dot_general(
                low[i, pl.ds(first, 2)].reshape(2 * shard, local),
                w_v[i, pl.ds(start, tile), :],
                NT,
                preferred_element_type=f32,
            )
            new = one if new is None else new + one
        return new.astype(bf).reshape(2, shard, tile)

    finish(there)
    for h in range(2):
        for j in range(half // tile):
            pown[h, :, :, pl.ds(j * tile, tile)] = result(there, h * half + j * tile)
        part_mate(h).start()
        part_mate(h).wait_recv()
        xsend[h] = (pown[h, c].astype(f32) + pmate[h].astype(f32)).astype(bf)
        part_across(h).start()
    finish(here)
    more = [
        pltpu.make_async_copy(low.at[i], r, st_sem.at[1 + i]) for i, r in enumerate((dq_ref, dk_ref, dv_ref))
    ]
    for cp in more:
        cp.start()
    stores += more
    for j in range(width // tile):
        qown[:, :, pl.ds(j * tile, tile)] = result(here, j * tile)
    part_own.start()
    for cp in rows_x:
        cp.wait_recv()
    for cp in rows_c:
        cp.start()
    swap_y.wait_recv()
    for b in range(4):
        part[b] = (part[b].astype(f32) + full[b, y].astype(f32)).astype(bf)
    keep = pltpu.make_async_copy(part, po_ref, st_sem.at[0])
    keep.start()
    stores.append(keep)
    part_own.wait_recv()
    for h in range(2):
        part_across(h).wait_recv()
        cols = slice(h * half, (h + 1) * half)
        gt_ref[:, cols] = (
            ghid_ref[:, cols]
            + (qown[c, :, cols].astype(f32) + qmate[:, cols].astype(f32) + xrecv[h].astype(f32))
        ).astype(bf)
    for cp in stores:
        cp.wait()
    for cp in rows_c:
        cp.wait_recv()
    pl.when(middle)(climb(0, (z + 3) % 4).wait_send)
    pl.when(middle)(sink(0, (z + 1) % 4).wait_send)
    pl.when(z == 2)(climb(1, 0).wait_send)
    pl.when(z == 1)(sink(1, 3).wait_send)
    pl.when(z == 3)(climb(1, 0).wait_recv)
    pl.when(z == 0)(sink(1, 3).wait_recv)
    for cp in [send_x, send_m, forward, part_own, swap_y] + stats + rows_x + rows_c:
        cp.wait_send()
    for h in range(2):
        part_mate(h).wait_send()
        part_across(h).wait_send()


def attend_back_both(dat, ghid, cos, sin, gq, gk, inv, wq, wk, wv, wo, qh, kh, qr, kr, v, p, mix, gh, gd):
    shard, width = dat.shape
    local = wq.shape[1]
    heads = local // HD
    bf = jnp.bfloat16
    f32 = jnp.float32
    dma = pltpu.SemaphoreType.DMA
    vm = pl.BlockSpec(memory_space=pltpu.VMEM)
    shape = jax.ShapeDtypeStruct
    half = width // 2
    total = 4 * shard
    return pl.pallas_call(
        attend_back_kernel,
        name="attend_backward",
        out_shape=(
            shape((shard, width), bf),
            shape((2, local), f32),
            shape((4, shard, local), bf),
            shape((4, shard, local), bf),
            shape((4, shard, local), bf),
            shape((4, local, width // 8), bf),
            shape(gh.shape, bf),
            shape(gd.shape, bf),
        ),
        in_specs=[vm] * 7 + [FULL] * 13,
        out_specs=(vm,) * 2 + (FULL,) * 6,
        input_output_aliases={18: 6, 19: 7},
        scratch_shapes=[
            pltpu.VMEM((3, width, local), bf),
            pltpu.VMEM((local, width), bf),
            pltpu.VMEM((4, shard, width), bf),
            pltpu.VMEM((2, 4, shard, local), f32),
            pltpu.VMEM((2, 4, shard, local), bf),
            pltpu.VMEM((4, shard, local), bf),
            pltpu.VMEM((4, shard, local), bf),
            pltpu.VMEM((4, heads, shard, total), f32),
            pltpu.VMEM((2, 4, shard, local), f32),
            pltpu.VMEM((3, 4, shard, local), bf),
            pltpu.VMEM((4, shard, local), bf),
            pltpu.VMEM((local, total), bf),
            pltpu.VMEM((4, 2, local, width // 8), bf),
            pltpu.VMEM((4, local, width // 8), bf),
            pltpu.VMEM((4, 16, shard), f32),
            pltpu.VMEM((3, 4, 16, shard), f32),
            pltpu.VMEM((2, 2, shard, half), bf),
            pltpu.VMEM((2, shard, half), bf),
            pltpu.VMEM((2, shard, half), bf),
            pltpu.VMEM((2, shard, half), bf),
            pltpu.VMEM((2, shard, width), bf),
            pltpu.VMEM((shard, width), bf),
            dma((11,)),
            dma((3,)), dma((3,)), dma((3,)), dma((3,)),
            dma((2,)), dma((2,)), dma((2,)), dma((2,)),
            dma(()), dma(()), dma((2,)), dma((2,)), dma((2, 2)), dma((2, 2)), dma(()), dma(()),
            dma((2, 2)), dma((2, 2)),
            dma((4,)),
        ],
        compiler_params=pltpu.CompilerParams(
            collective_id=3, has_side_effects=True, vmem_limit_bytes=56 * 1024 * 1024
        ),
        cost_estimate=pl.CostEstimate(
            flops=2 * total * width * local * 4 + 10 * heads * total * total * HD,
            bytes_accessed=24 * 1024 * 1024,
            transcendentals=0,
        ),
    )(
        dat, ghid, cos.reshape(4, shard, HD), sin.reshape(4, shard, HD), gq.reshape(1, -1), gk.reshape(1, -1), inv,
        wq, wk, wv, wo, qh, kh, qr, kr, v, p, mix, gh, gd,
    )


def place_kernel(a_ref, p_ref, m_ref, q_ref, k_ref, v_ref, o_ref, g_ref, u_ref, d_ref):
    f32 = jnp.float32
    n = a_ref.shape[2]
    for w, ref in ((0, v_ref), (1, q_ref), (2, k_ref)):
        for i in range(2):
            ref[:, i * n : (i + 1) * n] = a_ref[w, i].astype(f32).T
    new = p_ref[0].astype(f32)
    for i in range(1, 4):
        new = new + p_ref[i].astype(f32)
    o_ref[...] = new
    f = m_ref.shape[2]
    for i in range(2):
        d_ref[i * f : (i + 1) * f, :] = m_ref[0, i].astype(f32)
        g_ref[:, i * f : (i + 1) * f] = m_ref[1, i].astype(f32).T
        u_ref[:, i * f : (i + 1) * f] = m_ref[2, i].astype(f32).T


def place_grads(attn, proj, mlp):
    _, f, block = proj.shape
    f32 = jnp.float32
    vm = pl.BlockSpec(memory_space=pltpu.VMEM)
    shape = jax.ShapeDtypeStruct
    return pl.pallas_call(
        place_kernel,
        name="place_grads",
        out_shape=(
            shape((block, f), f32),
            shape((block, f), f32),
            shape((block, f), f32),
            shape((f, block), f32),
            shape((block, 4 * f), f32),
            shape((block, 4 * f), f32),
            shape((4 * f, block), f32),
        ),
        in_specs=[vm] * 3,
        out_specs=(vm,) * 7,
        compiler_params=pltpu.CompilerParams(vmem_limit_bytes=40 * 1024 * 1024),
    )(attn, proj, mlp)


def plain_body(
    tokens,
    lengths,
    w_query,
    w_key,
    w_value,
    w_out,
    w_gate,
    w_up,
    w_down,
    gain_query,
    gain_key,
    gain_attn,
    gain_mlp,
    cotangent,
):
    rows_dev = lengths.shape[0]
    model_width = w_query.shape[0]
    local_width = w_query.shape[1]
    head_count = local_width // HD
    gathered = lax.all_gather(tokens, "tensor", axis=0, tiled=True)
    row_count = gathered.shape[0]
    segment, offsets = jax.vmap(row_layout)(lengths)
    queries = jnp.dot(gathered, w_query, preferred_element_type=jnp.float32)
    keys_raw = jnp.dot(gathered, w_key, preferred_element_type=jnp.float32)
    values_low = jnp.dot(gathered, w_value, preferred_element_type=jnp.float32).astype(jnp.bfloat16)
    q_total, k_total = lax.psum(
        (jnp.sum(queries * queries, axis=1), jnp.sum(keys_raw * keys_raw, axis=1)), "tensor"
    )
    q_inv = lax.rsqrt(q_total / model_width + EPS)[:, None]
    k_inv = lax.rsqrt(k_total / model_width + EPS)[:, None]
    q_unit = queries * q_inv
    k_unit = keys_raw * k_inv

    def to_heads(values):
        return values.reshape(rows_dev, ROW_LEN, head_count, HD)

    queries_low = rotate(to_heads(q_unit * gain_query), offsets, 1.0).astype(jnp.bfloat16)
    keys_low = rotate(to_heads(k_unit * gain_key), offsets, 1.0).astype(jnp.bfloat16)
    values_heads = to_heads(values_low)
    mixed_heads, log_total = jax.vmap(lambda *a: attend(a))(
        queries_low, keys_low, values_heads, segment
    )
    mixed_low = mixed_heads.reshape(row_count, local_width)
    attn_out = lax.psum_scatter(
        jnp.dot(mixed_low, w_out, preferred_element_type=jnp.float32).astype(jnp.bfloat16),
        "tensor",
        scatter_dimension=0,
        tiled=True,
    ).astype(jnp.float32)
    inner_count = lax.axis_size("dp") // OUTER
    a_inv = lax.rsqrt(jnp.mean(attn_out * attn_out, axis=1, keepdims=True) + EPS)
    a_unit = attn_out * a_inv
    hidden = tokens.astype(jnp.float32) + a_unit * gain_attn
    hidden_low = hidden.astype(jnp.bfloat16)
    hidden_all = lax.all_gather(hidden_low, "tensor", axis=0, tiled=True)
    outer_index = lax.axis_index("dp") // inner_count

    def gather_group(shard):
        groups = [[z * inner_count + i for z in range(OUTER)] for i in range(inner_count)]
        part = lax.all_gather(shard, "dp", axis=0, tiled=True, axis_index_groups=groups)
        return lax.all_gather(part, "tensor", axis=0, tiled=True)

    hidden_group = gather_group(hidden_low)
    gate_acts = jnp.dot(hidden_all, w_gate, preferred_element_type=jnp.float32)
    up_acts = jnp.dot(hidden_all, w_up, preferred_element_type=jnp.float32)
    gate_sigmoid = jax.nn.sigmoid(gate_acts)
    inner_low = (gate_acts * gate_sigmoid * up_acts).astype(jnp.bfloat16)
    mlp_out = lax.psum_scatter(
        jnp.dot(inner_low, w_down, preferred_element_type=jnp.float32).astype(jnp.bfloat16),
        "tensor",
        scatter_dimension=0,
        tiled=True,
    ).astype(jnp.float32)
    f_inv = lax.rsqrt(jnp.mean(mlp_out * mlp_out, axis=1, keepdims=True) + EPS)
    f_unit = mlp_out * f_inv
    output = (hidden + f_unit * gain_mlp).astype(jnp.bfloat16)
    grad_output = cotangent.astype(jnp.float32)
    grad_mlp, grad_gain_mlp_part = post_norm_back(grad_output, f_unit, f_inv, gain_mlp)
    grad_mlp_low = grad_mlp.astype(jnp.bfloat16)
    mlp_grad_all = lax.all_gather(grad_mlp_low, "tensor", axis=0, tiled=True)
    mlp_grad_group = gather_group(grad_mlp_low)
    grad_inner = times_t(mlp_grad_all, w_down)
    grad_gate_low = (
        grad_inner * up_acts * gate_sigmoid * (1.0 + gate_acts * (1.0 - gate_sigmoid))
    ).astype(jnp.bfloat16)
    grad_up_low = (grad_inner * gate_acts * gate_sigmoid).astype(jnp.bfloat16)
    part_width = w_gate.shape[1] // OUTER
    gate_part = lax.dynamic_slice_in_dim(w_gate, outer_index * part_width, part_width, 1)
    up_part = lax.dynamic_slice_in_dim(w_up, outer_index * part_width, part_width, 1)
    down_part = lax.dynamic_slice_in_dim(w_down, outer_index * part_width, part_width, 0)
    gate_g = jnp.dot(hidden_group, gate_part, preferred_element_type=jnp.float32)
    up_g = jnp.dot(hidden_group, up_part, preferred_element_type=jnp.float32)
    sig_g = jax.nn.sigmoid(gate_g)
    inner_g = (gate_g * sig_g * up_g).astype(jnp.bfloat16)
    grad_inner_g = times_t(mlp_grad_group, down_part)
    grad_gate_g = (grad_inner_g * up_g * sig_g * (1.0 + gate_g * (1.0 - sig_g))).astype(
        jnp.bfloat16
    )
    grad_up_g = (grad_inner_g * gate_g * sig_g).astype(jnp.bfloat16)
    sum_down = scatter_join(split_cols(t_times(inner_g, mlp_grad_group), inner_count), inner_count, 0)
    sum_gate = scatter_join(split_rows(t_times(hidden_group, grad_gate_g), inner_count), inner_count, 1)
    sum_up = scatter_join(split_rows(t_times(hidden_group, grad_up_g), inner_count), inner_count, 1)
    grad_hidden = grad_output + lax.psum_scatter(
        (times_t(grad_gate_low, w_gate) + times_t(grad_up_low, w_up)).astype(jnp.bfloat16),
        "tensor",
        scatter_dimension=0,
        tiled=True,
    ).astype(jnp.float32)
    grad_attn, grad_gain_attn_part = post_norm_back(grad_hidden, a_unit, a_inv, gain_attn)
    grad_attn_low = grad_attn.astype(jnp.bfloat16)
    attn_grad_all = lax.all_gather(grad_attn_low, "tensor", axis=0, tiled=True)
    grad_mixed = times_t(attn_grad_all, w_out).astype(jnp.bfloat16)
    grad_q_rot, grad_k_rot, grad_values_low = jax.vmap(lambda *a: attend_back(a))(
        queries_low, keys_low, values_heads, segment, log_total, to_heads(grad_mixed)
    )
    grad_q_norm = rotate(grad_q_rot, offsets, -1.0).reshape(row_count, local_width)
    grad_k_norm = rotate(grad_k_rot, offsets, -1.0).reshape(row_count, local_width)
    grad_gain_query_part = jnp.sum(grad_q_norm * q_unit, axis=0)
    grad_gain_key_part = jnp.sum(grad_k_norm * k_unit, axis=0)
    q_scaled = grad_q_norm * gain_query
    k_scaled = grad_k_norm * gain_key
    q_dots, k_dots = lax.psum(
        (jnp.sum(q_scaled * q_unit, axis=1), jnp.sum(k_scaled * k_unit, axis=1)), "tensor"
    )
    grad_queries_low = (q_inv * (q_scaled - q_unit * (q_dots / model_width)[:, None])).astype(
        jnp.bfloat16
    )
    grad_keys_low = (k_inv * (k_scaled - k_unit * (k_dots / model_width)[:, None])).astype(
        jnp.bfloat16
    )
    grad_values_flat = grad_values_low.reshape(row_count, local_width)
    grad_tokens = (
        grad_hidden
        + lax.psum_scatter(
            (
                times_t(grad_queries_low, w_query)
                + times_t(grad_keys_low, w_key)
                + times_t(grad_values_flat, w_value)
            ).astype(jnp.bfloat16),
            "tensor",
            scatter_dimension=0,
            tiled=True,
        ).astype(jnp.float32)
    ).astype(jnp.bfloat16)
    tensor_start = lax.axis_index("tensor") * local_width
    zero_row = jnp.zeros((model_width,), jnp.float32)
    q_full = lax.dynamic_update_slice(zero_row, grad_gain_query_part, (tensor_start,))
    k_full = lax.dynamic_update_slice(zero_row, grad_gain_key_part, (tensor_start,))
    gain_stack = jnp.stack([q_full, k_full, grad_gain_attn_part, grad_gain_mlp_part])
    gain_total = lax.psum(gain_stack, ("dp", "tensor"))
    grad_gain_query = lax.dynamic_slice(gain_total[0], (tensor_start,), (local_width,))
    grad_gain_key = lax.dynamic_slice(gain_total[1], (tensor_start,), (local_width,))
    summed = (
        scatter_sum(split_rows(t_times(gathered, grad_queries_low), inner_count), inner_count),
        scatter_sum(split_rows(t_times(gathered, grad_keys_low), inner_count), inner_count),
        scatter_sum(split_rows(t_times(gathered, grad_values_flat), inner_count), inner_count),
        scatter_sum(split_cols(t_times(mixed_low, attn_grad_all), inner_count), inner_count),
        sum_gate,
        sum_up,
        sum_down,
    )
    return (
        output,
        grad_tokens,
        summed[0],
        summed[1],
        summed[2],
        summed[3],
        summed[4],
        summed[5],
        summed[6],
        grad_gain_query,
        grad_gain_key,
        gain_total[2],
        gain_total[3],
    )


def fused_body(
    tokens,
    lengths,
    w_query,
    w_key,
    w_value,
    w_out,
    w_gate,
    w_up,
    w_down,
    gain_query,
    gain_key,
    gain_attn,
    gain_mlp,
    cotangent,
):
    local_width = w_query.shape[1]
    segment, offsets = row_layout(lengths[0])
    half_width = HD // 2
    frequency = jnp.exp(
        jnp.arange(half_width, dtype=jnp.float32) * (-2.0 * math.log(THETA) / HD)
    )
    angles = offsets.astype(jnp.float32)[:, None] * frequency
    cosines = jnp.cos(angles)
    sines = jnp.sin(angles)
    cosines = jnp.concatenate([cosines, cosines], axis=1)
    sines = jnp.concatenate([-sines, sines], axis=1)
    attn_out, tokens_all, tokens_next, q_unit, k_unit, q_rot, k_rot, values, mixed, weights, inverse = attend_both(
        tokens, cosines, sines, segment, gain_query, gain_key, w_query, w_key, w_value, w_out
    )
    output, grad_hidden, grad_attn, gain_parts, group_h, group_d = mlp_both(
        attn_out, tokens, cotangent, gain_attn, gain_mlp, w_gate, w_up, w_down
    )
    grad_tokens, head_gains, grad_q, grad_k, grad_v, proj, group_h, group_d = attend_back_both(
        grad_attn, grad_hidden, cosines, sines, gain_query, gain_key, inverse,
        w_query, w_key, w_value, w_out, q_unit, k_unit, q_rot, k_rot, values, weights, mixed, group_h, group_d,
    )
    gains, attn_blocks, proj_blocks, mlp_blocks, _, _ = weight_grads(
        gain_parts, head_gains, group_h, group_d, w_gate, w_up, w_down, tokens_all, tokens_next,
        grad_q, grad_k, grad_v, proj,
    )
    return (
        output,
        grad_tokens,
        *place_grads(attn_blocks, proj_blocks, mlp_blocks),
        gains[2, :local_width],
        gains[3, :local_width],
        gains[0],
        gains[1],
    )


def solution(mesh):
    placed = (
        P(("dp", "tensor"), None),
        P("dp", None),
        P(None, "tensor"),
        P(None, "tensor"),
        P(None, "tensor"),
        P("tensor", None),
        P(None, "tensor"),
        P(None, "tensor"),
        P("tensor", None),
        P("tensor"),
        P("tensor"),
        P(),
        P(),
        P(("dp", "tensor"), None),
    )
    return jax.shard_map(
        fused_body if tuple(mesh.shape.values()) == (8, 4) else plain_body,
        mesh=mesh,
        in_specs=placed,
        out_specs=(
            P(("dp", "tensor"), None),
            P(("dp", "tensor"), None),
            P("dp", "tensor"),
            P("dp", "tensor"),
            P("dp", "tensor"),
            P("tensor", "dp"),
            P("dp", "tensor"),
            P("dp", "tensor"),
            P("tensor", "dp"),
            P("tensor"),
            P("tensor"),
            P(),
            P(),
        ),
        check_vma=False,
    )
```

```python
import math

import jax
import jax.numpy as jnp
from jax import lax
from jax.experimental import pallas as pl
from jax.experimental.pallas import tpu as pltpu
from jax.sharding import PartitionSpec as P

HD = 128
ROW_LEN = 512


EPS = 1e-06
THETA = 500000.0


def rotate(values, offsets, rot_sign):
    half_width = values.shape[-1] // 2
    frequency = jnp.exp(
        jnp.arange(half_width, dtype=jnp.float32) * (-2.0 * math.log(THETA) / values.shape[-1])
    )
    angles = offsets.astype(jnp.float32)[..., None, None] * frequency
    cosines = jnp.cos(angles)
    sine_part = rot_sign * jnp.sin(angles)
    first_half = values[..., :half_width]
    second_half = values[..., half_width:]
    return jnp.concatenate(
        [
            first_half * cosines - second_half * sine_part,
            second_half * cosines + first_half * sine_part,
        ],
        axis=-1,
    )


def row_layout(lengths_row):
    slots = jnp.arange(lengths_row.shape[0], dtype=jnp.int32)
    seq_ends = jnp.sum(
        jnp.where(slots[None, :] <= slots[:, None], lengths_row[None, :], 0), axis=1
    )
    position = jnp.arange(ROW_LEN, dtype=jnp.int32)
    passed = (position[:, None] >= seq_ends[None, :]).astype(jnp.int32)
    segment = jnp.sum(passed, axis=1)
    seq_start = jnp.sum(passed * lengths_row[None, :], axis=1)
    return (segment, position - seq_start)


def allowed_mask(segment):
    position = jnp.arange(segment.shape[0], dtype=jnp.int32)
    return (segment[:, None] == segment[None, :]) & (position[None, :] <= position[:, None])


def times_t(left_mat, right_mat):
    return lax.dot_general(
        left_mat, right_mat, (((1,), (1,)), ((), ())), preferred_element_type=jnp.float32
    )


def t_times(left_mat, right_mat):
    return lax.dot_general(
        left_mat, right_mat, (((0,), (0,)), ((), ())), preferred_element_type=jnp.float32
    )


def masked_scores(queries_low, keys_low, segment):
    scale_factor = 1.0 / math.sqrt(queries_low.shape[-1])
    scores = (
        jnp.einsum("qhd,khd->hqk", queries_low, keys_low, preferred_element_type=jnp.float32)
        * scale_factor
    )
    return jnp.where(allowed_mask(segment)[None], scores, -1e30)


def attend(block_item):
    queries_low, keys_low, values_low, segment = block_item
    scores = masked_scores(queries_low, keys_low, segment)
    row_max = jnp.max(scores, axis=-1, keepdims=True)
    shifted = jnp.exp(scores - row_max)
    row_total = jnp.sum(shifted, axis=-1, keepdims=True)
    attn_weights = (shifted / row_total).astype(jnp.bfloat16)
    mixed = jnp.einsum("hqk,khd->qhd", attn_weights, values_low, preferred_element_type=jnp.float32)
    return (mixed.astype(jnp.bfloat16), (row_max + jnp.log(row_total))[..., 0])


def attend_back(block_item):
    queries_low, keys_low, values_low, segment, log_total, grad_mixed = block_item
    scale_factor = 1.0 / math.sqrt(queries_low.shape[-1])
    scores = masked_scores(queries_low, keys_low, segment)
    attn_weights = jnp.exp(scores - log_total[..., None])
    grad_weights = jnp.einsum(
        "qhd,khd->hqk", grad_mixed, values_low, preferred_element_type=jnp.float32
    )
    row_dots = jnp.sum(attn_weights * grad_weights, axis=-1, keepdims=True)
    grad_scores = (attn_weights * (grad_weights - row_dots)).astype(jnp.bfloat16)
    grad_queries = scale_factor * jnp.einsum(
        "hqk,khd->qhd", grad_scores, keys_low, preferred_element_type=jnp.float32
    )
    grad_keys = scale_factor * jnp.einsum(
        "hqk,qhd->khd", grad_scores, queries_low, preferred_element_type=jnp.float32
    )
    grad_values = jnp.einsum(
        "hqk,qhd->khd",
        attn_weights.astype(jnp.bfloat16),
        grad_mixed,
        preferred_element_type=jnp.float32,
    )
    return (grad_queries, grad_keys, grad_values.astype(jnp.bfloat16))


def post_norm_back(grad_in, unit_rows, inv_scale, gain_vec):
    scaled = grad_in * gain_vec
    mean_dots = jnp.mean(scaled * unit_rows, axis=-1, keepdims=True)
    return (inv_scale * (scaled - unit_rows * mean_dots), jnp.sum(grad_in * unit_rows, axis=0))


OUTER = 4


def swap(value, shift):
    size = lax.axis_size("dp")
    return lax.ppermute(value, "dp", [(d, d ^ shift) for d in range(size)])


def pick(parts, index):
    return lax.dynamic_index_in_dim(parts, index, 0, keepdims=False)


def sum_inner(parts):
    inner = parts.shape[0]
    mine = lax.axis_index("dp") % inner
    total = pick(parts, mine)
    for k in range(1, inner):
        sent = pick(parts, mine ^ k).astype(jnp.bfloat16)
        total = total + swap(sent, k).astype(jnp.float32)
    return total


def trade_outer(parts, inner):
    mine = lax.axis_index("dp") // inner
    got = [(mine, pick(parts, mine))]
    for k in range(1, OUTER):
        got.append((mine ^ k, swap(pick(parts, mine ^ k), k * inner)))
    return got


def split_rows(grad, inner):
    cols = grad.shape[1]
    return grad.reshape(OUTER, inner, -1, cols).transpose(1, 0, 2, 3)


def split_cols(grad, inner):
    rows = grad.shape[0]
    return grad.reshape(rows, OUTER, inner, -1).transpose(2, 1, 0, 3)


def scatter_sum(parts, inner):
    half = sum_inner(parts).astype(jnp.bfloat16)
    got = trade_outer(half, inner)
    return sum(g.astype(jnp.float32) for _, g in got)


def scatter_join(parts, inner, axis):
    half = sum_inner(parts).astype(jnp.bfloat16)
    got = trade_outer(half, inner)
    stack = jnp.zeros((OUTER, *got[0][1].shape), jnp.bfloat16)
    for place, block in got:
        stack = lax.dynamic_update_index_in_dim(stack, block, place, 0)
    joined = jnp.concatenate([stack[z] for z in range(OUTER)], axis=axis)
    return joined.astype(jnp.float32)


MESH = pl.DeviceIdType.MESH
FULL = pl.BlockSpec(memory_space=pl.ANY)


def grads_kernel(
    gp_ref, gqk_ref, gh_in, gm_in, lhs_ref, wgt_ref, wut_ref, wd_ref, tok_ref, nxt_ref, dq_ref, dk_ref, dv_ref, po_ref,
    gain_ref, attn_ref, proj_ref, mlp_ref, gh_ref, gm_ref,
    hb_v, hb_w, tip_v, dm_v, wd_v, lhs_in, lhs_q, lhs_t, quad, quad_in, pair, full, part, gbuf, gin,
    ld_sem, xs_s, xs_r, cs_s, cs_r, qs_s, qs_r, os_s, os_r, qz_s, qz_r, qy_s, qy_r, ys_s, ys_r, ts_s, ts_r, own_s, gs_s, gs_r, lhs_sem,
):
    d = lax.axis_index("dp")
    t = lax.axis_index("tensor")
    z = d // 2
    y = d % 2
    side = z % 2
    top = z // 2
    mate = t + 1 - 2 * (t % 2)
    across = (t + 2) % 4
    twin = z * 2 + 1 - y
    pal = (z + 1 - 2 * side) * 2 + y
    bf = jnp.bfloat16
    f32 = jnp.float32
    f = lhs_t.shape[1]
    width = hb_v.shape[3]
    shard = hb_v.shape[2]
    span = width // 2
    hc = lhs_in.shape[4]
    total = 4 * shard

    def peer(k):
        return ((z + k) % 4) * 2 + y

    heads = (dv_ref, dq_ref, dk_ref)
    parts = (top, 1 - top)
    ranks = rank_rows(z)
    slow = [
        pltpu.make_async_copy(
            wd_ref.at[pl.ds(side * f, f), pl.ds(parts[i] * span, span)], wd_v.at[i], ld_sem.at[4 + i]
        )
        for i in range(2)
    ] + [
        pltpu.make_async_copy(r.at[:, :, pl.ds(y * hc, hc)], lhs_in.at[w, 0], ld_sem.at[6 + w])
        for w, r in enumerate(heads)
    ]
    toks = [
        pltpu.make_async_copy(r, hb_v.at[i], ld_sem.at[i]) for i, r in enumerate((tok_ref, nxt_ref))
    ]

    def lhs_load(n, w):
        return pltpu.make_async_copy(
            lhs_ref.at[n, w], lhs_t.at[w, :, pl.ds(n * total, total)], lhs_sem.at[n, w]
        )

    def dm_load(n, i):
        return pltpu.make_async_copy(
            gm_ref.at[ranks[n], :, :, pl.ds(parts[i] * span, span)], dm_v.at[n, i], ld_sem.at[9 + n * 2 + i]
        )

    def hb_load(n):
        return pltpu.make_async_copy(gh_ref.at[ranks[n]], hb_w, ld_sem.at[2 + n % 2])

    tips = [
        pltpu.make_async_copy(r, tip_v.at[i], ld_sem.at[21 + i]) for i, r in enumerate((wgt_ref, wut_ref))
    ]
    hb_load(2).start()
    for cp in tips + slow[2:] + toks + slow[:2]:
        cp.start()
    for n in range(2):
        for w in range(3):
            lhs_load(n, w).start()
    for n in range(3):
        for i in range(2):
            dm_load(n, i).start()

    greet([(peer(1), t), (peer(2), t), (peer(3), t), (twin, t), (d, mate), (d, across)])

    groups = (gh_ref, gm_ref)

    def head_swap(w):
        return far_copy(
            heads[w].at[:, :, pl.ds((1 - y) * hc, hc)], lhs_in.at[w, 1], qs_s.at[w], qs_r.at[w], twin, t
        )

    def proj_trade(k):
        return far_copy(po_ref.at[(z + k) % 4], proj_ref.at[z], os_s.at[k - 1], os_r.at[k - 1], peer(k), t)

    def piece(i):
        return gm_ref, ranks[3], pl.ds(parts[i] * span, span)

    def cell(i, q):
        ref, r, cols = piece(i)
        return ref.at[r, q, :, cols]

    def forward_x(i):
        return far_copy(cell(i, t), cell(i, t), xs_s.at[i], xs_r.at[i], d, across)

    def forward_c(i, h):
        q = t if h == 0 else across
        return far_copy(cell(i, q), cell(i, q), cs_s.at[i, h], cs_r.at[i, h], d, mate)

    def advance(i):
        pl.when(edge)(forward_x(i).wait_recv)
        for h in range(2):
            forward_c(i, h).start()

    def arrive(i):
        for h in range(2):
            forward_c(i, h).wait_recv()

    def gain_copy(i):
        stage, who = ((0, (peer(1), t)), (0, (peer(2), t)), (0, (peer(3), t)), (1, (twin, t)), (2, (d, across)), (3, (d, mate)))[i]
        return far_copy(gbuf.at[stage], gin.at[i], gs_s.at[i], gs_r.at[i], *who)

    gbuf[0] = jnp.zeros_like(gbuf[0])
    gbuf[0, 0:2, :] = gp_ref[...]
    gbuf[0, 2:4, 0 : gqk_ref.shape[1]] = gqk_ref[...]
    for i in range(3):
        gain_copy(i).start()
    for w in range(3):
        head_swap(w).start()
    edge = (z == 0) | (z == 3)
    for i in range(2):
        pl.when(edge)(forward_x(i).start)
    for k in (2, 1, 3):
        proj_trade(k).start()
    keep_proj = pltpu.make_async_copy(po_ref.at[z], proj_ref.at[z], own_s.at[0])
    keep_proj.start()

    def gain_step(stage):
        new = gbuf[stage]
        for i in ((0, 1, 2), (3,), (4,), (5,))[stage]:
            gain_copy(i).wait_recv()
            new = new + gin[i]
        if stage < 3:
            gbuf[stage + 1] = new
            gain_copy(stage + 3).start()
        if stage == 1:
            gain_ref[2:4, :] = new[2:4, :]
        if stage == 3:
            gain_ref[0:2, :] = new[0:2, :]

    step = 256

    def remake(n):
        def wide(j, carry):
            cols = pl.ds(pl.multiple_of(j * step, step), step)
            hb = hb_w[...].reshape(total, width)
            g = lax.dot_general(tip_v[0, cols, :], hb, NT, preferred_element_type=f32)
            u = lax.dot_general(tip_v[1, cols, :], hb, NT, preferred_element_type=f32)
            sg = jax.nn.sigmoid(g)
            gs = g * sg
            spot = slice(n * total, (n + 1) * total)
            lhs_t[0, cols, spot] = (gs * u).astype(bf)
            lhs_t[1, cols, spot] = (u * sg * (1.0 + g * (1.0 - sg))).astype(bf)
            lhs_t[2, cols, spot] = gs.astype(bf)
            return carry

        lax.fori_loop(0, f // step, wide, 0)

    def scale_back(n):
        if n < 2:
            for w in (1, 2):
                lhs_load(n, w).wait()

        def wide(j, carry):
            cols = pl.ds(pl.multiple_of(j * step, step), step)
            di = None
            for i in range(2):
                one = lax.dot_general(
                    wd_v[i, cols, :], dm_v[n, i].reshape(total, span), NT, preferred_element_type=f32
                )
                di = one if di is None else di + one
            toks = slice(n * total, (n + 1) * total)
            for w in (1, 2):
                lhs_t[w, cols, toks] = (lhs_t[w, cols, toks].astype(f32) * di).astype(bf)
            return carry

        lax.fori_loop(0, f // step, wide, 0)

    def hb_half(n):
        return pltpu.make_async_copy(
            gh_ref.at[ranks[n], :, :, pl.ds(top * span, span)],
            hb_v.at[n // 2, :, :, pl.ds((n % 2) * span, span)],
            ld_sem.at[17 + n],
        )

    hb_load(2).wait()
    for cp in tips:
        cp.wait()
    remake(2)
    hb_load(3).start()

    block = quad.shape[4]

    def quad_trade(w, k):
        return far_copy(quad.at[w, (z + k) % 4], quad_in.at[w, k - 1], qz_s.at[w, k - 1], qz_r.at[w, k - 1], peer(k), t)

    def head_grad(w):
        slow[2 + w].wait()
        head_swap(w).wait_recv()
        for i in range(2):
            lhs_q[:, i * total : (i + 1) * total] = lhs_in[w, i].reshape(total, hc).astype(f32).T.astype(bf)

        def tile(j, carry):
            cols = pl.ds(pl.multiple_of(j * block, block), block)
            quad[w, j // 2, j % 2] = jnp.dot(
                lhs_q[...], hb_v[:, :, :, cols].reshape(2 * total, block), preferred_element_type=f32
            ).astype(bf)
            return carry

        lax.fori_loop(0, 8, tile, 0)
        for k in (2, 1, 3):
            quad_trade(w, k).start()

    for cp in toks:
        cp.wait()
    head_grad(0)
    advance(0)
    hb_load(3).wait()
    remake(3)
    gain_step(0)
    head_grad(1)
    head_grad(2)
    advance(1)
    for n in range(4):
        hb_half(n).start()
    for i in range(2):
        arrive(i)
        dm_load(3, i).start()
    gain_step(1)

    def swap_y(w):
        return far_copy(full.at[w, :, 1 - y], part.at[w], ys_s.at[w], ys_r.at[w], twin, t)

    def trade_z(w):
        return far_copy(part.at[w, 1 - side], mlp_ref.at[w, side], ts_s.at[w], ts_r.at[w], pal, t)

    def keep(w):
        return pltpu.make_async_copy(part.at[w, side], mlp_ref.at[w, side], own_s.at[1 + w])

    def finish_y(w):
        swap_y(w).wait()
        for b in range(2):
            part[w, b] = (part[w, b].astype(f32) + full[w, b, y].astype(f32)).astype(bf)
        trade_z(w).start()
        keep(w).start()

    def emit(w):
        for b in range(4):
            new = None
            for n in range(4):
                one = jnp.dot(
                    lhs_t[w, :, n * total : (n + 1) * total],
                    (dm_v[n, 0, :, :, b * block : (b + 1) * block] if w == 0 else hb_v[
                        n // 2, :, :, (n % 2) * span + b * block : (n % 2) * span + (b + 1) * block
                    ]).reshape(total, block),
                    preferred_element_type=f32,
                )
                new = one if new is None else new + one
            full[w, b // 2, b % 2] = new.astype(bf)
        swap_y(w).start()

    for n in range(2):
        lhs_load(n, 0).wait()
    for n in range(4):
        dm_load(n, 0).wait()
    emit(0)
    for i in range(2):
        slow[i].wait()
    for n in range(4):
        dm_load(n, 1).wait()
        scale_back(n)
    gain_step(2)
    for n in range(4):
        hb_half(n).wait()
    emit(1)
    emit(2)
    gain_step(3)

    def head_swap_back(w):
        return far_copy(pair.at[w, 1 - y], attn_ref.at[w, y], qy_s.at[w], qy_r.at[w], twin, t)

    def head_keep(w):
        return pltpu.make_async_copy(pair.at[w, y], attn_ref.at[w, y], own_s.at[4 + w])

    def finish_head(w):
        for k in range(1, 4):
            quad_trade(w, k).wait_recv()
        for b in range(2):
            new = quad[w, z, b].astype(f32)
            for i in range(3):
                new = new + quad_in[w, i, b].astype(f32)
            pair[w, b] = new.astype(bf)
        head_swap_back(w).start()
        head_keep(w).start()

    finish_y(0)
    finish_head(0)
    finish_y(1)
    finish_head(1)
    finish_head(2)
    finish_y(2)

    keep_proj.wait()
    for i in range(6):
        gain_copy(i).wait_send()
    for i in range(2):
        pl.when(edge)(forward_x(i).wait_send)
        for h in range(2):
            forward_c(i, h).wait_send()
    for k in range(1, 4):
        proj_trade(k).wait()
    for w in range(3):
        head_swap(w).wait_send()
        for k in range(1, 4):
            quad_trade(w, k).wait_send()
        head_keep(w).wait()
        keep(w).wait()
        head_swap_back(w).wait()
        trade_z(w).wait()


def weight_grads(gp, gqk, gh, gd, lhs, wgt, wut, wd, tok, nxt, dq, dk, dv, po):
    shard, width = tok.shape[1], tok.shape[2]
    f = lhs.shape[2]
    local = dq.shape[2]
    block = width // 8
    bf = jnp.bfloat16
    f32 = jnp.float32
    dma = pltpu.SemaphoreType.DMA
    shape = jax.ShapeDtypeStruct
    vm = pl.BlockSpec(memory_space=pltpu.VMEM)
    flops = 2 * 4 * shard * 4 * f * (3 * width + 3 * width // 2)
    return pl.pallas_call(
        grads_kernel,
        name="weight_grads",
        input_output_aliases={2: 4, 3: 5},
        out_shape=(
            shape((4, width), f32),
            shape((3, 2, local // 2, block), bf),
            shape((4, local, block), bf),
            shape((3, 2, f, block), bf),
            shape(gh.shape, bf),
            shape(gd.shape, bf),
        ),
        in_specs=[vm] * 2 + [FULL] * 12,
        out_specs=(vm,) + (FULL,) * 5,
        scratch_shapes=[
            pltpu.VMEM((2, 4, shard, width), bf),
            pltpu.VMEM((4, shard, width), bf),
            pltpu.VMEM((2, f, width), bf),
            pltpu.VMEM((4, 2, 4, shard, width // 2), bf),
            pltpu.VMEM((2, f, width // 2), bf),
            pltpu.VMEM((3, 2, 4, shard, local // 2), bf),
            pltpu.VMEM((local // 2, 8 * shard), bf),
            pltpu.VMEM((3, f, 16 * shard), bf),
            pltpu.VMEM((3, 4, 2, local // 2, block), bf),
            pltpu.VMEM((3, 3, 2, local // 2, block), bf),
            pltpu.VMEM((3, 2, local // 2, block), bf),
            pltpu.VMEM((3, 2, 2, f, block), bf),
            pltpu.VMEM((3, 2, f, block), bf),
            pltpu.VMEM((4, 8, width), f32),
            pltpu.VMEM((6, 8, width), f32),
            dma((23,)),
            dma((2,)), dma((2,)), dma((2, 2)), dma((2, 2)),
            dma((3,)), dma((3,)), dma((3,)), dma((3,)),
            dma((3, 3)), dma((3, 3)), dma((3,)), dma((3,)),
            dma((3,)), dma((3,)), dma((3,)), dma((3,)),
            dma((7,)), dma((6,)), dma((6,)), dma((2, 3)),
        ],
        compiler_params=pltpu.CompilerParams(
            collective_id=0, has_side_effects=True, vmem_limit_bytes=60 * 1024 * 1024
        ),
        cost_estimate=pl.CostEstimate(flops=flops, bytes_accessed=60 * 1024 * 1024, transcendentals=0),
    )(gp, gqk, gh, gd, lhs, wgt, wut, wd, tok, nxt, dq, dk, dv, po)


def far_copy(src, dst, ss, rs, dd, tt):
    return pltpu.make_async_remote_copy(
        src_ref=src, dst_ref=dst, send_sem=ss, recv_sem=rs, device_id=(dd, tt), device_id_type=MESH
    )


def mean_inv(values):
    return lax.rsqrt(jnp.mean(values * values, axis=1, keepdims=True) + EPS)


def mlp_kernel(
    att_ref, tok_ref, cot_ref, ga_ref, gm_ref, wg_ref, wu_ref, wd_ref,
    out_ref, ghid_ref, dat_ref, gain_ref, gh_ref, gd_ref,
    wg_v, wu_v, wd_v, slope_g, slope_u, own, oth, low_a, low_b, pown, pmate, xsend, xrecv, qown, qmate, hid,
    w_sem, as_s, as_r, ax_s, ax_r, af_s, af_r, ps_s, ps_r, px_s, px_r, pq_s, pq_r, zs_s, zs_r, ds_s, ds_r, hc_s, hc_r, st_sem,
):
    d = lax.axis_index("dp")
    t = lax.axis_index("tensor")
    z = d // 2
    y = d % 2
    c = t % 2
    chip = t // 2
    mate = t + 1 - 2 * c
    across = (t + 2) % 4
    shard, width = att_ref.shape
    ff = wg_v.shape[1]
    bf = jnp.bfloat16
    f32 = jnp.float32
    tile = 512
    tiles = ff // tile

    def wcopy(i, j):
        cols = pl.ds(j * tile, tile)
        if i == 0:
            return pltpu.make_async_copy(wg_ref.at[:, cols], wg_v.at[:, cols], w_sem.at[0, j])
        if i == 1:
            return pltpu.make_async_copy(wu_ref.at[:, cols], wu_v.at[:, cols], w_sem.at[1, j])
        return pltpu.make_async_copy(wd_ref.at[cols, :], wd_v.at[cols, :], w_sem.at[2, j])

    for j in range(tiles):
        wcopy(0, j).start()
        wcopy(1, j).start()
    for j in range(tiles):
        wcopy(2, j).start()

    barrier = pltpu.get_barrier_semaphore()
    for dd, tt in [(((z + 1) % 4) * 2 + y, t), (((z + 3) % 4) * 2 + y, t), (d, mate), (d, across)]:
        pl.semaphore_signal(barrier, inc=1, device_id=(dd, tt), device_id_type=MESH)
    pl.semaphore_wait(barrier, 4)

    def send_mate(p):
        return far_copy(own.at[p, c], own.at[p, c], as_s.at[p], as_r.at[p], d, mate)

    def send_across(p):
        return far_copy(own.at[p, c], oth.at[p, c], ax_s.at[p], ax_r.at[p], d, across)

    def forward(p):
        return far_copy(oth.at[p, c], oth.at[p, c], af_s.at[p], af_r.at[p], d, mate)

    half = width // 2

    def part_mate(p, h):
        return far_copy(
            pown.at[p, h, 1 - c], pmate.at[p, h], ps_s.at[p, h], ps_r.at[p, h], d, mate
        )

    def part_across(p, h):
        return far_copy(xsend.at[p, h], xrecv.at[p, h], px_s.at[p, h], px_r.at[p, h], d, across)

    def part_own(p):
        return far_copy(qown.at[p, 1 - c], qmate.at[p], pq_s.at[p], pq_r.at[p], d, mate)

    lines_h = [Line(gh_ref, z, y, t, q, zs_s.at[i], zs_r.at[i]) for i, q in enumerate((t, across))]
    lines_d = [Line(gd_ref, z, y, t, q, ds_s.at[i], ds_r.at[i]) for i, q in enumerate((t, across))]
    ranks = rank_rows(z)

    def row_c(p, i):
        cell = gh_ref.at[ranks[1 + p], t if i == 0 else across]
        return far_copy(cell, cell, hc_s.at[p, i], hc_r.at[p, i], d, mate)

    def store_row(p, ref):
        mine = ref.at[z]
        return [
            pltpu.make_async_copy(own.at[p, 0], mine.at[chip * 2], st_sem.at[p, 0]),
            pltpu.make_async_copy(own.at[p, 1], mine.at[chip * 2 + 1], st_sem.at[p, 1]),
            pltpu.make_async_copy(oth.at[p, 0], mine.at[2 - chip * 2], st_sem.at[p, 2]),
            pltpu.make_async_copy(oth.at[p, 1], mine.at[3 - chip * 2], st_sem.at[p, 3]),
        ]

    two = 2 * shard

    def forward_in(lhs, base, wait):
        for j in range(tiles):
            if wait:
                wcopy(0, j).wait()
                wcopy(1, j).wait()
            cols = pl.ds(j * tile, tile)
            rows = pl.ds(base, two)
            both = lhs[...].reshape(two, width)
            g = jnp.dot(both, wg_v[:, cols], preferred_element_type=f32)
            u = jnp.dot(both, wu_v[:, cols], preferred_element_type=f32)
            sg = jax.nn.sigmoid(g)
            gs = g * sg
            low_a[:, cols] = (gs * u).astype(bf)
            slope_u[rows, cols] = gs
            slope_g[rows, cols] = u * sg * (1.0 + g * (1.0 - sg))

    def backward_in(lhs, base, wait):
        for j in range(tiles):
            cols = pl.ds(j * tile, tile)
            rows = pl.ds(base, two)
            di = lax.dot_general(
                lhs[...].reshape(two, width), wd_v[cols, :], (((1,), (1,)), ((), ())), preferred_element_type=f32
            )
            low_a[:, cols] = (di * slope_g[rows, cols]).astype(bf)
            low_b[:, cols] = (di * slope_u[rows, cols]).astype(bf)

    def result(p, cols):
        if p == 0:
            return jnp.dot(low_a[...], wd_v[:, cols], preferred_element_type=f32)
        nt = (((1,), (1,)), ((), ()))
        return lax.dot_general(
            low_a[...], wg_v[cols, :], nt, preferred_element_type=f32
        ) + lax.dot_general(low_b[...], wu_v[cols, :], nt, preferred_element_type=f32)

    def run(p, first, wait):
        send_across(p).start()
        send_mate(p).start()
        (lines_h, lines_d)[p][0].start(0, own.at[p, c])
        send_mate(p).wait_recv()
        first(own.at[p], 0, wait)
        if wait:
            for j in range(tiles):
                wcopy(2, j).wait()
        for j in range(width // tile):
            cols = pl.ds(j * tile, tile)
            new = result(p, cols).astype(bf)
            for s in range(2):
                qown[p, s, :, cols] = new[s * shard : (s + 1) * shard]
        part_own(p).start()
        send_across(p).wait_recv()
        forward(p).start()
        forward(p).wait_recv()
        (lines_h, lines_d)[p][1].start(0, oth.at[p, c])
        if p == 0:
            lines_h[0].landed(0)
            lines_h[0].start(1)
        for cp in store_row(p, gh_ref if p == 0 else gd_ref):
            cp.start()
        first(oth.at[p], two, False)
        for h in range(2):
            for j in range(half // tile):
                new = result(p, pl.ds(h * half + j * tile, tile)).astype(bf)
                for s in range(2):
                    pown[p, h, s, :, pl.ds(j * tile, tile)] = new[s * shard : (s + 1) * shard]
            part_mate(p, h).start()
            part_mate(p, h).wait_recv()
            xsend[p, h] = (pown[p, h, c].astype(f32) + pmate[p, h].astype(f32)).astype(bf)
            part_across(p, h).start()
        if p == 0:
            lines_h[1].landed(0)
            lines_h[1].start(1)
            for i in range(2):
                row_c(0, i).start()
        else:
            for line in lines_h:
                line.landed(1)
            for i in range(2):
                row_c(1, i).start()
        part_own(p).wait_recv()
        sums = []
        for h in range(2):
            part_across(p, h).wait_recv()
            cols = slice(h * half, (h + 1) * half)
            sums.append(
                qown[p, c, :, cols].astype(f32) + qmate[p, :, cols].astype(f32) + xrecv[p, h].astype(f32)
            )
        return jnp.concatenate(sums, axis=1)

    att = att_ref[...]
    hid[...] = tok_ref[...].astype(f32) + att * mean_inv(att) * ga_ref[...]
    own[0, c] = hid[...].astype(bf)
    mlp = run(0, forward_in, True)
    rf = mean_inv(mlp)
    fh = mlp * rf
    gy = cot_ref[...].astype(f32)
    out_ref[...] = (hid[...] + fh * gm_ref[...]).astype(bf)
    scaled = gy * gm_ref[...]
    dm = (rf * (scaled - fh * jnp.mean(scaled * fh, axis=1, keepdims=True))).astype(bf)
    gain_ref[1:2, :] = jnp.sum(gy * fh, axis=0, keepdims=True)
    own[1, c] = dm
    back = run(1, backward_in, False)
    gh = cot_ref[...].astype(f32) + back
    ghid_ref[...] = gh
    ra = mean_inv(att_ref[...])
    ah = att_ref[...] * ra
    gain_ref[0:1, :] = jnp.sum(gh * ah, axis=0, keepdims=True)
    scaled = gh * ga_ref[...]
    dat_ref[...] = (ra * (scaled - ah * jnp.mean(scaled * ah, axis=1, keepdims=True))).astype(bf)

    for p in range(2):
        send_across(p).wait_send()
        send_mate(p).wait_send()
        forward(p).wait_send()
        part_own(p).wait_send()
        for h in range(2):
            part_mate(p, h).wait_send()
            part_across(p, h).wait_send()
        for cp in store_row(p, gh_ref if p == 0 else gd_ref):
            cp.wait()
    for i in range(2):
        lines_h[i].sent(0, (own, oth)[i].at[0, c])
        lines_h[i].sent(1)
        lines_d[i].landed(0)
        lines_d[i].sent(0, (own, oth)[i].at[1, c])
    for p in range(2):
        for i in range(2):
            row_c(p, i).wait()


def mlp_both(att, tok, cot, ga, gm, wg, wu, wd):
    shard, width = tok.shape
    ff = wg.shape[1]
    bf = jnp.bfloat16
    f32 = jnp.float32
    dma = pltpu.SemaphoreType.DMA
    half = width // 2
    vm = pl.BlockSpec(memory_space=pltpu.VMEM)
    shape = jax.ShapeDtypeStruct
    return pl.pallas_call(
        mlp_kernel,
        name="feed_forward",
        out_shape=(
            shape((shard, width), bf),
            shape((shard, width), f32),
            shape((shard, width), bf),
            shape((2, width), f32),
            shape((4, 4, shard, width), bf),
            shape((4, 4, shard, width), bf),
        ),
        in_specs=[vm] * 5 + [FULL] * 3,
        out_specs=(vm,) * 4 + (FULL,) * 2,
        scratch_shapes=[
            pltpu.VMEM((width, ff), bf),
            pltpu.VMEM((width, ff), bf),
            pltpu.VMEM((ff, width), bf),
            pltpu.VMEM((4 * shard, ff), f32),
            pltpu.VMEM((4 * shard, ff), f32),
            pltpu.VMEM((2, 2, shard, width), bf),
            pltpu.VMEM((2, 2, shard, width), bf),
            pltpu.VMEM((2 * shard, ff), bf),
            pltpu.VMEM((2 * shard, ff), bf),
            pltpu.VMEM((2, 2, 2, shard, half), bf),
            pltpu.VMEM((2, 2, shard, half), bf),
            pltpu.VMEM((2, 2, shard, half), bf),
            pltpu.VMEM((2, 2, shard, half), bf),
            pltpu.VMEM((2, 2, shard, width), bf),
            pltpu.VMEM((2, shard, width), bf),
            pltpu.VMEM((shard, width), f32),
            dma((3, ff // 512)),
            dma((2,)), dma((2,)), dma((2,)), dma((2,)), dma((2,)), dma((2,)),
            dma((2, 2)), dma((2, 2)), dma((2, 2)), dma((2, 2)),
            dma((2,)), dma((2,)),
            dma((2, 2, 2)), dma((2, 2, 2)), dma((2, 2, 1)), dma((2, 2, 1)),
            dma((2, 2)), dma((2, 2)),
            dma((2, 4)),
        ],
        compiler_params=pltpu.CompilerParams(
            collective_id=1, has_side_effects=True, vmem_limit_bytes=60 * 1024 * 1024
        ),
        cost_estimate=pl.CostEstimate(
            flops=2 * 6 * 4 * shard * width * ff, bytes_accessed=40 * 1024 * 1024, transcendentals=4 * shard * ff
        ),
    )(att, tok, cot, ga.reshape(1, -1), gm.reshape(1, -1), wg, wu, wd)


NT = (((1,), (1,)), ((), ()))
TN = (((0,), (0,)), ((), ()))


def places():
    d = lax.axis_index("dp")
    t = lax.axis_index("tensor")
    c = t % 2
    return d, t, d // 2, d % 2, c, t // 2, t + 1 - 2 * c, (t + 2) % 4


def greet(targets):
    barrier = pltpu.get_barrier_semaphore()
    for dd, tt in targets:
        pl.semaphore_signal(barrier, inc=1, device_id=(dd, tt), device_id_type=MESH)
    pl.semaphore_wait(barrier, len(targets))


def to_rows(column):
    n = column.shape[0]
    return jnp.broadcast_to(column, (n, n)).T[0:8, :]


def to_column(rows):
    n = rows.shape[1]
    return jnp.broadcast_to(rows[0:1, :], (n, n)).T[:, 0:1]


def attend_kernel(
    tok_ref, cos_ref, sin_ref, segc_ref, segr_ref, gq_ref, gk_ref, wq_ref, wk_ref, wv_ref, wo_ref, wg_ref, wu_ref,
    att_ref, tall_ref, tnext_ref, qh_ref, kh_ref, qr_ref, kr_ref, v_ref, mix_ref, p_ref, inv_ref, wgt_ref, wut_ref,
    w_v, wo_v, wide, tipped, tall, raw, rot, val, mixed, prob, stat, stat_in, pown, pmate, xsend, xrecv, qown, qmate,
    w_sem, as_s, as_r, ss_s, ss_r, ps_s, ps_r, px_s, px_r, pq_s, pq_r, st_sem, ns_s, ns_r, tw_sem,
):
    d, t, z, y, c, chip, mate, across = places()
    far = (mate + 2) % 4
    shard, width = tok_ref.shape
    local = w_v.shape[2]
    bf = jnp.bfloat16
    f32 = jnp.float32
    heads = local // HD
    weights = [
        pltpu.make_async_copy(r, w_v.at[i], w_sem.at[i]) for i, r in enumerate((wq_ref, wk_ref, wv_ref))
    ] + [pltpu.make_async_copy(wo_ref, wo_v, w_sem.at[3])]
    for cp in weights:
        cp.start()
    span = wide.shape[2]
    side = z % 2
    tips = [
        pltpu.make_async_copy(r.at[:, pl.ds(side * span, span)], wide.at[i], tw_sem.at[i])
        for i, r in enumerate((wg_ref, wu_ref))
    ]
    for cp in tips:
        cp.start()
    drops = [
        pltpu.make_async_copy(tipped.at[i], r, tw_sem.at[2 + i]) for i, r in enumerate((wgt_ref, wut_ref))
    ]

    def tip(i):
        tips[i].wait()

        def one(j, carry):
            cols = pl.ds(pl.multiple_of(j * 128, 128), 128)
            tipped[i, cols, :] = wide[i, :, cols].T
            return carry

        lax.fori_loop(0, span // 128, one, 0)
        drops[i].start()

    tall[t] = tok_ref[...]
    twin = z * 2 + 1 - y
    greet([(d, mate), (d, across), (d, far), (twin, t)])

    send_x = far_copy(tall.at[t], tall.at[t], as_s.at[0], as_r.at[0], d, across)
    send_m = far_copy(tall.at[t], tall.at[t], as_s.at[1], as_r.at[1], d, mate)
    forward = far_copy(tall.at[across], tall.at[across], as_s.at[2], as_r.at[2], d, mate)
    send_x.start()
    send_m.start()
    next_y = far_copy(tall.at[t], tnext_ref.at[t], ns_s.at[0], ns_r.at[0], twin, t)
    halves = (pl.ds(0, shard // 2), pl.ds(shard // 2, shard // 2))
    next_x = [
        far_copy(tnext_ref.at[t, rows], tnext_ref.at[t, rows], ns_s.at[i], ns_r.at[i], d, across)
        for i, rows in ((1, halves[0]), (4, halves[1]))
    ]
    next_c = [
        far_copy(tnext_ref.at[q], tnext_ref.at[q], ns_s.at[2 + i], ns_r.at[2 + i], d, mate)
        for i, q in enumerate((t, across))
    ]
    next_y.start()

    def project(first):
        rows = tall[pl.ds(first, 2)].reshape(2 * shard, width)
        for i in range(3):
            new = jnp.dot(rows, w_v[i], preferred_element_type=f32).reshape(2, shard, local)
            if i == 2:
                val[pl.ds(first, 2)] = new.astype(bf)
            else:
                raw[i, pl.ds(first, 2)] = new
                for s in range(2):
                    stat[first + s, i * 8 : i * 8 + 8, :] = to_rows(
                        jnp.sum(new[s] * new[s], axis=1, keepdims=True)
                    )

    here = chip * 2
    there = 2 - chip * 2
    for cp in weights[:3]:
        cp.wait()
    send_m.wait_recv()
    project(here)
    tip(0)
    send_x.wait_recv()
    forward.start()
    forward.wait_recv()
    next_y.wait_recv()
    next_x[0].start()
    project(there)

    stats = [
        far_copy(stat, stat_in.at[i], ss_s.at[i], ss_r.at[i], d, who)
        for i, who in enumerate((mate, across, far))
    ]
    for cp in stats:
        cp.start()
    next_x[1].start()
    stores = [
        pltpu.make_async_copy(tall, tall_ref, st_sem.at[0]),
        pltpu.make_async_copy(val, v_ref, st_sem.at[1]),
    ]
    for cp in stores:
        cp.start()
    for cp in stats:
        cp.wait_recv()

    for q in range(4):
        inv = lax.rsqrt((stat[q] + stat_in[0, q] + stat_in[1, q] + stat_in[2, q]) / width + EPS)
        inv_ref[q] = inv
        for i, gain in ((0, gq_ref), (1, gk_ref)):
            unit = raw[i, q] * to_column(inv[i * 8 : i * 8 + 8])
            raw[i, q] = unit
            unit = unit * gain[...]
            for h in range(heads):
                cols = slice(h * HD, (h + 1) * HD)
                one = unit[:, cols]
                rot[i, q, :, cols] = (
                    one * cos_ref[q] + pltpu.roll(one, HD // 2, 1) * sin_ref[q]
                ).astype(bf)
    more = [
        pltpu.make_async_copy(raw.at[0], qh_ref, st_sem.at[2]),
        pltpu.make_async_copy(raw.at[1], kh_ref, st_sem.at[3]),
        pltpu.make_async_copy(rot.at[0], qr_ref, st_sem.at[4]),
        pltpu.make_async_copy(rot.at[1], kr_ref, st_sem.at[5]),
    ]
    for cp in more:
        cp.start()
    stores += more

    scale = 1.0 / math.sqrt(HD)
    total = 4 * shard

    def mix(first, n):
        ids = first * shard + lax.broadcasted_iota(jnp.int32, (2 * shard, total), 0)
        keys = lax.broadcasted_iota(jnp.int32, (2 * shard, total), 1)
        same = segc_ref[pl.ds(first, 2)].reshape(2 * shard, 1) == segr_ref[...]
        ok = same & (keys <= ids)
        for h in range(heads):
            cols = slice(h * HD, (h + 1) * HD)
            s = lax.dot_general(
                rot[0, pl.ds(first, 2), :, cols].reshape(2 * shard, HD),
                rot[1, :, :, cols].reshape(total, HD),
                NT,
                preferred_element_type=f32,
            )
            s = jnp.where(ok, s * scale, -1e30)
            e = jnp.exp(s - jnp.max(s, axis=1, keepdims=True))
            p = e / jnp.sum(e, axis=1, keepdims=True)
            prob[pl.ds(first, 2), h] = p.reshape(2, shard, total)
            mixed[pl.ds(first, 2), :, cols] = (
                jnp.dot(p.astype(bf), val[:, :, cols].reshape(total, HD), preferred_element_type=f32)
                .astype(bf)
                .reshape(2, shard, HD)
            )
        cp = pltpu.make_async_copy(prob.at[pl.ds(first, 2)], p_ref.at[pl.ds(first, 2)], st_sem.at[6 + n])
        cp.start()
        stores.append(cp)

    half = width // 2
    tile = 512

    def part_mate(h):
        return far_copy(pown.at[h, 1 - c], pmate.at[h], ps_s.at[h], ps_r.at[h], d, mate)

    def part_across(h):
        return far_copy(xsend.at[h], xrecv.at[h], px_s.at[h], px_r.at[h], d, across)

    part_own = far_copy(qown.at[1 - c], qmate, pq_s, pq_r, d, mate)

    mix(there, 0)
    for cp in next_x:
        cp.wait_recv()
    for cp in next_c:
        cp.start()
    weights[3].wait()
    for h in range(2):
        for j in range(half // tile):
            new = jnp.dot(
                mixed[pl.ds(there, 2)].reshape(2 * shard, local),
                wo_v[:, pl.ds(h * half + j * tile, tile)],
                preferred_element_type=f32,
            ).astype(bf)
            pown[h, :, :, pl.ds(j * tile, tile)] = new.reshape(2, shard, tile)
        part_mate(h).start()
    for h in range(2):
        part_mate(h).wait_recv()
        xsend[h] = (pown[h, c].astype(f32) + pmate[h].astype(f32)).astype(bf)
        part_across(h).start()
    mix(here, 1)
    for j in range(width // tile):
        new = jnp.dot(
            mixed[pl.ds(here, 2)].reshape(2 * shard, local),
            wo_v[:, pl.ds(j * tile, tile)],
            preferred_element_type=f32,
        ).astype(bf)
        qown[:, :, pl.ds(j * tile, tile)] = new.reshape(2, shard, tile)
    part_own.start()
    cp = pltpu.make_async_copy(mixed, mix_ref, st_sem.at[8])
    cp.start()
    stores.append(cp)
    tip(1)
    stores += drops
    part_own.wait_recv()
    for h in range(2):
        part_across(h).wait_recv()
        cols = slice(h * half, (h + 1) * half)
        att_ref[:, cols] = (
            qown[c, :, cols].astype(f32) + qmate[:, cols].astype(f32) + xrecv[h].astype(f32)
        )
    for cp in stores:
        cp.wait()
    for cp in next_c:
        cp.wait_recv()
    for cp in [send_x, send_m, forward, part_own, next_y] + next_x + next_c + stats:
        cp.wait_send()
    for h in range(2):
        part_mate(h).wait_send()
        part_across(h).wait_send()


def attend_both(tok, cos, sin, seg, gq, gk, wq, wk, wv, wo, wg, wu):
    shard, width = tok.shape
    local = wq.shape[1]
    heads = local // HD
    bf = jnp.bfloat16
    f32 = jnp.float32
    dma = pltpu.SemaphoreType.DMA
    vm = pl.BlockSpec(memory_space=pltpu.VMEM)
    shape = jax.ShapeDtypeStruct
    half = width // 2
    total = 4 * shard
    return pl.pallas_call(
        attend_kernel,
        name="attend_forward",
        out_shape=(
            shape((shard, width), f32),
            shape((4, shard, width), bf),
            shape((4, shard, width), bf),
            shape((4, shard, local), f32),
            shape((4, shard, local), f32),
            shape((4, shard, local), bf),
            shape((4, shard, local), bf),
            shape((4, shard, local), bf),
            shape((4, shard, local), bf),
            shape((4, heads, shard, total), f32),
            shape((4, 16, shard), f32),
            shape((wg.shape[1] // 2, width), bf),
            shape((wg.shape[1] // 2, width), bf),
        ),
        in_specs=[vm] * 7 + [FULL] * 6,
        out_specs=(vm,) + (FULL,) * 9 + (vm,) + (FULL,) * 2,
        scratch_shapes=[
            pltpu.VMEM((3, width, local), bf),
            pltpu.VMEM((local, width), bf),
            pltpu.VMEM((2, width, wg.shape[1] // 2), bf),
            pltpu.VMEM((2, wg.shape[1] // 2, width), bf),
            pltpu.VMEM((4, shard, width), bf),
            pltpu.VMEM((2, 4, shard, local), f32),
            pltpu.VMEM((2, 4, shard, local), bf),
            pltpu.VMEM((4, shard, local), bf),
            pltpu.VMEM((4, shard, local), bf),
            pltpu.VMEM((4, heads, shard, total), f32),
            pltpu.VMEM((4, 16, shard), f32),
            pltpu.VMEM((3, 4, 16, shard), f32),
            pltpu.VMEM((2, 2, shard, half), bf),
            pltpu.VMEM((2, shard, half), bf),
            pltpu.VMEM((2, shard, half), bf),
            pltpu.VMEM((2, shard, half), bf),
            pltpu.VMEM((2, shard, width), bf),
            pltpu.VMEM((shard, width), bf),
            dma((4,)),
            dma((3,)), dma((3,)), dma((3,)), dma((3,)),
            dma((2,)), dma((2,)), dma((2,)), dma((2,)),
            dma(()), dma(()),
            dma((9,)),
            dma((5,)), dma((5,)), dma((4,)),
        ],
        compiler_params=pltpu.CompilerParams(
            collective_id=2, has_side_effects=True, vmem_limit_bytes=56 * 1024 * 1024
        ),
        cost_estimate=pl.CostEstimate(
            flops=2 * total * width * local * 4, bytes_accessed=24 * 1024 * 1024, transcendentals=heads * total * total
        ),
    )(
        tok, cos.reshape(4, shard, HD), sin.reshape(4, shard, HD), seg.reshape(4, shard, 1), seg.reshape(1, total),
        gq.reshape(1, -1), gk.reshape(1, -1), wq, wk, wv, wo, wg, wu,
    )


def rank_rows(z):
    return (z, z + 1 - 2 * (z % 2), 2 - z // 2, 3 - 3 * (z // 2))


class Line:
    def __init__(self, ref, z, y, t, q, send, recv):
        self.ref, self.z, self.t, self.q, self.send, self.recv = ref, z, t, q, send, recv
        self.up = ((z + 1) % 4) * 2 + y
        self.down = ((z + 3) % 4) * 2 + y

    def go(self, way, i, r, src=None):
        cell = self.ref.at[r, self.q]
        return far_copy(
            cell if src is None else src, cell, self.send.at[way, i], self.recv.at[way, i], (self.up, self.down)[way], self.t
        )

    def hops(self, step, src=None):
        z = self.z
        if step == 0:
            return [(z < 3, 0, z), (z > 0, 1, z)]
        if step == 1:
            middle = (z > 0) & (z < 3)
            return [(middle, 0, (z + 3) % 4), (middle, 1, (z + 1) % 4)]
        return [(z == 2, 0, 0), (z == 1, 1, 3)]

    def lands(self, step):
        z = self.z
        if step == 0:
            return [(z > 0, 0, (z + 3) % 4), (z < 3, 1, (z + 1) % 4)]
        if step == 1:
            return [(z > 1, 0, (z + 2) % 4), (z < 2, 1, (z + 2) % 4)]
        return [(z == 3, 0, 0), (z == 0, 1, 3)]

    def start(self, step, src=None):
        for ok, way, r in self.hops(step):
            pl.when(ok)(self.go(way, step, r, src).start)

    def sent(self, step, src=None):
        for ok, way, r in self.hops(step):
            pl.when(ok)(self.go(way, step, r, src).wait_send)

    def landed(self, step):
        for ok, way, r in self.lands(step):
            pl.when(ok)(self.go(way, step, r).wait_recv)


def attend_back_kernel(
    dat_ref, ghid_ref, cos_ref, sin_ref, gq_ref, gk_ref, inv_ref,
    wq_ref, wk_ref, wv_ref, wo_ref, qh_ref, kh_ref, qr_ref, kr_ref, v_ref, p_ref, mix_ref, wgt_ref, wut_ref, gh_in, gd_in,
    gt_ref, gain_ref, dq_ref, dk_ref, dv_ref, po_ref, lhs_ref, gh_ref, gd_ref,
    w_v, wo_v, dall, unit, rot, val, dmix, prob, scaled, low, mixed, lhs_t, full, part, tip_v, hb_v, made, stat, stat_in, pown, pmate, xsend, xrecv, qown, qmate,
    w_sem, as_s, as_r, ss_s, ss_r, ps_s, ps_r, px_s, px_r, pq_s, pq_r, hx_s, hx_r, hc_s, hc_r, dc_s, dc_r, ys_s, ys_r, zs_s, zs_r, hz_s, hz_r, st_sem, hb_sem, made_sem,
):
    d, t, z, y, c, chip, mate, across = places()
    far = (mate + 2) % 4
    shard, width = dat_ref.shape
    local = w_v.shape[2]
    bf = jnp.bfloat16
    f32 = jnp.float32
    heads = local // HD
    total = 4 * shard
    sources = (wo_ref, wgt_ref, wut_ref, mix_ref, v_ref, p_ref, qr_ref, kr_ref, qh_ref, kh_ref, wq_ref, wk_ref, wv_ref)
    homes = (wo_v, tip_v.at[0], tip_v.at[1], mixed, val, prob, rot.at[0], rot.at[1], unit.at[0], unit.at[1], w_v.at[0], w_v.at[1], w_v.at[2])
    loads = [pltpu.make_async_copy(a, b, w_sem.at[i]) for i, (a, b) in enumerate(zip(sources, homes))]
    for cp in loads:
        cp.start()
    dall[t] = dat_ref[...]
    twin = z * 2 + 1 - y
    above = ((z + 1) % 4) * 2 + y
    below = ((z + 3) % 4) * 2 + y
    greet([(d, mate), (d, across), (d, far), (twin, t), (above, t), (below, t)])

    line_h = Line(gh_ref, z, y, t, t, hz_s, hz_r)
    lines_d = [Line(gd_ref, z, y, t, q, zs_s.at[i], zs_r.at[i]) for i, q in enumerate((t, across))]
    line_h.start(2)
    for line in lines_d:
        line.start(1)
    ranks = rank_rows(z)
    edge = (z == 0) | (z == 3)

    def hb_load(n):
        return pltpu.make_async_copy(gh_ref.at[ranks[n]], hb_v.at[n % 2], hb_sem.at[n])

    hb_load(0).start()
    hb_load(1).start()

    def made_out(n):
        return pltpu.make_async_copy(made, lhs_ref.at[n], made_sem.at[n])

    def remake(n):
        hb_load(n).wait()
        if n > 0:
            made_out(n - 1).wait()

        def wide(j, carry):
            cols = pl.ds(pl.multiple_of(j * 256, 256), 256)
            hb = hb_v[n % 2].reshape(total, width)
            g = lax.dot_general(tip_v[0, cols, :], hb, NT, preferred_element_type=f32)
            u = lax.dot_general(tip_v[1, cols, :], hb, NT, preferred_element_type=f32)
            sg = jax.nn.sigmoid(g)
            gs = g * sg
            made[0, cols, :] = (gs * u).astype(bf)
            made[1, cols, :] = (u * sg * (1.0 + g * (1.0 - sg))).astype(bf)
            made[2, cols, :] = gs.astype(bf)
            return carry

        lax.fori_loop(0, made.shape[1] // 256, wide, 0)
        made_out(n).start()

    send_x = far_copy(dall.at[t], dall.at[t], as_s.at[0], as_r.at[0], d, across)
    send_m = far_copy(dall.at[t], dall.at[t], as_s.at[1], as_r.at[1], d, mate)
    forward = far_copy(dall.at[across], dall.at[across], as_s.at[2], as_r.at[2], d, mate)
    send_x.start()
    send_m.start()
    last = ranks[3]
    row_x = far_copy(gh_ref.at[last, t], gh_ref.at[last, t], hx_s, hx_r, d, across)
    row_c = [
        far_copy(gh_ref.at[last, q], gh_ref.at[last, q], hc_s.at[j], hc_r.at[j], d, mate)
        for j, q in enumerate((t, across))
    ]
    dm_c = [
        [
            far_copy(gd_ref.at[r, q], gd_ref.at[r, q], dc_s.at[i, j], dc_r.at[i, j], d, mate)
            for j, q in enumerate((t, across))
        ]
        for i, r in enumerate(ranks[1:3])
    ]
    for cp in dm_c[0]:
        cp.start()
    swap_y = far_copy(full.at[:, 1 - y], part, ys_s, ys_r, twin, t)

    def project(first):
        rows = dall[pl.ds(first, 2)].reshape(2 * shard, width)
        dmix[pl.ds(first, 2)] = (
            lax.dot_general(rows, wo_v[...], NT, preferred_element_type=f32).astype(bf).reshape(2, shard, local)
        )

    here = chip * 2
    there = 2 - chip * 2
    loads[0].wait()
    send_m.wait_recv()
    project(here)
    for cp in loads[1:]:
        cp.wait()
    remake(0)
    send_x.wait_recv()
    forward.start()
    forward.wait_recv()
    line_h.landed(2)
    pl.when(edge)(row_x.start)
    project(there)
    lhs_t[...] = mixed[...].reshape(total, local).astype(f32).T.astype(bf)
    block = full.shape[3]
    for b in range(8):
        full[b // 2, b % 2] = jnp.dot(
            lhs_t[...], dall[:, :, b * block : (b + 1) * block].reshape(total, block), preferred_element_type=f32
        ).astype(bf)
    swap_y.start()
    stores = []

    scale = 1.0 / math.sqrt(HD)
    cos = cos_ref[...].reshape(total, HD)
    sin = sin_ref[...].reshape(total, HD)
    dots = [jnp.zeros((total, 1), f32), jnp.zeros((total, 1), f32)]
    for h in range(heads):
        cols = slice(h * HD, (h + 1) * HD)
        dm = dmix[:, :, cols].reshape(total, HD)
        p = prob[:, h].reshape(total, total)
        dp = lax.dot_general(dm, val[:, :, cols].reshape(total, HD), NT, preferred_element_type=f32)
        ds = (p * (dp - jnp.sum(p * dp, axis=1, keepdims=True))).astype(bf)
        low[2, :, :, cols] = (
            lax.dot_general(p.astype(bf), dm, TN, preferred_element_type=f32).astype(bf).reshape(4, shard, HD)
        )
        back = (
            jnp.dot(ds, rot[1, :, :, cols].reshape(total, HD), preferred_element_type=f32) * scale,
            lax.dot_general(ds, rot[0, :, :, cols].reshape(total, HD), TN, preferred_element_type=f32) * scale,
        )
        for i, gain in ((0, gq_ref), (1, gk_ref)):
            g = back[i]
            g = g * cos - pltpu.roll(g, HD // 2, 1) * sin
            u = unit[i, :, :, cols].reshape(total, HD)
            prod = g * u
            gain_ref[i : i + 1, cols] = jnp.sum(prod, axis=0, keepdims=True)
            dots[i] = dots[i] + jnp.sum(prod * gain[:, cols], axis=1, keepdims=True)
            scaled[i, :, :, cols] = (g * gain[:, cols]).reshape(4, shard, HD)
    for q in range(4):
        for i in range(2):
            stat[q, i * 8 : i * 8 + 8, :] = to_rows(dots[i][q * shard : (q + 1) * shard])
    stats = [
        far_copy(stat, stat_in.at[i], ss_s.at[i], ss_r.at[i], d, who)
        for i, who in enumerate((mate, across, far))
    ]
    for cp in stats:
        cp.start()
    pl.when(edge)(row_x.wait_recv)
    for cp in row_c:
        cp.start()
    for line in lines_d:
        line.landed(1)
    lines_d[0].start(2)
    for cp in dm_c[1]:
        cp.start()
    for cp in stats:
        cp.wait_recv()

    def finish(first):
        for s in range(2):
            q = first + s
            mean = (stat[q] + stat_in[0, q] + stat_in[1, q] + stat_in[2, q]) / width
            inv = inv_ref[q]
            for i in range(2):
                low[i, q] = (
                    to_column(inv[i * 8 : i * 8 + 8])
                    * (scaled[i, q] - unit[i, q] * to_column(mean[i * 8 : i * 8 + 8]))
                ).astype(bf)

    half = width // 2
    tile = 512

    def part_mate(h):
        return far_copy(pown.at[h, 1 - c], pmate.at[h], ps_s.at[h], ps_r.at[h], d, mate)

    def part_across(h):
        return far_copy(xsend.at[h], xrecv.at[h], px_s.at[h], px_r.at[h], d, across)

    part_own = far_copy(qown.at[1 - c], qmate, pq_s, pq_r, d, mate)

    def result(first, start):
        new = None
        for i in range(3):
            one = lax.dot_general(
                low[i, pl.ds(first, 2)].reshape(2 * shard, local),
                w_v[i, pl.ds(start, tile), :],
                NT,
                preferred_element_type=f32,
            )
            new = one if new is None else new + one
        return new.astype(bf).reshape(2, shard, tile)

    finish(there)
    for h in range(2):
        for j in range(half // tile):
            pown[h, :, :, pl.ds(j * tile, tile)] = result(there, h * half + j * tile)
        part_mate(h).start()
        part_mate(h).wait_recv()
        xsend[h] = (pown[h, c].astype(f32) + pmate[h].astype(f32)).astype(bf)
        part_across(h).start()
    finish(here)
    more = [
        pltpu.make_async_copy(low.at[i], r, st_sem.at[1 + i]) for i, r in enumerate((dq_ref, dk_ref, dv_ref))
    ]
    for cp in more:
        cp.start()
    stores += more
    for j in range(width // tile):
        qown[:, :, pl.ds(j * tile, tile)] = result(here, j * tile)
    part_own.start()
    remake(1)
    swap_y.wait_recv()
    for b in range(4):
        part[b] = (part[b].astype(f32) + full[b, y].astype(f32)).astype(bf)
    keep = pltpu.make_async_copy(part, po_ref, st_sem.at[0])
    keep.start()
    stores.append(keep)
    part_own.wait_recv()
    for h in range(2):
        part_across(h).wait_recv()
        cols = slice(h * half, (h + 1) * half)
        gt_ref[:, cols] = (
            ghid_ref[:, cols]
            + (qown[c, :, cols].astype(f32) + qmate[:, cols].astype(f32) + xrecv[h].astype(f32))
        ).astype(bf)
    for cp in stores:
        cp.wait()
    for cp in row_c + dm_c[0] + dm_c[1]:
        cp.wait()
    line_h.sent(2)
    for line in lines_d:
        line.sent(1)
    lines_d[0].landed(2)
    lines_d[0].sent(2)
    pl.when(edge)(row_x.wait_send)
    made_out(1).wait()
    for cp in [send_x, send_m, forward, part_own, swap_y] + stats:
        cp.wait_send()
    for h in range(2):
        part_mate(h).wait_send()
        part_across(h).wait_send()


def attend_back_both(dat, ghid, cos, sin, gq, gk, inv, wq, wk, wv, wo, qh, kh, qr, kr, v, p, mix, wgt, wut, gh, gd):
    shard, width = dat.shape
    local = wq.shape[1]
    heads = local // HD
    bf = jnp.bfloat16
    f32 = jnp.float32
    dma = pltpu.SemaphoreType.DMA
    vm = pl.BlockSpec(memory_space=pltpu.VMEM)
    shape = jax.ShapeDtypeStruct
    half = width // 2
    total = 4 * shard
    return pl.pallas_call(
        attend_back_kernel,
        name="attend_backward",
        out_shape=(
            shape((shard, width), bf),
            shape((2, local), f32),
            shape((4, shard, local), bf),
            shape((4, shard, local), bf),
            shape((4, shard, local), bf),
            shape((4, local, width // 8), bf),
            shape((2, 3, wgt.shape[0], total), bf),
            shape(gh.shape, bf),
            shape(gd.shape, bf),
        ),
        in_specs=[vm] * 7 + [FULL] * 15,
        out_specs=(vm,) * 2 + (FULL,) * 7,
        input_output_aliases={20: 7, 21: 8},
        scratch_shapes=[
            pltpu.VMEM((3, width, local), bf),
            pltpu.VMEM((local, width), bf),
            pltpu.VMEM((4, shard, width), bf),
            pltpu.VMEM((2, 4, shard, local), f32),
            pltpu.VMEM((2, 4, shard, local), bf),
            pltpu.VMEM((4, shard, local), bf),
            pltpu.VMEM((4, shard, local), bf),
            pltpu.VMEM((4, heads, shard, total), f32),
            pltpu.VMEM((2, 4, shard, local), f32),
            pltpu.VMEM((3, 4, shard, local), bf),
            pltpu.VMEM((4, shard, local), bf),
            pltpu.VMEM((local, total), bf),
            pltpu.VMEM((4, 2, local, width // 8), bf),
            pltpu.VMEM((4, local, width // 8), bf),
            pltpu.VMEM((2, wgt.shape[0], width), bf),
            pltpu.VMEM((2, 4, shard, width), bf),
            pltpu.VMEM((3, wgt.shape[0], total), bf),
            pltpu.VMEM((4, 16, shard), f32),
            pltpu.VMEM((3, 4, 16, shard), f32),
            pltpu.VMEM((2, 2, shard, half), bf),
            pltpu.VMEM((2, shard, half), bf),
            pltpu.VMEM((2, shard, half), bf),
            pltpu.VMEM((2, shard, half), bf),
            pltpu.VMEM((2, shard, width), bf),
            pltpu.VMEM((shard, width), bf),
            dma((13,)),
            dma((3,)), dma((3,)), dma((3,)), dma((3,)),
            dma((2,)), dma((2,)), dma((2,)), dma((2,)),
            dma(()), dma(()), dma(()), dma(()), dma((2,)), dma((2,)), dma((2, 2)), dma((2, 2)), dma(()), dma(()),
            dma((2, 2, 3)), dma((2, 2, 3)), dma((2, 3)), dma((2, 3)),
            dma((4,)), dma((2,)), dma((2,)),
        ],
        compiler_params=pltpu.CompilerParams(
            collective_id=3, has_side_effects=True, vmem_limit_bytes=56 * 1024 * 1024
        ),
        cost_estimate=pl.CostEstimate(
            flops=2 * total * width * local * 4 + 10 * heads * total * total * HD,
            bytes_accessed=24 * 1024 * 1024,
            transcendentals=0,
        ),
    )(
        dat, ghid, cos.reshape(4, shard, HD), sin.reshape(4, shard, HD), gq.reshape(1, -1), gk.reshape(1, -1), inv,
        wq, wk, wv, wo, qh, kh, qr, kr, v, p, mix, wgt, wut, gh, gd,
    )


def place_kernel(a_ref, p_ref, m_ref, q_ref, k_ref, v_ref, o_ref, g_ref, u_ref, d_ref):
    f32 = jnp.float32
    n = a_ref.shape[2]
    for w, ref in ((0, v_ref), (1, q_ref), (2, k_ref)):
        for i in range(2):
            ref[:, i * n : (i + 1) * n] = a_ref[w, i].astype(f32).T
    new = p_ref[0].astype(f32)
    for i in range(1, 4):
        new = new + p_ref[i].astype(f32)
    o_ref[...] = new
    f = m_ref.shape[2]
    for i in range(2):
        d_ref[i * f : (i + 1) * f, :] = m_ref[0, i].astype(f32)
        g_ref[:, i * f : (i + 1) * f] = m_ref[1, i].astype(f32).T
        u_ref[:, i * f : (i + 1) * f] = m_ref[2, i].astype(f32).T


def place_grads(attn, proj, mlp):
    _, f, block = proj.shape
    f32 = jnp.float32
    vm = pl.BlockSpec(memory_space=pltpu.VMEM)
    shape = jax.ShapeDtypeStruct
    return pl.pallas_call(
        place_kernel,
        name="place_grads",
        out_shape=(
            shape((block, f), f32),
            shape((block, f), f32),
            shape((block, f), f32),
            shape((f, block), f32),
            shape((block, 4 * f), f32),
            shape((block, 4 * f), f32),
            shape((4 * f, block), f32),
        ),
        in_specs=[vm] * 3,
        out_specs=(vm,) * 7,
        compiler_params=pltpu.CompilerParams(vmem_limit_bytes=40 * 1024 * 1024),
    )(attn, proj, mlp)


def plain_body(
    tokens,
    lengths,
    w_query,
    w_key,
    w_value,
    w_out,
    w_gate,
    w_up,
    w_down,
    gain_query,
    gain_key,
    gain_attn,
    gain_mlp,
    cotangent,
):
    rows_dev = lengths.shape[0]
    model_width = w_query.shape[0]
    local_width = w_query.shape[1]
    head_count = local_width // HD
    gathered = lax.all_gather(tokens, "tensor", axis=0, tiled=True)
    row_count = gathered.shape[0]
    segment, offsets = jax.vmap(row_layout)(lengths)
    queries = jnp.dot(gathered, w_query, preferred_element_type=jnp.float32)
    keys_raw = jnp.dot(gathered, w_key, preferred_element_type=jnp.float32)
    values_low = jnp.dot(gathered, w_value, preferred_element_type=jnp.float32).astype(jnp.bfloat16)
    q_total, k_total = lax.psum(
        (jnp.sum(queries * queries, axis=1), jnp.sum(keys_raw * keys_raw, axis=1)), "tensor"
    )
    q_inv = lax.rsqrt(q_total / model_width + EPS)[:, None]
    k_inv = lax.rsqrt(k_total / model_width + EPS)[:, None]
    q_unit = queries * q_inv
    k_unit = keys_raw * k_inv

    def to_heads(values):
        return values.reshape(rows_dev, ROW_LEN, head_count, HD)

    queries_low = rotate(to_heads(q_unit * gain_query), offsets, 1.0).astype(jnp.bfloat16)
    keys_low = rotate(to_heads(k_unit * gain_key), offsets, 1.0).astype(jnp.bfloat16)
    values_heads = to_heads(values_low)
    mixed_heads, log_total = jax.vmap(lambda *a: attend(a))(
        queries_low, keys_low, values_heads, segment
    )
    mixed_low = mixed_heads.reshape(row_count, local_width)
    attn_out = lax.psum_scatter(
        jnp.dot(mixed_low, w_out, preferred_element_type=jnp.float32).astype(jnp.bfloat16),
        "tensor",
        scatter_dimension=0,
        tiled=True,
    ).astype(jnp.float32)
    inner_count = lax.axis_size("dp") // OUTER
    a_inv = lax.rsqrt(jnp.mean(attn_out * attn_out, axis=1, keepdims=True) + EPS)
    a_unit = attn_out * a_inv
    hidden = tokens.astype(jnp.float32) + a_unit * gain_attn
    hidden_low = hidden.astype(jnp.bfloat16)
    hidden_all = lax.all_gather(hidden_low, "tensor", axis=0, tiled=True)
    outer_index = lax.axis_index("dp") // inner_count

    def gather_group(shard):
        groups = [[z * inner_count + i for z in range(OUTER)] for i in range(inner_count)]
        part = lax.all_gather(shard, "dp", axis=0, tiled=True, axis_index_groups=groups)
        return lax.all_gather(part, "tensor", axis=0, tiled=True)

    hidden_group = gather_group(hidden_low)
    gate_acts = jnp.dot(hidden_all, w_gate, preferred_element_type=jnp.float32)
    up_acts = jnp.dot(hidden_all, w_up, preferred_element_type=jnp.float32)
    gate_sigmoid = jax.nn.sigmoid(gate_acts)
    inner_low = (gate_acts * gate_sigmoid * up_acts).astype(jnp.bfloat16)
    mlp_out = lax.psum_scatter(
        jnp.dot(inner_low, w_down, preferred_element_type=jnp.float32).astype(jnp.bfloat16),
        "tensor",
        scatter_dimension=0,
        tiled=True,
    ).astype(jnp.float32)
    f_inv = lax.rsqrt(jnp.mean(mlp_out * mlp_out, axis=1, keepdims=True) + EPS)
    f_unit = mlp_out * f_inv
    output = (hidden + f_unit * gain_mlp).astype(jnp.bfloat16)
    grad_output = cotangent.astype(jnp.float32)
    grad_mlp, grad_gain_mlp_part = post_norm_back(grad_output, f_unit, f_inv, gain_mlp)
    grad_mlp_low = grad_mlp.astype(jnp.bfloat16)
    mlp_grad_all = lax.all_gather(grad_mlp_low, "tensor", axis=0, tiled=True)
    mlp_grad_group = gather_group(grad_mlp_low)
    grad_inner = times_t(mlp_grad_all, w_down)
    grad_gate_low = (
        grad_inner * up_acts * gate_sigmoid * (1.0 + gate_acts * (1.0 - gate_sigmoid))
    ).astype(jnp.bfloat16)
    grad_up_low = (grad_inner * gate_acts * gate_sigmoid).astype(jnp.bfloat16)
    part_width = w_gate.shape[1] // OUTER
    gate_part = lax.dynamic_slice_in_dim(w_gate, outer_index * part_width, part_width, 1)
    up_part = lax.dynamic_slice_in_dim(w_up, outer_index * part_width, part_width, 1)
    down_part = lax.dynamic_slice_in_dim(w_down, outer_index * part_width, part_width, 0)
    gate_g = jnp.dot(hidden_group, gate_part, preferred_element_type=jnp.float32)
    up_g = jnp.dot(hidden_group, up_part, preferred_element_type=jnp.float32)
    sig_g = jax.nn.sigmoid(gate_g)
    inner_g = (gate_g * sig_g * up_g).astype(jnp.bfloat16)
    grad_inner_g = times_t(mlp_grad_group, down_part)
    grad_gate_g = (grad_inner_g * up_g * sig_g * (1.0 + gate_g * (1.0 - sig_g))).astype(
        jnp.bfloat16
    )
    grad_up_g = (grad_inner_g * gate_g * sig_g).astype(jnp.bfloat16)
    sum_down = scatter_join(split_cols(t_times(inner_g, mlp_grad_group), inner_count), inner_count, 0)
    sum_gate = scatter_join(split_rows(t_times(hidden_group, grad_gate_g), inner_count), inner_count, 1)
    sum_up = scatter_join(split_rows(t_times(hidden_group, grad_up_g), inner_count), inner_count, 1)
    grad_hidden = grad_output + lax.psum_scatter(
        (times_t(grad_gate_low, w_gate) + times_t(grad_up_low, w_up)).astype(jnp.bfloat16),
        "tensor",
        scatter_dimension=0,
        tiled=True,
    ).astype(jnp.float32)
    grad_attn, grad_gain_attn_part = post_norm_back(grad_hidden, a_unit, a_inv, gain_attn)
    grad_attn_low = grad_attn.astype(jnp.bfloat16)
    attn_grad_all = lax.all_gather(grad_attn_low, "tensor", axis=0, tiled=True)
    grad_mixed = times_t(attn_grad_all, w_out).astype(jnp.bfloat16)
    grad_q_rot, grad_k_rot, grad_values_low = jax.vmap(lambda *a: attend_back(a))(
        queries_low, keys_low, values_heads, segment, log_total, to_heads(grad_mixed)
    )
    grad_q_norm = rotate(grad_q_rot, offsets, -1.0).reshape(row_count, local_width)
    grad_k_norm = rotate(grad_k_rot, offsets, -1.0).reshape(row_count, local_width)
    grad_gain_query_part = jnp.sum(grad_q_norm * q_unit, axis=0)
    grad_gain_key_part = jnp.sum(grad_k_norm * k_unit, axis=0)
    q_scaled = grad_q_norm * gain_query
    k_scaled = grad_k_norm * gain_key
    q_dots, k_dots = lax.psum(
        (jnp.sum(q_scaled * q_unit, axis=1), jnp.sum(k_scaled * k_unit, axis=1)), "tensor"
    )
    grad_queries_low = (q_inv * (q_scaled - q_unit * (q_dots / model_width)[:, None])).astype(
        jnp.bfloat16
    )
    grad_keys_low = (k_inv * (k_scaled - k_unit * (k_dots / model_width)[:, None])).astype(
        jnp.bfloat16
    )
    grad_values_flat = grad_values_low.reshape(row_count, local_width)
    grad_tokens = (
        grad_hidden
        + lax.psum_scatter(
            (
                times_t(grad_queries_low, w_query)
                + times_t(grad_keys_low, w_key)
                + times_t(grad_values_flat, w_value)
            ).astype(jnp.bfloat16),
            "tensor",
            scatter_dimension=0,
            tiled=True,
        ).astype(jnp.float32)
    ).astype(jnp.bfloat16)
    tensor_start = lax.axis_index("tensor") * local_width
    zero_row = jnp.zeros((model_width,), jnp.float32)
    q_full = lax.dynamic_update_slice(zero_row, grad_gain_query_part, (tensor_start,))
    k_full = lax.dynamic_update_slice(zero_row, grad_gain_key_part, (tensor_start,))
    gain_stack = jnp.stack([q_full, k_full, grad_gain_attn_part, grad_gain_mlp_part])
    gain_total = lax.psum(gain_stack, ("dp", "tensor"))
    grad_gain_query = lax.dynamic_slice(gain_total[0], (tensor_start,), (local_width,))
    grad_gain_key = lax.dynamic_slice(gain_total[1], (tensor_start,), (local_width,))
    summed = (
        scatter_sum(split_rows(t_times(gathered, grad_queries_low), inner_count), inner_count),
        scatter_sum(split_rows(t_times(gathered, grad_keys_low), inner_count), inner_count),
        scatter_sum(split_rows(t_times(gathered, grad_values_flat), inner_count), inner_count),
        scatter_sum(split_cols(t_times(mixed_low, attn_grad_all), inner_count), inner_count),
        sum_gate,
        sum_up,
        sum_down,
    )
    return (
        output,
        grad_tokens,
        summed[0],
        summed[1],
        summed[2],
        summed[3],
        summed[4],
        summed[5],
        summed[6],
        grad_gain_query,
        grad_gain_key,
        gain_total[2],
        gain_total[3],
    )


def fused_body(
    tokens,
    lengths,
    w_query,
    w_key,
    w_value,
    w_out,
    w_gate,
    w_up,
    w_down,
    gain_query,
    gain_key,
    gain_attn,
    gain_mlp,
    cotangent,
):
    local_width = w_query.shape[1]
    segment, offsets = row_layout(lengths[0])
    half_width = HD // 2
    frequency = jnp.exp(
        jnp.arange(half_width, dtype=jnp.float32) * (-2.0 * math.log(THETA) / HD)
    )
    angles = offsets.astype(jnp.float32)[:, None] * frequency
    cosines = jnp.cos(angles)
    sines = jnp.sin(angles)
    cosines = jnp.concatenate([cosines, cosines], axis=1)
    sines = jnp.concatenate([-sines, sines], axis=1)
    (
        attn_out, tokens_all, tokens_next, q_unit, k_unit, q_rot, k_rot, values, mixed, weights, inverse, gate_t, up_t,
    ) = attend_both(
        tokens, cosines, sines, segment, gain_query, gain_key, w_query, w_key, w_value, w_out, w_gate, w_up
    )
    output, grad_hidden, grad_attn, gain_parts, group_h, group_d = mlp_both(
        attn_out, tokens, cotangent, gain_attn, gain_mlp, w_gate, w_up, w_down
    )
    grad_tokens, head_gains, grad_q, grad_k, grad_v, proj, made, group_h, group_d = attend_back_both(
        grad_attn, grad_hidden, cosines, sines, gain_query, gain_key, inverse,
        w_query, w_key, w_value, w_out, q_unit, k_unit, q_rot, k_rot, values, weights, mixed, gate_t, up_t,
        group_h, group_d,
    )
    gains, attn_blocks, proj_blocks, mlp_blocks, _, _ = weight_grads(
        gain_parts, head_gains, group_h, group_d, made, gate_t, up_t, w_down, tokens_all, tokens_next, grad_q, grad_k, grad_v, proj,
    )
    return (
        output,
        grad_tokens,
        *place_grads(attn_blocks, proj_blocks, mlp_blocks),
        gains[2, :local_width],
        gains[3, :local_width],
        gains[0],
        gains[1],
    )


def solution(mesh):
    placed = (
        P(("dp", "tensor"), None),
        P("dp", None),
        P(None, "tensor"),
        P(None, "tensor"),
        P(None, "tensor"),
        P("tensor", None),
        P(None, "tensor"),
        P(None, "tensor"),
        P("tensor", None),
        P("tensor"),
        P("tensor"),
        P(),
        P(),
        P(("dp", "tensor"), None),
    )
    return jax.shard_map(
        fused_body if tuple(mesh.shape.values()) == (8, 4) else plain_body,
        mesh=mesh,
        in_specs=placed,
        out_specs=(
            P(("dp", "tensor"), None),
            P(("dp", "tensor"), None),
            P("dp", "tensor"),
            P("dp", "tensor"),
            P("dp", "tensor"),
            P("tensor", "dp"),
            P("dp", "tensor"),
            P("dp", "tensor"),
            P("tensor", "dp"),
            P("tensor"),
            P("tensor"),
            P(),
            P(),
        ),
        check_vma=False,
    )
```

```python
import math

import jax
import jax.numpy as jnp
from jax import lax
from jax.experimental import pallas as pl
from jax.experimental.pallas import tpu as pltpu
from jax.sharding import PartitionSpec as P

HD = 128
ROW_LEN = 512


EPS = 1e-06
THETA = 500000.0


def rotate(values, offsets, rot_sign):
    half_width = values.shape[-1] // 2
    frequency = jnp.exp(
        jnp.arange(half_width, dtype=jnp.float32) * (-2.0 * math.log(THETA) / values.shape[-1])
    )
    angles = offsets.astype(jnp.float32)[..., None, None] * frequency
    cosines = jnp.cos(angles)
    sine_part = rot_sign * jnp.sin(angles)
    first_half = values[..., :half_width]
    second_half = values[..., half_width:]
    return jnp.concatenate(
        [
            first_half * cosines - second_half * sine_part,
            second_half * cosines + first_half * sine_part,
        ],
        axis=-1,
    )


def row_layout(lengths_row):
    slots = jnp.arange(lengths_row.shape[0], dtype=jnp.int32)
    seq_ends = jnp.sum(
        jnp.where(slots[None, :] <= slots[:, None], lengths_row[None, :], 0), axis=1
    )
    position = jnp.arange(ROW_LEN, dtype=jnp.int32)
    passed = (position[:, None] >= seq_ends[None, :]).astype(jnp.int32)
    segment = jnp.sum(passed, axis=1)
    seq_start = jnp.sum(passed * lengths_row[None, :], axis=1)
    return (segment, position - seq_start)


def allowed_mask(segment):
    position = jnp.arange(segment.shape[0], dtype=jnp.int32)
    return (segment[:, None] == segment[None, :]) & (position[None, :] <= position[:, None])


def times_t(left_mat, right_mat):
    return lax.dot_general(
        left_mat, right_mat, (((1,), (1,)), ((), ())), preferred_element_type=jnp.float32
    )


def t_times(left_mat, right_mat):
    return lax.dot_general(
        left_mat, right_mat, (((0,), (0,)), ((), ())), preferred_element_type=jnp.float32
    )


def masked_scores(queries_low, keys_low, segment):
    scale_factor = 1.0 / math.sqrt(queries_low.shape[-1])
    scores = (
        jnp.einsum("qhd,khd->hqk", queries_low, keys_low, preferred_element_type=jnp.float32)
        * scale_factor
    )
    return jnp.where(allowed_mask(segment)[None], scores, -1e30)


def attend(block_item):
    queries_low, keys_low, values_low, segment = block_item
    scores = masked_scores(queries_low, keys_low, segment)
    row_max = jnp.max(scores, axis=-1, keepdims=True)
    shifted = jnp.exp(scores - row_max)
    row_total = jnp.sum(shifted, axis=-1, keepdims=True)
    attn_weights = (shifted / row_total).astype(jnp.bfloat16)
    mixed = jnp.einsum("hqk,khd->qhd", attn_weights, values_low, preferred_element_type=jnp.float32)
    return (mixed.astype(jnp.bfloat16), (row_max + jnp.log(row_total))[..., 0])


def attend_back(block_item):
    queries_low, keys_low, values_low, segment, log_total, grad_mixed = block_item
    scale_factor = 1.0 / math.sqrt(queries_low.shape[-1])
    scores = masked_scores(queries_low, keys_low, segment)
    attn_weights = jnp.exp(scores - log_total[..., None])
    grad_weights = jnp.einsum(
        "qhd,khd->hqk", grad_mixed, values_low, preferred_element_type=jnp.float32
    )
    row_dots = jnp.sum(attn_weights * grad_weights, axis=-1, keepdims=True)
    grad_scores = (attn_weights * (grad_weights - row_dots)).astype(jnp.bfloat16)
    grad_queries = scale_factor * jnp.einsum(
        "hqk,khd->qhd", grad_scores, keys_low, preferred_element_type=jnp.float32
    )
    grad_keys = scale_factor * jnp.einsum(
        "hqk,qhd->khd", grad_scores, queries_low, preferred_element_type=jnp.float32
    )
    grad_values = jnp.einsum(
        "hqk,qhd->khd",
        attn_weights.astype(jnp.bfloat16),
        grad_mixed,
        preferred_element_type=jnp.float32,
    )
    return (grad_queries, grad_keys, grad_values.astype(jnp.bfloat16))


def post_norm_back(grad_in, unit_rows, inv_scale, gain_vec):
    scaled = grad_in * gain_vec
    mean_dots = jnp.mean(scaled * unit_rows, axis=-1, keepdims=True)
    return (inv_scale * (scaled - unit_rows * mean_dots), jnp.sum(grad_in * unit_rows, axis=0))


OUTER = 4


def swap(value, shift):
    size = lax.axis_size("dp")
    return lax.ppermute(value, "dp", [(d, d ^ shift) for d in range(size)])


def pick(parts, index):
    return lax.dynamic_index_in_dim(parts, index, 0, keepdims=False)


def sum_inner(parts):
    inner = parts.shape[0]
    mine = lax.axis_index("dp") % inner
    total = pick(parts, mine)
    for k in range(1, inner):
        sent = pick(parts, mine ^ k).astype(jnp.bfloat16)
        total = total + swap(sent, k).astype(jnp.float32)
    return total


def trade_outer(parts, inner):
    mine = lax.axis_index("dp") // inner
    got = [(mine, pick(parts, mine))]
    for k in range(1, OUTER):
        got.append((mine ^ k, swap(pick(parts, mine ^ k), k * inner)))
    return got


def split_rows(grad, inner):
    cols = grad.shape[1]
    return grad.reshape(OUTER, inner, -1, cols).transpose(1, 0, 2, 3)


def split_cols(grad, inner):
    rows = grad.shape[0]
    return grad.reshape(rows, OUTER, inner, -1).transpose(2, 1, 0, 3)


def scatter_sum(parts, inner):
    half = sum_inner(parts).astype(jnp.bfloat16)
    got = trade_outer(half, inner)
    return sum(g.astype(jnp.float32) for _, g in got)


def scatter_join(parts, inner, axis):
    half = sum_inner(parts).astype(jnp.bfloat16)
    got = trade_outer(half, inner)
    stack = jnp.zeros((OUTER, *got[0][1].shape), jnp.bfloat16)
    for place, block in got:
        stack = lax.dynamic_update_index_in_dim(stack, block, place, 0)
    joined = jnp.concatenate([stack[z] for z in range(OUTER)], axis=axis)
    return joined.astype(jnp.float32)


MESH = pl.DeviceIdType.MESH
FULL = pl.BlockSpec(memory_space=pl.ANY)


def grads_kernel(
    gp_ref, gqk_ref, gh_in, gm_in, lhs_ref, wgt_ref, wut_ref, wd_ref, tok_ref, nxt_ref, dq_ref, dk_ref, dv_ref, po_ref,
    gain_ref, attn_ref, proj_ref, mlp_ref, gh_ref, gm_ref,
    hb_v, tip_v, dm_v, wd_v, lhs_in, lhs_q, lhs_t, quad, quad_in, pair, full, part, gbuf, gin,
    ld_sem, xs_s, xs_r, cs_s, cs_r, qs_s, qs_r, os_s, os_r, qz_s, qz_r, qy_s, qy_r, ys_s, ys_r, ts_s, ts_r, own_s, gs_s, gs_r, lhs_sem,
):
    d = lax.axis_index("dp")
    t = lax.axis_index("tensor")
    z = d // 2
    y = d % 2
    side = z % 2
    top = z // 2
    mate = t + 1 - 2 * (t % 2)
    across = (t + 2) % 4
    twin = z * 2 + 1 - y
    pal = (z + 1 - 2 * side) * 2 + y
    bf = jnp.bfloat16
    f32 = jnp.float32
    f = lhs_t.shape[1]
    width = hb_v.shape[3]
    shard = hb_v.shape[2]
    span = width // 2
    hc = lhs_in.shape[4]
    total = 4 * shard

    def peer(k):
        return ((z + k) % 4) * 2 + y

    heads = (dv_ref, dq_ref, dk_ref)
    parts = (top, 1 - top)
    ranks = rank_rows(z)
    slow = [
        pltpu.make_async_copy(
            wd_ref.at[pl.ds(side * f, f), pl.ds(parts[i] * span, span)], wd_v.at[i], ld_sem.at[4 + i]
        )
        for i in range(2)
    ] + [
        pltpu.make_async_copy(r.at[:, :, pl.ds(y * hc, hc)], lhs_in.at[w, 0], ld_sem.at[6 + w])
        for w, r in enumerate(heads)
    ]
    toks = [
        pltpu.make_async_copy(r, hb_v.at[i], ld_sem.at[i]) for i, r in enumerate((tok_ref, nxt_ref))
    ]

    def lhs_load(n, w):
        return pltpu.make_async_copy(
            lhs_ref.at[n, w], lhs_t.at[w, :, pl.ds(n * total, total)], lhs_sem.at[n, w]
        )

    def dm_load(n, i):
        return pltpu.make_async_copy(
            gm_ref.at[ranks[n], :, :, pl.ds(parts[i] * span, span)], dm_v.at[n, i], ld_sem.at[9 + n * 2 + i]
        )

    def hb_load(n):
        return [
            pltpu.make_async_copy(
                gh_ref.at[ranks[n], :, :, pl.ds(i * span, span)], dm_v.at[3, i], ld_sem.at[2 + i]
            )
            for i in range(2)
        ]

    tips = [
        pltpu.make_async_copy(r, tip_v.at[i], ld_sem.at[21 + i]) for i, r in enumerate((wgt_ref, wut_ref))
    ]
    for cp in hb_load(3) + tips + slow[2:] + toks + slow[:2]:
        cp.start()
    for w in range(3):
        for n in range(3):
            lhs_load(n, w).start()
    for i in range(2):
        dm_load(0, i).start()

    greet([(peer(1), t), (peer(2), t), (peer(3), t), (twin, t), (d, mate), (d, across)])

    groups = (gh_ref, gm_ref)

    def head_swap(w):
        return far_copy(
            heads[w].at[:, :, pl.ds((1 - y) * hc, hc)], lhs_in.at[w, 1], qs_s.at[w], qs_r.at[w], twin, t
        )

    def proj_trade(k):
        return far_copy(po_ref.at[(z + k) % 4], proj_ref.at[z], os_s.at[k - 1], os_r.at[k - 1], peer(k), t)

    def piece(i):
        return gm_ref, ranks[1 + i % 3], pl.ds(parts[i // 3] * span, span)

    def cell(i, q):
        ref, r, cols = piece(i)
        return ref.at[r, q, :, cols]

    def forward_x(i):
        return far_copy(cell(i, t), cell(i, t), xs_s.at[i], xs_r.at[i], d, across)

    def forward_c(i, h):
        q = t if h == 0 else across
        return far_copy(cell(i, q), cell(i, q), cs_s.at[i, h], cs_r.at[i, h], d, mate)

    def advance(i):
        forward_x(i).wait_recv()
        for h in range(2):
            forward_c(i, h).start()

    def arrive(i):
        for h in range(2):
            forward_c(i, h).wait_recv()

    def gain_copy(i):
        stage, who = ((0, (peer(1), t)), (0, (peer(2), t)), (0, (peer(3), t)), (1, (twin, t)), (2, (d, across)), (3, (d, mate)))[i]
        return far_copy(gbuf.at[stage], gin.at[i], gs_s.at[i], gs_r.at[i], *who)

    gbuf[0] = jnp.zeros_like(gbuf[0])
    gbuf[0, 0:2, :] = gp_ref[...]
    gbuf[0, 2:4, 0 : gqk_ref.shape[1]] = gqk_ref[...]
    for i in range(3):
        gain_copy(i).start()
    for w in range(3):
        head_swap(w).start()
    for i in range(6):
        forward_x(i).start()
    for k in (2, 1, 3):
        proj_trade(k).start()
    keep_proj = pltpu.make_async_copy(po_ref.at[z], proj_ref.at[z], own_s.at[0])
    keep_proj.start()

    def gain_step(stage):
        new = gbuf[stage]
        for i in ((0, 1, 2), (3,), (4,), (5,))[stage]:
            gain_copy(i).wait_recv()
            new = new + gin[i]
        if stage < 3:
            gbuf[stage + 1] = new
            gain_copy(stage + 3).start()
        if stage == 1:
            gain_ref[2:4, :] = new[2:4, :]
        if stage == 3:
            gain_ref[0:2, :] = new[0:2, :]

    step = 512

    def remake(n):
        def wide(j, carry):
            cols = pl.ds(pl.multiple_of(j * step, step), step)
            hb = [dm_v[3, i].reshape(total, span) for i in range(2)]
            g, u = [
                lax.dot_general(tip_v[w, cols, :span], hb[0], NT, preferred_element_type=f32)
                + lax.dot_general(tip_v[w, cols, span:], hb[1], NT, preferred_element_type=f32)
                for w in range(2)
            ]
            sg = jax.nn.sigmoid(g)
            gs = g * sg
            spot = slice(n * total, (n + 1) * total)
            lhs_t[0, cols, spot] = (gs * u).astype(bf)
            lhs_t[1, cols, spot] = (u * sg * (1.0 + g * (1.0 - sg))).astype(bf)
            lhs_t[2, cols, spot] = gs.astype(bf)
            return carry

        lax.fori_loop(0, f // step, wide, 0)

    def scale_back(n):
        if n < 3:
            for w in (1, 2):
                lhs_load(n, w).wait()

        def wide(j, carry):
            cols = pl.ds(pl.multiple_of(j * step, step), step)
            di = None
            for i in range(2):
                one = lax.dot_general(
                    wd_v[i, cols, :], dm_v[n, i].reshape(total, span), NT, preferred_element_type=f32
                )
                di = one if di is None else di + one
            toks = slice(n * total, (n + 1) * total)
            for w in (1, 2):
                lhs_t[w, cols, toks] = (lhs_t[w, cols, toks].astype(f32) * di).astype(bf)
            return carry

        lax.fori_loop(0, f // step, wide, 0)

    def hb_half(n):
        return pltpu.make_async_copy(
            gh_ref.at[ranks[n], :, :, pl.ds(top * span, span)],
            hb_v.at[n // 2, :, :, pl.ds((n % 2) * span, span)],
            ld_sem.at[17 + n],
        )

    for cp in hb_load(3) + tips:
        cp.wait()
    remake(3)

    block = quad.shape[4]

    def quad_trade(w, k):
        return far_copy(quad.at[w, (z + k) % 4], quad_in.at[w, k - 1], qz_s.at[w, k - 1], qz_r.at[w, k - 1], peer(k), t)

    def head_grad(w):
        slow[2 + w].wait()
        head_swap(w).wait_recv()
        for i in range(2):
            lhs_q[:, i * total : (i + 1) * total] = lhs_in[w, i].reshape(total, hc).astype(f32).T.astype(bf)

        def tile(j, carry):
            cols = pl.ds(pl.multiple_of(j * block, block), block)
            quad[w, j // 2, j % 2] = jnp.dot(
                lhs_q[...], hb_v[:, :, :, cols].reshape(2 * total, block), preferred_element_type=f32
            ).astype(bf)
            return carry

        lax.fori_loop(0, 8, tile, 0)
        for k in (2, 1, 3):
            quad_trade(w, k).start()

    for cp in toks:
        cp.wait()
    head_grad(0)
    advance(0)
    head_grad(1)
    advance(1)
    advance(2)
    head_grad(2)
    for n in range(4):
        hb_half(n).start()
    for n in (1, 2, 3):
        arrive(n - 1)
        dm_load(n, 0).start()
    gain_step(0)

    def swap_y(w):
        return far_copy(full.at[w, :, 1 - y], part.at[w], ys_s.at[w], ys_r.at[w], twin, t)

    def trade_z(w):
        return far_copy(part.at[w, 1 - side], mlp_ref.at[w, side], ts_s.at[w], ts_r.at[w], pal, t)

    def keep(w):
        return pltpu.make_async_copy(part.at[w, side], mlp_ref.at[w, side], own_s.at[1 + w])

    def finish_y(w):
        swap_y(w).wait()
        for b in range(2):
            part[w, b] = (part[w, b].astype(f32) + full[w, b, y].astype(f32)).astype(bf)
        trade_z(w).start()
        keep(w).start()

    def emit(w):
        for b in range(4):
            new = None
            for n in range(4):
                one = jnp.dot(
                    lhs_t[w, :, n * total : (n + 1) * total],
                    (dm_v[n, 0, :, :, b * block : (b + 1) * block] if w == 0 else hb_v[
                        n // 2, :, :, (n % 2) * span + b * block : (n % 2) * span + (b + 1) * block
                    ]).reshape(total, block),
                    preferred_element_type=f32,
                )
                new = one if new is None else new + one
            full[w, b // 2, b % 2] = new.astype(bf)
        swap_y(w).start()

    for n in range(3):
        lhs_load(n, 0).wait()
    for n in range(4):
        dm_load(n, 0).wait()
    emit(0)
    gain_step(1)
    advance(3)
    for i in range(2):
        slow[i].wait()
    dm_load(0, 1).wait()
    arrive(3)
    dm_load(1, 1).start()
    scale_back(0)
    for n in (1, 2, 3):
        if n < 3:
            advance(3 + n)
        dm_load(n, 1).wait()
        scale_back(n)
        if n < 3:
            arrive(3 + n)
            dm_load(n + 1, 1).start()
    gain_step(2)
    for n in range(4):
        hb_half(n).wait()
    emit(1)
    emit(2)
    gain_step(3)

    def head_swap_back(w):
        return far_copy(pair.at[w, 1 - y], attn_ref.at[w, y], qy_s.at[w], qy_r.at[w], twin, t)

    def head_keep(w):
        return pltpu.make_async_copy(pair.at[w, y], attn_ref.at[w, y], own_s.at[4 + w])

    def finish_head(w):
        for k in range(1, 4):
            quad_trade(w, k).wait_recv()
        for b in range(2):
            new = quad[w, z, b].astype(f32)
            for i in range(3):
                new = new + quad_in[w, i, b].astype(f32)
            pair[w, b] = new.astype(bf)
        head_swap_back(w).start()
        head_keep(w).start()

    finish_y(0)
    finish_head(0)
    finish_y(1)
    finish_head(1)
    finish_y(2)
    finish_head(2)

    keep_proj.wait()
    for i in range(6):
        gain_copy(i).wait_send()
    for i in range(6):
        forward_x(i).wait_send()
        for h in range(2):
            forward_c(i, h).wait_send()
    for k in range(1, 4):
        proj_trade(k).wait()
    for w in range(3):
        head_swap(w).wait_send()
        for k in range(1, 4):
            quad_trade(w, k).wait_send()
        head_keep(w).wait()
        keep(w).wait()
        head_swap_back(w).wait()
        trade_z(w).wait()


def weight_grads(gp, gqk, gh, gd, lhs, wgt, wut, wd, tok, nxt, dq, dk, dv, po):
    shard, width = tok.shape[1], tok.shape[2]
    f = lhs.shape[2]
    local = dq.shape[2]
    block = width // 8
    bf = jnp.bfloat16
    f32 = jnp.float32
    dma = pltpu.SemaphoreType.DMA
    shape = jax.ShapeDtypeStruct
    vm = pl.BlockSpec(memory_space=pltpu.VMEM)
    flops = 2 * 4 * shard * 4 * f * (3 * width + 3 * width // 2)
    return pl.pallas_call(
        grads_kernel,
        name="weight_grads",
        input_output_aliases={2: 4, 3: 5},
        out_shape=(
            shape((4, width), f32),
            shape((3, 2, local // 2, block), bf),
            shape((4, local, block), bf),
            shape((3, 2, f, block), bf),
            shape(gh.shape, bf),
            shape(gd.shape, bf),
        ),
        in_specs=[vm] * 2 + [FULL] * 12,
        out_specs=(vm,) + (FULL,) * 5,
        scratch_shapes=[
            pltpu.VMEM((2, 4, shard, width), bf),
            pltpu.VMEM((2, f, width), bf),
            pltpu.VMEM((4, 2, 4, shard, width // 2), bf),
            pltpu.VMEM((2, f, width // 2), bf),
            pltpu.VMEM((3, 2, 4, shard, local // 2), bf),
            pltpu.VMEM((local // 2, 8 * shard), bf),
            pltpu.VMEM((3, f, 16 * shard), bf),
            pltpu.VMEM((3, 4, 2, local // 2, block), bf),
            pltpu.VMEM((3, 3, 2, local // 2, block), bf),
            pltpu.VMEM((3, 2, local // 2, block), bf),
            pltpu.VMEM((3, 2, 2, f, block), bf),
            pltpu.VMEM((3, 2, f, block), bf),
            pltpu.VMEM((4, 8, width), f32),
            pltpu.VMEM((6, 8, width), f32),
            dma((25,)),
            dma((6,)), dma((6,)), dma((6, 2)), dma((6, 2)),
            dma((3,)), dma((3,)), dma((3,)), dma((3,)),
            dma((3, 3)), dma((3, 3)), dma((3,)), dma((3,)),
            dma((3,)), dma((3,)), dma((3,)), dma((3,)),
            dma((7,)), dma((6,)), dma((6,)), dma((3, 3)),
        ],
        compiler_params=pltpu.CompilerParams(
            collective_id=0, has_side_effects=True, vmem_limit_bytes=60 * 1024 * 1024
        ),
        cost_estimate=pl.CostEstimate(flops=flops, bytes_accessed=60 * 1024 * 1024, transcendentals=0),
    )(gp, gqk, gh, gd, lhs, wgt, wut, wd, tok, nxt, dq, dk, dv, po)


def far_copy(src, dst, ss, rs, dd, tt):
    return pltpu.make_async_remote_copy(
        src_ref=src, dst_ref=dst, send_sem=ss, recv_sem=rs, device_id=(dd, tt), device_id_type=MESH
    )


def mean_inv(values):
    return lax.rsqrt(jnp.mean(values * values, axis=1, keepdims=True) + EPS)


def mlp_kernel(
    att_ref, tok_ref, cot_ref, ga_ref, gm_ref, wg_ref, wu_ref, wd_ref,
    out_ref, ghid_ref, dat_ref, gain_ref, gh_ref, gd_ref,
    wg_v, wu_v, wd_v, slope_g, slope_u, buf, low_a, low_b, part, pmate, xsend, xrecv, hid,
    w_sem, as_s, as_r, ax_s, ax_r, af_s, af_r, ps_s, ps_r, px_s, px_r, zs_s, zs_r, ds_s, ds_r, hc_s, hc_r, st_sem,
):
    d, t, z, y, c, chip, mate, across = places()
    shard, width = att_ref.shape
    ff = wg_v.shape[1]
    bf = jnp.bfloat16
    f32 = jnp.float32
    tile = 512
    tiles = ff // tile
    small = shard // 2
    two = 2 * shard
    half = width // 2

    def wcopy(i, j):
        cols = pl.ds(j * tile, tile)
        if i == 0:
            return pltpu.make_async_copy(wg_ref.at[:, cols], wg_v.at[:, cols], w_sem.at[0, j])
        if i == 1:
            return pltpu.make_async_copy(wu_ref.at[:, cols], wu_v.at[:, cols], w_sem.at[1, j])
        return pltpu.make_async_copy(wd_ref.at[cols, :], wd_v.at[cols, :], w_sem.at[2, j])

    for j in range(tiles):
        wcopy(0, j).start()
        wcopy(1, j).start()
    for j in range(tiles):
        wcopy(2, j).start()
    greet([(((z + 1) % 4) * 2 + y, t), (((z + 3) % 4) * 2 + y, t), (d, mate), (d, across)])

    def send_mate(p, b):
        return far_copy(buf.at[p, b, c], buf.at[p, b, c], as_s.at[p, b], as_r.at[p, b], d, mate)

    def send_across(p, b):
        return far_copy(buf.at[p, b, c], buf.at[p, b, 2 + c], ax_s.at[p, b], ax_r.at[p, b], d, across)

    def forward(p, b):
        return far_copy(buf.at[p, b, 2 + c], buf.at[p, b, 2 + c], af_s.at[p, b], af_r.at[p, b], d, mate)

    def part_mate(p, b, h):
        return far_copy(part.at[p, b, h, 1 - c], pmate.at[p, b, h], ps_s.at[p, b, h], ps_r.at[p, b, h], d, mate)

    def part_across(p, b, h):
        return far_copy(xsend.at[p, b, h], xrecv.at[p, b, h], px_s.at[p, b, h], px_r.at[p, b, h], d, across)

    groups = (gh_ref, gd_ref)
    lines_h = [Line(gh_ref, z, y, t, q, zs_s.at[i], zs_r.at[i]) for i, q in enumerate((t, across))]
    lines_d = [Line(gd_ref, z, y, t, t, ds_s, ds_r)]
    ranks = rank_rows(z)

    def line_src(p, i):
        return buf.at[p, :, c if i == 0 else 2 + c]

    def row_c(n, i):
        cell = gh_ref.at[ranks[1 + n], t if i == 0 else across]
        return far_copy(cell, cell, hc_s.at[n, i], hc_r.at[n, i], d, mate)

    def store_row(p):
        mine = groups[p].at[z]
        return [
            pltpu.make_async_copy(buf.at[p, :, i], mine.at[q], st_sem.at[p, i])
            for i, q in enumerate((chip * 2, chip * 2 + 1, 2 - chip * 2, 3 - chip * 2))
        ]

    def inner(p, b):
        rows = pl.ds(b * two, two)
        both = buf[p, b].reshape(two, width)
        for j in range(tiles):
            cols = pl.ds(j * tile, tile)
            if p == 0:
                if b == 0:
                    wcopy(0, j).wait()
                    wcopy(1, j).wait()
                g = jnp.dot(both, wg_v[:, cols], preferred_element_type=f32)
                u = jnp.dot(both, wu_v[:, cols], preferred_element_type=f32)
                sg = jax.nn.sigmoid(g)
                gs = g * sg
                low_a[:, cols] = (gs * u).astype(bf)
                slope_u[rows, cols] = gs
                slope_g[rows, cols] = u * sg * (1.0 + g * (1.0 - sg))
            else:
                di = lax.dot_general(both, wd_v[cols, :], NT, preferred_element_type=f32)
                low_a[:, cols] = (di * slope_g[rows, cols]).astype(bf)
                low_b[:, cols] = (di * slope_u[rows, cols]).astype(bf)

    def combine(p, b, h):
        part_mate(p, b, h).wait_recv()
        xsend[p, b, h] = (part[p, b, h, c, 1].astype(f32) + pmate[p, b, h, 1].astype(f32)).astype(bf)
        part_across(p, b, h).start()

    def outer(p, b):
        if p == 0 and b == 0:
            for j in range(tiles):
                wcopy(2, j).wait()
        for h in range(2):
            for j in range(half // tile):
                cols = pl.ds(h * half + j * tile, tile)
                if p == 0:
                    new = jnp.dot(low_a[...], wd_v[:, cols], preferred_element_type=f32)
                else:
                    new = lax.dot_general(
                        low_a[...], wg_v[cols, :], NT, preferred_element_type=f32
                    ) + lax.dot_general(low_b[...], wu_v[cols, :], NT, preferred_element_type=f32)
                new = new.astype(bf)
                for i in range(4):
                    part[p, b, h, i % 2, i // 2, :, pl.ds(j * tile, tile)] = new[i * small : (i + 1) * small]
            part_mate(p, b, h).start()
            if h == 1:
                combine(p, b, 0)
        combine(p, b, 1)

    def whole(p, b):
        sums = []
        for h in range(2):
            part_across(p, b, h).wait_recv()
            sums.append(
                part[p, b, h, c, 0].astype(f32) + pmate[p, b, h, 0].astype(f32) + xrecv[p, b, h].astype(f32)
            )
        return jnp.concatenate(sums, axis=1)

    def launch(p, b):
        send_across(p, b).start()
        send_mate(p, b).start()

    def arrive(p, b):
        send_mate(p, b).wait_recv()
        send_across(p, b).wait_recv()
        forward(p, b).start()
        forward(p, b).wait_recv()

    def rows_of(b):
        return slice(b * small, (b + 1) * small)

    def middle(b):
        r = rows_of(b)
        mlp = whole(0, b)
        rf = mean_inv(mlp)
        fh = mlp * rf
        gy = cot_ref[r, :].astype(f32)
        out_ref[r, :] = (hid[r, :] + fh * gm_ref[...]).astype(bf)
        scaled = gy * gm_ref[...]
        buf[1, b, c] = (rf * (scaled - fh * jnp.mean(scaled * fh, axis=1, keepdims=True))).astype(bf)
        launch(1, b)
        gain = jnp.sum(gy * fh, axis=0, keepdims=True)
        gain_ref[1:2, :] = gain if b == 0 else gain_ref[1:2, :] + gain

    def last(b):
        r = rows_of(b)
        gh = cot_ref[r, :].astype(f32) + whole(1, b)
        ghid_ref[r, :] = gh
        att = att_ref[r, :]
        ra = mean_inv(att)
        ah = att * ra
        gain = jnp.sum(gh * ah, axis=0, keepdims=True)
        gain_ref[0:1, :] = gain if b == 0 else gain_ref[0:1, :] + gain
        scaled = gh * ga_ref[...]
        dat_ref[r, :] = (ra * (scaled - ah * jnp.mean(scaled * ah, axis=1, keepdims=True))).astype(bf)

    for b in range(2):
        r = rows_of(b)
        att = att_ref[r, :]
        hid[r, :] = tok_ref[r, :].astype(f32) + att * mean_inv(att) * ga_ref[...]
        buf[0, b, c] = hid[r, :].astype(bf)
        launch(0, b)
    lines_h[0].start(0, line_src(0, 0))
    arrive(0, 0)
    inner(0, 0)
    outer(0, 0)
    arrive(0, 1)
    lines_h[1].start(0, line_src(0, 1))
    for cp in store_row(0):
        cp.start()
    inner(0, 1)
    middle(0)
    lines_h[0].landed(0)
    lines_h[0].start(1)
    outer(0, 1)
    arrive(1, 0)
    lines_h[1].landed(0)
    lines_h[1].start(1)
    for i in range(2):
        row_c(0, i).start()
    inner(1, 0)
    middle(1)
    lines_d[0].start(0, line_src(1, 0))
    outer(1, 0)
    arrive(1, 1)
    for cp in store_row(1):
        cp.start()
    inner(1, 1)
    outer(1, 1)
    for line in lines_h:
        line.landed(1)
    for i in range(2):
        row_c(1, i).start()
    last(0)
    last(1)

    for p in range(2):
        for b in range(2):
            send_across(p, b).wait_send()
            send_mate(p, b).wait_send()
            forward(p, b).wait_send()
            for h in range(2):
                part_mate(p, b, h).wait_send()
                part_across(p, b, h).wait_send()
        for cp in store_row(p):
            cp.wait()
        for i in range(2):
            row_c(p, i).wait()
    for i in range(2):
        lines_h[i].sent(0, line_src(0, i))
        lines_h[i].sent(1)
    lines_d[0].sent(0, line_src(1, 0))
    lines_d[0].landed(0)


def mlp_both(att, tok, cot, ga, gm, wg, wu, wd):
    shard, width = tok.shape
    ff = wg.shape[1]
    bf = jnp.bfloat16
    f32 = jnp.float32
    dma = pltpu.SemaphoreType.DMA
    half = width // 2
    small = shard // 2
    vm = pl.BlockSpec(memory_space=pltpu.VMEM)
    shape = jax.ShapeDtypeStruct
    out = pl.pallas_call(
        mlp_kernel,
        name="feed_forward",
        out_shape=(
            shape((shard, width), bf),
            shape((shard, width), f32),
            shape((shard, width), bf),
            shape((2, width), f32),
            shape((4, 4, 2, small, width), bf),
            shape((4, 4, 2, small, width), bf),
        ),
        in_specs=[vm] * 5 + [FULL] * 3,
        out_specs=(vm,) * 4 + (FULL,) * 2,
        scratch_shapes=[
            pltpu.VMEM((width, ff), bf),
            pltpu.VMEM((width, ff), bf),
            pltpu.VMEM((ff, width), bf),
            pltpu.VMEM((4 * shard, ff), f32),
            pltpu.VMEM((4 * shard, ff), f32),
            pltpu.VMEM((2, 2, 4, small, width), bf),
            pltpu.VMEM((2 * shard, ff), bf),
            pltpu.VMEM((2 * shard, ff), bf),
            pltpu.VMEM((2, 2, 2, 2, 2, small, half), bf),
            pltpu.VMEM((2, 2, 2, 2, small, half), bf),
            pltpu.VMEM((2, 2, 2, small, half), bf),
            pltpu.VMEM((2, 2, 2, small, half), bf),
            pltpu.VMEM((shard, width), f32),
            dma((3, ff // 512)),
            dma((2, 2)), dma((2, 2)), dma((2, 2)), dma((2, 2)), dma((2, 2)), dma((2, 2)),
            dma((2, 2, 2)), dma((2, 2, 2)), dma((2, 2, 2)), dma((2, 2, 2)),
            dma((2, 2, 2)), dma((2, 2, 2)), dma((2, 1)), dma((2, 1)),
            dma((2, 2)), dma((2, 2)),
            dma((2, 4)),
        ],
        compiler_params=pltpu.CompilerParams(
            collective_id=1, has_side_effects=True, vmem_limit_bytes=60 * 1024 * 1024
        ),
        cost_estimate=pl.CostEstimate(
            flops=2 * 6 * 4 * shard * width * ff, bytes_accessed=40 * 1024 * 1024, transcendentals=4 * shard * ff
        ),
    )(att, tok, cot, ga.reshape(1, -1), gm.reshape(1, -1), wg, wu, wd)
    return (*out[:4], out[4].reshape(4, 4, shard, width), out[5].reshape(4, 4, shard, width))


NT = (((1,), (1,)), ((), ()))
TN = (((0,), (0,)), ((), ()))


def places():
    d = lax.axis_index("dp")
    t = lax.axis_index("tensor")
    c = t % 2
    return d, t, d // 2, d % 2, c, t // 2, t + 1 - 2 * c, (t + 2) % 4


def greet(targets):
    barrier = pltpu.get_barrier_semaphore()
    for dd, tt in targets:
        pl.semaphore_signal(barrier, inc=1, device_id=(dd, tt), device_id_type=MESH)
    pl.semaphore_wait(barrier, len(targets))


def to_rows(column):
    n = column.shape[0]
    return jnp.broadcast_to(column, (n, n)).T[0:8, :]


def to_column(rows):
    n = rows.shape[1]
    return jnp.broadcast_to(rows[0:1, :], (n, n)).T[:, 0:1]


def attend_kernel(
    len_ref, tok_ref, gq_ref, gk_ref, wq_ref, wk_ref, wv_ref, wo_ref, wg_ref, wu_ref,
    att_ref, tall_ref, tnext_ref, qh_ref, kh_ref, qr_ref, kr_ref, v_ref, mix_ref, p_ref, inv_ref, cos_ref, sin_ref, wgt_ref, wut_ref,
    w_v, wo_v, wide, tipped, tall, raw, rot, val, mixed, prob, stat, stat_in, pown, pmate, xsend, xrecv, qown, qmate,
    w_sem, as_s, as_r, ss_s, ss_r, ps_s, ps_r, px_s, px_r, pq_s, pq_r, st_sem, ns_s, ns_r, tw_sem,
):
    d, t, z, y, c, chip, mate, across = places()
    far = (mate + 2) % 4
    shard, width = tok_ref.shape
    local = w_v.shape[2]
    bf = jnp.bfloat16
    f32 = jnp.float32
    heads = local // HD
    weights = [
        pltpu.make_async_copy(r, w_v.at[i], w_sem.at[i]) for i, r in enumerate((wq_ref, wk_ref, wv_ref))
    ] + [pltpu.make_async_copy(wo_ref, wo_v, w_sem.at[3])]
    for cp in weights:
        cp.start()
    span = wide.shape[2]
    side = z % 2
    tips = [
        pltpu.make_async_copy(r.at[:, pl.ds(side * span, span)], wide.at[i], tw_sem.at[i])
        for i, r in enumerate((wg_ref, wu_ref))
    ]
    for cp in tips:
        cp.start()
    drops = [
        pltpu.make_async_copy(tipped.at[i], r, tw_sem.at[2 + i]) for i, r in enumerate((wgt_ref, wut_ref))
    ]

    def tip(i):
        tips[i].wait()

        def one(j, carry):
            cols = pl.ds(pl.multiple_of(j * 128, 128), 128)
            tipped[i, cols, :] = wide[i, :, cols].T
            return carry

        lax.fori_loop(0, span // 128, one, 0)
        drops[i].start()

    tall[t] = tok_ref[...]
    twin = z * 2 + 1 - y
    greet([(d, mate), (d, across), (d, far), (twin, t)])

    send_x = far_copy(tall.at[t], tall.at[t], as_s.at[0], as_r.at[0], d, across)
    send_m = far_copy(tall.at[t], tall.at[t], as_s.at[1], as_r.at[1], d, mate)
    forward = far_copy(tall.at[across], tall.at[across], as_s.at[2], as_r.at[2], d, mate)
    send_x.start()
    send_m.start()
    next_y = [
        far_copy(tall.at[q], tnext_ref.at[q], ns_s.at[i], ns_r.at[i], twin, t) for i, q in enumerate((t, across))
    ]
    next_c = [
        far_copy(tnext_ref.at[q], tnext_ref.at[q], ns_s.at[2 + i], ns_r.at[2 + i], d, mate)
        for i, q in enumerate((t, across))
    ]
    next_y[0].start()

    total = 4 * shard

    def layout(shape, dim):
        spot = lax.broadcasted_iota(jnp.int32, shape, dim)
        end = 0
        seg = jnp.zeros(shape, jnp.int32)
        start = jnp.zeros(shape, jnp.int32)
        for i in range(len_ref.shape[1]):
            size = len_ref[0, i]
            end = end + size
            past = spot >= end
            seg = seg + jnp.where(past, 1, 0)
            start = start + jnp.where(past, size, 0)
        return seg, spot - start

    def tables():
        lane = lax.broadcasted_iota(jnp.int32, (total, HD), 1)
        near = lane < HD // 2
        freq = jnp.exp(jnp.where(near, lane, lane - HD // 2).astype(f32) * (-2.0 * math.log(THETA) / HD))
        angle = layout((total, HD), 0)[1].astype(f32) * freq
        cos_ref[...] = jnp.cos(angle).reshape(4, shard, HD)
        sines = jnp.sin(angle)
        sin_ref[...] = jnp.where(near, -sines, sines).reshape(4, shard, HD)

    def project(first):
        rows = tall[pl.ds(first, 2)].reshape(2 * shard, width)
        for i in range(3):
            new = jnp.dot(rows, w_v[i], preferred_element_type=f32).reshape(2, shard, local)
            if i == 2:
                val[pl.ds(first, 2)] = new.astype(bf)
            else:
                raw[i, pl.ds(first, 2)] = new
                for s in range(2):
                    stat[first + s, i * 8 : i * 8 + 8, :] = to_rows(
                        jnp.sum(new[s] * new[s], axis=1, keepdims=True)
                    )

    here = chip * 2
    there = 2 - chip * 2
    for cp in weights[:3]:
        cp.wait()
    send_m.wait_recv()
    project(here)
    tables()
    tip(0)
    send_x.wait_recv()
    forward.start()
    next_y[1].start()
    forward.wait_recv()
    project(there)

    stats = [
        far_copy(stat, stat_in.at[i], ss_s.at[i], ss_r.at[i], d, who)
        for i, who in enumerate((mate, across, far))
    ]
    for cp in stats:
        cp.start()
    stores = [
        pltpu.make_async_copy(tall, tall_ref, st_sem.at[0]),
        pltpu.make_async_copy(val, v_ref, st_sem.at[1]),
    ]
    for cp in stores:
        cp.start()
    for cp in stats:
        cp.wait_recv()

    for q in range(4):
        inv = lax.rsqrt((stat[q] + stat_in[0, q] + stat_in[1, q] + stat_in[2, q]) / width + EPS)
        inv_ref[q] = inv
        for i, gain in ((0, gq_ref), (1, gk_ref)):
            unit = raw[i, q] * to_column(inv[i * 8 : i * 8 + 8])
            raw[i, q] = unit
            unit = unit * gain[...]
            for h in range(heads):
                cols = slice(h * HD, (h + 1) * HD)
                one = unit[:, cols]
                rot[i, q, :, cols] = (
                    one * cos_ref[q] + pltpu.roll(one, HD // 2, 1) * sin_ref[q]
                ).astype(bf)
    more = [
        pltpu.make_async_copy(raw.at[0], qh_ref, st_sem.at[2]),
        pltpu.make_async_copy(raw.at[1], kh_ref, st_sem.at[3]),
        pltpu.make_async_copy(rot.at[0], qr_ref, st_sem.at[4]),
        pltpu.make_async_copy(rot.at[1], kr_ref, st_sem.at[5]),
    ]
    for cp in more:
        cp.start()
    stores += more

    scale = 1.0 / math.sqrt(HD)
    def mix(first, n):
        ids = first * shard + lax.broadcasted_iota(jnp.int32, (2 * shard, total), 0)
        keys = lax.broadcasted_iota(jnp.int32, (2 * shard, total), 1)
        rows = first * shard + lax.broadcasted_iota(jnp.int32, (2 * shard, 1), 0)
        seg_rows = jnp.zeros((2 * shard, 1), jnp.int32)
        end = 0
        for i in range(len_ref.shape[1]):
            end = end + len_ref[0, i]
            seg_rows = seg_rows + jnp.where(rows >= end, 1, 0)
        same = seg_rows == layout((1, total), 1)[0]
        ok = same & (keys <= ids)
        for h in range(heads):
            cols = slice(h * HD, (h + 1) * HD)
            s = lax.dot_general(
                rot[0, pl.ds(first, 2), :, cols].reshape(2 * shard, HD),
                rot[1, :, :, cols].reshape(total, HD),
                NT,
                preferred_element_type=f32,
            )
            s = jnp.where(ok, s * scale, -1e30)
            e = jnp.exp(s - jnp.max(s, axis=1, keepdims=True))
            p = e / jnp.sum(e, axis=1, keepdims=True)
            prob[pl.ds(first, 2), h] = p.reshape(2, shard, total)
            mixed[pl.ds(first, 2), :, cols] = (
                jnp.dot(p.astype(bf), val[:, :, cols].reshape(total, HD), preferred_element_type=f32)
                .astype(bf)
                .reshape(2, shard, HD)
            )
        cp = pltpu.make_async_copy(prob.at[pl.ds(first, 2)], p_ref.at[pl.ds(first, 2)], st_sem.at[6 + n])
        cp.start()
        stores.append(cp)

    half = width // 2
    tile = 512

    def part_mate(h):
        return far_copy(pown.at[h, 1 - c], pmate.at[h], ps_s.at[h], ps_r.at[h], d, mate)

    def part_across(h):
        return far_copy(xsend.at[h], xrecv.at[h], px_s.at[h], px_r.at[h], d, across)

    part_own = far_copy(qown.at[1 - c], qmate, pq_s, pq_r, d, mate)

    mix(there, 0)
    weights[3].wait()
    for h in range(2):
        for j in range(half // tile):
            new = jnp.dot(
                mixed[pl.ds(there, 2)].reshape(2 * shard, local),
                wo_v[:, pl.ds(h * half + j * tile, tile)],
                preferred_element_type=f32,
            ).astype(bf)
            pown[h, :, :, pl.ds(j * tile, tile)] = new.reshape(2, shard, tile)
        part_mate(h).start()
    for h in range(2):
        part_mate(h).wait_recv()
        xsend[h] = (pown[h, c].astype(f32) + pmate[h].astype(f32)).astype(bf)
        part_across(h).start()
    mix(here, 1)
    for j in range(width // tile):
        new = jnp.dot(
            mixed[pl.ds(here, 2)].reshape(2 * shard, local),
            wo_v[:, pl.ds(j * tile, tile)],
            preferred_element_type=f32,
        ).astype(bf)
        qown[:, :, pl.ds(j * tile, tile)] = new.reshape(2, shard, tile)
    part_own.start()
    cp = pltpu.make_async_copy(mixed, mix_ref, st_sem.at[8])
    cp.start()
    stores.append(cp)
    for cp in next_y:
        cp.wait_recv()
    for cp in next_c:
        cp.start()
    tip(1)
    stores += drops
    part_own.wait_recv()
    for h in range(2):
        part_across(h).wait_recv()
        cols = slice(h * half, (h + 1) * half)
        att_ref[:, cols] = (
            qown[c, :, cols].astype(f32) + qmate[:, cols].astype(f32) + xrecv[h].astype(f32)
        )
    for cp in stores:
        cp.wait()
    for cp in next_c:
        cp.wait_recv()
    for cp in [send_x, send_m, forward, part_own] + next_y + next_c + stats:
        cp.wait_send()
    for h in range(2):
        part_mate(h).wait_send()
        part_across(h).wait_send()


def attend_both(lengths, tok, gq, gk, wq, wk, wv, wo, wg, wu):
    shard, width = tok.shape
    local = wq.shape[1]
    heads = local // HD
    bf = jnp.bfloat16
    f32 = jnp.float32
    dma = pltpu.SemaphoreType.DMA
    vm = pl.BlockSpec(memory_space=pltpu.VMEM)
    shape = jax.ShapeDtypeStruct
    half = width // 2
    total = 4 * shard
    return pl.pallas_call(
        attend_kernel,
        name="attend_forward",
        out_shape=(
            shape((shard, width), f32),
            shape((4, shard, width), bf),
            shape((4, shard, width), bf),
            shape((4, shard, local), f32),
            shape((4, shard, local), f32),
            shape((4, shard, local), bf),
            shape((4, shard, local), bf),
            shape((4, shard, local), bf),
            shape((4, shard, local), bf),
            shape((4, heads, shard, total), f32),
            shape((4, 16, shard), f32),
            shape((4, shard, HD), f32),
            shape((4, shard, HD), f32),
            shape((wg.shape[1] // 2, width), bf),
            shape((wg.shape[1] // 2, width), bf),
        ),
        in_specs=[pl.BlockSpec(memory_space=pltpu.SMEM)] + [vm] * 3 + [FULL] * 6,
        out_specs=(vm,) + (FULL,) * 9 + (vm,) * 3 + (FULL,) * 2,
        scratch_shapes=[
            pltpu.VMEM((3, width, local), bf),
            pltpu.VMEM((local, width), bf),
            pltpu.VMEM((2, width, wg.shape[1] // 2), bf),
            pltpu.VMEM((2, wg.shape[1] // 2, width), bf),
            pltpu.VMEM((4, shard, width), bf),
            pltpu.VMEM((2, 4, shard, local), f32),
            pltpu.VMEM((2, 4, shard, local), bf),
            pltpu.VMEM((4, shard, local), bf),
            pltpu.VMEM((4, shard, local), bf),
            pltpu.VMEM((4, heads, shard, total), f32),
            pltpu.VMEM((4, 16, shard), f32),
            pltpu.VMEM((3, 4, 16, shard), f32),
            pltpu.VMEM((2, 2, shard, half), bf),
            pltpu.VMEM((2, shard, half), bf),
            pltpu.VMEM((2, shard, half), bf),
            pltpu.VMEM((2, shard, half), bf),
            pltpu.VMEM((2, shard, width), bf),
            pltpu.VMEM((shard, width), bf),
            dma((4,)),
            dma((3,)), dma((3,)), dma((3,)), dma((3,)),
            dma((2,)), dma((2,)), dma((2,)), dma((2,)),
            dma(()), dma(()),
            dma((9,)),
            dma((4,)), dma((4,)), dma((4,)),
        ],
        compiler_params=pltpu.CompilerParams(
            collective_id=2, has_side_effects=True, vmem_limit_bytes=56 * 1024 * 1024
        ),
        cost_estimate=pl.CostEstimate(
            flops=2 * total * width * local * 4, bytes_accessed=24 * 1024 * 1024, transcendentals=heads * total * total
        ),
    )(
        lengths, tok, gq.reshape(1, -1), gk.reshape(1, -1), wq, wk, wv, wo, wg, wu,
    )


def rank_rows(z):
    return (z, z + 1 - 2 * (z % 2), 2 - z // 2, 3 - 3 * (z // 2))


class Line:
    def __init__(self, ref, z, y, t, q, send, recv):
        self.ref, self.z, self.t, self.q, self.send, self.recv = ref, z, t, q, send, recv
        self.up = ((z + 1) % 4) * 2 + y
        self.down = ((z + 3) % 4) * 2 + y

    def go(self, way, i, r, src=None):
        cell = self.ref.at[r, self.q]
        return far_copy(
            cell if src is None else src, cell, self.send.at[way, i], self.recv.at[way, i], (self.up, self.down)[way], self.t
        )

    def hops(self, step, src=None):
        z = self.z
        if step == 0:
            return [(z < 3, 0, z), (z > 0, 1, z)]
        if step == 1:
            middle = (z > 0) & (z < 3)
            return [(middle, 0, (z + 3) % 4), (middle, 1, (z + 1) % 4)]
        return [(z == 2, 0, 0), (z == 1, 1, 3)]

    def lands(self, step):
        z = self.z
        if step == 0:
            return [(z > 0, 0, (z + 3) % 4), (z < 3, 1, (z + 1) % 4)]
        if step == 1:
            return [(z > 1, 0, (z + 2) % 4), (z < 2, 1, (z + 2) % 4)]
        return [(z == 3, 0, 0), (z == 0, 1, 3)]

    def start(self, step, src=None):
        for ok, way, r in self.hops(step):
            pl.when(ok)(self.go(way, step, r, src).start)

    def sent(self, step, src=None):
        for ok, way, r in self.hops(step):
            pl.when(ok)(self.go(way, step, r, src).wait_send)

    def landed(self, step):
        for ok, way, r in self.lands(step):
            pl.when(ok)(self.go(way, step, r).wait_recv)


def attend_back_kernel(
    dat_ref, ghid_ref, cos_ref, sin_ref, gq_ref, gk_ref, inv_ref,
    wq_ref, wk_ref, wv_ref, wo_ref, qh_ref, kh_ref, qr_ref, kr_ref, v_ref, p_ref, mix_ref, wgt_ref, wut_ref, gh_in, gd_in,
    gt_ref, gain_ref, dq_ref, dk_ref, dv_ref, po_ref, lhs_ref, gh_ref, gd_ref,
    w_v, wo_v, dall, unit, rot, val, dmix, prob, scaled, low, mixed, lhs_t, full, part, tip_v, hb_v, made, stat, stat_in, pown, pmate, xsend, xrecv, qown, qmate,
    w_sem, as_s, as_r, hx_s, hx_r, hc_s, hc_r, ss_s, ss_r, ps_s, ps_r, px_s, px_r, pq_s, pq_r, ys_s, ys_r, zs_s, zs_r, hz_s, hz_r, st_sem, hb_sem, made_sem,
):
    d, t, z, y, c, chip, mate, across = places()
    far = (mate + 2) % 4
    shard, width = dat_ref.shape
    local = w_v.shape[2]
    bf = jnp.bfloat16
    f32 = jnp.float32
    heads = local // HD
    total = 4 * shard
    sources = (wo_ref, wgt_ref, wut_ref, mix_ref, v_ref, p_ref, qr_ref, kr_ref, qh_ref, kh_ref, wq_ref, wk_ref, wv_ref)
    homes = (wo_v, tip_v.at[0], tip_v.at[1], mixed, val, prob, rot.at[0], rot.at[1], unit.at[0], unit.at[1], w_v.at[0], w_v.at[1], w_v.at[2])
    loads = [pltpu.make_async_copy(a, b, w_sem.at[i]) for i, (a, b) in enumerate(zip(sources, homes))]
    for cp in loads:
        cp.start()
    dall[t] = dat_ref[...]
    twin = z * 2 + 1 - y
    above = ((z + 1) % 4) * 2 + y
    below = ((z + 3) % 4) * 2 + y
    greet([(d, mate), (d, across), (d, far), (twin, t), (above, t), (below, t)])

    line_h = Line(gh_ref, z, y, t, t, hz_s, hz_r)
    line_d = Line(gd_ref, z, y, t, t, zs_s, zs_r)
    line_h.start(2)
    line_d.start(1)
    ranks = rank_rows(z)
    edge = (z == 0) | (z == 3)

    def hb_load(n):
        return pltpu.make_async_copy(gh_ref.at[ranks[n]], hb_v.at[n % 2], hb_sem.at[n])

    hb_load(0).start()
    hb_load(1).start()

    def made_out(n):
        return pltpu.make_async_copy(made, lhs_ref.at[n], made_sem.at[n])

    def remake(n):
        hb_load(n).wait()
        if n > 0:
            made_out(n - 1).wait()

        def wide(j, carry):
            cols = pl.ds(pl.multiple_of(j * 512, 512), 512)
            hb = hb_v[n % 2].reshape(total, width)
            g = lax.dot_general(tip_v[0, cols, :], hb, NT, preferred_element_type=f32)
            u = lax.dot_general(tip_v[1, cols, :], hb, NT, preferred_element_type=f32)
            sg = jax.nn.sigmoid(g)
            gs = g * sg
            made[0, cols, :] = (gs * u).astype(bf)
            made[1, cols, :] = (u * sg * (1.0 + g * (1.0 - sg))).astype(bf)
            made[2, cols, :] = gs.astype(bf)
            return carry

        lax.fori_loop(0, made.shape[1] // 512, wide, 0)
        made_out(n).start()

    send_x = far_copy(dall.at[t], dall.at[t], as_s.at[0], as_r.at[0], d, across)
    send_m = far_copy(dall.at[t], dall.at[t], as_s.at[1], as_r.at[1], d, mate)
    forward = far_copy(dall.at[across], dall.at[across], as_s.at[2], as_r.at[2], d, mate)
    send_x.start()
    send_m.start()
    last = ranks[3]
    row_x = far_copy(gh_ref.at[last, t], gh_ref.at[last, t], hx_s, hx_r, d, across)
    row_c = [
        far_copy(gh_ref.at[last, q], gh_ref.at[last, q], hc_s.at[j], hc_r.at[j], d, mate)
        for j, q in enumerate((t, across))
    ]
    swap_y = far_copy(full.at[:, 1 - y], part, ys_s, ys_r, twin, t)

    def project(first):
        rows = dall[pl.ds(first, 2)].reshape(2 * shard, width)
        dmix[pl.ds(first, 2)] = (
            lax.dot_general(rows, wo_v[...], NT, preferred_element_type=f32).astype(bf).reshape(2, shard, local)
        )

    here = chip * 2
    there = 2 - chip * 2
    loads[0].wait()
    send_m.wait_recv()
    project(here)
    for cp in loads[1:3]:
        cp.wait()
    remake(0)
    hb_load(2).start()
    for cp in loads[3:]:
        cp.wait()
    send_x.wait_recv()
    forward.start()
    forward.wait_recv()
    line_h.landed(2)
    pl.when(edge)(row_x.start)
    project(there)
    lhs_t[...] = mixed[...].reshape(total, local).astype(f32).T.astype(bf)
    block = full.shape[3]
    for b in range(8):
        full[b // 2, b % 2] = jnp.dot(
            lhs_t[...], dall[:, :, b * block : (b + 1) * block].reshape(total, block), preferred_element_type=f32
        ).astype(bf)
    swap_y.start()
    stores = []

    scale = 1.0 / math.sqrt(HD)
    cos = cos_ref[...].reshape(total, HD)
    sin = sin_ref[...].reshape(total, HD)
    dots = [jnp.zeros((total, 1), f32), jnp.zeros((total, 1), f32)]
    for h in range(heads):
        cols = slice(h * HD, (h + 1) * HD)
        dm = dmix[:, :, cols].reshape(total, HD)
        p = prob[:, h].reshape(total, total)
        dp = lax.dot_general(dm, val[:, :, cols].reshape(total, HD), NT, preferred_element_type=f32)
        ds = (p * (dp - jnp.sum(p * dp, axis=1, keepdims=True))).astype(bf)
        low[2, :, :, cols] = (
            lax.dot_general(p.astype(bf), dm, TN, preferred_element_type=f32).astype(bf).reshape(4, shard, HD)
        )
        back = (
            jnp.dot(ds, rot[1, :, :, cols].reshape(total, HD), preferred_element_type=f32) * scale,
            lax.dot_general(ds, rot[0, :, :, cols].reshape(total, HD), TN, preferred_element_type=f32) * scale,
        )
        for i, gain in ((0, gq_ref), (1, gk_ref)):
            g = back[i]
            g = g * cos - pltpu.roll(g, HD // 2, 1) * sin
            u = unit[i, :, :, cols].reshape(total, HD)
            prod = g * u
            gain_ref[i : i + 1, cols] = jnp.sum(prod, axis=0, keepdims=True)
            dots[i] = dots[i] + jnp.sum(prod * gain[:, cols], axis=1, keepdims=True)
            scaled[i, :, :, cols] = (g * gain[:, cols]).reshape(4, shard, HD)
    for q in range(4):
        for i in range(2):
            stat[q, i * 8 : i * 8 + 8, :] = to_rows(dots[i][q * shard : (q + 1) * shard])
    stats = [
        far_copy(stat, stat_in.at[i], ss_s.at[i], ss_r.at[i], d, who)
        for i, who in enumerate((mate, across, far))
    ]
    for cp in stats:
        cp.start()
    for cp in stats:
        cp.wait_recv()

    def finish(first):
        for s in range(2):
            q = first + s
            mean = (stat[q] + stat_in[0, q] + stat_in[1, q] + stat_in[2, q]) / width
            inv = inv_ref[q]
            for i in range(2):
                low[i, q] = (
                    to_column(inv[i * 8 : i * 8 + 8])
                    * (scaled[i, q] - unit[i, q] * to_column(mean[i * 8 : i * 8 + 8]))
                ).astype(bf)

    half = width // 2
    tile = 512

    def part_mate(h):
        return far_copy(pown.at[h, 1 - c], pmate.at[h], ps_s.at[h], ps_r.at[h], d, mate)

    def part_across(h):
        return far_copy(xsend.at[h], xrecv.at[h], px_s.at[h], px_r.at[h], d, across)

    part_own = far_copy(qown.at[1 - c], qmate, pq_s, pq_r, d, mate)

    def result(first, start):
        new = None
        for i in range(3):
            one = lax.dot_general(
                low[i, pl.ds(first, 2)].reshape(2 * shard, local),
                w_v[i, pl.ds(start, tile), :],
                NT,
                preferred_element_type=f32,
            )
            new = one if new is None else new + one
        return new.astype(bf).reshape(2, shard, tile)

    finish(there)
    for h in range(2):
        for j in range(half // tile):
            pown[h, :, :, pl.ds(j * tile, tile)] = result(there, h * half + j * tile)
        part_mate(h).start()
        part_mate(h).wait_recv()
        xsend[h] = (pown[h, c].astype(f32) + pmate[h].astype(f32)).astype(bf)
        part_across(h).start()
    line_d.landed(1)
    line_d.start(2)
    pl.when(edge)(row_x.wait_recv)
    for cp in row_c:
        cp.start()
    finish(here)
    more = [
        pltpu.make_async_copy(low.at[i], r, st_sem.at[1 + i]) for i, r in enumerate((dq_ref, dk_ref, dv_ref))
    ]
    for cp in more:
        cp.start()
    stores += more
    for j in range(width // tile):
        qown[:, :, pl.ds(j * tile, tile)] = result(here, j * tile)
    part_own.start()
    remake(1)
    swap_y.wait_recv()
    for b in range(4):
        part[b] = (part[b].astype(f32) + full[b, y].astype(f32)).astype(bf)
    keep = pltpu.make_async_copy(part, po_ref, st_sem.at[0])
    keep.start()
    stores.append(keep)
    remake(2)
    part_own.wait_recv()
    for h in range(2):
        part_across(h).wait_recv()
        cols = slice(h * half, (h + 1) * half)
        gt_ref[:, cols] = (
            ghid_ref[:, cols]
            + (qown[c, :, cols].astype(f32) + qmate[:, cols].astype(f32) + xrecv[h].astype(f32))
        ).astype(bf)
    for cp in stores:
        cp.wait()
    for cp in row_c:
        cp.wait()
    pl.when(edge)(row_x.wait_send)
    line_h.sent(2)
    line_d.sent(1)
    line_d.landed(2)
    line_d.sent(2)
    made_out(2).wait()
    for cp in [send_x, send_m, forward, part_own, swap_y] + stats:
        cp.wait_send()
    for h in range(2):
        part_mate(h).wait_send()
        part_across(h).wait_send()


def attend_back_both(dat, ghid, cos, sin, gq, gk, inv, wq, wk, wv, wo, qh, kh, qr, kr, v, p, mix, wgt, wut, gh, gd):
    shard, width = dat.shape
    local = wq.shape[1]
    heads = local // HD
    bf = jnp.bfloat16
    f32 = jnp.float32
    dma = pltpu.SemaphoreType.DMA
    vm = pl.BlockSpec(memory_space=pltpu.VMEM)
    shape = jax.ShapeDtypeStruct
    half = width // 2
    total = 4 * shard
    return pl.pallas_call(
        attend_back_kernel,
        name="attend_backward",
        out_shape=(
            shape((shard, width), bf),
            shape((2, local), f32),
            shape((4, shard, local), bf),
            shape((4, shard, local), bf),
            shape((4, shard, local), bf),
            shape((4, local, width // 8), bf),
            shape((3, 3, wgt.shape[0], total), bf),
            shape(gh.shape, bf),
            shape(gd.shape, bf),
        ),
        in_specs=[vm] * 7 + [FULL] * 15,
        out_specs=(vm,) * 2 + (FULL,) * 7,
        input_output_aliases={20: 7, 21: 8},
        scratch_shapes=[
            pltpu.VMEM((3, width, local), bf),
            pltpu.VMEM((local, width), bf),
            pltpu.VMEM((4, shard, width), bf),
            pltpu.VMEM((2, 4, shard, local), f32),
            pltpu.VMEM((2, 4, shard, local), bf),
            pltpu.VMEM((4, shard, local), bf),
            pltpu.VMEM((4, shard, local), bf),
            pltpu.VMEM((4, heads, shard, total), f32),
            pltpu.VMEM((2, 4, shard, local), f32),
            pltpu.VMEM((3, 4, shard, local), bf),
            pltpu.VMEM((4, shard, local), bf),
            pltpu.VMEM((local, total), bf),
            pltpu.VMEM((4, 2, local, width // 8), bf),
            pltpu.VMEM((4, local, width // 8), bf),
            pltpu.VMEM((2, wgt.shape[0], width), bf),
            pltpu.VMEM((2, 4, shard, width), bf),
            pltpu.VMEM((3, wgt.shape[0], total), bf),
            pltpu.VMEM((4, 16, shard), f32),
            pltpu.VMEM((3, 4, 16, shard), f32),
            pltpu.VMEM((2, 2, shard, half), bf),
            pltpu.VMEM((2, shard, half), bf),
            pltpu.VMEM((2, shard, half), bf),
            pltpu.VMEM((2, shard, half), bf),
            pltpu.VMEM((2, shard, width), bf),
            pltpu.VMEM((shard, width), bf),
            dma((13,)),
            dma((3,)), dma((3,)), dma(()), dma(()), dma((2,)), dma((2,)), dma((3,)), dma((3,)),
            dma((2,)), dma((2,)), dma((2,)), dma((2,)),
            dma(()), dma(()), dma(()), dma(()),
            dma((2, 3)), dma((2, 3)), dma((2, 3)), dma((2, 3)),
            dma((4,)), dma((3,)), dma((3,)),
        ],
        compiler_params=pltpu.CompilerParams(
            collective_id=3, has_side_effects=True, vmem_limit_bytes=56 * 1024 * 1024
        ),
        cost_estimate=pl.CostEstimate(
            flops=2 * total * width * local * 4 + 10 * heads * total * total * HD,
            bytes_accessed=24 * 1024 * 1024,
            transcendentals=0,
        ),
    )(
        dat, ghid, cos.reshape(4, shard, HD), sin.reshape(4, shard, HD), gq.reshape(1, -1), gk.reshape(1, -1), inv,
        wq, wk, wv, wo, qh, kh, qr, kr, v, p, mix, wgt, wut, gh, gd,
    )


def place_kernel(
    a_ref, p_ref, m_ref, n_ref, q_ref, k_ref, v_ref, o_ref, g_ref, u_ref, d_ref, gq_ref, gk_ref, ga_ref, gm_ref,
    a_v, p_v, m_v, head_v, o_v, gu_v, d_v, in_sem, out_sem,
):
    f32 = jnp.float32
    n = a_v.shape[2]
    f = m_v.shape[2]
    loads = [pltpu.make_async_copy(m_ref.at[w], m_v.at[w], in_sem.at[w]) for w in range(3)] + [
        pltpu.make_async_copy(p_ref, p_v, in_sem.at[3]),
        pltpu.make_async_copy(a_ref, a_v, in_sem.at[4]),
    ]
    for cp in loads:
        cp.start()
    stores = []

    def store(src, dst):
        cp = pltpu.make_async_copy(src, dst, out_sem.at[len(stores)])
        cp.start()
        stores.append(cp)

    local = gq_ref.shape[1]
    gq_ref[...] = n_ref[2:3, :local]
    gk_ref[...] = n_ref[3:4, :local]
    ga_ref[...] = n_ref[0:1, :]
    gm_ref[...] = n_ref[1:2, :]
    loads[0].wait()
    for i in range(2):
        d_v[i * f : (i + 1) * f, :] = m_v[0, i].astype(f32)
    store(d_v, d_ref)
    for w, ref in ((1, g_ref), (2, u_ref)):
        loads[w].wait()
        for i in range(2):
            gu_v[w - 1, :, i * f : (i + 1) * f] = m_v[w, i].T.astype(f32)
        store(gu_v.at[w - 1], ref)
    loads[3].wait()
    new = p_v[0].astype(f32)
    for i in range(1, 4):
        new = new + p_v[i].astype(f32)
    o_v[...] = new
    store(o_v, o_ref)
    loads[4].wait()
    for w, ref in ((0, v_ref), (1, q_ref), (2, k_ref)):
        for i in range(2):
            head_v[w, :, i * n : (i + 1) * n] = a_v[w, i].T.astype(f32)
        store(head_v.at[w], ref)
    for cp in stores:
        cp.wait()


def place_grads(attn, proj, mlp, gains):
    _, f, block = proj.shape
    width = gains.shape[1]
    f32 = jnp.float32
    vm = pl.BlockSpec(memory_space=pltpu.VMEM)
    shape = jax.ShapeDtypeStruct
    return pl.pallas_call(
        place_kernel,
        name="place_grads",
        out_shape=(
            shape((block, f), f32),
            shape((block, f), f32),
            shape((block, f), f32),
            shape((f, block), f32),
            shape((block, 4 * f), f32),
            shape((block, 4 * f), f32),
            shape((4 * f, block), f32),
            shape((1, f), f32),
            shape((1, f), f32),
            shape((1, width), f32),
            shape((1, width), f32),
        ),
        in_specs=[FULL] * 3 + [vm],
        out_specs=(FULL,) * 7 + (vm,) * 4,
        scratch_shapes=[
            pltpu.VMEM(attn.shape, attn.dtype),
            pltpu.VMEM(proj.shape, proj.dtype),
            pltpu.VMEM(mlp.shape, mlp.dtype),
            pltpu.VMEM((3, block, f), f32),
            pltpu.VMEM((f, block), f32),
            pltpu.VMEM((2, block, 4 * f), f32),
            pltpu.VMEM((4 * f, block), f32),
            pltpu.SemaphoreType.DMA((5,)),
            pltpu.SemaphoreType.DMA((7,)),
        ],
        compiler_params=pltpu.CompilerParams(vmem_limit_bytes=60 * 1024 * 1024),
    )(attn, proj, mlp, gains)


def plain_body(
    tokens,
    lengths,
    w_query,
    w_key,
    w_value,
    w_out,
    w_gate,
    w_up,
    w_down,
    gain_query,
    gain_key,
    gain_attn,
    gain_mlp,
    cotangent,
):
    rows_dev = lengths.shape[0]
    model_width = w_query.shape[0]
    local_width = w_query.shape[1]
    head_count = local_width // HD
    gathered = lax.all_gather(tokens, "tensor", axis=0, tiled=True)
    row_count = gathered.shape[0]
    segment, offsets = jax.vmap(row_layout)(lengths)
    queries = jnp.dot(gathered, w_query, preferred_element_type=jnp.float32)
    keys_raw = jnp.dot(gathered, w_key, preferred_element_type=jnp.float32)
    values_low = jnp.dot(gathered, w_value, preferred_element_type=jnp.float32).astype(jnp.bfloat16)
    q_total, k_total = lax.psum(
        (jnp.sum(queries * queries, axis=1), jnp.sum(keys_raw * keys_raw, axis=1)), "tensor"
    )
    q_inv = lax.rsqrt(q_total / model_width + EPS)[:, None]
    k_inv = lax.rsqrt(k_total / model_width + EPS)[:, None]
    q_unit = queries * q_inv
    k_unit = keys_raw * k_inv

    def to_heads(values):
        return values.reshape(rows_dev, ROW_LEN, head_count, HD)

    queries_low = rotate(to_heads(q_unit * gain_query), offsets, 1.0).astype(jnp.bfloat16)
    keys_low = rotate(to_heads(k_unit * gain_key), offsets, 1.0).astype(jnp.bfloat16)
    values_heads = to_heads(values_low)
    mixed_heads, log_total = jax.vmap(lambda *a: attend(a))(
        queries_low, keys_low, values_heads, segment
    )
    mixed_low = mixed_heads.reshape(row_count, local_width)
    attn_out = lax.psum_scatter(
        jnp.dot(mixed_low, w_out, preferred_element_type=jnp.float32).astype(jnp.bfloat16),
        "tensor",
        scatter_dimension=0,
        tiled=True,
    ).astype(jnp.float32)
    inner_count = lax.axis_size("dp") // OUTER
    a_inv = lax.rsqrt(jnp.mean(attn_out * attn_out, axis=1, keepdims=True) + EPS)
    a_unit = attn_out * a_inv
    hidden = tokens.astype(jnp.float32) + a_unit * gain_attn
    hidden_low = hidden.astype(jnp.bfloat16)
    hidden_all = lax.all_gather(hidden_low, "tensor", axis=0, tiled=True)
    outer_index = lax.axis_index("dp") // inner_count

    def gather_group(shard):
        groups = [[z * inner_count + i for z in range(OUTER)] for i in range(inner_count)]
        part = lax.all_gather(shard, "dp", axis=0, tiled=True, axis_index_groups=groups)
        return lax.all_gather(part, "tensor", axis=0, tiled=True)

    hidden_group = gather_group(hidden_low)
    gate_acts = jnp.dot(hidden_all, w_gate, preferred_element_type=jnp.float32)
    up_acts = jnp.dot(hidden_all, w_up, preferred_element_type=jnp.float32)
    gate_sigmoid = jax.nn.sigmoid(gate_acts)
    inner_low = (gate_acts * gate_sigmoid * up_acts).astype(jnp.bfloat16)
    mlp_out = lax.psum_scatter(
        jnp.dot(inner_low, w_down, preferred_element_type=jnp.float32).astype(jnp.bfloat16),
        "tensor",
        scatter_dimension=0,
        tiled=True,
    ).astype(jnp.float32)
    f_inv = lax.rsqrt(jnp.mean(mlp_out * mlp_out, axis=1, keepdims=True) + EPS)
    f_unit = mlp_out * f_inv
    output = (hidden + f_unit * gain_mlp).astype(jnp.bfloat16)
    grad_output = cotangent.astype(jnp.float32)
    grad_mlp, grad_gain_mlp_part = post_norm_back(grad_output, f_unit, f_inv, gain_mlp)
    grad_mlp_low = grad_mlp.astype(jnp.bfloat16)
    mlp_grad_all = lax.all_gather(grad_mlp_low, "tensor", axis=0, tiled=True)
    mlp_grad_group = gather_group(grad_mlp_low)
    grad_inner = times_t(mlp_grad_all, w_down)
    grad_gate_low = (
        grad_inner * up_acts * gate_sigmoid * (1.0 + gate_acts * (1.0 - gate_sigmoid))
    ).astype(jnp.bfloat16)
    grad_up_low = (grad_inner * gate_acts * gate_sigmoid).astype(jnp.bfloat16)
    part_width = w_gate.shape[1] // OUTER
    gate_part = lax.dynamic_slice_in_dim(w_gate, outer_index * part_width, part_width, 1)
    up_part = lax.dynamic_slice_in_dim(w_up, outer_index * part_width, part_width, 1)
    down_part = lax.dynamic_slice_in_dim(w_down, outer_index * part_width, part_width, 0)
    gate_g = jnp.dot(hidden_group, gate_part, preferred_element_type=jnp.float32)
    up_g = jnp.dot(hidden_group, up_part, preferred_element_type=jnp.float32)
    sig_g = jax.nn.sigmoid(gate_g)
    inner_g = (gate_g * sig_g * up_g).astype(jnp.bfloat16)
    grad_inner_g = times_t(mlp_grad_group, down_part)
    grad_gate_g = (grad_inner_g * up_g * sig_g * (1.0 + gate_g * (1.0 - sig_g))).astype(
        jnp.bfloat16
    )
    grad_up_g = (grad_inner_g * gate_g * sig_g).astype(jnp.bfloat16)
    sum_down = scatter_join(split_cols(t_times(inner_g, mlp_grad_group), inner_count), inner_count, 0)
    sum_gate = scatter_join(split_rows(t_times(hidden_group, grad_gate_g), inner_count), inner_count, 1)
    sum_up = scatter_join(split_rows(t_times(hidden_group, grad_up_g), inner_count), inner_count, 1)
    grad_hidden = grad_output + lax.psum_scatter(
        (times_t(grad_gate_low, w_gate) + times_t(grad_up_low, w_up)).astype(jnp.bfloat16),
        "tensor",
        scatter_dimension=0,
        tiled=True,
    ).astype(jnp.float32)
    grad_attn, grad_gain_attn_part = post_norm_back(grad_hidden, a_unit, a_inv, gain_attn)
    grad_attn_low = grad_attn.astype(jnp.bfloat16)
    attn_grad_all = lax.all_gather(grad_attn_low, "tensor", axis=0, tiled=True)
    grad_mixed = times_t(attn_grad_all, w_out).astype(jnp.bfloat16)
    grad_q_rot, grad_k_rot, grad_values_low = jax.vmap(lambda *a: attend_back(a))(
        queries_low, keys_low, values_heads, segment, log_total, to_heads(grad_mixed)
    )
    grad_q_norm = rotate(grad_q_rot, offsets, -1.0).reshape(row_count, local_width)
    grad_k_norm = rotate(grad_k_rot, offsets, -1.0).reshape(row_count, local_width)
    grad_gain_query_part = jnp.sum(grad_q_norm * q_unit, axis=0)
    grad_gain_key_part = jnp.sum(grad_k_norm * k_unit, axis=0)
    q_scaled = grad_q_norm * gain_query
    k_scaled = grad_k_norm * gain_key
    q_dots, k_dots = lax.psum(
        (jnp.sum(q_scaled * q_unit, axis=1), jnp.sum(k_scaled * k_unit, axis=1)), "tensor"
    )
    grad_queries_low = (q_inv * (q_scaled - q_unit * (q_dots / model_width)[:, None])).astype(
        jnp.bfloat16
    )
    grad_keys_low = (k_inv * (k_scaled - k_unit * (k_dots / model_width)[:, None])).astype(
        jnp.bfloat16
    )
    grad_values_flat = grad_values_low.reshape(row_count, local_width)
    grad_tokens = (
        grad_hidden
        + lax.psum_scatter(
            (
                times_t(grad_queries_low, w_query)
                + times_t(grad_keys_low, w_key)
                + times_t(grad_values_flat, w_value)
            ).astype(jnp.bfloat16),
            "tensor",
            scatter_dimension=0,
            tiled=True,
        ).astype(jnp.float32)
    ).astype(jnp.bfloat16)
    tensor_start = lax.axis_index("tensor") * local_width
    zero_row = jnp.zeros((model_width,), jnp.float32)
    q_full = lax.dynamic_update_slice(zero_row, grad_gain_query_part, (tensor_start,))
    k_full = lax.dynamic_update_slice(zero_row, grad_gain_key_part, (tensor_start,))
    gain_stack = jnp.stack([q_full, k_full, grad_gain_attn_part, grad_gain_mlp_part])
    gain_total = lax.psum(gain_stack, ("dp", "tensor"))
    grad_gain_query = lax.dynamic_slice(gain_total[0], (tensor_start,), (local_width,))
    grad_gain_key = lax.dynamic_slice(gain_total[1], (tensor_start,), (local_width,))
    summed = (
        scatter_sum(split_rows(t_times(gathered, grad_queries_low), inner_count), inner_count),
        scatter_sum(split_rows(t_times(gathered, grad_keys_low), inner_count), inner_count),
        scatter_sum(split_rows(t_times(gathered, grad_values_flat), inner_count), inner_count),
        scatter_sum(split_cols(t_times(mixed_low, attn_grad_all), inner_count), inner_count),
        sum_gate,
        sum_up,
        sum_down,
    )
    return (
        output,
        grad_tokens,
        summed[0],
        summed[1],
        summed[2],
        summed[3],
        summed[4],
        summed[5],
        summed[6],
        grad_gain_query,
        grad_gain_key,
        gain_total[2],
        gain_total[3],
    )


def fused_body(
    tokens,
    lengths,
    w_query,
    w_key,
    w_value,
    w_out,
    w_gate,
    w_up,
    w_down,
    gain_query,
    gain_key,
    gain_attn,
    gain_mlp,
    cotangent,
):
    (
        attn_out, tokens_all, tokens_next, q_unit, k_unit, q_rot, k_rot, values, mixed, weights, inverse,
        cosines, sines, gate_t, up_t,
    ) = attend_both(
        lengths, tokens, gain_query, gain_key, w_query, w_key, w_value, w_out, w_gate, w_up
    )
    output, grad_hidden, grad_attn, gain_parts, group_h, group_d = mlp_both(
        attn_out, tokens, cotangent, gain_attn, gain_mlp, w_gate, w_up, w_down
    )
    grad_tokens, head_gains, grad_q, grad_k, grad_v, proj, made, group_h, group_d = attend_back_both(
        grad_attn, grad_hidden, cosines, sines, gain_query, gain_key, inverse,
        w_query, w_key, w_value, w_out, q_unit, k_unit, q_rot, k_rot, values, weights, mixed, gate_t, up_t,
        group_h, group_d,
    )
    gains, attn_blocks, proj_blocks, mlp_blocks, _, _ = weight_grads(
        gain_parts, head_gains, group_h, group_d, made, gate_t, up_t, w_down, tokens_all, tokens_next, grad_q, grad_k, grad_v, proj,
    )
    placed = place_grads(attn_blocks, proj_blocks, mlp_blocks, gains)
    return (
        output,
        grad_tokens,
        *placed[:7],
        *(g.reshape(-1) for g in placed[7:]),
    )


def solution(mesh):
    placed = (
        P(("dp", "tensor"), None),
        P("dp", None),
        P(None, "tensor"),
        P(None, "tensor"),
        P(None, "tensor"),
        P("tensor", None),
        P(None, "tensor"),
        P(None, "tensor"),
        P("tensor", None),
        P("tensor"),
        P("tensor"),
        P(),
        P(),
        P(("dp", "tensor"), None),
    )
    return jax.shard_map(
        fused_body if tuple(mesh.shape.values()) == (8, 4) else plain_body,
        mesh=mesh,
        in_specs=placed,
        out_specs=(
            P(("dp", "tensor"), None),
            P(("dp", "tensor"), None),
            P("dp", "tensor"),
            P("dp", "tensor"),
            P("dp", "tensor"),
            P("tensor", "dp"),
            P("dp", "tensor"),
            P("dp", "tensor"),
            P("tensor", "dp"),
            P("tensor"),
            P("tensor"),
            P(),
            P(),
        ),
        check_vma=False,
    )
```

```python
import math

import jax
import jax.numpy as jnp
from jax import lax
from jax.experimental import pallas as pl
from jax.experimental.pallas import tpu as pltpu
from jax.sharding import PartitionSpec as P

HD = 128
ROW_LEN = 512


EPS = 1e-06
THETA = 500000.0


def rotate(values, offsets, rot_sign):
    half_width = values.shape[-1] // 2
    frequency = jnp.exp(
        jnp.arange(half_width, dtype=jnp.float32) * (-2.0 * math.log(THETA) / values.shape[-1])
    )
    angles = offsets.astype(jnp.float32)[..., None, None] * frequency
    cosines = jnp.cos(angles)
    sine_part = rot_sign * jnp.sin(angles)
    first_half = values[..., :half_width]
    second_half = values[..., half_width:]
    return jnp.concatenate(
        [
            first_half * cosines - second_half * sine_part,
            second_half * cosines + first_half * sine_part,
        ],
        axis=-1,
    )


def row_layout(lengths_row):
    slots = jnp.arange(lengths_row.shape[0], dtype=jnp.int32)
    seq_ends = jnp.sum(
        jnp.where(slots[None, :] <= slots[:, None], lengths_row[None, :], 0), axis=1
    )
    position = jnp.arange(ROW_LEN, dtype=jnp.int32)
    passed = (position[:, None] >= seq_ends[None, :]).astype(jnp.int32)
    segment = jnp.sum(passed, axis=1)
    seq_start = jnp.sum(passed * lengths_row[None, :], axis=1)
    return (segment, position - seq_start)


def allowed_mask(segment):
    position = jnp.arange(segment.shape[0], dtype=jnp.int32)
    return (segment[:, None] == segment[None, :]) & (position[None, :] <= position[:, None])


def times_t(left_mat, right_mat):
    return lax.dot_general(
        left_mat, right_mat, (((1,), (1,)), ((), ())), preferred_element_type=jnp.float32
    )


def t_times(left_mat, right_mat):
    return lax.dot_general(
        left_mat, right_mat, (((0,), (0,)), ((), ())), preferred_element_type=jnp.float32
    )


def masked_scores(queries_low, keys_low, segment):
    scale_factor = 1.0 / math.sqrt(queries_low.shape[-1])
    scores = (
        jnp.einsum("qhd,khd->hqk", queries_low, keys_low, preferred_element_type=jnp.float32)
        * scale_factor
    )
    return jnp.where(allowed_mask(segment)[None], scores, -1e30)


def attend(block_item):
    queries_low, keys_low, values_low, segment = block_item
    scores = masked_scores(queries_low, keys_low, segment)
    row_max = jnp.max(scores, axis=-1, keepdims=True)
    shifted = jnp.exp(scores - row_max)
    row_total = jnp.sum(shifted, axis=-1, keepdims=True)
    attn_weights = (shifted / row_total).astype(jnp.bfloat16)
    mixed = jnp.einsum("hqk,khd->qhd", attn_weights, values_low, preferred_element_type=jnp.float32)
    return (mixed.astype(jnp.bfloat16), (row_max + jnp.log(row_total))[..., 0])


def attend_back(block_item):
    queries_low, keys_low, values_low, segment, log_total, grad_mixed = block_item
    scale_factor = 1.0 / math.sqrt(queries_low.shape[-1])
    scores = masked_scores(queries_low, keys_low, segment)
    attn_weights = jnp.exp(scores - log_total[..., None])
    grad_weights = jnp.einsum(
        "qhd,khd->hqk", grad_mixed, values_low, preferred_element_type=jnp.float32
    )
    row_dots = jnp.sum(attn_weights * grad_weights, axis=-1, keepdims=True)
    grad_scores = (attn_weights * (grad_weights - row_dots)).astype(jnp.bfloat16)
    grad_queries = scale_factor * jnp.einsum(
        "hqk,khd->qhd", grad_scores, keys_low, preferred_element_type=jnp.float32
    )
    grad_keys = scale_factor * jnp.einsum(
        "hqk,qhd->khd", grad_scores, queries_low, preferred_element_type=jnp.float32
    )
    grad_values = jnp.einsum(
        "hqk,qhd->khd",
        attn_weights.astype(jnp.bfloat16),
        grad_mixed,
        preferred_element_type=jnp.float32,
    )
    return (grad_queries, grad_keys, grad_values.astype(jnp.bfloat16))


def post_norm_back(grad_in, unit_rows, inv_scale, gain_vec):
    scaled = grad_in * gain_vec
    mean_dots = jnp.mean(scaled * unit_rows, axis=-1, keepdims=True)
    return (inv_scale * (scaled - unit_rows * mean_dots), jnp.sum(grad_in * unit_rows, axis=0))


OUTER = 4


def swap(value, shift):
    size = lax.axis_size("dp")
    return lax.ppermute(value, "dp", [(d, d ^ shift) for d in range(size)])


def pick(parts, index):
    return lax.dynamic_index_in_dim(parts, index, 0, keepdims=False)


def sum_inner(parts):
    inner = parts.shape[0]
    mine = lax.axis_index("dp") % inner
    total = pick(parts, mine)
    for k in range(1, inner):
        sent = pick(parts, mine ^ k).astype(jnp.bfloat16)
        total = total + swap(sent, k).astype(jnp.float32)
    return total


def trade_outer(parts, inner):
    mine = lax.axis_index("dp") // inner
    got = [(mine, pick(parts, mine))]
    for k in range(1, OUTER):
        got.append((mine ^ k, swap(pick(parts, mine ^ k), k * inner)))
    return got


def split_rows(grad, inner):
    cols = grad.shape[1]
    return grad.reshape(OUTER, inner, -1, cols).transpose(1, 0, 2, 3)


def split_cols(grad, inner):
    rows = grad.shape[0]
    return grad.reshape(rows, OUTER, inner, -1).transpose(2, 1, 0, 3)


def scatter_sum(parts, inner):
    half = sum_inner(parts).astype(jnp.bfloat16)
    got = trade_outer(half, inner)
    return sum(g.astype(jnp.float32) for _, g in got)


def scatter_join(parts, inner, axis):
    half = sum_inner(parts).astype(jnp.bfloat16)
    got = trade_outer(half, inner)
    stack = jnp.zeros((OUTER, *got[0][1].shape), jnp.bfloat16)
    for place, block in got:
        stack = lax.dynamic_update_index_in_dim(stack, block, place, 0)
    joined = jnp.concatenate([stack[z] for z in range(OUTER)], axis=axis)
    return joined.astype(jnp.float32)


MESH = pl.DeviceIdType.MESH
FULL = pl.BlockSpec(memory_space=pl.ANY)


def grads_kernel(
    gp_ref, gqk_ref, gh_in, gm_in, lhs_ref, wgt_ref, wut_ref, wd_ref, tok_ref, nxt_ref, dq_ref, dk_ref, dv_ref, po_ref,
    gain_ref, attn_ref, proj_ref, mlp_ref, gh_ref, gm_ref,
    hb_v, tip_v, dm_v, wd_v, lhs_in, lhs_q, lhs_t, quad, quad_in, pair, full, part, gbuf, gin,
    ld_sem, xs_s, xs_r, cs_s, cs_r, qs_s, qs_r, os_s, os_r, qz_s, qz_r, qy_s, qy_r, ys_s, ys_r, ts_s, ts_r, own_s, gs_s, gs_r, lhs_sem, pc_sem, hb_sem,
):
    d = lax.axis_index("dp")
    t = lax.axis_index("tensor")
    z = d // 2
    y = d % 2
    side = z % 2
    top = z // 2
    mate = t + 1 - 2 * (t % 2)
    across = (t + 2) % 4
    twin = z * 2 + 1 - y
    pal = (z + 1 - 2 * side) * 2 + y
    bf = jnp.bfloat16
    f32 = jnp.float32
    f = lhs_t.shape[1]
    width = hb_v.shape[3]
    shard = hb_v.shape[2]
    span = width // 2
    hc = lhs_in.shape[4]
    total = 4 * shard

    def peer(k):
        return ((z + k) % 4) * 2 + y

    heads = (dv_ref, dq_ref, dk_ref)
    parts = (top, 1 - top)
    ranks = rank_rows(z)
    slow = [
        pltpu.make_async_copy(
            wd_ref.at[pl.ds(side * f, f), pl.ds(parts[i] * span, span)], wd_v.at[i], ld_sem.at[4 + i]
        )
        for i in range(2)
    ] + [
        pltpu.make_async_copy(r.at[:, :, pl.ds(y * hc, hc)], lhs_in.at[w, 0], ld_sem.at[6 + w])
        for w, r in enumerate(heads)
    ]
    toks = [
        pltpu.make_async_copy(r, hb_v.at[i], ld_sem.at[i]) for i, r in enumerate((tok_ref, nxt_ref))
    ]

    def lhs_load(n, w):
        return pltpu.make_async_copy(
            lhs_ref.at[n, w], lhs_t.at[w, :, pl.ds(n * total, total)], lhs_sem.at[n, w]
        )

    def dm_load(n, i):
        return pltpu.make_async_copy(
            gm_ref.at[ranks[n], :, :, pl.ds(parts[i] * span, span)], dm_v.at[n, i], ld_sem.at[9 + n * 2 + i]
        )

    def hb_load(n):
        return [
            pltpu.make_async_copy(
                gh_ref.at[ranks[n], :, :, pl.ds(i * span, span)], dm_v.at[n, i], hb_sem.at[n - 2, i]
            )
            for i in range(2)
        ]

    tips = [
        pltpu.make_async_copy(r, tip_v.at[i], ld_sem.at[21 + i]) for i, r in enumerate((wgt_ref, wut_ref))
    ]
    for cp in hb_load(2) + tips + hb_load(3) + slow[2:] + toks:
        cp.start()
    for w in range(3):
        for n in range(2):
            lhs_load(n, w).start()
    for cp in [dm_load(0, 0), dm_load(0, 1)] + slow[:2]:
        cp.start()

    greet([(peer(1), t), (peer(2), t), (peer(3), t), (twin, t), (d, mate), (d, across)])

    groups = (gh_ref, gm_ref)

    def head_swap(w):
        return far_copy(
            heads[w].at[:, :, pl.ds((1 - y) * hc, hc)], lhs_in.at[w, 1], qs_s.at[w], qs_r.at[w], twin, t
        )

    block = quad.shape[4]

    def proj_trade(k):
        return far_copy(po_ref.at[(z + k) % 4], proj_ref.at[z], os_s.at[k - 1], os_r.at[k - 1], peer(k), t)

    keep_proj = pltpu.make_async_copy(po_ref.at[z], proj_ref.at[z], own_s.at[0])
    keep_proj.start()

    def piece(i):
        if i >= 12:
            return i - 11, pl.ds(parts[1] * span, span), pl.ds(0, span)
        spot = ((i // 3) % 2) * 2 + (1 - y if i < 6 else y)
        return 1 + i % 3, pl.ds(top * span + spot * block, block), pl.ds(spot * block, block)

    def cell(i, q):
        n, cols, _ = piece(i)
        return gm_ref.at[ranks[n], q, :, cols]

    def piece_load(i):
        n, cols, spot = piece(i)
        return pltpu.make_async_copy(
            gm_ref.at[ranks[n], :, :, cols], dm_v.at[n, i // 12, :, :, spot], pc_sem.at[i]
        )

    def forward_x(i):
        return far_copy(cell(i, t), cell(i, t), xs_s.at[i], xs_r.at[i], d, across)

    def forward_c(i, h):
        q = t if h == 0 else across
        return far_copy(cell(i, q), cell(i, q), cs_s.at[i, h], cs_r.at[i, h], d, mate)

    def advance(i):
        forward_x(i).wait_recv()
        for h in range(2):
            forward_c(i, h).start()

    def arrive(i):
        for h in range(2):
            forward_c(i, h).wait_recv()

    def gain_copy(i):
        stage, who = ((0, (peer(1), t)), (0, (peer(2), t)), (0, (peer(3), t)), (1, (twin, t)), (2, (d, across)), (3, (d, mate)))[i]
        return far_copy(gbuf.at[stage], gin.at[i], gs_s.at[i], gs_r.at[i], *who)

    gbuf[0] = jnp.zeros_like(gbuf[0])
    gbuf[0, 0:2, :] = gp_ref[...]
    gbuf[0, 2:4, 0 : gqk_ref.shape[1]] = gqk_ref[...]
    for i in range(3):
        gain_copy(i).start()
    for w in range(3):
        head_swap(w).start()
    for k in (2, 1, 3):
        proj_trade(k).start()
    for i in range(15):
        forward_x(i).start()
    def gain_step(stage):
        new = gbuf[stage]
        for i in ((0, 1, 2), (3,), (4,), (5,))[stage]:
            gain_copy(i).wait_recv()
            new = new + gin[i]
        if stage < 3:
            gbuf[stage + 1] = new
            gain_copy(stage + 3).start()
        if stage == 1:
            gain_ref[2:4, :] = new[2:4, :]
        if stage == 3:
            gain_ref[0:2, :] = new[0:2, :]

    step = 512

    def remake(n):
        def wide(j, carry):
            cols = pl.ds(pl.multiple_of(j * step, step), step)
            hb = [dm_v[n, i].reshape(total, span) for i in range(2)]
            g, u = [
                lax.dot_general(tip_v[w, cols, :span], hb[0], NT, preferred_element_type=f32)
                + lax.dot_general(tip_v[w, cols, span:], hb[1], NT, preferred_element_type=f32)
                for w in range(2)
            ]
            sg = jax.nn.sigmoid(g)
            gs = g * sg
            spot = slice(n * total, (n + 1) * total)
            lhs_t[0, cols, spot] = (gs * u).astype(bf)
            lhs_t[1, cols, spot] = (u * sg * (1.0 + g * (1.0 - sg))).astype(bf)
            lhs_t[2, cols, spot] = gs.astype(bf)
            return carry

        lax.fori_loop(0, f // step, wide, 0)

    def scale_back(n):
        if n < 2:
            for w in (1, 2):
                lhs_load(n, w).wait()

        def wide(j, carry):
            cols = pl.ds(pl.multiple_of(j * step, step), step)
            di = None
            for i in range(2):
                one = lax.dot_general(
                    wd_v[i, cols, :], dm_v[n, i].reshape(total, span), NT, preferred_element_type=f32
                )
                di = one if di is None else di + one
            toks = slice(n * total, (n + 1) * total)
            for w in (1, 2):
                lhs_t[w, cols, toks] = (lhs_t[w, cols, toks].astype(f32) * di).astype(bf)
            return carry

        lax.fori_loop(0, f // step, wide, 0)

    def hb_half(n):
        return pltpu.make_async_copy(
            gh_ref.at[ranks[n], :, :, pl.ds(top * span, span)],
            hb_v.at[n // 2, :, :, pl.ds((n % 2) * span, span)],
            ld_sem.at[17 + n],
        )

    for cp in hb_load(2) + tips:
        cp.wait()
    remake(2)

    def quad_trade(w, k):
        return far_copy(quad.at[w, (z + k) % 4], quad_in.at[w, k - 1], qz_s.at[w, k - 1], qz_r.at[w, k - 1], peer(k), t)

    def head_grad(w):
        slow[2 + w].wait()
        head_swap(w).wait_recv()
        for i in range(2):
            lhs_q[:, i * total : (i + 1) * total] = lhs_in[w, i].reshape(total, hc).astype(f32).T.astype(bf)

        def tile(j, carry):
            cols = pl.ds(pl.multiple_of(j * block, block), block)
            quad[w, j // 2, j % 2] = jnp.dot(
                lhs_q[...], hb_v[:, :, :, cols].reshape(2 * total, block), preferred_element_type=f32
            ).astype(bf)
            return carry

        lax.fori_loop(0, 8, tile, 0)
        for k in (2, 1, 3):
            quad_trade(w, k).start()

    for cp in toks:
        cp.wait()
    head_grad(0)
    for cp in hb_load(3):
        cp.wait()
    remake(3)
    for i in range(6):
        advance(i)
    for i in range(6):
        arrive(i)
        piece_load(i).start()
    gain_step(0)

    def swap_y(w):
        return far_copy(full.at[w, :, 1 - y], part.at[w], ys_s.at[w], ys_r.at[w], twin, t)

    def trade_z(w):
        return far_copy(part.at[w, 1 - side], mlp_ref.at[w, side], ts_s.at[w], ts_r.at[w], pal, t)

    def keep(w):
        return pltpu.make_async_copy(part.at[w, side], mlp_ref.at[w, side], own_s.at[1 + w])

    def finish_y(w):
        swap_y(w).wait()
        for b in range(2):
            part[w, b] = (part[w, b].astype(f32) + full[w, b, y].astype(f32)).astype(bf)
        trade_z(w).start()
        keep(w).start()

    def emit(w, yy):
        for zz in range(2):
            off = (zz * 2 + yy) * block
            new = None
            for n in range(4):
                base = 0 if w == 0 else (n % 2) * span
                cols = pl.ds(pl.multiple_of(base + off, block), block)
                rows = dm_v[n, 0, :, :, cols] if w == 0 else hb_v[n // 2, :, :, cols]
                one = jnp.dot(
                    lhs_t[w, :, n * total : (n + 1) * total],
                    rows.reshape(total, block),
                    preferred_element_type=f32,
                )
                new = one if new is None else new + one
            full[w, zz, yy] = new.astype(bf)

    for n in range(2):
        lhs_load(n, 0).wait()
    dm_load(0, 0).wait()
    for i in range(6):
        piece_load(i).wait()
    emit(0, 1 - y)
    swap_y(0).start()
    head_grad(1)
    head_grad(2)
    for n in range(4):
        hb_half(n).start()
    for i in range(6, 12):
        advance(i)
    for i in range(6, 12):
        arrive(i)
        piece_load(i).start()
    gain_step(1)
    for i in range(6, 12):
        piece_load(i).wait()
    emit(0, y)
    for i in range(2):
        slow[i].wait()
    dm_load(0, 1).wait()
    scale_back(0)
    advance(12)
    advance(13)
    for i in (12, 13):
        arrive(i)
        piece_load(i).start()
    piece_load(12).wait()
    scale_back(1)
    advance(14)
    piece_load(13).wait()
    scale_back(2)
    arrive(14)
    piece_load(14).start()
    piece_load(14).wait()
    scale_back(3)
    gain_step(2)
    for n in range(4):
        hb_half(n).wait()
    for w in (1, 2):
        emit(w, 1 - y)
        swap_y(w).start()
    for w in (1, 2):
        emit(w, y)
    gain_step(3)

    def head_swap_back(w):
        return far_copy(pair.at[w, 1 - y], attn_ref.at[w, y], qy_s.at[w], qy_r.at[w], twin, t)

    def head_keep(w):
        return pltpu.make_async_copy(pair.at[w, y], attn_ref.at[w, y], own_s.at[4 + w])

    def finish_head(w):
        for k in range(1, 4):
            quad_trade(w, k).wait_recv()
        for b in range(2):
            new = quad[w, z, b].astype(f32)
            for i in range(3):
                new = new + quad_in[w, i, b].astype(f32)
            pair[w, b] = new.astype(bf)
        head_swap_back(w).start()
        head_keep(w).start()

    finish_y(0)
    finish_head(0)
    finish_y(1)
    finish_head(1)
    finish_y(2)
    finish_head(2)

    keep_proj.wait()
    for k in range(1, 4):
        proj_trade(k).wait()
    for i in range(6):
        gain_copy(i).wait_send()
    for i in range(15):
        forward_x(i).wait_send()
        for h in range(2):
            forward_c(i, h).wait_send()
    for w in range(3):
        head_swap(w).wait_send()
        for k in range(1, 4):
            quad_trade(w, k).wait_send()
        head_keep(w).wait()
        keep(w).wait()
        head_swap_back(w).wait()
        trade_z(w).wait()


def weight_grads(gp, gqk, gh, gd, lhs, wgt, wut, wd, tok, nxt, dq, dk, dv, po):
    shard, width = tok.shape[1], tok.shape[2]
    f = lhs.shape[2]
    local = dq.shape[2]
    block = width // 8
    bf = jnp.bfloat16
    f32 = jnp.float32
    dma = pltpu.SemaphoreType.DMA
    shape = jax.ShapeDtypeStruct
    vm = pl.BlockSpec(memory_space=pltpu.VMEM)
    flops = 2 * 4 * shard * 4 * f * (3 * width + 3 * width // 2)
    return pl.pallas_call(
        grads_kernel,
        name="weight_grads",
        input_output_aliases={2: 4, 3: 5},
        out_shape=(
            shape((4, width), f32),
            shape((3, 2, local // 2, block), bf),
            shape((4, local, block), bf),
            shape((3, 2, f, block), bf),
            shape(gh.shape, bf),
            shape(gd.shape, bf),
        ),
        in_specs=[vm] * 2 + [FULL] * 12,
        out_specs=(vm,) + (FULL,) * 5,
        scratch_shapes=[
            pltpu.VMEM((2, 4, shard, width), bf),
            pltpu.VMEM((2, f, width), bf),
            pltpu.VMEM((4, 2, 4, shard, width // 2), bf),
            pltpu.VMEM((2, f, width // 2), bf),
            pltpu.VMEM((3, 2, 4, shard, local // 2), bf),
            pltpu.VMEM((local // 2, 8 * shard), bf),
            pltpu.VMEM((3, f, 16 * shard), bf),
            pltpu.VMEM((3, 4, 2, local // 2, block), bf),
            pltpu.VMEM((3, 3, 2, local // 2, block), bf),
            pltpu.VMEM((3, 2, local // 2, block), bf),
            pltpu.VMEM((3, 2, 2, f, block), bf),
            pltpu.VMEM((3, 2, f, block), bf),
            pltpu.VMEM((4, 8, width), f32),
            pltpu.VMEM((6, 8, width), f32),
            dma((25,)),
            dma((15,)), dma((15,)), dma((15, 2)), dma((15, 2)),
            dma((3,)), dma((3,)), dma((3,)), dma((3,)),
            dma((3, 3)), dma((3, 3)), dma((3,)), dma((3,)),
            dma((3,)), dma((3,)), dma((3,)), dma((3,)),
            dma((7,)), dma((6,)), dma((6,)), dma((3, 3)), dma((15,)), dma((2, 2)),
        ],
        compiler_params=pltpu.CompilerParams(
            collective_id=0, has_side_effects=True, vmem_limit_bytes=60 * 1024 * 1024
        ),
        cost_estimate=pl.CostEstimate(flops=flops, bytes_accessed=60 * 1024 * 1024, transcendentals=0),
    )(gp, gqk, gh, gd, lhs, wgt, wut, wd, tok, nxt, dq, dk, dv, po)


def far_copy(src, dst, ss, rs, dd, tt):
    return pltpu.make_async_remote_copy(
        src_ref=src, dst_ref=dst, send_sem=ss, recv_sem=rs, device_id=(dd, tt), device_id_type=MESH
    )


def mean_inv(values):
    return lax.rsqrt(jnp.mean(values * values, axis=1, keepdims=True) + EPS)


def mlp_kernel(
    att_ref, tok_ref, cot_ref, ga_ref, gm_ref, wg_ref, wu_ref, wd_ref,
    out_ref, ghid_ref, dat_ref, gain_ref, gh_ref, gd_ref,
    wg_v, wu_v, wd_v, slope_g, slope_u, buf, low_a, low_b, part, pmate, xsend, xrecv, hid,
    w_sem, as_s, as_r, ax_s, ax_r, af_s, af_r, ps_s, ps_r, px_s, px_r, zs_s, zs_r, ds_s, ds_r, hc_s, hc_r, st_sem,
):
    d, t, z, y, c, chip, mate, across = places()
    shard, width = att_ref.shape
    ff = wg_v.shape[1]
    bf = jnp.bfloat16
    f32 = jnp.float32
    tile = 512
    tiles = ff // tile
    small = shard // 2
    two = 2 * shard
    half = width // 2

    def wcopy(i, j):
        cols = pl.ds(j * tile, tile)
        if i == 0:
            return pltpu.make_async_copy(wg_ref.at[:, cols], wg_v.at[:, cols], w_sem.at[0, j])
        if i == 1:
            return pltpu.make_async_copy(wu_ref.at[:, cols], wu_v.at[:, cols], w_sem.at[1, j])
        return pltpu.make_async_copy(wd_ref.at[cols, :], wd_v.at[cols, :], w_sem.at[2, j])

    for j in range(tiles):
        wcopy(0, j).start()
        wcopy(1, j).start()
    for j in range(tiles):
        wcopy(2, j).start()
    greet([(((z + 1) % 4) * 2 + y, t), (((z + 3) % 4) * 2 + y, t), (d, mate), (d, across)])

    def send_mate(p, b):
        return far_copy(buf.at[p, b, c], buf.at[p, b, c], as_s.at[p, b], as_r.at[p, b], d, mate)

    def send_across(p, b):
        return far_copy(buf.at[p, b, c], buf.at[p, b, 2 + c], ax_s.at[p, b], ax_r.at[p, b], d, across)

    def forward(p, b):
        return far_copy(buf.at[p, b, 2 + c], buf.at[p, b, 2 + c], af_s.at[p, b], af_r.at[p, b], d, mate)

    def part_mate(p, b, h):
        return far_copy(part.at[p, b, h, 1 - c], pmate.at[p, b, h], ps_s.at[p, b, h], ps_r.at[p, b, h], d, mate)

    def part_across(p, b, h):
        return far_copy(xsend.at[p, b, h], xrecv.at[p, b, h], px_s.at[p, b, h], px_r.at[p, b, h], d, across)

    groups = (gh_ref, gd_ref)
    lines_h = [Line(gh_ref, z, y, t, q, zs_s.at[i], zs_r.at[i]) for i, q in enumerate((t, across))]
    lines_d = [Line(gd_ref, z, y, t, t, ds_s, ds_r)]
    ranks = rank_rows(z)

    def line_src(p, i):
        return buf.at[p, :, c if i == 0 else 2 + c]

    def row_c(n, i):
        cell = gh_ref.at[ranks[1 + n], t if i == 0 else across]
        return far_copy(cell, cell, hc_s.at[n, i], hc_r.at[n, i], d, mate)

    def store_row(p):
        mine = groups[p].at[z]
        return [
            pltpu.make_async_copy(buf.at[p, :, i], mine.at[q], st_sem.at[p, i])
            for i, q in enumerate((chip * 2, chip * 2 + 1, 2 - chip * 2, 3 - chip * 2))
        ]

    def inner(p, b):
        rows = pl.ds(b * two, two)
        both = buf[p, b].reshape(two, width)
        for j in range(tiles):
            cols = pl.ds(j * tile, tile)
            if p == 0:
                if b == 0:
                    wcopy(0, j).wait()
                    wcopy(1, j).wait()
                g = jnp.dot(both, wg_v[:, cols], preferred_element_type=f32)
                u = jnp.dot(both, wu_v[:, cols], preferred_element_type=f32)
                sg = jax.nn.sigmoid(g)
                gs = g * sg
                low_a[:, cols] = (gs * u).astype(bf)
                slope_u[rows, cols] = gs
                slope_g[rows, cols] = u * sg * (1.0 + g * (1.0 - sg))
            else:
                di = lax.dot_general(both, wd_v[cols, :], NT, preferred_element_type=f32)
                low_a[:, cols] = (di * slope_g[rows, cols]).astype(bf)
                low_b[:, cols] = (di * slope_u[rows, cols]).astype(bf)

    def combine(p, b, h):
        part_mate(p, b, h).wait_recv()
        xsend[p, b, h] = (part[p, b, h, c, 1].astype(f32) + pmate[p, b, h, 1].astype(f32)).astype(bf)
        part_across(p, b, h).start()

    def outer(p, b):
        if p == 0 and b == 0:
            for j in range(tiles):
                wcopy(2, j).wait()
        for h in range(2):
            for j in range(half // tile):
                cols = pl.ds(h * half + j * tile, tile)
                if p == 0:
                    new = jnp.dot(low_a[...], wd_v[:, cols], preferred_element_type=f32)
                else:
                    new = lax.dot_general(
                        low_a[...], wg_v[cols, :], NT, preferred_element_type=f32
                    ) + lax.dot_general(low_b[...], wu_v[cols, :], NT, preferred_element_type=f32)
                new = new.astype(bf)
                for i in range(4):
                    part[p, b, h, i % 2, i // 2, :, pl.ds(j * tile, tile)] = new[i * small : (i + 1) * small]
            part_mate(p, b, h).start()
            if h == 1:
                combine(p, b, 0)
        combine(p, b, 1)

    def whole(p, b):
        sums = []
        for h in range(2):
            part_across(p, b, h).wait_recv()
            sums.append(
                part[p, b, h, c, 0].astype(f32) + pmate[p, b, h, 0].astype(f32) + xrecv[p, b, h].astype(f32)
            )
        return jnp.concatenate(sums, axis=1)

    def launch(p, b):
        send_across(p, b).start()
        send_mate(p, b).start()

    def arrive(p, b):
        send_mate(p, b).wait_recv()
        send_across(p, b).wait_recv()
        forward(p, b).start()
        forward(p, b).wait_recv()

    def rows_of(b):
        return slice(b * small, (b + 1) * small)

    def middle(b):
        r = rows_of(b)
        mlp = whole(0, b)
        rf = mean_inv(mlp)
        fh = mlp * rf
        gy = cot_ref[r, :].astype(f32)
        out_ref[r, :] = (hid[r, :] + fh * gm_ref[...]).astype(bf)
        scaled = gy * gm_ref[...]
        buf[1, b, c] = (rf * (scaled - fh * jnp.mean(scaled * fh, axis=1, keepdims=True))).astype(bf)
        launch(1, b)
        gain = jnp.sum(gy * fh, axis=0, keepdims=True)
        gain_ref[1:2, :] = gain if b == 0 else gain_ref[1:2, :] + gain

    def last(b):
        r = rows_of(b)
        gh = cot_ref[r, :].astype(f32) + whole(1, b)
        ghid_ref[r, :] = gh
        att = att_ref[r, :]
        ra = mean_inv(att)
        ah = att * ra
        gain = jnp.sum(gh * ah, axis=0, keepdims=True)
        gain_ref[0:1, :] = gain if b == 0 else gain_ref[0:1, :] + gain
        scaled = gh * ga_ref[...]
        dat_ref[r, :] = (ra * (scaled - ah * jnp.mean(scaled * ah, axis=1, keepdims=True))).astype(bf)

    for b in range(2):
        r = rows_of(b)
        att = att_ref[r, :]
        hid[r, :] = tok_ref[r, :].astype(f32) + att * mean_inv(att) * ga_ref[...]
        buf[0, b, c] = hid[r, :].astype(bf)
        launch(0, b)
    lines_h[0].start(0, line_src(0, 0))
    arrive(0, 0)
    inner(0, 0)
    outer(0, 0)
    arrive(0, 1)
    lines_h[1].start(0, line_src(0, 1))
    for cp in store_row(0):
        cp.start()
    inner(0, 1)
    middle(0)
    lines_h[0].landed(0)
    lines_h[0].start(1)
    outer(0, 1)
    arrive(1, 0)
    lines_h[1].landed(0)
    lines_h[1].start(1)
    for i in range(2):
        row_c(0, i).start()
    inner(1, 0)
    middle(1)
    lines_d[0].start(0, line_src(1, 0))
    outer(1, 0)
    arrive(1, 1)
    for cp in store_row(1):
        cp.start()
    inner(1, 1)
    outer(1, 1)
    for line in lines_h:
        line.landed(1)
    for i in range(2):
        row_c(1, i).start()
    last(0)
    last(1)

    for p in range(2):
        for b in range(2):
            send_across(p, b).wait_send()
            send_mate(p, b).wait_send()
            forward(p, b).wait_send()
            for h in range(2):
                part_mate(p, b, h).wait_send()
                part_across(p, b, h).wait_send()
        for cp in store_row(p):
            cp.wait()
        for i in range(2):
            row_c(p, i).wait()
    for i in range(2):
        lines_h[i].sent(0, line_src(0, i))
        lines_h[i].sent(1)
    lines_d[0].sent(0, line_src(1, 0))
    lines_d[0].landed(0)


def mlp_both(att, tok, cot, ga, gm, wg, wu, wd):
    shard, width = tok.shape
    ff = wg.shape[1]
    bf = jnp.bfloat16
    f32 = jnp.float32
    dma = pltpu.SemaphoreType.DMA
    half = width // 2
    small = shard // 2
    vm = pl.BlockSpec(memory_space=pltpu.VMEM)
    shape = jax.ShapeDtypeStruct
    out = pl.pallas_call(
        mlp_kernel,
        name="feed_forward",
        out_shape=(
            shape((shard, width), bf),
            shape((shard, width), f32),
            shape((shard, width), bf),
            shape((2, width), f32),
            shape((4, 4, 2, small, width), bf),
            shape((4, 4, 2, small, width), bf),
        ),
        in_specs=[vm] * 5 + [FULL] * 3,
        out_specs=(vm,) * 4 + (FULL,) * 2,
        scratch_shapes=[
            pltpu.VMEM((width, ff), bf),
            pltpu.VMEM((width, ff), bf),
            pltpu.VMEM((ff, width), bf),
            pltpu.VMEM((4 * shard, ff), f32),
            pltpu.VMEM((4 * shard, ff), f32),
            pltpu.VMEM((2, 2, 4, small, width), bf),
            pltpu.VMEM((2 * shard, ff), bf),
            pltpu.VMEM((2 * shard, ff), bf),
            pltpu.VMEM((2, 2, 2, 2, 2, small, half), bf),
            pltpu.VMEM((2, 2, 2, 2, small, half), bf),
            pltpu.VMEM((2, 2, 2, small, half), bf),
            pltpu.VMEM((2, 2, 2, small, half), bf),
            pltpu.VMEM((shard, width), f32),
            dma((3, ff // 512)),
            dma((2, 2)), dma((2, 2)), dma((2, 2)), dma((2, 2)), dma((2, 2)), dma((2, 2)),
            dma((2, 2, 2)), dma((2, 2, 2)), dma((2, 2, 2)), dma((2, 2, 2)),
            dma((2, 2, 2)), dma((2, 2, 2)), dma((2, 1)), dma((2, 1)),
            dma((2, 2)), dma((2, 2)),
            dma((2, 4)),
        ],
        compiler_params=pltpu.CompilerParams(
            collective_id=1, has_side_effects=True, vmem_limit_bytes=60 * 1024 * 1024
        ),
        cost_estimate=pl.CostEstimate(
            flops=2 * 6 * 4 * shard * width * ff, bytes_accessed=40 * 1024 * 1024, transcendentals=4 * shard * ff
        ),
    )(att, tok, cot, ga.reshape(1, -1), gm.reshape(1, -1), wg, wu, wd)
    return (*out[:4], out[4].reshape(4, 4, shard, width), out[5].reshape(4, 4, shard, width))


NT = (((1,), (1,)), ((), ()))
TN = (((0,), (0,)), ((), ()))


def places():
    d = lax.axis_index("dp")
    t = lax.axis_index("tensor")
    c = t % 2
    return d, t, d // 2, d % 2, c, t // 2, t + 1 - 2 * c, (t + 2) % 4


def greet(targets):
    barrier = pltpu.get_barrier_semaphore()
    for dd, tt in targets:
        pl.semaphore_signal(barrier, inc=1, device_id=(dd, tt), device_id_type=MESH)
    pl.semaphore_wait(barrier, len(targets))


def to_rows(column):
    n = column.shape[0]
    return jnp.broadcast_to(column, (n, n)).T[0:8, :]


def to_column(rows):
    n = rows.shape[1]
    return jnp.broadcast_to(rows[0:1, :], (n, n)).T[:, 0:1]


def attend_kernel(
    len_ref, tok_ref, gq_ref, gk_ref, wq_ref, wk_ref, wv_ref, wo_ref, wg_ref, wu_ref,
    att_ref, tall_ref, tnext_ref, qh_ref, kh_ref, qr_ref, kr_ref, v_ref, mix_ref, p_ref, inv_ref, cos_ref, sin_ref, wgt_ref, wut_ref,
    w_v, wo_v, wide, tipped, tall, raw, rot, val, mixed, prob, stat, stat_in, pown, pmate, xsend, xrecv, qown, qmate,
    w_sem, as_s, as_r, ss_s, ss_r, ps_s, ps_r, px_s, px_r, pq_s, pq_r, st_sem, ns_s, ns_r, tw_sem,
):
    d, t, z, y, c, chip, mate, across = places()
    far = (mate + 2) % 4
    shard, width = tok_ref.shape
    local = w_v.shape[2]
    bf = jnp.bfloat16
    f32 = jnp.float32
    heads = local // HD
    weights = [
        pltpu.make_async_copy(r, w_v.at[i], w_sem.at[i]) for i, r in enumerate((wq_ref, wk_ref, wv_ref))
    ] + [pltpu.make_async_copy(wo_ref, wo_v, w_sem.at[3])]
    for cp in weights:
        cp.start()
    span = wide.shape[2]
    side = z % 2
    tips = [
        pltpu.make_async_copy(r.at[:, pl.ds(side * span, span)], wide.at[i], tw_sem.at[i])
        for i, r in enumerate((wg_ref, wu_ref))
    ]
    for cp in tips:
        cp.start()
    drops = [
        pltpu.make_async_copy(tipped.at[i], r, tw_sem.at[2 + i]) for i, r in enumerate((wgt_ref, wut_ref))
    ]

    def tip(i):
        tips[i].wait()

        def one(j, carry):
            cols = pl.ds(pl.multiple_of(j * 128, 128), 128)
            tipped[i, cols, :] = wide[i, :, cols].T
            return carry

        lax.fori_loop(0, span // 128, one, 0)
        drops[i].start()

    tall[t] = tok_ref[...]
    twin = z * 2 + 1 - y
    greet([(d, mate), (d, across), (d, far), (twin, t)])

    send_x = far_copy(tall.at[t], tall.at[t], as_s.at[0], as_r.at[0], d, across)
    send_m = far_copy(tall.at[t], tall.at[t], as_s.at[1], as_r.at[1], d, mate)
    forward = far_copy(tall.at[across], tall.at[across], as_s.at[2], as_r.at[2], d, mate)
    send_x.start()
    send_m.start()
    next_y = [
        far_copy(tall.at[q], tnext_ref.at[q], ns_s.at[i], ns_r.at[i], twin, t) for i, q in enumerate((t, across))
    ]
    next_c = [
        far_copy(tnext_ref.at[q], tnext_ref.at[q], ns_s.at[2 + i], ns_r.at[2 + i], d, mate)
        for i, q in enumerate((t, across))
    ]
    next_y[0].start()

    total = 4 * shard

    def layout(shape, dim):
        spot = lax.broadcasted_iota(jnp.int32, shape, dim)
        end = 0
        seg = jnp.zeros(shape, jnp.int32)
        start = jnp.zeros(shape, jnp.int32)
        for i in range(len_ref.shape[1]):
            size = len_ref[0, i]
            end = end + size
            past = spot >= end
            seg = seg + jnp.where(past, 1, 0)
            start = start + jnp.where(past, size, 0)
        return seg, spot - start

    def tables():
        lane = lax.broadcasted_iota(jnp.int32, (total, HD), 1)
        near = lane < HD // 2
        freq = jnp.exp(jnp.where(near, lane, lane - HD // 2).astype(f32) * (-2.0 * math.log(THETA) / HD))
        angle = layout((total, HD), 0)[1].astype(f32) * freq
        cos_ref[...] = jnp.cos(angle).reshape(4, shard, HD)
        sines = jnp.sin(angle)
        sin_ref[...] = jnp.where(near, -sines, sines).reshape(4, shard, HD)

    def project(first):
        rows = tall[pl.ds(first, 2)].reshape(2 * shard, width)
        for i in range(3):
            new = jnp.dot(rows, w_v[i], preferred_element_type=f32).reshape(2, shard, local)
            if i == 2:
                val[pl.ds(first, 2)] = new.astype(bf)
            else:
                raw[i, pl.ds(first, 2)] = new
                for s in range(2):
                    stat[first + s, i * 8 : i * 8 + 8, :] = to_rows(
                        jnp.sum(new[s] * new[s], axis=1, keepdims=True)
                    )

    here = chip * 2
    there = 2 - chip * 2
    for cp in weights[:3]:
        cp.wait()
    send_m.wait_recv()
    project(here)
    tables()
    tip(0)
    send_x.wait_recv()
    forward.start()
    next_y[1].start()
    forward.wait_recv()
    project(there)

    stats = [
        far_copy(stat, stat_in.at[i], ss_s.at[i], ss_r.at[i], d, who)
        for i, who in enumerate((mate, across, far))
    ]
    for cp in stats:
        cp.start()
    stores = [
        pltpu.make_async_copy(tall, tall_ref, st_sem.at[0]),
        pltpu.make_async_copy(val, v_ref, st_sem.at[1]),
    ]
    for cp in stores:
        cp.start()
    for cp in stats:
        cp.wait_recv()

    for q in range(4):
        inv = lax.rsqrt((stat[q] + stat_in[0, q] + stat_in[1, q] + stat_in[2, q]) / width + EPS)
        inv_ref[q] = inv
        for i, gain in ((0, gq_ref), (1, gk_ref)):
            unit = raw[i, q] * to_column(inv[i * 8 : i * 8 + 8])
            raw[i, q] = unit
            unit = unit * gain[...]
            for h in range(heads):
                cols = slice(h * HD, (h + 1) * HD)
                one = unit[:, cols]
                rot[i, q, :, cols] = (
                    one * cos_ref[q] + pltpu.roll(one, HD // 2, 1) * sin_ref[q]
                ).astype(bf)
    more = [
        pltpu.make_async_copy(raw.at[0], qh_ref, st_sem.at[2]),
        pltpu.make_async_copy(raw.at[1], kh_ref, st_sem.at[3]),
        pltpu.make_async_copy(rot.at[0], qr_ref, st_sem.at[4]),
        pltpu.make_async_copy(rot.at[1], kr_ref, st_sem.at[5]),
    ]
    for cp in more:
        cp.start()
    stores += more

    scale = 1.0 / math.sqrt(HD)
    def mix(first, n):
        ids = first * shard + lax.broadcasted_iota(jnp.int32, (2 * shard, total), 0)
        keys = lax.broadcasted_iota(jnp.int32, (2 * shard, total), 1)
        rows = first * shard + lax.broadcasted_iota(jnp.int32, (2 * shard, 1), 0)
        seg_rows = jnp.zeros((2 * shard, 1), jnp.int32)
        end = 0
        for i in range(len_ref.shape[1]):
            end = end + len_ref[0, i]
            seg_rows = seg_rows + jnp.where(rows >= end, 1, 0)
        same = seg_rows == layout((1, total), 1)[0]
        ok = same & (keys <= ids)
        for h in range(heads):
            cols = slice(h * HD, (h + 1) * HD)
            s = lax.dot_general(
                rot[0, pl.ds(first, 2), :, cols].reshape(2 * shard, HD),
                rot[1, :, :, cols].reshape(total, HD),
                NT,
                preferred_element_type=f32,
            )
            s = jnp.where(ok, s * scale, -1e30)
            e = jnp.exp(s - jnp.max(s, axis=1, keepdims=True))
            p = e / jnp.sum(e, axis=1, keepdims=True)
            prob[pl.ds(first, 2), h] = p.reshape(2, shard, total)
            mixed[pl.ds(first, 2), :, cols] = (
                jnp.dot(p.astype(bf), val[:, :, cols].reshape(total, HD), preferred_element_type=f32)
                .astype(bf)
                .reshape(2, shard, HD)
            )
        cp = pltpu.make_async_copy(prob.at[pl.ds(first, 2)], p_ref.at[pl.ds(first, 2)], st_sem.at[6 + n])
        cp.start()
        stores.append(cp)

    half = width // 2
    tile = 512

    def part_mate(h):
        return far_copy(pown.at[h, 1 - c], pmate.at[h], ps_s.at[h], ps_r.at[h], d, mate)

    def part_across(h):
        return far_copy(xsend.at[h], xrecv.at[h], px_s.at[h], px_r.at[h], d, across)

    part_own = far_copy(qown.at[1 - c], qmate, pq_s, pq_r, d, mate)

    mix(there, 0)
    weights[3].wait()
    for h in range(2):
        for j in range(half // tile):
            new = jnp.dot(
                mixed[pl.ds(there, 2)].reshape(2 * shard, local),
                wo_v[:, pl.ds(h * half + j * tile, tile)],
                preferred_element_type=f32,
            ).astype(bf)
            pown[h, :, :, pl.ds(j * tile, tile)] = new.reshape(2, shard, tile)
        part_mate(h).start()
    for h in range(2):
        part_mate(h).wait_recv()
        xsend[h] = (pown[h, c].astype(f32) + pmate[h].astype(f32)).astype(bf)
        part_across(h).start()
    mix(here, 1)
    for j in range(width // tile):
        new = jnp.dot(
            mixed[pl.ds(here, 2)].reshape(2 * shard, local),
            wo_v[:, pl.ds(j * tile, tile)],
            preferred_element_type=f32,
        ).astype(bf)
        qown[:, :, pl.ds(j * tile, tile)] = new.reshape(2, shard, tile)
    part_own.start()
    cp = pltpu.make_async_copy(mixed, mix_ref, st_sem.at[8])
    cp.start()
    stores.append(cp)
    for cp in next_y:
        cp.wait_recv()
    for cp in next_c:
        cp.start()
    tip(1)
    stores += drops
    part_own.wait_recv()
    for h in range(2):
        part_across(h).wait_recv()
        cols = slice(h * half, (h + 1) * half)
        att_ref[:, cols] = (
            qown[c, :, cols].astype(f32) + qmate[:, cols].astype(f32) + xrecv[h].astype(f32)
        )
    for cp in stores:
        cp.wait()
    for cp in next_c:
        cp.wait_recv()
    for cp in [send_x, send_m, forward, part_own] + next_y + next_c + stats:
        cp.wait_send()
    for h in range(2):
        part_mate(h).wait_send()
        part_across(h).wait_send()


def attend_both(lengths, tok, gq, gk, wq, wk, wv, wo, wg, wu):
    shard, width = tok.shape
    local = wq.shape[1]
    heads = local // HD
    bf = jnp.bfloat16
    f32 = jnp.float32
    dma = pltpu.SemaphoreType.DMA
    vm = pl.BlockSpec(memory_space=pltpu.VMEM)
    shape = jax.ShapeDtypeStruct
    half = width // 2
    total = 4 * shard
    return pl.pallas_call(
        attend_kernel,
        name="attend_forward",
        out_shape=(
            shape((shard, width), f32),
            shape((4, shard, width), bf),
            shape((4, shard, width), bf),
            shape((4, shard, local), f32),
            shape((4, shard, local), f32),
            shape((4, shard, local), bf),
            shape((4, shard, local), bf),
            shape((4, shard, local), bf),
            shape((4, shard, local), bf),
            shape((4, heads, shard, total), f32),
            shape((4, 16, shard), f32),
            shape((4, shard, HD), f32),
            shape((4, shard, HD), f32),
            shape((wg.shape[1] // 2, width), bf),
            shape((wg.shape[1] // 2, width), bf),
        ),
        in_specs=[pl.BlockSpec(memory_space=pltpu.SMEM)] + [vm] * 3 + [FULL] * 6,
        out_specs=(vm,) + (FULL,) * 9 + (vm,) * 3 + (FULL,) * 2,
        scratch_shapes=[
            pltpu.VMEM((3, width, local), bf),
            pltpu.VMEM((local, width), bf),
            pltpu.VMEM((2, width, wg.shape[1] // 2), bf),
            pltpu.VMEM((2, wg.shape[1] // 2, width), bf),
            pltpu.VMEM((4, shard, width), bf),
            pltpu.VMEM((2, 4, shard, local), f32),
            pltpu.VMEM((2, 4, shard, local), bf),
            pltpu.VMEM((4, shard, local), bf),
            pltpu.VMEM((4, shard, local), bf),
            pltpu.VMEM((4, heads, shard, total), f32),
            pltpu.VMEM((4, 16, shard), f32),
            pltpu.VMEM((3, 4, 16, shard), f32),
            pltpu.VMEM((2, 2, shard, half), bf),
            pltpu.VMEM((2, shard, half), bf),
            pltpu.VMEM((2, shard, half), bf),
            pltpu.VMEM((2, shard, half), bf),
            pltpu.VMEM((2, shard, width), bf),
            pltpu.VMEM((shard, width), bf),
            dma((4,)),
            dma((3,)), dma((3,)), dma((3,)), dma((3,)),
            dma((2,)), dma((2,)), dma((2,)), dma((2,)),
            dma(()), dma(()),
            dma((9,)),
            dma((4,)), dma((4,)), dma((4,)),
        ],
        compiler_params=pltpu.CompilerParams(
            collective_id=2, has_side_effects=True, vmem_limit_bytes=56 * 1024 * 1024
        ),
        cost_estimate=pl.CostEstimate(
            flops=2 * total * width * local * 4, bytes_accessed=24 * 1024 * 1024, transcendentals=heads * total * total
        ),
    )(
        lengths, tok, gq.reshape(1, -1), gk.reshape(1, -1), wq, wk, wv, wo, wg, wu,
    )


def rank_rows(z):
    return (z, z + 1 - 2 * (z % 2), 2 - z // 2, 3 - 3 * (z // 2))


class Line:
    def __init__(self, ref, z, y, t, q, send, recv):
        self.ref, self.z, self.t, self.q, self.send, self.recv = ref, z, t, q, send, recv
        self.up = ((z + 1) % 4) * 2 + y
        self.down = ((z + 3) % 4) * 2 + y

    def go(self, way, i, r, src=None):
        cell = self.ref.at[r, self.q]
        return far_copy(
            cell if src is None else src, cell, self.send.at[way, i], self.recv.at[way, i], (self.up, self.down)[way], self.t
        )

    def hops(self, step, src=None):
        z = self.z
        if step == 0:
            return [(z < 3, 0, z), (z > 0, 1, z)]
        if step == 1:
            middle = (z > 0) & (z < 3)
            return [(middle, 0, (z + 3) % 4), (middle, 1, (z + 1) % 4)]
        return [(z == 2, 0, 0), (z == 1, 1, 3)]

    def lands(self, step):
        z = self.z
        if step == 0:
            return [(z > 0, 0, (z + 3) % 4), (z < 3, 1, (z + 1) % 4)]
        if step == 1:
            return [(z > 1, 0, (z + 2) % 4), (z < 2, 1, (z + 2) % 4)]
        return [(z == 3, 0, 0), (z == 0, 1, 3)]

    def start(self, step, src=None):
        for ok, way, r in self.hops(step):
            pl.when(ok)(self.go(way, step, r, src).start)

    def sent(self, step, src=None):
        for ok, way, r in self.hops(step):
            pl.when(ok)(self.go(way, step, r, src).wait_send)

    def landed(self, step):
        for ok, way, r in self.lands(step):
            pl.when(ok)(self.go(way, step, r).wait_recv)


def attend_back_kernel(
    dat_ref, ghid_ref, cos_ref, sin_ref, gq_ref, gk_ref, inv_ref,
    wq_ref, wk_ref, wv_ref, wo_ref, qh_ref, kh_ref, qr_ref, kr_ref, v_ref, p_ref, mix_ref, wgt_ref, wut_ref, gh_in, gd_in,
    gt_ref, gain_ref, dq_ref, dk_ref, dv_ref, po_ref, lhs_ref, gh_ref, gd_ref,
    w_v, wo_v, dall, unit, rot, val, dmix, prob, scaled, low, mixed, lhs_t, full, part, tip_v, hb_v, made, stat, stat_in, pown, pmate, xsend, xrecv, qown, qmate,
    w_sem, as_s, as_r, hx_s, hx_r, hc_s, hc_r, ss_s, ss_r, ps_s, ps_r, px_s, px_r, pq_s, pq_r, ys_s, ys_r, zs_s, zs_r, hz_s, hz_r, st_sem, hb_sem, made_sem,
):
    d, t, z, y, c, chip, mate, across = places()
    far = (mate + 2) % 4
    shard, width = dat_ref.shape
    local = w_v.shape[2]
    bf = jnp.bfloat16
    f32 = jnp.float32
    heads = local // HD
    total = 4 * shard
    sources = (wo_ref, wgt_ref, wut_ref, mix_ref, v_ref, p_ref, qr_ref, kr_ref, qh_ref, kh_ref, wq_ref, wk_ref, wv_ref)
    homes = (wo_v, tip_v.at[0], tip_v.at[1], mixed, val, prob, rot.at[0], rot.at[1], unit.at[0], unit.at[1], w_v.at[0], w_v.at[1], w_v.at[2])
    loads = [pltpu.make_async_copy(a, b, w_sem.at[i]) for i, (a, b) in enumerate(zip(sources, homes))]
    for cp in loads:
        cp.start()
    dall[t] = dat_ref[...]
    twin = z * 2 + 1 - y
    above = ((z + 1) % 4) * 2 + y
    below = ((z + 3) % 4) * 2 + y
    greet([(d, mate), (d, across), (d, far), (twin, t), (above, t), (below, t)])

    line_h = Line(gh_ref, z, y, t, t, hz_s, hz_r)
    line_d = Line(gd_ref, z, y, t, t, zs_s, zs_r)
    line_h.start(2)
    line_d.start(1)
    ranks = rank_rows(z)
    edge = (z == 0) | (z == 3)

    def hb_load(n):
        return pltpu.make_async_copy(gh_ref.at[ranks[n]], hb_v.at[n % 2], hb_sem.at[n])

    hb_load(0).start()
    hb_load(1).start()

    def made_out(n):
        return pltpu.make_async_copy(made, lhs_ref.at[n], made_sem.at[n])

    def remake(n):
        hb_load(n).wait()
        if n > 0:
            made_out(n - 1).wait()

        def wide(j, carry):
            cols = pl.ds(pl.multiple_of(j * 512, 512), 512)
            hb = hb_v[n % 2].reshape(total, width)
            g = lax.dot_general(tip_v[0, cols, :], hb, NT, preferred_element_type=f32)
            u = lax.dot_general(tip_v[1, cols, :], hb, NT, preferred_element_type=f32)
            sg = jax.nn.sigmoid(g)
            gs = g * sg
            made[0, cols, :] = (gs * u).astype(bf)
            made[1, cols, :] = (u * sg * (1.0 + g * (1.0 - sg))).astype(bf)
            made[2, cols, :] = gs.astype(bf)
            return carry

        lax.fori_loop(0, made.shape[1] // 512, wide, 0)
        made_out(n).start()

    send_x = far_copy(dall.at[t], dall.at[t], as_s.at[0], as_r.at[0], d, across)
    send_m = far_copy(dall.at[t], dall.at[t], as_s.at[1], as_r.at[1], d, mate)
    forward = far_copy(dall.at[across], dall.at[across], as_s.at[2], as_r.at[2], d, mate)
    send_x.start()
    send_m.start()
    last = ranks[3]
    row_x = far_copy(gh_ref.at[last, t], gh_ref.at[last, t], hx_s, hx_r, d, across)
    row_c = [
        far_copy(gh_ref.at[last, q], gh_ref.at[last, q], hc_s.at[j], hc_r.at[j], d, mate)
        for j, q in enumerate((t, across))
    ]
    swap_y = far_copy(full.at[:, 1 - y], part, ys_s, ys_r, twin, t)

    def project(first):
        rows = dall[pl.ds(first, 2)].reshape(2 * shard, width)
        dmix[pl.ds(first, 2)] = (
            lax.dot_general(rows, wo_v[...], NT, preferred_element_type=f32).astype(bf).reshape(2, shard, local)
        )

    here = chip * 2
    there = 2 - chip * 2
    loads[0].wait()
    send_m.wait_recv()
    project(here)
    for cp in loads[1:3]:
        cp.wait()
    remake(0)
    for cp in loads[3:]:
        cp.wait()
    send_x.wait_recv()
    forward.start()
    forward.wait_recv()
    line_h.landed(2)
    pl.when(edge)(row_x.start)
    project(there)
    lhs_t[...] = mixed[...].reshape(total, local).astype(f32).T.astype(bf)
    block = full.shape[3]
    for b in range(8):
        full[b // 2, b % 2] = jnp.dot(
            lhs_t[...], dall[:, :, b * block : (b + 1) * block].reshape(total, block), preferred_element_type=f32
        ).astype(bf)
    swap_y.start()
    stores = []

    scale = 1.0 / math.sqrt(HD)
    cos = cos_ref[...].reshape(total, HD)
    sin = sin_ref[...].reshape(total, HD)
    dots = [jnp.zeros((total, 1), f32), jnp.zeros((total, 1), f32)]
    for h in range(heads):
        cols = slice(h * HD, (h + 1) * HD)
        dm = dmix[:, :, cols].reshape(total, HD)
        p = prob[:, h].reshape(total, total)
        dp = lax.dot_general(dm, val[:, :, cols].reshape(total, HD), NT, preferred_element_type=f32)
        ds = (p * (dp - jnp.sum(p * dp, axis=1, keepdims=True))).astype(bf)
        low[2, :, :, cols] = (
            lax.dot_general(p.astype(bf), dm, TN, preferred_element_type=f32).astype(bf).reshape(4, shard, HD)
        )
        back = (
            jnp.dot(ds, rot[1, :, :, cols].reshape(total, HD), preferred_element_type=f32) * scale,
            lax.dot_general(ds, rot[0, :, :, cols].reshape(total, HD), TN, preferred_element_type=f32) * scale,
        )
        for i, gain in ((0, gq_ref), (1, gk_ref)):
            g = back[i]
            g = g * cos - pltpu.roll(g, HD // 2, 1) * sin
            u = unit[i, :, :, cols].reshape(total, HD)
            prod = g * u
            gain_ref[i : i + 1, cols] = jnp.sum(prod, axis=0, keepdims=True)
            dots[i] = dots[i] + jnp.sum(prod * gain[:, cols], axis=1, keepdims=True)
            scaled[i, :, :, cols] = (g * gain[:, cols]).reshape(4, shard, HD)
    for q in range(4):
        for i in range(2):
            stat[q, i * 8 : i * 8 + 8, :] = to_rows(dots[i][q * shard : (q + 1) * shard])
    stats = [
        far_copy(stat, stat_in.at[i], ss_s.at[i], ss_r.at[i], d, who)
        for i, who in enumerate((mate, across, far))
    ]
    for cp in stats:
        cp.start()
    for cp in stats:
        cp.wait_recv()

    def finish(first):
        for s in range(2):
            q = first + s
            mean = (stat[q] + stat_in[0, q] + stat_in[1, q] + stat_in[2, q]) / width
            inv = inv_ref[q]
            for i in range(2):
                low[i, q] = (
                    to_column(inv[i * 8 : i * 8 + 8])
                    * (scaled[i, q] - unit[i, q] * to_column(mean[i * 8 : i * 8 + 8]))
                ).astype(bf)

    half = width // 2
    tile = 512

    def part_mate(h):
        return far_copy(pown.at[h, 1 - c], pmate.at[h], ps_s.at[h], ps_r.at[h], d, mate)

    def part_across(h):
        return far_copy(xsend.at[h], xrecv.at[h], px_s.at[h], px_r.at[h], d, across)

    part_own = far_copy(qown.at[1 - c], qmate, pq_s, pq_r, d, mate)

    def result(first, start):
        new = None
        for i in range(3):
            one = lax.dot_general(
                low[i, pl.ds(first, 2)].reshape(2 * shard, local),
                w_v[i, pl.ds(start, tile), :],
                NT,
                preferred_element_type=f32,
            )
            new = one if new is None else new + one
        return new.astype(bf).reshape(2, shard, tile)

    finish(there)
    for h in range(2):
        for j in range(half // tile):
            pown[h, :, :, pl.ds(j * tile, tile)] = result(there, h * half + j * tile)
        part_mate(h).start()
        part_mate(h).wait_recv()
        xsend[h] = (pown[h, c].astype(f32) + pmate[h].astype(f32)).astype(bf)
        part_across(h).start()
    line_d.landed(1)
    line_d.start(2)
    pl.when(edge)(row_x.wait_recv)
    for cp in row_c:
        cp.start()
    finish(here)
    more = [
        pltpu.make_async_copy(low.at[i], r, st_sem.at[1 + i]) for i, r in enumerate((dq_ref, dk_ref, dv_ref))
    ]
    for cp in more:
        cp.start()
    stores += more
    for j in range(width // tile):
        qown[:, :, pl.ds(j * tile, tile)] = result(here, j * tile)
    part_own.start()
    remake(1)
    swap_y.wait_recv()
    for b in range(4):
        part[b] = (part[b].astype(f32) + full[b, y].astype(f32)).astype(bf)
    keep = pltpu.make_async_copy(part, po_ref, st_sem.at[0])
    keep.start()
    stores.append(keep)
    part_own.wait_recv()
    for h in range(2):
        part_across(h).wait_recv()
        cols = slice(h * half, (h + 1) * half)
        gt_ref[:, cols] = (
            ghid_ref[:, cols]
            + (qown[c, :, cols].astype(f32) + qmate[:, cols].astype(f32) + xrecv[h].astype(f32))
        ).astype(bf)
    for cp in stores:
        cp.wait()
    for cp in row_c:
        cp.wait()
    pl.when(edge)(row_x.wait_send)
    line_h.sent(2)
    line_d.sent(1)
    line_d.landed(2)
    line_d.sent(2)
    made_out(1).wait()
    for cp in [send_x, send_m, forward, part_own, swap_y] + stats:
        cp.wait_send()
    for h in range(2):
        part_mate(h).wait_send()
        part_across(h).wait_send()


def attend_back_both(dat, ghid, cos, sin, gq, gk, inv, wq, wk, wv, wo, qh, kh, qr, kr, v, p, mix, wgt, wut, gh, gd):
    shard, width = dat.shape
    local = wq.shape[1]
    heads = local // HD
    bf = jnp.bfloat16
    f32 = jnp.float32
    dma = pltpu.SemaphoreType.DMA
    vm = pl.BlockSpec(memory_space=pltpu.VMEM)
    shape = jax.ShapeDtypeStruct
    half = width // 2
    total = 4 * shard
    return pl.pallas_call(
        attend_back_kernel,
        name="attend_backward",
        out_shape=(
            shape((shard, width), bf),
            shape((2, local), f32),
            shape((4, shard, local), bf),
            shape((4, shard, local), bf),
            shape((4, shard, local), bf),
            shape((4, local, width // 8), bf),
            shape((2, 3, wgt.shape[0], total), bf),
            shape(gh.shape, bf),
            shape(gd.shape, bf),
        ),
        in_specs=[vm] * 7 + [FULL] * 15,
        out_specs=(vm,) * 2 + (FULL,) * 7,
        input_output_aliases={20: 7, 21: 8},
        scratch_shapes=[
            pltpu.VMEM((3, width, local), bf),
            pltpu.VMEM((local, width), bf),
            pltpu.VMEM((4, shard, width), bf),
            pltpu.VMEM((2, 4, shard, local), f32),
            pltpu.VMEM((2, 4, shard, local), bf),
            pltpu.VMEM((4, shard, local), bf),
            pltpu.VMEM((4, shard, local), bf),
            pltpu.VMEM((4, heads, shard, total), f32),
            pltpu.VMEM((2, 4, shard, local), f32),
            pltpu.VMEM((3, 4, shard, local), bf),
            pltpu.VMEM((4, shard, local), bf),
            pltpu.VMEM((local, total), bf),
            pltpu.VMEM((4, 2, local, width // 8), bf),
            pltpu.VMEM((4, local, width // 8), bf),
            pltpu.VMEM((2, wgt.shape[0], width), bf),
            pltpu.VMEM((2, 4, shard, width), bf),
            pltpu.VMEM((3, wgt.shape[0], total), bf),
            pltpu.VMEM((4, 16, shard), f32),
            pltpu.VMEM((3, 4, 16, shard), f32),
            pltpu.VMEM((2, 2, shard, half), bf),
            pltpu.VMEM((2, shard, half), bf),
            pltpu.VMEM((2, shard, half), bf),
            pltpu.VMEM((2, shard, half), bf),
            pltpu.VMEM((2, shard, width), bf),
            pltpu.VMEM((shard, width), bf),
            dma((13,)),
            dma((3,)), dma((3,)), dma(()), dma(()), dma((2,)), dma((2,)), dma((3,)), dma((3,)),
            dma((2,)), dma((2,)), dma((2,)), dma((2,)),
            dma(()), dma(()), dma(()), dma(()),
            dma((2, 3)), dma((2, 3)), dma((2, 3)), dma((2, 3)),
            dma((4,)), dma((3,)), dma((3,)),
        ],
        compiler_params=pltpu.CompilerParams(
            collective_id=3, has_side_effects=True, vmem_limit_bytes=56 * 1024 * 1024
        ),
        cost_estimate=pl.CostEstimate(
            flops=2 * total * width * local * 4 + 10 * heads * total * total * HD,
            bytes_accessed=24 * 1024 * 1024,
            transcendentals=0,
        ),
    )(
        dat, ghid, cos.reshape(4, shard, HD), sin.reshape(4, shard, HD), gq.reshape(1, -1), gk.reshape(1, -1), inv,
        wq, wk, wv, wo, qh, kh, qr, kr, v, p, mix, wgt, wut, gh, gd,
    )


def place_kernel(
    a_ref, p_ref, m_ref, n_ref, q_ref, k_ref, v_ref, o_ref, g_ref, u_ref, d_ref, gq_ref, gk_ref, ga_ref, gm_ref,
    a_v, p_v, m_v, head_v, o_v, gu_v, d_v, in_sem, out_sem,
):
    f32 = jnp.float32
    n = a_v.shape[2]
    f = m_v.shape[2]
    loads = [pltpu.make_async_copy(m_ref.at[w], m_v.at[w], in_sem.at[w]) for w in range(3)] + [
        pltpu.make_async_copy(p_ref, p_v, in_sem.at[3]),
        pltpu.make_async_copy(a_ref, a_v, in_sem.at[4]),
    ]
    for cp in loads:
        cp.start()
    stores = []

    def store(src, dst):
        cp = pltpu.make_async_copy(src, dst, out_sem.at[len(stores)])
        cp.start()
        stores.append(cp)

    local = gq_ref.shape[1]
    gq_ref[...] = n_ref[2:3, :local]
    gk_ref[...] = n_ref[3:4, :local]
    ga_ref[...] = n_ref[0:1, :]
    gm_ref[...] = n_ref[1:2, :]
    loads[0].wait()
    for i in range(2):
        d_v[i * f : (i + 1) * f, :] = m_v[0, i].astype(f32)
    store(d_v, d_ref)
    for w, ref in ((1, g_ref), (2, u_ref)):
        loads[w].wait()
        for i in range(2):
            gu_v[w - 1, :, i * f : (i + 1) * f] = m_v[w, i].T.astype(f32)
        store(gu_v.at[w - 1], ref)
    loads[3].wait()
    new = p_v[0].astype(f32)
    for i in range(1, 4):
        new = new + p_v[i].astype(f32)
    o_v[...] = new
    store(o_v, o_ref)
    loads[4].wait()
    for w, ref in ((0, v_ref), (1, q_ref), (2, k_ref)):
        for i in range(2):
            head_v[w, :, i * n : (i + 1) * n] = a_v[w, i].T.astype(f32)
        store(head_v.at[w], ref)
    for cp in stores:
        cp.wait()


def place_grads(attn, proj, mlp, gains):
    _, f, block = proj.shape
    width = gains.shape[1]
    f32 = jnp.float32
    vm = pl.BlockSpec(memory_space=pltpu.VMEM)
    shape = jax.ShapeDtypeStruct
    return pl.pallas_call(
        place_kernel,
        name="place_grads",
        out_shape=(
            shape((block, f), f32),
            shape((block, f), f32),
            shape((block, f), f32),
            shape((f, block), f32),
            shape((block, 4 * f), f32),
            shape((block, 4 * f), f32),
            shape((4 * f, block), f32),
            shape((1, f), f32),
            shape((1, f), f32),
            shape((1, width), f32),
            shape((1, width), f32),
        ),
        in_specs=[FULL] * 3 + [vm],
        out_specs=(FULL,) * 7 + (vm,) * 4,
        scratch_shapes=[
            pltpu.VMEM(attn.shape, attn.dtype),
            pltpu.VMEM(proj.shape, proj.dtype),
            pltpu.VMEM(mlp.shape, mlp.dtype),
            pltpu.VMEM((3, block, f), f32),
            pltpu.VMEM((f, block), f32),
            pltpu.VMEM((2, block, 4 * f), f32),
            pltpu.VMEM((4 * f, block), f32),
            pltpu.SemaphoreType.DMA((5,)),
            pltpu.SemaphoreType.DMA((7,)),
        ],
        compiler_params=pltpu.CompilerParams(vmem_limit_bytes=60 * 1024 * 1024),
    )(attn, proj, mlp, gains)


def plain_body(
    tokens,
    lengths,
    w_query,
    w_key,
    w_value,
    w_out,
    w_gate,
    w_up,
    w_down,
    gain_query,
    gain_key,
    gain_attn,
    gain_mlp,
    cotangent,
):
    rows_dev = lengths.shape[0]
    model_width = w_query.shape[0]
    local_width = w_query.shape[1]
    head_count = local_width // HD
    gathered = lax.all_gather(tokens, "tensor", axis=0, tiled=True)
    row_count = gathered.shape[0]
    segment, offsets = jax.vmap(row_layout)(lengths)
    queries = jnp.dot(gathered, w_query, preferred_element_type=jnp.float32)
    keys_raw = jnp.dot(gathered, w_key, preferred_element_type=jnp.float32)
    values_low = jnp.dot(gathered, w_value, preferred_element_type=jnp.float32).astype(jnp.bfloat16)
    q_total, k_total = lax.psum(
        (jnp.sum(queries * queries, axis=1), jnp.sum(keys_raw * keys_raw, axis=1)), "tensor"
    )
    q_inv = lax.rsqrt(q_total / model_width + EPS)[:, None]
    k_inv = lax.rsqrt(k_total / model_width + EPS)[:, None]
    q_unit = queries * q_inv
    k_unit = keys_raw * k_inv

    def to_heads(values):
        return values.reshape(rows_dev, ROW_LEN, head_count, HD)

    queries_low = rotate(to_heads(q_unit * gain_query), offsets, 1.0).astype(jnp.bfloat16)
    keys_low = rotate(to_heads(k_unit * gain_key), offsets, 1.0).astype(jnp.bfloat16)
    values_heads = to_heads(values_low)
    mixed_heads, log_total = jax.vmap(lambda *a: attend(a))(
        queries_low, keys_low, values_heads, segment
    )
    mixed_low = mixed_heads.reshape(row_count, local_width)
    attn_out = lax.psum_scatter(
        jnp.dot(mixed_low, w_out, preferred_element_type=jnp.float32).astype(jnp.bfloat16),
        "tensor",
        scatter_dimension=0,
        tiled=True,
    ).astype(jnp.float32)
    inner_count = lax.axis_size("dp") // OUTER
    a_inv = lax.rsqrt(jnp.mean(attn_out * attn_out, axis=1, keepdims=True) + EPS)
    a_unit = attn_out * a_inv
    hidden = tokens.astype(jnp.float32) + a_unit * gain_attn
    hidden_low = hidden.astype(jnp.bfloat16)
    hidden_all = lax.all_gather(hidden_low, "tensor", axis=0, tiled=True)
    outer_index = lax.axis_index("dp") // inner_count

    def gather_group(shard):
        groups = [[z * inner_count + i for z in range(OUTER)] for i in range(inner_count)]
        part = lax.all_gather(shard, "dp", axis=0, tiled=True, axis_index_groups=groups)
        return lax.all_gather(part, "tensor", axis=0, tiled=True)

    hidden_group = gather_group(hidden_low)
    gate_acts = jnp.dot(hidden_all, w_gate, preferred_element_type=jnp.float32)
    up_acts = jnp.dot(hidden_all, w_up, preferred_element_type=jnp.float32)
    gate_sigmoid = jax.nn.sigmoid(gate_acts)
    inner_low = (gate_acts * gate_sigmoid * up_acts).astype(jnp.bfloat16)
    mlp_out = lax.psum_scatter(
        jnp.dot(inner_low, w_down, preferred_element_type=jnp.float32).astype(jnp.bfloat16),
        "tensor",
        scatter_dimension=0,
        tiled=True,
    ).astype(jnp.float32)
    f_inv = lax.rsqrt(jnp.mean(mlp_out * mlp_out, axis=1, keepdims=True) + EPS)
    f_unit = mlp_out * f_inv
    output = (hidden + f_unit * gain_mlp).astype(jnp.bfloat16)
    grad_output = cotangent.astype(jnp.float32)
    grad_mlp, grad_gain_mlp_part = post_norm_back(grad_output, f_unit, f_inv, gain_mlp)
    grad_mlp_low = grad_mlp.astype(jnp.bfloat16)
    mlp_grad_all = lax.all_gather(grad_mlp_low, "tensor", axis=0, tiled=True)
    mlp_grad_group = gather_group(grad_mlp_low)
    grad_inner = times_t(mlp_grad_all, w_down)
    grad_gate_low = (
        grad_inner * up_acts * gate_sigmoid * (1.0 + gate_acts * (1.0 - gate_sigmoid))
    ).astype(jnp.bfloat16)
    grad_up_low = (grad_inner * gate_acts * gate_sigmoid).astype(jnp.bfloat16)
    part_width = w_gate.shape[1] // OUTER
    gate_part = lax.dynamic_slice_in_dim(w_gate, outer_index * part_width, part_width, 1)
    up_part = lax.dynamic_slice_in_dim(w_up, outer_index * part_width, part_width, 1)
    down_part = lax.dynamic_slice_in_dim(w_down, outer_index * part_width, part_width, 0)
    gate_g = jnp.dot(hidden_group, gate_part, preferred_element_type=jnp.float32)
    up_g = jnp.dot(hidden_group, up_part, preferred_element_type=jnp.float32)
    sig_g = jax.nn.sigmoid(gate_g)
    inner_g = (gate_g * sig_g * up_g).astype(jnp.bfloat16)
    grad_inner_g = times_t(mlp_grad_group, down_part)
    grad_gate_g = (grad_inner_g * up_g * sig_g * (1.0 + gate_g * (1.0 - sig_g))).astype(
        jnp.bfloat16
    )
    grad_up_g = (grad_inner_g * gate_g * sig_g).astype(jnp.bfloat16)
    sum_down = scatter_join(split_cols(t_times(inner_g, mlp_grad_group), inner_count), inner_count, 0)
    sum_gate = scatter_join(split_rows(t_times(hidden_group, grad_gate_g), inner_count), inner_count, 1)
    sum_up = scatter_join(split_rows(t_times(hidden_group, grad_up_g), inner_count), inner_count, 1)
    grad_hidden = grad_output + lax.psum_scatter(
        (times_t(grad_gate_low, w_gate) + times_t(grad_up_low, w_up)).astype(jnp.bfloat16),
        "tensor",
        scatter_dimension=0,
        tiled=True,
    ).astype(jnp.float32)
    grad_attn, grad_gain_attn_part = post_norm_back(grad_hidden, a_unit, a_inv, gain_attn)
    grad_attn_low = grad_attn.astype(jnp.bfloat16)
    attn_grad_all = lax.all_gather(grad_attn_low, "tensor", axis=0, tiled=True)
    grad_mixed = times_t(attn_grad_all, w_out).astype(jnp.bfloat16)
    grad_q_rot, grad_k_rot, grad_values_low = jax.vmap(lambda *a: attend_back(a))(
        queries_low, keys_low, values_heads, segment, log_total, to_heads(grad_mixed)
    )
    grad_q_norm = rotate(grad_q_rot, offsets, -1.0).reshape(row_count, local_width)
    grad_k_norm = rotate(grad_k_rot, offsets, -1.0).reshape(row_count, local_width)
    grad_gain_query_part = jnp.sum(grad_q_norm * q_unit, axis=0)
    grad_gain_key_part = jnp.sum(grad_k_norm * k_unit, axis=0)
    q_scaled = grad_q_norm * gain_query
    k_scaled = grad_k_norm * gain_key
    q_dots, k_dots = lax.psum(
        (jnp.sum(q_scaled * q_unit, axis=1), jnp.sum(k_scaled * k_unit, axis=1)), "tensor"
    )
    grad_queries_low = (q_inv * (q_scaled - q_unit * (q_dots / model_width)[:, None])).astype(
        jnp.bfloat16
    )
    grad_keys_low = (k_inv * (k_scaled - k_unit * (k_dots / model_width)[:, None])).astype(
        jnp.bfloat16
    )
    grad_values_flat = grad_values_low.reshape(row_count, local_width)
    grad_tokens = (
        grad_hidden
        + lax.psum_scatter(
            (
                times_t(grad_queries_low, w_query)
                + times_t(grad_keys_low, w_key)
                + times_t(grad_values_flat, w_value)
            ).astype(jnp.bfloat16),
            "tensor",
            scatter_dimension=0,
            tiled=True,
        ).astype(jnp.float32)
    ).astype(jnp.bfloat16)
    tensor_start = lax.axis_index("tensor") * local_width
    zero_row = jnp.zeros((model_width,), jnp.float32)
    q_full = lax.dynamic_update_slice(zero_row, grad_gain_query_part, (tensor_start,))
    k_full = lax.dynamic_update_slice(zero_row, grad_gain_key_part, (tensor_start,))
    gain_stack = jnp.stack([q_full, k_full, grad_gain_attn_part, grad_gain_mlp_part])
    gain_total = lax.psum(gain_stack, ("dp", "tensor"))
    grad_gain_query = lax.dynamic_slice(gain_total[0], (tensor_start,), (local_width,))
    grad_gain_key = lax.dynamic_slice(gain_total[1], (tensor_start,), (local_width,))
    summed = (
        scatter_sum(split_rows(t_times(gathered, grad_queries_low), inner_count), inner_count),
        scatter_sum(split_rows(t_times(gathered, grad_keys_low), inner_count), inner_count),
        scatter_sum(split_rows(t_times(gathered, grad_values_flat), inner_count), inner_count),
        scatter_sum(split_cols(t_times(mixed_low, attn_grad_all), inner_count), inner_count),
        sum_gate,
        sum_up,
        sum_down,
    )
    return (
        output,
        grad_tokens,
        summed[0],
        summed[1],
        summed[2],
        summed[3],
        summed[4],
        summed[5],
        summed[6],
        grad_gain_query,
        grad_gain_key,
        gain_total[2],
        gain_total[3],
    )


def fused_body(
    tokens,
    lengths,
    w_query,
    w_key,
    w_value,
    w_out,
    w_gate,
    w_up,
    w_down,
    gain_query,
    gain_key,
    gain_attn,
    gain_mlp,
    cotangent,
):
    (
        attn_out, tokens_all, tokens_next, q_unit, k_unit, q_rot, k_rot, values, mixed, weights, inverse,
        cosines, sines, gate_t, up_t,
    ) = attend_both(
        lengths, tokens, gain_query, gain_key, w_query, w_key, w_value, w_out, w_gate, w_up
    )
    output, grad_hidden, grad_attn, gain_parts, group_h, group_d = mlp_both(
        attn_out, tokens, cotangent, gain_attn, gain_mlp, w_gate, w_up, w_down
    )
    grad_tokens, head_gains, grad_q, grad_k, grad_v, proj, made, group_h, group_d = attend_back_both(
        grad_attn, grad_hidden, cosines, sines, gain_query, gain_key, inverse,
        w_query, w_key, w_value, w_out, q_unit, k_unit, q_rot, k_rot, values, weights, mixed, gate_t, up_t,
        group_h, group_d,
    )
    gains, attn_blocks, proj_blocks, mlp_blocks, _, _ = weight_grads(
        gain_parts, head_gains, group_h, group_d, made, gate_t, up_t, w_down, tokens_all, tokens_next, grad_q, grad_k, grad_v, proj,
    )
    placed = place_grads(attn_blocks, proj_blocks, mlp_blocks, gains)
    return (
        output,
        grad_tokens,
        *placed[:7],
        *(g.reshape(-1) for g in placed[7:]),
    )


def solution(mesh):
    placed = (
        P(("dp", "tensor"), None),
        P("dp", None),
        P(None, "tensor"),
        P(None, "tensor"),
        P(None, "tensor"),
        P("tensor", None),
        P(None, "tensor"),
        P(None, "tensor"),
        P("tensor", None),
        P("tensor"),
        P("tensor"),
        P(),
        P(),
        P(("dp", "tensor"), None),
    )
    return jax.shard_map(
        fused_body if tuple(mesh.shape.values()) == (8, 4) else plain_body,
        mesh=mesh,
        in_specs=placed,
        out_specs=(
            P(("dp", "tensor"), None),
            P(("dp", "tensor"), None),
            P("dp", "tensor"),
            P("dp", "tensor"),
            P("dp", "tensor"),
            P("tensor", "dp"),
            P("dp", "tensor"),
            P("dp", "tensor"),
            P("tensor", "dp"),
            P("tensor"),
            P("tensor"),
            P(),
            P(),
        ),
        check_vma=False,
    )
```

```python
import math

import jax
import jax.numpy as jnp
from jax import lax
from jax.experimental import pallas as pl
from jax.experimental.pallas import tpu as pltpu
from jax.sharding import PartitionSpec as P

HD = 128
ROW_LEN = 512


EPS = 1e-06
THETA = 500000.0


def rotate(values, offsets, rot_sign):
    half_width = values.shape[-1] // 2
    frequency = jnp.exp(
        jnp.arange(half_width, dtype=jnp.float32) * (-2.0 * math.log(THETA) / values.shape[-1])
    )
    angles = offsets.astype(jnp.float32)[..., None, None] * frequency
    cosines = jnp.cos(angles)
    sine_part = rot_sign * jnp.sin(angles)
    first_half = values[..., :half_width]
    second_half = values[..., half_width:]
    return jnp.concatenate(
        [
            first_half * cosines - second_half * sine_part,
            second_half * cosines + first_half * sine_part,
        ],
        axis=-1,
    )


def row_layout(lengths_row):
    slots = jnp.arange(lengths_row.shape[0], dtype=jnp.int32)
    seq_ends = jnp.sum(
        jnp.where(slots[None, :] <= slots[:, None], lengths_row[None, :], 0), axis=1
    )
    position = jnp.arange(ROW_LEN, dtype=jnp.int32)
    passed = (position[:, None] >= seq_ends[None, :]).astype(jnp.int32)
    segment = jnp.sum(passed, axis=1)
    seq_start = jnp.sum(passed * lengths_row[None, :], axis=1)
    return (segment, position - seq_start)


def allowed_mask(segment):
    position = jnp.arange(segment.shape[0], dtype=jnp.int32)
    return (segment[:, None] == segment[None, :]) & (position[None, :] <= position[:, None])


def times_t(left_mat, right_mat):
    return lax.dot_general(
        left_mat, right_mat, (((1,), (1,)), ((), ())), preferred_element_type=jnp.float32
    )


def t_times(left_mat, right_mat):
    return lax.dot_general(
        left_mat, right_mat, (((0,), (0,)), ((), ())), preferred_element_type=jnp.float32
    )


def masked_scores(queries_low, keys_low, segment):
    scale_factor = 1.0 / math.sqrt(queries_low.shape[-1])
    scores = (
        jnp.einsum("qhd,khd->hqk", queries_low, keys_low, preferred_element_type=jnp.float32)
        * scale_factor
    )
    return jnp.where(allowed_mask(segment)[None], scores, -1e30)


def attend(block_item):
    queries_low, keys_low, values_low, segment = block_item
    scores = masked_scores(queries_low, keys_low, segment)
    row_max = jnp.max(scores, axis=-1, keepdims=True)
    shifted = jnp.exp(scores - row_max)
    row_total = jnp.sum(shifted, axis=-1, keepdims=True)
    attn_weights = (shifted / row_total).astype(jnp.bfloat16)
    mixed = jnp.einsum("hqk,khd->qhd", attn_weights, values_low, preferred_element_type=jnp.float32)
    return (mixed.astype(jnp.bfloat16), (row_max + jnp.log(row_total))[..., 0])


def attend_back(block_item):
    queries_low, keys_low, values_low, segment, log_total, grad_mixed = block_item
    scale_factor = 1.0 / math.sqrt(queries_low.shape[-1])
    scores = masked_scores(queries_low, keys_low, segment)
    attn_weights = jnp.exp(scores - log_total[..., None])
    grad_weights = jnp.einsum(
        "qhd,khd->hqk", grad_mixed, values_low, preferred_element_type=jnp.float32
    )
    row_dots = jnp.sum(attn_weights * grad_weights, axis=-1, keepdims=True)
    grad_scores = (attn_weights * (grad_weights - row_dots)).astype(jnp.bfloat16)
    grad_queries = scale_factor * jnp.einsum(
        "hqk,khd->qhd", grad_scores, keys_low, preferred_element_type=jnp.float32
    )
    grad_keys = scale_factor * jnp.einsum(
        "hqk,qhd->khd", grad_scores, queries_low, preferred_element_type=jnp.float32
    )
    grad_values = jnp.einsum(
        "hqk,qhd->khd",
        attn_weights.astype(jnp.bfloat16),
        grad_mixed,
        preferred_element_type=jnp.float32,
    )
    return (grad_queries, grad_keys, grad_values.astype(jnp.bfloat16))


def post_norm_back(grad_in, unit_rows, inv_scale, gain_vec):
    scaled = grad_in * gain_vec
    mean_dots = jnp.mean(scaled * unit_rows, axis=-1, keepdims=True)
    return (inv_scale * (scaled - unit_rows * mean_dots), jnp.sum(grad_in * unit_rows, axis=0))


OUTER = 4


def swap(value, shift):
    size = lax.axis_size("dp")
    return lax.ppermute(value, "dp", [(d, d ^ shift) for d in range(size)])


def pick(parts, index):
    return lax.dynamic_index_in_dim(parts, index, 0, keepdims=False)


def sum_inner(parts):
    inner = parts.shape[0]
    mine = lax.axis_index("dp") % inner
    total = pick(parts, mine)
    for k in range(1, inner):
        sent = pick(parts, mine ^ k).astype(jnp.bfloat16)
        total = total + swap(sent, k).astype(jnp.float32)
    return total


def trade_outer(parts, inner):
    mine = lax.axis_index("dp") // inner
    got = [(mine, pick(parts, mine))]
    for k in range(1, OUTER):
        got.append((mine ^ k, swap(pick(parts, mine ^ k), k * inner)))
    return got


def split_rows(grad, inner):
    cols = grad.shape[1]
    return grad.reshape(OUTER, inner, -1, cols).transpose(1, 0, 2, 3)


def split_cols(grad, inner):
    rows = grad.shape[0]
    return grad.reshape(rows, OUTER, inner, -1).transpose(2, 1, 0, 3)


def scatter_sum(parts, inner):
    half = sum_inner(parts).astype(jnp.bfloat16)
    got = trade_outer(half, inner)
    return sum(g.astype(jnp.float32) for _, g in got)


def scatter_join(parts, inner, axis):
    half = sum_inner(parts).astype(jnp.bfloat16)
    got = trade_outer(half, inner)
    stack = jnp.zeros((OUTER, *got[0][1].shape), jnp.bfloat16)
    for place, block in got:
        stack = lax.dynamic_update_index_in_dim(stack, block, place, 0)
    joined = jnp.concatenate([stack[z] for z in range(OUTER)], axis=axis)
    return joined.astype(jnp.float32)


MESH = pl.DeviceIdType.MESH
FULL = pl.BlockSpec(memory_space=pl.ANY)


def grads_kernel(
    gp_ref, gqk_ref, gh_in, gm_in, lhs_ref, wgt_ref, wut_ref, wd_ref, tok_ref, nxt_ref, dq_ref, dk_ref, dv_ref, po_ref,
    gain_ref, attn_ref, proj_ref, mlp_ref, gh_ref, gm_ref,
    hb_v, tip_v, dm_v, wd_v, lhs_in, lhs_q, lhs_t, quad, quad_in, pair, full, part, gbuf, gin,
    ld_sem, xs_s, xs_r, cs_s, cs_r, qs_s, qs_r, os_s, os_r, qz_s, qz_r, qy_s, qy_r, ys_s, ys_r, ts_s, ts_r, own_s, gs_s, gs_r, lhs_sem, pc_sem, hb_sem,
):
    d = lax.axis_index("dp")
    t = lax.axis_index("tensor")
    z = d // 2
    y = d % 2
    side = z % 2
    top = z // 2
    mate = t + 1 - 2 * (t % 2)
    across = (t + 2) % 4
    twin = z * 2 + 1 - y
    pal = (z + 1 - 2 * side) * 2 + y
    bf = jnp.bfloat16
    f32 = jnp.float32
    f = lhs_t.shape[1]
    width = hb_v.shape[3]
    shard = hb_v.shape[2]
    span = width // 2
    hc = lhs_in.shape[4]
    total = 4 * shard

    def peer(k):
        return ((z + k) % 4) * 2 + y

    heads = (dv_ref, dq_ref, dk_ref)
    parts = (top, 1 - top)
    ranks = rank_rows(z)
    slow = [
        pltpu.make_async_copy(
            wd_ref.at[pl.ds(side * f, f), pl.ds(parts[i] * span, span)], wd_v.at[i], ld_sem.at[4 + i]
        )
        for i in range(2)
    ] + [
        pltpu.make_async_copy(r.at[:, :, pl.ds(y * hc, hc)], lhs_in.at[w, 0], ld_sem.at[6 + w])
        for w, r in enumerate(heads)
    ]
    toks = [
        pltpu.make_async_copy(r, hb_v.at[i], ld_sem.at[i]) for i, r in enumerate((tok_ref, nxt_ref))
    ]

    def lhs_load(n, w):
        return pltpu.make_async_copy(
            lhs_ref.at[n, w], lhs_t.at[w, :, pl.ds(n * total, total)], lhs_sem.at[n, w]
        )

    def dm_load(n, i):
        return pltpu.make_async_copy(
            gm_ref.at[ranks[n], :, :, pl.ds(parts[i] * span, span)], dm_v.at[n, i], ld_sem.at[9 + n * 2 + i]
        )

    def hb_load(n):
        return [
            pltpu.make_async_copy(
                gh_ref.at[ranks[n], :, :, pl.ds(i * span, span)], dm_v.at[n, i], hb_sem.at[n - 2, i]
            )
            for i in range(2)
        ]

    tips = [
        pltpu.make_async_copy(r, tip_v.at[i], ld_sem.at[21 + i]) for i, r in enumerate((wgt_ref, wut_ref))
    ]
    for cp in hb_load(2) + tips + hb_load(3) + slow[2:] + toks:
        cp.start()
    for w in range(3):
        for n in range(2):
            lhs_load(n, w).start()
    for cp in [dm_load(0, 0), dm_load(0, 1)] + slow[:2]:
        cp.start()

    greet([(peer(1), t), (peer(2), t), (peer(3), t), (twin, t), (d, mate), (d, across)])

    groups = (gh_ref, gm_ref)

    def head_swap(w):
        return far_copy(
            heads[w].at[:, :, pl.ds((1 - y) * hc, hc)], lhs_in.at[w, 1], qs_s.at[w], qs_r.at[w], twin, t
        )

    block = quad.shape[4]

    def proj_trade(k):
        return far_copy(po_ref.at[(z + k) % 4], proj_ref.at[z], os_s.at[k - 1], os_r.at[k - 1], peer(k), t)

    keep_proj = pltpu.make_async_copy(po_ref.at[z], proj_ref.at[z], own_s.at[0])
    keep_proj.start()

    def piece(i):
        if i >= 12:
            return i - 11, pl.ds(parts[1] * span, span), pl.ds(0, span)
        spot = ((i // 3) % 2) * 2 + (1 - y if i < 6 else y)
        return 1 + i % 3, pl.ds(top * span + spot * block, block), pl.ds(spot * block, block)

    def cell(i, q):
        n, cols, _ = piece(i)
        return gm_ref.at[ranks[n], q, :, cols]

    def piece_load(i):
        n, cols, spot = piece(i)
        return pltpu.make_async_copy(
            gm_ref.at[ranks[n], :, :, cols], dm_v.at[n, i // 12, :, :, spot], pc_sem.at[i]
        )

    def forward_x(i):
        return far_copy(cell(i, t), cell(i, t), xs_s.at[i], xs_r.at[i], d, across)

    def forward_c(i, h):
        q = t if h == 0 else across
        return far_copy(cell(i, q), cell(i, q), cs_s.at[i, h], cs_r.at[i, h], d, mate)

    def advance(i):
        forward_x(i).wait_recv()
        for h in range(2):
            forward_c(i, h).start()

    def arrive(i):
        for h in range(2):
            forward_c(i, h).wait_recv()

    def gain_copy(i):
        stage, who = ((0, (peer(1), t)), (0, (peer(2), t)), (0, (peer(3), t)), (1, (twin, t)), (2, (d, across)), (3, (d, mate)))[i]
        return far_copy(gbuf.at[stage], gin.at[i], gs_s.at[i], gs_r.at[i], *who)

    gbuf[0] = jnp.zeros_like(gbuf[0])
    gbuf[0, 0:2, :] = gp_ref[...]
    gbuf[0, 2:4, 0 : gqk_ref.shape[1]] = gqk_ref[...]
    for i in range(3):
        gain_copy(i).start()
    for w in range(3):
        head_swap(w).start()
    for k in (2, 1, 3):
        proj_trade(k).start()
    for i in range(15):
        forward_x(i).start()
    def gain_step(stage):
        new = gbuf[stage]
        for i in ((0, 1, 2), (3,), (4,), (5,))[stage]:
            gain_copy(i).wait_recv()
            new = new + gin[i]
        if stage < 3:
            gbuf[stage + 1] = new
            gain_copy(stage + 3).start()
        if stage == 1:
            gain_ref[2:4, :] = new[2:4, :]
        if stage == 3:
            gain_ref[0:2, :] = new[0:2, :]

    step = 512

    def remake(n):
        def wide(j, carry):
            cols = pl.ds(pl.multiple_of(j * step, step), step)
            hb = [dm_v[n, i].reshape(total, span) for i in range(2)]
            g, u = [
                lax.dot_general(tip_v[w, cols, :span], hb[0], NT, preferred_element_type=f32)
                + lax.dot_general(tip_v[w, cols, span:], hb[1], NT, preferred_element_type=f32)
                for w in range(2)
            ]
            sg = jax.nn.sigmoid(g)
            gs = g * sg
            spot = slice(n * total, (n + 1) * total)
            lhs_t[0, cols, spot] = (gs * u).astype(bf)
            lhs_t[1, cols, spot] = (u * sg * (1.0 + g * (1.0 - sg))).astype(bf)
            lhs_t[2, cols, spot] = gs.astype(bf)
            return carry

        lax.fori_loop(0, f // step, wide, 0)

    def scale_back(n):
        if n < 2:
            for w in (1, 2):
                lhs_load(n, w).wait()

        def wide(j, carry):
            cols = pl.ds(pl.multiple_of(j * step, step), step)
            di = None
            for i in range(2):
                one = lax.dot_general(
                    wd_v[i, cols, :], dm_v[n, i].reshape(total, span), NT, preferred_element_type=f32
                )
                di = one if di is None else di + one
            toks = slice(n * total, (n + 1) * total)
            for w in (1, 2):
                lhs_t[w, cols, toks] = (lhs_t[w, cols, toks].astype(f32) * di).astype(bf)
            return carry

        lax.fori_loop(0, f // step, wide, 0)

    def hb_half(n):
        return pltpu.make_async_copy(
            gh_ref.at[ranks[n], :, :, pl.ds(top * span, span)],
            hb_v.at[n // 2, :, :, pl.ds((n % 2) * span, span)],
            ld_sem.at[17 + n],
        )

    for cp in hb_load(2) + tips:
        cp.wait()
    remake(2)

    def quad_trade(w, k):
        return far_copy(quad.at[w, (z + k) % 4], quad_in.at[w, k - 1], qz_s.at[w, k - 1], qz_r.at[w, k - 1], peer(k), t)

    def head_grad(w):
        slow[2 + w].wait()
        head_swap(w).wait_recv()
        for i in range(2):
            lhs_q[:, i * total : (i + 1) * total] = lhs_in[w, i].reshape(total, hc).astype(f32).T.astype(bf)

        def tile(j, carry):
            cols = pl.ds(pl.multiple_of(j * block, block), block)
            quad[w, j // 2, j % 2] = jnp.dot(
                lhs_q[...], hb_v[:, :, :, cols].reshape(2 * total, block), preferred_element_type=f32
            ).astype(bf)
            return carry

        lax.fori_loop(0, 8, tile, 0)
        for k in (2, 1, 3):
            quad_trade(w, k).start()

    for cp in toks:
        cp.wait()
    head_grad(0)
    for cp in hb_load(3):
        cp.wait()
    remake(3)
    for i in range(6):
        advance(i)
    for i in range(6):
        arrive(i)
        piece_load(i).start()
    gain_step(0)

    def swap_y(w):
        return far_copy(full.at[w, :, 1 - y], part.at[w], ys_s.at[w], ys_r.at[w], twin, t)

    def trade_z(w):
        return far_copy(part.at[w, 1 - side], mlp_ref.at[w, side], ts_s.at[w], ts_r.at[w], pal, t)

    def keep(w):
        return pltpu.make_async_copy(part.at[w, side], mlp_ref.at[w, side], own_s.at[1 + w])

    def finish_y(w):
        swap_y(w).wait()
        for b in range(2):
            part[w, b] = (part[w, b].astype(f32) + full[w, b, y].astype(f32)).astype(bf)
        trade_z(w).start()
        keep(w).start()

    def emit(w, yy):
        for zz in range(2):
            off = (zz * 2 + yy) * block
            new = None
            for n in range(4):
                base = 0 if w == 0 else (n % 2) * span
                cols = pl.ds(pl.multiple_of(base + off, block), block)
                rows = dm_v[n, 0, :, :, cols] if w == 0 else hb_v[n // 2, :, :, cols]
                one = jnp.dot(
                    lhs_t[w, :, n * total : (n + 1) * total],
                    rows.reshape(total, block),
                    preferred_element_type=f32,
                )
                new = one if new is None else new + one
            full[w, zz, yy] = new.astype(bf)

    for n in range(2):
        lhs_load(n, 0).wait()
    dm_load(0, 0).wait()
    for i in range(6):
        piece_load(i).wait()
    emit(0, 1 - y)
    swap_y(0).start()
    head_grad(1)
    head_grad(2)
    for n in range(4):
        hb_half(n).start()
    for i in range(6, 12):
        advance(i)
    for i in range(6, 12):
        arrive(i)
        piece_load(i).start()
    gain_step(1)
    for i in range(6, 12):
        piece_load(i).wait()
    emit(0, y)
    for i in range(2):
        slow[i].wait()
    dm_load(0, 1).wait()
    scale_back(0)
    advance(12)
    advance(13)
    for i in (12, 13):
        arrive(i)
        piece_load(i).start()
    piece_load(12).wait()
    scale_back(1)
    advance(14)
    piece_load(13).wait()
    scale_back(2)
    arrive(14)
    piece_load(14).start()
    piece_load(14).wait()
    scale_back(3)
    gain_step(2)
    for n in range(4):
        hb_half(n).wait()
    for w in (1, 2):
        emit(w, 1 - y)
        swap_y(w).start()
    for w in (1, 2):
        emit(w, y)
    gain_step(3)

    def head_swap_back(w):
        return far_copy(pair.at[w, 1 - y], attn_ref.at[w, y], qy_s.at[w], qy_r.at[w], twin, t)

    def head_keep(w):
        return pltpu.make_async_copy(pair.at[w, y], attn_ref.at[w, y], own_s.at[4 + w])

    def finish_head(w):
        for k in range(1, 4):
            quad_trade(w, k).wait_recv()
        for b in range(2):
            new = quad[w, z, b].astype(f32)
            for i in range(3):
                new = new + quad_in[w, i, b].astype(f32)
            pair[w, b] = new.astype(bf)
        head_swap_back(w).start()
        head_keep(w).start()

    finish_y(0)
    finish_head(0)
    finish_y(1)
    finish_head(1)
    finish_y(2)
    finish_head(2)

    keep_proj.wait()
    for k in range(1, 4):
        proj_trade(k).wait()
    for i in range(6):
        gain_copy(i).wait_send()
    for i in range(15):
        forward_x(i).wait_send()
        for h in range(2):
            forward_c(i, h).wait_send()
    for w in range(3):
        head_swap(w).wait_send()
        for k in range(1, 4):
            quad_trade(w, k).wait_send()
        head_keep(w).wait()
        keep(w).wait()
        head_swap_back(w).wait()
        trade_z(w).wait()


def weight_grads(gp, gqk, gh, gd, lhs, wgt, wut, wd, tok, nxt, dq, dk, dv, po):
    shard, width = tok.shape[1], tok.shape[2]
    f = lhs.shape[2]
    local = dq.shape[2]
    block = width // 8
    bf = jnp.bfloat16
    f32 = jnp.float32
    dma = pltpu.SemaphoreType.DMA
    shape = jax.ShapeDtypeStruct
    vm = pl.BlockSpec(memory_space=pltpu.VMEM)
    flops = 2 * 4 * shard * 4 * f * (3 * width + 3 * width // 2)
    return pl.pallas_call(
        grads_kernel,
        name="weight_grads",
        input_output_aliases={2: 4, 3: 5},
        out_shape=(
            shape((4, width), f32),
            shape((3, 2, local // 2, block), bf),
            shape((4, local, block), bf),
            shape((3, 2, f, block), bf),
            shape(gh.shape, bf),
            shape(gd.shape, bf),
        ),
        in_specs=[vm] * 2 + [FULL] * 12,
        out_specs=(vm,) + (FULL,) * 5,
        scratch_shapes=[
            pltpu.VMEM((2, 4, shard, width), bf),
            pltpu.VMEM((2, f, width), bf),
            pltpu.VMEM((4, 2, 4, shard, width // 2), bf),
            pltpu.VMEM((2, f, width // 2), bf),
            pltpu.VMEM((3, 2, 4, shard, local // 2), bf),
            pltpu.VMEM((local // 2, 8 * shard), bf),
            pltpu.VMEM((3, f, 16 * shard), bf),
            pltpu.VMEM((3, 4, 2, local // 2, block), bf),
            pltpu.VMEM((3, 3, 2, local // 2, block), bf),
            pltpu.VMEM((3, 2, local // 2, block), bf),
            pltpu.VMEM((3, 2, 2, f, block), bf),
            pltpu.VMEM((3, 2, f, block), bf),
            pltpu.VMEM((4, 8, width), f32),
            pltpu.VMEM((6, 8, width), f32),
            dma((25,)),
            dma((15,)), dma((15,)), dma((15, 2)), dma((15, 2)),
            dma((3,)), dma((3,)), dma((3,)), dma((3,)),
            dma((3, 3)), dma((3, 3)), dma((3,)), dma((3,)),
            dma((3,)), dma((3,)), dma((3,)), dma((3,)),
            dma((7,)), dma((6,)), dma((6,)), dma((3, 3)), dma((15,)), dma((2, 2)),
        ],
        compiler_params=pltpu.CompilerParams(
            collective_id=0, has_side_effects=True, vmem_limit_bytes=60 * 1024 * 1024
        ),
        cost_estimate=pl.CostEstimate(flops=flops, bytes_accessed=60 * 1024 * 1024, transcendentals=0),
    )(gp, gqk, gh, gd, lhs, wgt, wut, wd, tok, nxt, dq, dk, dv, po)


def far_copy(src, dst, ss, rs, dd, tt):
    return pltpu.make_async_remote_copy(
        src_ref=src, dst_ref=dst, send_sem=ss, recv_sem=rs, device_id=(dd, tt), device_id_type=MESH
    )


def mean_inv(values):
    return lax.rsqrt(jnp.mean(values * values, axis=1, keepdims=True) + EPS)


def mlp_kernel(
    att_ref, tok_ref, cot_ref, ga_ref, gm_ref, wg_ref, wu_ref, wd_ref,
    out_ref, ghid_ref, dat_ref, gain_ref, gh_ref, gd_ref,
    wg_v, wu_v, wd_v, slope_g, slope_u, buf, low_a, low_b, part, pmate, xsend, xrecv, hid,
    w_sem, as_s, as_r, ax_s, ax_r, af_s, af_r, ps_s, ps_r, px_s, px_r, zs_s, zs_r, ds_s, ds_r, hc_s, hc_r, st_sem,
):
    d, t, z, y, c, chip, mate, across = places()
    shard, width = att_ref.shape
    ff = wg_v.shape[1]
    bf = jnp.bfloat16
    f32 = jnp.float32
    tile = 512
    tiles = ff // tile
    small = shard // 2
    two = 2 * shard
    half = width // 2

    def wcopy(i, j):
        cols = pl.ds(j * tile, tile)
        if i == 0:
            return pltpu.make_async_copy(wg_ref.at[:, cols], wg_v.at[:, cols], w_sem.at[0, j])
        if i == 1:
            return pltpu.make_async_copy(wu_ref.at[:, cols], wu_v.at[:, cols], w_sem.at[1, j])
        return pltpu.make_async_copy(wd_ref.at[cols, :], wd_v.at[cols, :], w_sem.at[2, j])

    for j in range(tiles):
        wcopy(0, j).start()
        wcopy(1, j).start()
    for j in range(tiles):
        wcopy(2, j).start()
    greet([(((z + 1) % 4) * 2 + y, t), (((z + 3) % 4) * 2 + y, t), (d, mate), (d, across)])

    def send_mate(p, b):
        return far_copy(buf.at[p, b, c], buf.at[p, b, c], as_s.at[p, b], as_r.at[p, b], d, mate)

    def send_across(p, b):
        return far_copy(buf.at[p, b, c], buf.at[p, b, 2 + c], ax_s.at[p, b], ax_r.at[p, b], d, across)

    def forward(p, b):
        return far_copy(buf.at[p, b, 2 + c], buf.at[p, b, 2 + c], af_s.at[p, b], af_r.at[p, b], d, mate)

    def part_mate(p, b, h):
        return far_copy(part.at[p, b, h, 1 - c], pmate.at[p, b, h], ps_s.at[p, b, h], ps_r.at[p, b, h], d, mate)

    def part_across(p, b, h):
        return far_copy(xsend.at[p, b, h], xrecv.at[p, b, h], px_s.at[p, b, h], px_r.at[p, b, h], d, across)

    groups = (gh_ref, gd_ref)
    lines_h = [Line(gh_ref, z, y, t, q, zs_s.at[i], zs_r.at[i]) for i, q in enumerate((t, across))]
    lines_d = [Line(gd_ref, z, y, t, t, ds_s, ds_r)]
    ranks = rank_rows(z)

    def line_src(p, i):
        return buf.at[p, :, c if i == 0 else 2 + c]

    def row_c(n, i):
        cell = gh_ref.at[ranks[1 + n], t if i == 0 else across]
        return far_copy(cell, cell, hc_s.at[n, i], hc_r.at[n, i], d, mate)

    def store_row(p):
        mine = groups[p].at[z]
        return [
            pltpu.make_async_copy(buf.at[p, :, i], mine.at[q], st_sem.at[p, i])
            for i, q in enumerate((chip * 2, chip * 2 + 1, 2 - chip * 2, 3 - chip * 2))
        ]

    def inner(p, b):
        rows = pl.ds(b * two, two)
        both = buf[p, b].reshape(two, width)
        for j in range(tiles):
            cols = pl.ds(j * tile, tile)
            if p == 0:
                if b == 0:
                    wcopy(0, j).wait()
                    wcopy(1, j).wait()
                g = jnp.dot(both, wg_v[:, cols], preferred_element_type=f32)
                u = jnp.dot(both, wu_v[:, cols], preferred_element_type=f32)
                sg = jax.nn.sigmoid(g)
                gs = g * sg
                low_a[:, cols] = (gs * u).astype(bf)
                slope_u[rows, cols] = gs
                slope_g[rows, cols] = u * sg * (1.0 + g * (1.0 - sg))
            else:
                di = lax.dot_general(both, wd_v[cols, :], NT, preferred_element_type=f32)
                low_a[:, cols] = (di * slope_g[rows, cols]).astype(bf)
                low_b[:, cols] = (di * slope_u[rows, cols]).astype(bf)

    def combine(p, b, h):
        part_mate(p, b, h).wait_recv()
        xsend[p, b, h] = (part[p, b, h, c, 1].astype(f32) + pmate[p, b, h, 1].astype(f32)).astype(bf)
        part_across(p, b, h).start()

    def outer(p, b):
        if p == 0 and b == 0:
            for j in range(tiles):
                wcopy(2, j).wait()
        for h in range(2):
            for j in range(half // tile):
                cols = pl.ds(h * half + j * tile, tile)
                if p == 0:
                    new = jnp.dot(low_a[...], wd_v[:, cols], preferred_element_type=f32)
                else:
                    new = lax.dot_general(
                        low_a[...], wg_v[cols, :], NT, preferred_element_type=f32
                    ) + lax.dot_general(low_b[...], wu_v[cols, :], NT, preferred_element_type=f32)
                new = new.astype(bf)
                for i in range(4):
                    part[p, b, h, i % 2, i // 2, :, pl.ds(j * tile, tile)] = new[i * small : (i + 1) * small]
            part_mate(p, b, h).start()
            if h == 1:
                combine(p, b, 0)
        combine(p, b, 1)

    def whole(p, b):
        sums = []
        for h in range(2):
            part_across(p, b, h).wait_recv()
            sums.append(
                part[p, b, h, c, 0].astype(f32) + pmate[p, b, h, 0].astype(f32) + xrecv[p, b, h].astype(f32)
            )
        return jnp.concatenate(sums, axis=1)

    def launch(p, b):
        send_across(p, b).start()
        send_mate(p, b).start()

    def arrive(p, b):
        send_mate(p, b).wait_recv()
        send_across(p, b).wait_recv()
        forward(p, b).start()
        forward(p, b).wait_recv()

    def rows_of(b):
        return slice(b * small, (b + 1) * small)

    def middle(b):
        r = rows_of(b)
        mlp = whole(0, b)
        rf = mean_inv(mlp)
        fh = mlp * rf
        gy = cot_ref[r, :].astype(f32)
        out_ref[r, :] = (hid[r, :] + fh * gm_ref[...]).astype(bf)
        scaled = gy * gm_ref[...]
        buf[1, b, c] = (rf * (scaled - fh * jnp.mean(scaled * fh, axis=1, keepdims=True))).astype(bf)
        launch(1, b)
        gain = jnp.sum(gy * fh, axis=0, keepdims=True)
        gain_ref[1:2, :] = gain if b == 0 else gain_ref[1:2, :] + gain

    def last(b):
        r = rows_of(b)
        gh = cot_ref[r, :].astype(f32) + whole(1, b)
        ghid_ref[r, :] = gh
        att = att_ref[r, :]
        ra = mean_inv(att)
        ah = att * ra
        gain = jnp.sum(gh * ah, axis=0, keepdims=True)
        gain_ref[0:1, :] = gain if b == 0 else gain_ref[0:1, :] + gain
        scaled = gh * ga_ref[...]
        dat_ref[r, :] = (ra * (scaled - ah * jnp.mean(scaled * ah, axis=1, keepdims=True))).astype(bf)

    for b in range(2):
        r = rows_of(b)
        att = att_ref[r, :]
        hid[r, :] = tok_ref[r, :].astype(f32) + att * mean_inv(att) * ga_ref[...]
        buf[0, b, c] = hid[r, :].astype(bf)
        launch(0, b)
    lines_h[0].start(0, line_src(0, 0))
    arrive(0, 0)
    inner(0, 0)
    outer(0, 0)
    arrive(0, 1)
    lines_h[1].start(0, line_src(0, 1))
    for cp in store_row(0):
        cp.start()
    inner(0, 1)
    middle(0)
    lines_h[0].landed(0)
    lines_h[0].start(1)
    outer(0, 1)
    arrive(1, 0)
    lines_h[1].landed(0)
    lines_h[1].start(1)
    for i in range(2):
        row_c(0, i).start()
    inner(1, 0)
    middle(1)
    lines_d[0].start(0, line_src(1, 0))
    outer(1, 0)
    arrive(1, 1)
    for cp in store_row(1):
        cp.start()
    inner(1, 1)
    outer(1, 1)
    for line in lines_h:
        line.landed(1)
    for i in range(2):
        row_c(1, i).start()
    last(0)
    last(1)

    for p in range(2):
        for b in range(2):
            send_across(p, b).wait_send()
            send_mate(p, b).wait_send()
            forward(p, b).wait_send()
            for h in range(2):
                part_mate(p, b, h).wait_send()
                part_across(p, b, h).wait_send()
        for cp in store_row(p):
            cp.wait()
        for i in range(2):
            row_c(p, i).wait()
    for i in range(2):
        lines_h[i].sent(0, line_src(0, i))
        lines_h[i].sent(1)
    lines_d[0].sent(0, line_src(1, 0))
    lines_d[0].landed(0)


def mlp_both(att, tok, cot, ga, gm, wg, wu, wd):
    shard, width = tok.shape
    ff = wg.shape[1]
    bf = jnp.bfloat16
    f32 = jnp.float32
    dma = pltpu.SemaphoreType.DMA
    half = width // 2
    small = shard // 2
    vm = pl.BlockSpec(memory_space=pltpu.VMEM)
    shape = jax.ShapeDtypeStruct
    out = pl.pallas_call(
        mlp_kernel,
        name="feed_forward",
        out_shape=(
            shape((shard, width), bf),
            shape((shard, width), f32),
            shape((shard, width), bf),
            shape((2, width), f32),
            shape((4, 4, 2, small, width), bf),
            shape((4, 4, 2, small, width), bf),
        ),
        in_specs=[vm] * 5 + [FULL] * 3,
        out_specs=(vm,) * 4 + (FULL,) * 2,
        scratch_shapes=[
            pltpu.VMEM((width, ff), bf),
            pltpu.VMEM((width, ff), bf),
            pltpu.VMEM((ff, width), bf),
            pltpu.VMEM((4 * shard, ff), f32),
            pltpu.VMEM((4 * shard, ff), f32),
            pltpu.VMEM((2, 2, 4, small, width), bf),
            pltpu.VMEM((2 * shard, ff), bf),
            pltpu.VMEM((2 * shard, ff), bf),
            pltpu.VMEM((2, 2, 2, 2, 2, small, half), bf),
            pltpu.VMEM((2, 2, 2, 2, small, half), bf),
            pltpu.VMEM((2, 2, 2, small, half), bf),
            pltpu.VMEM((2, 2, 2, small, half), bf),
            pltpu.VMEM((shard, width), f32),
            dma((3, ff // 512)),
            dma((2, 2)), dma((2, 2)), dma((2, 2)), dma((2, 2)), dma((2, 2)), dma((2, 2)),
            dma((2, 2, 2)), dma((2, 2, 2)), dma((2, 2, 2)), dma((2, 2, 2)),
            dma((2, 2, 2)), dma((2, 2, 2)), dma((2, 1)), dma((2, 1)),
            dma((2, 2)), dma((2, 2)),
            dma((2, 4)),
        ],
        compiler_params=pltpu.CompilerParams(
            collective_id=1, has_side_effects=True, vmem_limit_bytes=60 * 1024 * 1024
        ),
        cost_estimate=pl.CostEstimate(
            flops=2 * 6 * 4 * shard * width * ff, bytes_accessed=40 * 1024 * 1024, transcendentals=4 * shard * ff
        ),
    )(att, tok, cot, ga.reshape(1, -1), gm.reshape(1, -1), wg, wu, wd)
    return (*out[:4], out[4].reshape(4, 4, shard, width), out[5].reshape(4, 4, shard, width))


NT = (((1,), (1,)), ((), ()))
TN = (((0,), (0,)), ((), ()))


def places():
    d = lax.axis_index("dp")
    t = lax.axis_index("tensor")
    c = t % 2
    return d, t, d // 2, d % 2, c, t // 2, t + 1 - 2 * c, (t + 2) % 4


def greet(targets):
    barrier = pltpu.get_barrier_semaphore()
    for dd, tt in targets:
        pl.semaphore_signal(barrier, inc=1, device_id=(dd, tt), device_id_type=MESH)
    pl.semaphore_wait(barrier, len(targets))


def to_rows(column):
    n = column.shape[0]
    return jnp.broadcast_to(column, (n, n)).T[0:4, :]


def to_column(rows):
    n = rows.shape[1]
    return jnp.broadcast_to(rows[0:1, :], (n, n)).T[:, 0:1]


def attend_kernel(
    len_ref, tok_ref, gq_ref, gk_ref, wq_ref, wk_ref, wv_ref, wo_ref, wg_ref, wu_ref,
    att_ref, tall_ref, tnext_ref, qh_ref, kh_ref, qr_ref, kr_ref, v_ref, mix_ref, p_ref, inv_ref, cos_ref, sin_ref, wgt_ref, wut_ref,
    w_v, wo_v, wide, tipped, tall, raw, rot, val, mixed, prob, stat, stat_in, pown, pmate, xsend, xrecv, qown, qmate,
    w_sem, as_s, as_r, ss_s, ss_r, ps_s, ps_r, px_s, px_r, pq_s, pq_r, st_sem, ns_s, ns_r, tw_sem,
):
    d, t, z, y, c, chip, mate, across = places()
    far = (mate + 2) % 4
    shard, width = tok_ref.shape
    local = w_v.shape[2]
    bf = jnp.bfloat16
    f32 = jnp.float32
    heads = local // HD
    weights = [
        pltpu.make_async_copy(r, w_v.at[i], w_sem.at[i]) for i, r in enumerate((wq_ref, wk_ref, wv_ref))
    ] + [pltpu.make_async_copy(wo_ref, wo_v, w_sem.at[3])]
    for cp in weights:
        cp.start()
    span = wide.shape[2]
    side = z % 2
    tips = [
        pltpu.make_async_copy(r.at[:, pl.ds(side * span, span)], wide.at[i], tw_sem.at[i])
        for i, r in enumerate((wg_ref, wu_ref))
    ]
    for cp in tips:
        cp.start()
    drops = [
        pltpu.make_async_copy(tipped.at[i], r, tw_sem.at[2 + i]) for i, r in enumerate((wgt_ref, wut_ref))
    ]

    def tip(i):
        tips[i].wait()

        def one(j, carry):
            cols = pl.ds(pl.multiple_of(j * 128, 128), 128)
            tipped[i, cols, :] = wide[i, :, cols].T
            return carry

        lax.fori_loop(0, span // 128, one, 0)
        drops[i].start()

    tall[t] = tok_ref[...]
    twin = z * 2 + 1 - y
    greet([(d, mate), (d, across), (d, far), (twin, t)])

    send_x = far_copy(tall.at[t], tall.at[t], as_s.at[0], as_r.at[0], d, across)
    send_m = far_copy(tall.at[t], tall.at[t], as_s.at[1], as_r.at[1], d, mate)
    forward = far_copy(tall.at[across], tall.at[across], as_s.at[2], as_r.at[2], d, mate)
    send_x.start()
    send_m.start()
    next_y = [
        far_copy(tall.at[q], tnext_ref.at[q], ns_s.at[i], ns_r.at[i], twin, t) for i, q in enumerate((t, across))
    ]
    next_c = [
        far_copy(tnext_ref.at[q], tnext_ref.at[q], ns_s.at[2 + i], ns_r.at[2 + i], d, mate)
        for i, q in enumerate((t, across))
    ]
    next_y[0].start()

    total = 4 * shard

    def layout(shape, dim):
        spot = lax.broadcasted_iota(jnp.int32, shape, dim)
        end = 0
        seg = jnp.zeros(shape, jnp.int32)
        start = jnp.zeros(shape, jnp.int32)
        for i in range(len_ref.shape[1]):
            size = len_ref[0, i]
            end = end + size
            past = spot >= end
            seg = seg + jnp.where(past, 1, 0)
            start = start + jnp.where(past, size, 0)
        return seg, spot - start

    def tables():
        lane = lax.broadcasted_iota(jnp.int32, (total, HD), 1)
        near = lane < HD // 2
        freq = jnp.exp(jnp.where(near, lane, lane - HD // 2).astype(f32) * (-2.0 * math.log(THETA) / HD))
        angle = layout((total, HD), 0)[1].astype(f32) * freq
        cos_ref[...] = jnp.cos(angle).reshape(4, shard, HD)
        sines = jnp.sin(angle)
        sin_ref[...] = jnp.where(near, -sines, sines).reshape(4, shard, HD)

    def project(first):
        rows = tall[pl.ds(first, 2)].reshape(2 * shard, width)
        for i in range(3):
            new = jnp.dot(rows, w_v[i], preferred_element_type=f32).reshape(2, shard, local)
            if i == 2:
                val[pl.ds(first, 2)] = new.astype(bf)
            else:
                raw[i, pl.ds(first, 2)] = new
                for s in range(2):
                    stat[first + s, i * 4 : i * 4 + 4, :] = to_rows(
                        jnp.sum(new[s] * new[s], axis=1, keepdims=True)
                    )

    here = chip * 2
    there = 2 - chip * 2
    for cp in weights[:3]:
        cp.wait()
    send_m.wait_recv()
    project(here)
    tables()
    tip(0)
    send_x.wait_recv()
    forward.start()
    next_y[1].start()
    forward.wait_recv()
    project(there)

    stats = [
        far_copy(stat, stat_in.at[i], ss_s.at[i], ss_r.at[i], d, who)
        for i, who in enumerate((mate, across, far))
    ]
    for cp in stats:
        cp.start()
    stores = [
        pltpu.make_async_copy(tall, tall_ref, st_sem.at[0]),
        pltpu.make_async_copy(val, v_ref, st_sem.at[1]),
    ]
    for cp in stores:
        cp.start()
    for cp in stats:
        cp.wait_recv()

    for q in range(4):
        inv = lax.rsqrt((stat[q] + stat_in[0, q] + stat_in[1, q] + stat_in[2, q]) / width + EPS)
        inv_ref[q] = inv
        for i, gain in ((0, gq_ref), (1, gk_ref)):
            unit = raw[i, q] * to_column(inv[i * 4 : i * 4 + 4])
            raw[i, q] = unit
            unit = unit * gain[...]
            for h in range(heads):
                cols = slice(h * HD, (h + 1) * HD)
                one = unit[:, cols]
                rot[i, q, :, cols] = (
                    one * cos_ref[q] + pltpu.roll(one, HD // 2, 1) * sin_ref[q]
                ).astype(bf)
    more = [
        pltpu.make_async_copy(raw.at[0], qh_ref, st_sem.at[2]),
        pltpu.make_async_copy(raw.at[1], kh_ref, st_sem.at[3]),
        pltpu.make_async_copy(rot.at[0], qr_ref, st_sem.at[4]),
        pltpu.make_async_copy(rot.at[1], kr_ref, st_sem.at[5]),
    ]
    for cp in more:
        cp.start()
    stores += more

    scale = 1.0 / math.sqrt(HD)
    def mix(first, n):
        ids = first * shard + lax.broadcasted_iota(jnp.int32, (2 * shard, total), 0)
        keys = lax.broadcasted_iota(jnp.int32, (2 * shard, total), 1)
        rows = first * shard + lax.broadcasted_iota(jnp.int32, (2 * shard, 1), 0)
        seg_rows = jnp.zeros((2 * shard, 1), jnp.int32)
        end = 0
        for i in range(len_ref.shape[1]):
            end = end + len_ref[0, i]
            seg_rows = seg_rows + jnp.where(rows >= end, 1, 0)
        same = seg_rows == layout((1, total), 1)[0]
        ok = same & (keys <= ids)
        for h in range(heads):
            cols = slice(h * HD, (h + 1) * HD)
            s = lax.dot_general(
                rot[0, pl.ds(first, 2), :, cols].reshape(2 * shard, HD),
                rot[1, :, :, cols].reshape(total, HD),
                NT,
                preferred_element_type=f32,
            )
            s = jnp.where(ok, s * scale, -1e30)
            e = jnp.exp(s - jnp.max(s, axis=1, keepdims=True))
            p = e / jnp.sum(e, axis=1, keepdims=True)
            prob[pl.ds(first, 2), h] = p.reshape(2, shard, total)
            mixed[pl.ds(first, 2), :, cols] = (
                jnp.dot(p.astype(bf), val[:, :, cols].reshape(total, HD), preferred_element_type=f32)
                .astype(bf)
                .reshape(2, shard, HD)
            )
        cp = pltpu.make_async_copy(prob.at[pl.ds(first, 2)], p_ref.at[pl.ds(first, 2)], st_sem.at[6 + n])
        cp.start()
        stores.append(cp)

    half = width // 2
    tile = 512

    def part_mate(h):
        return far_copy(pown.at[h, 1 - c], pmate.at[h], ps_s.at[h], ps_r.at[h], d, mate)

    def part_across(h):
        return far_copy(xsend.at[h], xrecv.at[h], px_s.at[h], px_r.at[h], d, across)

    part_own = far_copy(qown.at[1 - c], qmate, pq_s, pq_r, d, mate)

    mix(there, 0)
    weights[3].wait()
    for h in range(2):
        for j in range(half // tile):
            new = jnp.dot(
                mixed[pl.ds(there, 2)].reshape(2 * shard, local),
                wo_v[:, pl.ds(h * half + j * tile, tile)],
                preferred_element_type=f32,
            ).astype(bf)
            pown[h, :, :, pl.ds(j * tile, tile)] = new.reshape(2, shard, tile)
        part_mate(h).start()
    for h in range(2):
        part_mate(h).wait_recv()
        xsend[h] = (pown[h, c].astype(f32) + pmate[h].astype(f32)).astype(bf)
        part_across(h).start()
    mix(here, 1)
    for j in range(width // tile):
        new = jnp.dot(
            mixed[pl.ds(here, 2)].reshape(2 * shard, local),
            wo_v[:, pl.ds(j * tile, tile)],
            preferred_element_type=f32,
        ).astype(bf)
        qown[:, :, pl.ds(j * tile, tile)] = new.reshape(2, shard, tile)
    part_own.start()
    cp = pltpu.make_async_copy(mixed, mix_ref, st_sem.at[8])
    cp.start()
    stores.append(cp)
    for cp in next_y:
        cp.wait_recv()
    for cp in next_c:
        cp.start()
    tip(1)
    stores += drops
    part_own.wait_recv()
    for h in range(2):
        part_across(h).wait_recv()
        cols = slice(h * half, (h + 1) * half)
        att_ref[:, cols] = (
            qown[c, :, cols].astype(f32) + qmate[:, cols].astype(f32) + xrecv[h].astype(f32)
        )
    for cp in stores:
        cp.wait()
    for cp in next_c:
        cp.wait_recv()
    for cp in [send_x, send_m, forward, part_own] + next_y + next_c + stats:
        cp.wait_send()
    for h in range(2):
        part_mate(h).wait_send()
        part_across(h).wait_send()


def attend_both(lengths, tok, gq, gk, wq, wk, wv, wo, wg, wu):
    shard, width = tok.shape
    local = wq.shape[1]
    heads = local // HD
    bf = jnp.bfloat16
    f32 = jnp.float32
    dma = pltpu.SemaphoreType.DMA
    vm = pl.BlockSpec(memory_space=pltpu.VMEM)
    shape = jax.ShapeDtypeStruct
    half = width // 2
    total = 4 * shard
    return pl.pallas_call(
        attend_kernel,
        name="attend_forward",
        out_shape=(
            shape((shard, width), f32),
            shape((4, shard, width), bf),
            shape((4, shard, width), bf),
            shape((4, shard, local), f32),
            shape((4, shard, local), f32),
            shape((4, shard, local), bf),
            shape((4, shard, local), bf),
            shape((4, shard, local), bf),
            shape((4, shard, local), bf),
            shape((4, heads, shard, total), f32),
            shape((4, 8, shard), f32),
            shape((4, shard, HD), f32),
            shape((4, shard, HD), f32),
            shape((wg.shape[1] // 2, width), bf),
            shape((wg.shape[1] // 2, width), bf),
        ),
        in_specs=[pl.BlockSpec(memory_space=pltpu.SMEM)] + [vm] * 3 + [FULL] * 6,
        out_specs=(vm,) + (FULL,) * 9 + (vm,) * 3 + (FULL,) * 2,
        scratch_shapes=[
            pltpu.VMEM((3, width, local), bf),
            pltpu.VMEM((local, width), bf),
            pltpu.VMEM((2, width, wg.shape[1] // 2), bf),
            pltpu.VMEM((2, wg.shape[1] // 2, width), bf),
            pltpu.VMEM((4, shard, width), bf),
            pltpu.VMEM((2, 4, shard, local), f32),
            pltpu.VMEM((2, 4, shard, local), bf),
            pltpu.VMEM((4, shard, local), bf),
            pltpu.VMEM((4, shard, local), bf),
            pltpu.VMEM((4, heads, shard, total), f32),
            pltpu.VMEM((4, 8, shard), f32),
            pltpu.VMEM((3, 4, 8, shard), f32),
            pltpu.VMEM((2, 2, shard, half), bf),
            pltpu.VMEM((2, shard, half), bf),
            pltpu.VMEM((2, shard, half), bf),
            pltpu.VMEM((2, shard, half), bf),
            pltpu.VMEM((2, shard, width), bf),
            pltpu.VMEM((shard, width), bf),
            dma((4,)),
            dma((3,)), dma((3,)), dma((3,)), dma((3,)),
            dma((2,)), dma((2,)), dma((2,)), dma((2,)),
            dma(()), dma(()),
            dma((9,)),
            dma((4,)), dma((4,)), dma((4,)),
        ],
        compiler_params=pltpu.CompilerParams(
            collective_id=2, has_side_effects=True, vmem_limit_bytes=56 * 1024 * 1024
        ),
        cost_estimate=pl.CostEstimate(
            flops=2 * total * width * local * 4, bytes_accessed=24 * 1024 * 1024, transcendentals=heads * total * total
        ),
    )(
        lengths, tok, gq.reshape(1, -1), gk.reshape(1, -1), wq, wk, wv, wo, wg, wu,
    )


def rank_rows(z):
    return (z, z + 1 - 2 * (z % 2), 2 - z // 2, 3 - 3 * (z // 2))


class Line:
    def __init__(self, ref, z, y, t, q, send, recv):
        self.ref, self.z, self.t, self.q, self.send, self.recv = ref, z, t, q, send, recv
        self.up = ((z + 1) % 4) * 2 + y
        self.down = ((z + 3) % 4) * 2 + y

    def go(self, way, i, r, src=None):
        cell = self.ref.at[r, self.q]
        return far_copy(
            cell if src is None else src, cell, self.send.at[way, i], self.recv.at[way, i], (self.up, self.down)[way], self.t
        )

    def hops(self, step, src=None):
        z = self.z
        if step == 0:
            return [(z < 3, 0, z), (z > 0, 1, z)]
        if step == 1:
            middle = (z > 0) & (z < 3)
            return [(middle, 0, (z + 3) % 4), (middle, 1, (z + 1) % 4)]
        return [(z == 2, 0, 0), (z == 1, 1, 3)]

    def lands(self, step):
        z = self.z
        if step == 0:
            return [(z > 0, 0, (z + 3) % 4), (z < 3, 1, (z + 1) % 4)]
        if step == 1:
            return [(z > 1, 0, (z + 2) % 4), (z < 2, 1, (z + 2) % 4)]
        return [(z == 3, 0, 0), (z == 0, 1, 3)]

    def start(self, step, src=None):
        for ok, way, r in self.hops(step):
            pl.when(ok)(self.go(way, step, r, src).start)

    def sent(self, step, src=None):
        for ok, way, r in self.hops(step):
            pl.when(ok)(self.go(way, step, r, src).wait_send)

    def landed(self, step):
        for ok, way, r in self.lands(step):
            pl.when(ok)(self.go(way, step, r).wait_recv)


def attend_back_kernel(
    dat_ref, ghid_ref, cos_ref, sin_ref, gq_ref, gk_ref, inv_ref,
    wq_ref, wk_ref, wv_ref, wo_ref, qh_ref, kh_ref, qr_ref, kr_ref, v_ref, p_ref, mix_ref, wgt_ref, wut_ref, gh_in, gd_in,
    gt_ref, gain_ref, dq_ref, dk_ref, dv_ref, po_ref, lhs_ref, gh_ref, gd_ref,
    w_v, wo_v, dall, unit, rot, val, dmix, prob, scaled, low, mixed, lhs_t, full, part, tip_v, hb_v, made, stat, stat_in, pown, pmate, xsend, xrecv, qown, qmate,
    w_sem, as_s, as_r, hx_s, hx_r, hc_s, hc_r, ss_s, ss_r, ps_s, ps_r, px_s, px_r, pq_s, pq_r, ys_s, ys_r, zs_s, zs_r, hz_s, hz_r, st_sem, hb_sem, made_sem,
):
    d, t, z, y, c, chip, mate, across = places()
    far = (mate + 2) % 4
    shard, width = dat_ref.shape
    local = w_v.shape[2]
    bf = jnp.bfloat16
    f32 = jnp.float32
    heads = local // HD
    total = 4 * shard
    sources = (wo_ref, wgt_ref, wut_ref, mix_ref, v_ref, p_ref, qr_ref, kr_ref, qh_ref, kh_ref, wq_ref, wk_ref, wv_ref)
    homes = (wo_v, tip_v.at[0], tip_v.at[1], mixed, val, prob, rot.at[0], rot.at[1], unit.at[0], unit.at[1], w_v.at[0], w_v.at[1], w_v.at[2])
    loads = [pltpu.make_async_copy(a, b, w_sem.at[i]) for i, (a, b) in enumerate(zip(sources, homes))]
    for cp in loads:
        cp.start()
    dall[t] = dat_ref[...]
    twin = z * 2 + 1 - y
    above = ((z + 1) % 4) * 2 + y
    below = ((z + 3) % 4) * 2 + y
    greet([(d, mate), (d, across), (d, far), (twin, t), (above, t), (below, t)])

    line_h = Line(gh_ref, z, y, t, t, hz_s, hz_r)
    line_d = Line(gd_ref, z, y, t, t, zs_s, zs_r)
    line_h.start(2)
    line_d.start(1)
    ranks = rank_rows(z)
    edge = (z == 0) | (z == 3)

    def hb_load(n):
        return pltpu.make_async_copy(gh_ref.at[ranks[n]], hb_v.at[n % 2], hb_sem.at[n])

    hb_load(0).start()
    hb_load(1).start()

    def made_out(n):
        return pltpu.make_async_copy(made, lhs_ref.at[n], made_sem.at[n])

    def remake(n):
        hb_load(n).wait()
        if n > 0:
            made_out(n - 1).wait()

        def wide(j, carry):
            cols = pl.ds(pl.multiple_of(j * 512, 512), 512)
            hb = hb_v[n % 2].reshape(total, width)
            g = lax.dot_general(tip_v[0, cols, :], hb, NT, preferred_element_type=f32)
            u = lax.dot_general(tip_v[1, cols, :], hb, NT, preferred_element_type=f32)
            sg = jax.nn.sigmoid(g)
            gs = g * sg
            made[0, cols, :] = (gs * u).astype(bf)
            made[1, cols, :] = (u * sg * (1.0 + g * (1.0 - sg))).astype(bf)
            made[2, cols, :] = gs.astype(bf)
            return carry

        lax.fori_loop(0, made.shape[1] // 512, wide, 0)
        made_out(n).start()

    send_x = far_copy(dall.at[t], dall.at[t], as_s.at[0], as_r.at[0], d, across)
    send_m = far_copy(dall.at[t], dall.at[t], as_s.at[1], as_r.at[1], d, mate)
    forward = far_copy(dall.at[across], dall.at[across], as_s.at[2], as_r.at[2], d, mate)
    send_x.start()
    send_m.start()
    last = ranks[3]
    row_x = far_copy(gh_ref.at[last, t], gh_ref.at[last, t], hx_s, hx_r, d, across)
    row_c = [
        far_copy(gh_ref.at[last, q], gh_ref.at[last, q], hc_s.at[j], hc_r.at[j], d, mate)
        for j, q in enumerate((t, across))
    ]
    swap_y = far_copy(full.at[:, 1 - y], part, ys_s, ys_r, twin, t)

    def project(first):
        rows = dall[pl.ds(first, 2)].reshape(2 * shard, width)
        dmix[pl.ds(first, 2)] = (
            lax.dot_general(rows, wo_v[...], NT, preferred_element_type=f32).astype(bf).reshape(2, shard, local)
        )

    here = chip * 2
    there = 2 - chip * 2
    loads[0].wait()
    send_m.wait_recv()
    project(here)
    for cp in loads[1:3]:
        cp.wait()
    remake(0)
    for cp in loads[3:]:
        cp.wait()
    send_x.wait_recv()
    forward.start()
    forward.wait_recv()
    line_h.landed(2)
    pl.when(edge)(row_x.start)
    project(there)
    lhs_t[...] = mixed[...].reshape(total, local).astype(f32).T.astype(bf)
    block = full.shape[3]
    for b in range(8):
        full[b // 2, b % 2] = jnp.dot(
            lhs_t[...], dall[:, :, b * block : (b + 1) * block].reshape(total, block), preferred_element_type=f32
        ).astype(bf)
    swap_y.start()
    stores = []

    scale = 1.0 / math.sqrt(HD)
    cos = cos_ref[...].reshape(total, HD)
    sin = sin_ref[...].reshape(total, HD)
    dots = [jnp.zeros((total, 1), f32), jnp.zeros((total, 1), f32)]
    for h in range(heads):
        cols = slice(h * HD, (h + 1) * HD)
        dm = dmix[:, :, cols].reshape(total, HD)
        p = prob[:, h].reshape(total, total)
        dp = lax.dot_general(dm, val[:, :, cols].reshape(total, HD), NT, preferred_element_type=f32)
        ds = (p * (dp - jnp.sum(p * dp, axis=1, keepdims=True))).astype(bf)
        low[2, :, :, cols] = (
            lax.dot_general(p.astype(bf), dm, TN, preferred_element_type=f32).astype(bf).reshape(4, shard, HD)
        )
        back = (
            jnp.dot(ds, rot[1, :, :, cols].reshape(total, HD), preferred_element_type=f32) * scale,
            lax.dot_general(ds, rot[0, :, :, cols].reshape(total, HD), TN, preferred_element_type=f32) * scale,
        )
        for i, gain in ((0, gq_ref), (1, gk_ref)):
            g = back[i]
            g = g * cos - pltpu.roll(g, HD // 2, 1) * sin
            u = unit[i, :, :, cols].reshape(total, HD)
            prod = g * u
            gain_ref[i : i + 1, cols] = jnp.sum(prod, axis=0, keepdims=True)
            dots[i] = dots[i] + jnp.sum(prod * gain[:, cols], axis=1, keepdims=True)
            scaled[i, :, :, cols] = (g * gain[:, cols]).reshape(4, shard, HD)
    for q in range(4):
        for i in range(2):
            stat[q, i * 4 : i * 4 + 4, :] = to_rows(dots[i][q * shard : (q + 1) * shard])
    stats = [
        far_copy(stat, stat_in.at[i], ss_s.at[i], ss_r.at[i], d, who)
        for i, who in enumerate((mate, across, far))
    ]
    for cp in stats:
        cp.start()
    for cp in stats:
        cp.wait_recv()

    def finish(first):
        for s in range(2):
            q = first + s
            mean = (stat[q] + stat_in[0, q] + stat_in[1, q] + stat_in[2, q]) / width
            inv = inv_ref[q]
            for i in range(2):
                low[i, q] = (
                    to_column(inv[i * 4 : i * 4 + 4])
                    * (scaled[i, q] - unit[i, q] * to_column(mean[i * 4 : i * 4 + 4]))
                ).astype(bf)

    half = width // 2
    tile = 512

    def part_mate(h):
        return far_copy(pown.at[h, 1 - c], pmate.at[h], ps_s.at[h], ps_r.at[h], d, mate)

    def part_across(h):
        return far_copy(xsend.at[h], xrecv.at[h], px_s.at[h], px_r.at[h], d, across)

    part_own = far_copy(qown.at[1 - c], qmate, pq_s, pq_r, d, mate)

    def result(first, start):
        new = None
        for i in range(3):
            one = lax.dot_general(
                low[i, pl.ds(first, 2)].reshape(2 * shard, local),
                w_v[i, pl.ds(start, tile), :],
                NT,
                preferred_element_type=f32,
            )
            new = one if new is None else new + one
        return new.astype(bf).reshape(2, shard, tile)

    finish(there)
    for h in range(2):
        for j in range(half // tile):
            pown[h, :, :, pl.ds(j * tile, tile)] = result(there, h * half + j * tile)
        part_mate(h).start()
        part_mate(h).wait_recv()
        xsend[h] = (pown[h, c].astype(f32) + pmate[h].astype(f32)).astype(bf)
        part_across(h).start()
    line_d.landed(1)
    line_d.start(2)
    pl.when(edge)(row_x.wait_recv)
    for cp in row_c:
        cp.start()
    finish(here)
    more = [
        pltpu.make_async_copy(low.at[i], r, st_sem.at[1 + i]) for i, r in enumerate((dq_ref, dk_ref, dv_ref))
    ]
    for cp in more:
        cp.start()
    stores += more
    for j in range(width // tile):
        qown[:, :, pl.ds(j * tile, tile)] = result(here, j * tile)
    part_own.start()
    remake(1)
    swap_y.wait_recv()
    for b in range(4):
        part[b] = (part[b].astype(f32) + full[b, y].astype(f32)).astype(bf)
    keep = pltpu.make_async_copy(part, po_ref, st_sem.at[0])
    keep.start()
    stores.append(keep)
    part_own.wait_recv()
    for h in range(2):
        part_across(h).wait_recv()
        cols = slice(h * half, (h + 1) * half)
        gt_ref[:, cols] = (
            ghid_ref[:, cols]
            + (qown[c, :, cols].astype(f32) + qmate[:, cols].astype(f32) + xrecv[h].astype(f32))
        ).astype(bf)
    for cp in stores:
        cp.wait()
    for cp in row_c:
        cp.wait()
    pl.when(edge)(row_x.wait_send)
    line_h.sent(2)
    line_d.sent(1)
    line_d.landed(2)
    line_d.sent(2)
    made_out(1).wait()
    for cp in [send_x, send_m, forward, part_own, swap_y] + stats:
        cp.wait_send()
    for h in range(2):
        part_mate(h).wait_send()
        part_across(h).wait_send()


def attend_back_both(dat, ghid, cos, sin, gq, gk, inv, wq, wk, wv, wo, qh, kh, qr, kr, v, p, mix, wgt, wut, gh, gd):
    shard, width = dat.shape
    local = wq.shape[1]
    heads = local // HD
    bf = jnp.bfloat16
    f32 = jnp.float32
    dma = pltpu.SemaphoreType.DMA
    vm = pl.BlockSpec(memory_space=pltpu.VMEM)
    shape = jax.ShapeDtypeStruct
    half = width // 2
    total = 4 * shard
    return pl.pallas_call(
        attend_back_kernel,
        name="attend_backward",
        out_shape=(
            shape((shard, width), bf),
            shape((2, local), f32),
            shape((4, shard, local), bf),
            shape((4, shard, local), bf),
            shape((4, shard, local), bf),
            shape((4, local, width // 8), bf),
            shape((2, 3, wgt.shape[0], total), bf),
            shape(gh.shape, bf),
            shape(gd.shape, bf),
        ),
        in_specs=[vm] * 7 + [FULL] * 15,
        out_specs=(vm,) * 2 + (FULL,) * 7,
        input_output_aliases={20: 7, 21: 8},
        scratch_shapes=[
            pltpu.VMEM((3, width, local), bf),
            pltpu.VMEM((local, width), bf),
            pltpu.VMEM((4, shard, width), bf),
            pltpu.VMEM((2, 4, shard, local), f32),
            pltpu.VMEM((2, 4, shard, local), bf),
            pltpu.VMEM((4, shard, local), bf),
            pltpu.VMEM((4, shard, local), bf),
            pltpu.VMEM((4, heads, shard, total), f32),
            pltpu.VMEM((2, 4, shard, local), f32),
            pltpu.VMEM((3, 4, shard, local), bf),
            pltpu.VMEM((4, shard, local), bf),
            pltpu.VMEM((local, total), bf),
            pltpu.VMEM((4, 2, local, width // 8), bf),
            pltpu.VMEM((4, local, width // 8), bf),
            pltpu.VMEM((2, wgt.shape[0], width), bf),
            pltpu.VMEM((2, 4, shard, width), bf),
            pltpu.VMEM((3, wgt.shape[0], total), bf),
            pltpu.VMEM((4, 8, shard), f32),
            pltpu.VMEM((3, 4, 8, shard), f32),
            pltpu.VMEM((2, 2, shard, half), bf),
            pltpu.VMEM((2, shard, half), bf),
            pltpu.VMEM((2, shard, half), bf),
            pltpu.VMEM((2, shard, half), bf),
            pltpu.VMEM((2, shard, width), bf),
            pltpu.VMEM((shard, width), bf),
            dma((13,)),
            dma((3,)), dma((3,)), dma(()), dma(()), dma((2,)), dma((2,)), dma((3,)), dma((3,)),
            dma((2,)), dma((2,)), dma((2,)), dma((2,)),
            dma(()), dma(()), dma(()), dma(()),
            dma((2, 3)), dma((2, 3)), dma((2, 3)), dma((2, 3)),
            dma((4,)), dma((3,)), dma((3,)),
        ],
        compiler_params=pltpu.CompilerParams(
            collective_id=3, has_side_effects=True, vmem_limit_bytes=56 * 1024 * 1024
        ),
        cost_estimate=pl.CostEstimate(
            flops=2 * total * width * local * 4 + 10 * heads * total * total * HD,
            bytes_accessed=24 * 1024 * 1024,
            transcendentals=0,
        ),
    )(
        dat, ghid, cos.reshape(4, shard, HD), sin.reshape(4, shard, HD), gq.reshape(1, -1), gk.reshape(1, -1), inv,
        wq, wk, wv, wo, qh, kh, qr, kr, v, p, mix, wgt, wut, gh, gd,
    )


def place_kernel(
    a_ref, p_ref, m_ref, n_ref, q_ref, k_ref, v_ref, o_ref, g_ref, u_ref, d_ref, gq_ref, gk_ref, ga_ref, gm_ref,
    a_v, p_v, m_v, head_v, o_v, gu_v, d_v, in_sem, out_sem,
):
    f32 = jnp.float32
    n = a_v.shape[2]
    f = m_v.shape[2]
    loads = [pltpu.make_async_copy(m_ref.at[w], m_v.at[w], in_sem.at[w]) for w in range(3)] + [
        pltpu.make_async_copy(p_ref, p_v, in_sem.at[3]),
        pltpu.make_async_copy(a_ref, a_v, in_sem.at[4]),
    ]
    for cp in loads:
        cp.start()
    stores = []

    def store(src, dst):
        cp = pltpu.make_async_copy(src, dst, out_sem.at[len(stores)])
        cp.start()
        stores.append(cp)

    local = gq_ref.shape[1]
    gq_ref[...] = n_ref[2:3, :local]
    gk_ref[...] = n_ref[3:4, :local]
    ga_ref[...] = n_ref[0:1, :]
    gm_ref[...] = n_ref[1:2, :]
    loads[0].wait()
    for i in range(2):
        d_v[i * f : (i + 1) * f, :] = m_v[0, i].astype(f32)
    store(d_v, d_ref)
    for w, ref in ((1, g_ref), (2, u_ref)):
        loads[w].wait()
        for i in range(2):
            gu_v[w - 1, :, i * f : (i + 1) * f] = m_v[w, i].T.astype(f32)
        store(gu_v.at[w - 1], ref)
    loads[3].wait()
    new = p_v[0].astype(f32)
    for i in range(1, 4):
        new = new + p_v[i].astype(f32)
    o_v[...] = new
    store(o_v, o_ref)
    loads[4].wait()
    for w, ref in ((0, v_ref), (1, q_ref), (2, k_ref)):
        for i in range(2):
            head_v[w, :, i * n : (i + 1) * n] = a_v[w, i].T.astype(f32)
        store(head_v.at[w], ref)
    for cp in stores:
        cp.wait()


def place_grads(attn, proj, mlp, gains):
    _, f, block = proj.shape
    width = gains.shape[1]
    f32 = jnp.float32
    vm = pl.BlockSpec(memory_space=pltpu.VMEM)
    shape = jax.ShapeDtypeStruct
    return pl.pallas_call(
        place_kernel,
        name="place_grads",
        out_shape=(
            shape((block, f), f32),
            shape((block, f), f32),
            shape((block, f), f32),
            shape((f, block), f32),
            shape((block, 4 * f), f32),
            shape((block, 4 * f), f32),
            shape((4 * f, block), f32),
            shape((1, f), f32),
            shape((1, f), f32),
            shape((1, width), f32),
            shape((1, width), f32),
        ),
        in_specs=[FULL] * 3 + [vm],
        out_specs=(FULL,) * 7 + (vm,) * 4,
        scratch_shapes=[
            pltpu.VMEM(attn.shape, attn.dtype),
            pltpu.VMEM(proj.shape, proj.dtype),
            pltpu.VMEM(mlp.shape, mlp.dtype),
            pltpu.VMEM((3, block, f), f32),
            pltpu.VMEM((f, block), f32),
            pltpu.VMEM((2, block, 4 * f), f32),
            pltpu.VMEM((4 * f, block), f32),
            pltpu.SemaphoreType.DMA((5,)),
            pltpu.SemaphoreType.DMA((7,)),
        ],
        compiler_params=pltpu.CompilerParams(vmem_limit_bytes=60 * 1024 * 1024),
    )(attn, proj, mlp, gains)


def plain_body(
    tokens,
    lengths,
    w_query,
    w_key,
    w_value,
    w_out,
    w_gate,
    w_up,
    w_down,
    gain_query,
    gain_key,
    gain_attn,
    gain_mlp,
    cotangent,
):
    rows_dev = lengths.shape[0]
    model_width = w_query.shape[0]
    local_width = w_query.shape[1]
    head_count = local_width // HD
    gathered = lax.all_gather(tokens, "tensor", axis=0, tiled=True)
    row_count = gathered.shape[0]
    segment, offsets = jax.vmap(row_layout)(lengths)
    queries = jnp.dot(gathered, w_query, preferred_element_type=jnp.float32)
    keys_raw = jnp.dot(gathered, w_key, preferred_element_type=jnp.float32)
    values_low = jnp.dot(gathered, w_value, preferred_element_type=jnp.float32).astype(jnp.bfloat16)
    q_total, k_total = lax.psum(
        (jnp.sum(queries * queries, axis=1), jnp.sum(keys_raw * keys_raw, axis=1)), "tensor"
    )
    q_inv = lax.rsqrt(q_total / model_width + EPS)[:, None]
    k_inv = lax.rsqrt(k_total / model_width + EPS)[:, None]
    q_unit = queries * q_inv
    k_unit = keys_raw * k_inv

    def to_heads(values):
        return values.reshape(rows_dev, ROW_LEN, head_count, HD)

    queries_low = rotate(to_heads(q_unit * gain_query), offsets, 1.0).astype(jnp.bfloat16)
    keys_low = rotate(to_heads(k_unit * gain_key), offsets, 1.0).astype(jnp.bfloat16)
    values_heads = to_heads(values_low)
    mixed_heads, log_total = jax.vmap(lambda *a: attend(a))(
        queries_low, keys_low, values_heads, segment
    )
    mixed_low = mixed_heads.reshape(row_count, local_width)
    attn_out = lax.psum_scatter(
        jnp.dot(mixed_low, w_out, preferred_element_type=jnp.float32).astype(jnp.bfloat16),
        "tensor",
        scatter_dimension=0,
        tiled=True,
    ).astype(jnp.float32)
    inner_count = lax.axis_size("dp") // OUTER
    a_inv = lax.rsqrt(jnp.mean(attn_out * attn_out, axis=1, keepdims=True) + EPS)
    a_unit = attn_out * a_inv
    hidden = tokens.astype(jnp.float32) + a_unit * gain_attn
    hidden_low = hidden.astype(jnp.bfloat16)
    hidden_all = lax.all_gather(hidden_low, "tensor", axis=0, tiled=True)
    outer_index = lax.axis_index("dp") // inner_count

    def gather_group(shard):
        groups = [[z * inner_count + i for z in range(OUTER)] for i in range(inner_count)]
        part = lax.all_gather(shard, "dp", axis=0, tiled=True, axis_index_groups=groups)
        return lax.all_gather(part, "tensor", axis=0, tiled=True)

    hidden_group = gather_group(hidden_low)
    gate_acts = jnp.dot(hidden_all, w_gate, preferred_element_type=jnp.float32)
    up_acts = jnp.dot(hidden_all, w_up, preferred_element_type=jnp.float32)
    gate_sigmoid = jax.nn.sigmoid(gate_acts)
    inner_low = (gate_acts * gate_sigmoid * up_acts).astype(jnp.bfloat16)
    mlp_out = lax.psum_scatter(
        jnp.dot(inner_low, w_down, preferred_element_type=jnp.float32).astype(jnp.bfloat16),
        "tensor",
        scatter_dimension=0,
        tiled=True,
    ).astype(jnp.float32)
    f_inv = lax.rsqrt(jnp.mean(mlp_out * mlp_out, axis=1, keepdims=True) + EPS)
    f_unit = mlp_out * f_inv
    output = (hidden + f_unit * gain_mlp).astype(jnp.bfloat16)
    grad_output = cotangent.astype(jnp.float32)
    grad_mlp, grad_gain_mlp_part = post_norm_back(grad_output, f_unit, f_inv, gain_mlp)
    grad_mlp_low = grad_mlp.astype(jnp.bfloat16)
    mlp_grad_all = lax.all_gather(grad_mlp_low, "tensor", axis=0, tiled=True)
    mlp_grad_group = gather_group(grad_mlp_low)
    grad_inner = times_t(mlp_grad_all, w_down)
    grad_gate_low = (
        grad_inner * up_acts * gate_sigmoid * (1.0 + gate_acts * (1.0 - gate_sigmoid))
    ).astype(jnp.bfloat16)
    grad_up_low = (grad_inner * gate_acts * gate_sigmoid).astype(jnp.bfloat16)
    part_width = w_gate.shape[1] // OUTER
    gate_part = lax.dynamic_slice_in_dim(w_gate, outer_index * part_width, part_width, 1)
    up_part = lax.dynamic_slice_in_dim(w_up, outer_index * part_width, part_width, 1)
    down_part = lax.dynamic_slice_in_dim(w_down, outer_index * part_width, part_width, 0)
    gate_g = jnp.dot(hidden_group, gate_part, preferred_element_type=jnp.float32)
    up_g = jnp.dot(hidden_group, up_part, preferred_element_type=jnp.float32)
    sig_g = jax.nn.sigmoid(gate_g)
    inner_g = (gate_g * sig_g * up_g).astype(jnp.bfloat16)
    grad_inner_g = times_t(mlp_grad_group, down_part)
    grad_gate_g = (grad_inner_g * up_g * sig_g * (1.0 + gate_g * (1.0 - sig_g))).astype(
        jnp.bfloat16
    )
    grad_up_g = (grad_inner_g * gate_g * sig_g).astype(jnp.bfloat16)
    sum_down = scatter_join(split_cols(t_times(inner_g, mlp_grad_group), inner_count), inner_count, 0)
    sum_gate = scatter_join(split_rows(t_times(hidden_group, grad_gate_g), inner_count), inner_count, 1)
    sum_up = scatter_join(split_rows(t_times(hidden_group, grad_up_g), inner_count), inner_count, 1)
    grad_hidden = grad_output + lax.psum_scatter(
        (times_t(grad_gate_low, w_gate) + times_t(grad_up_low, w_up)).astype(jnp.bfloat16),
        "tensor",
        scatter_dimension=0,
        tiled=True,
    ).astype(jnp.float32)
    grad_attn, grad_gain_attn_part = post_norm_back(grad_hidden, a_unit, a_inv, gain_attn)
    grad_attn_low = grad_attn.astype(jnp.bfloat16)
    attn_grad_all = lax.all_gather(grad_attn_low, "tensor", axis=0, tiled=True)
    grad_mixed = times_t(attn_grad_all, w_out).astype(jnp.bfloat16)
    grad_q_rot, grad_k_rot, grad_values_low = jax.vmap(lambda *a: attend_back(a))(
        queries_low, keys_low, values_heads, segment, log_total, to_heads(grad_mixed)
    )
    grad_q_norm = rotate(grad_q_rot, offsets, -1.0).reshape(row_count, local_width)
    grad_k_norm = rotate(grad_k_rot, offsets, -1.0).reshape(row_count, local_width)
    grad_gain_query_part = jnp.sum(grad_q_norm * q_unit, axis=0)
    grad_gain_key_part = jnp.sum(grad_k_norm * k_unit, axis=0)
    q_scaled = grad_q_norm * gain_query
    k_scaled = grad_k_norm * gain_key
    q_dots, k_dots = lax.psum(
        (jnp.sum(q_scaled * q_unit, axis=1), jnp.sum(k_scaled * k_unit, axis=1)), "tensor"
    )
    grad_queries_low = (q_inv * (q_scaled - q_unit * (q_dots / model_width)[:, None])).astype(
        jnp.bfloat16
    )
    grad_keys_low = (k_inv * (k_scaled - k_unit * (k_dots / model_width)[:, None])).astype(
        jnp.bfloat16
    )
    grad_values_flat = grad_values_low.reshape(row_count, local_width)
    grad_tokens = (
        grad_hidden
        + lax.psum_scatter(
            (
                times_t(grad_queries_low, w_query)
                + times_t(grad_keys_low, w_key)
                + times_t(grad_values_flat, w_value)
            ).astype(jnp.bfloat16),
            "tensor",
            scatter_dimension=0,
            tiled=True,
        ).astype(jnp.float32)
    ).astype(jnp.bfloat16)
    tensor_start = lax.axis_index("tensor") * local_width
    zero_row = jnp.zeros((model_width,), jnp.float32)
    q_full = lax.dynamic_update_slice(zero_row, grad_gain_query_part, (tensor_start,))
    k_full = lax.dynamic_update_slice(zero_row, grad_gain_key_part, (tensor_start,))
    gain_stack = jnp.stack([q_full, k_full, grad_gain_attn_part, grad_gain_mlp_part])
    gain_total = lax.psum(gain_stack, ("dp", "tensor"))
    grad_gain_query = lax.dynamic_slice(gain_total[0], (tensor_start,), (local_width,))
    grad_gain_key = lax.dynamic_slice(gain_total[1], (tensor_start,), (local_width,))
    summed = (
        scatter_sum(split_rows(t_times(gathered, grad_queries_low), inner_count), inner_count),
        scatter_sum(split_rows(t_times(gathered, grad_keys_low), inner_count), inner_count),
        scatter_sum(split_rows(t_times(gathered, grad_values_flat), inner_count), inner_count),
        scatter_sum(split_cols(t_times(mixed_low, attn_grad_all), inner_count), inner_count),
        sum_gate,
        sum_up,
        sum_down,
    )
    return (
        output,
        grad_tokens,
        summed[0],
        summed[1],
        summed[2],
        summed[3],
        summed[4],
        summed[5],
        summed[6],
        grad_gain_query,
        grad_gain_key,
        gain_total[2],
        gain_total[3],
    )


def fused_body(
    tokens,
    lengths,
    w_query,
    w_key,
    w_value,
    w_out,
    w_gate,
    w_up,
    w_down,
    gain_query,
    gain_key,
    gain_attn,
    gain_mlp,
    cotangent,
):
    (
        attn_out, tokens_all, tokens_next, q_unit, k_unit, q_rot, k_rot, values, mixed, weights, inverse,
        cosines, sines, gate_t, up_t,
    ) = attend_both(
        lengths, tokens, gain_query, gain_key, w_query, w_key, w_value, w_out, w_gate, w_up
    )
    output, grad_hidden, grad_attn, gain_parts, group_h, group_d = mlp_both(
        attn_out, tokens, cotangent, gain_attn, gain_mlp, w_gate, w_up, w_down
    )
    grad_tokens, head_gains, grad_q, grad_k, grad_v, proj, made, group_h, group_d = attend_back_both(
        grad_attn, grad_hidden, cosines, sines, gain_query, gain_key, inverse,
        w_query, w_key, w_value, w_out, q_unit, k_unit, q_rot, k_rot, values, weights, mixed, gate_t, up_t,
        group_h, group_d,
    )
    gains, attn_blocks, proj_blocks, mlp_blocks, _, _ = weight_grads(
        gain_parts, head_gains, group_h, group_d, made, gate_t, up_t, w_down, tokens_all, tokens_next, grad_q, grad_k, grad_v, proj,
    )
    placed = place_grads(attn_blocks, proj_blocks, mlp_blocks, gains)
    return (
        output,
        grad_tokens,
        *placed[:7],
        *(g.reshape(-1) for g in placed[7:]),
    )


def solution(mesh):
    placed = (
        P(("dp", "tensor"), None),
        P("dp", None),
        P(None, "tensor"),
        P(None, "tensor"),
        P(None, "tensor"),
        P("tensor", None),
        P(None, "tensor"),
        P(None, "tensor"),
        P("tensor", None),
        P("tensor"),
        P("tensor"),
        P(),
        P(),
        P(("dp", "tensor"), None),
    )
    return jax.shard_map(
        fused_body if tuple(mesh.shape.values()) == (8, 4) else plain_body,
        mesh=mesh,
        in_specs=placed,
        out_specs=(
            P(("dp", "tensor"), None),
            P(("dp", "tensor"), None),
            P("dp", "tensor"),
            P("dp", "tensor"),
            P("dp", "tensor"),
            P("tensor", "dp"),
            P("dp", "tensor"),
            P("dp", "tensor"),
            P("tensor", "dp"),
            P("tensor"),
            P("tensor"),
            P(),
            P(),
        ),
        check_vma=False,
    )
```
